32 devices in a mesh: group: 2 (over x), seq: 16 (over z, y, core).
Axes of the slice: x: 2, y: 2, z: 4, core: 2. Of those that a mesh axis runs over, the one named last changes fastest.
Arguments:
- tokens: float32 [2, 16, 6, 96, 192], P('group', 'seq'), may hold values from -6 to 6
- cotangent: float32 [2, 16, 2, 6, 48, 384], P(None, 'seq', 'group'), may hold values from -6 to 6
- enc_params: float32 [2, 518784], P('group'), as said below
- enc_momentum: float32 [2, 518784], P('group', 'seq')
- enc_average: float32 [2, 518784], P('group', 'seq')
- fus_params: float32 [1774080], replicated, as said below
- fus_momentum: float32 [1774080], P(('group', 'seq'))
- fus_average: float32 [1774080], P(('group', 'seq'))
- earth_bias: float32 [8, 12, 3312], replicated, may hold values from -4 to 4
- bias_momentum: float32 [317952], P(('group', 'seq'))
- bias_average: float32 [317952], P(('group', 'seq')), may hold values from -4 to 4
Outputs:
- merged: float32 [2, 16, 2, 6, 48, 384], P(None, 'seq', 'group')
- tokens_grad: float32 [2, 16, 6, 96, 192], P('group', 'seq')
- enc_grad: float32 [2, 518784], P('group', 'seq')
- enc_new: float32 [2, 518784], P('group', 'seq')
- enc_momentum_new: float32 [2, 518784], P('group', 'seq')
- enc_average_new: float32 [2, 518784], P('group', 'seq')
- fus_grad: float32 [1774080], P(('group', 'seq'))
- fus_new: float32 [1774080], P(('group', 'seq'))
- fus_momentum_new: float32 [1774080], P(('group', 'seq'))
- fus_average_new: float32 [1774080], P(('group', 'seq'))
- bias_grad: float32 [317952], P(('group', 'seq'))
- bias_new: float32 [317952], P(('group', 'seq'))
- bias_momentum_new: float32 [317952], P(('group', 'seq'))
- bias_average_new: float32 [317952], P(('group', 'seq'))
The draws below stay inside these ranges and needn't reach their ends.
Inputs may be any that keep to these rules, and one draw needn't show every extreme that they name: `enc_params`: laid out as the first step states. `fus_params`: laid out as the first step states.
All inputs are finite; a program needn't handle non-finite values.
Results may differ from the reference program's by a relative error of at most 0.0003.
Values sent between devices are 32-bit elements; how exact they have to be, the bound alone decides.
A program may use at most 256 MiB of HBM per device.

```python
import math
from functools import partial
import jax
import jax.numpy as jnp
from jax import lax

CE = 192
CF = 384
HEADS_E = 6
HEADS_F = 12
MLP_E = 768
MLP_F = 1536
WIN_LAT = 6
WIN_LON = 12
WIN_MOD = 2
SAMPLES = 2
LON = 96
HALF_LON = 48
BANDS = 8
SLOTS = 16
LAT_E = 48
MODS = 2
HALVES = 2
REL = 3312
TABLE = 317952
ENC_RAW = 518784
ENC_P = 518784
FUS_RAW = 1774080
FUS_P = 1774080


def encoder_layout():
    return [(3 * CE * CE, 0.0, 1.2 / math.sqrt(CE)), (CE * CE, 0.0, 3.0 / math.sqrt(CE)), (CE * MLP_E, 0.0, 1.0 / math.sqrt(CE)), (MLP_E * CE, 0.0, 1.0 / math.sqrt(MLP_E)), (CE * CF, 0.0, 1.0 / math.sqrt(CE)), (CE, 1.0, 0.1), (CE, 0.0, 0.2), (CE, 0.0, 0.2), (CE, 0.0, 0.2), (CE, 0.0, 0.2), (CE, 1.0, 0.1), (CE, 0.0, 0.2), (MLP_E, 0.0, 0.2), (CE, 0.0, 0.2), (CF, 0.0, 0.2), (ENC_P - ENC_RAW, 0.0, 0.02)]


def merging_layout():
    return [(3 * CF * CF, 0.0, 1.2 / math.sqrt(CF)), (CF * CF, 0.0, 4.0 / math.sqrt(CF)), (CF * MLP_F, 0.0, 1.0 / math.sqrt(CF)), (MLP_F * CF, 0.0, 1.0 / math.sqrt(MLP_F)), (CF, 1.0, 0.1), (CF, 0.0, 0.2), (CF, 0.0, 0.2), (CF, 0.0, 0.2), (CF, 0.0, 0.2), (CF, 1.0, 0.1), (CF, 0.0, 0.2), (MLP_F, 0.0, 0.2), (CF, 0.0, 0.2), (FUS_P - FUS_RAW, 0.0, 0.02)]


def flat_draw(key, layout):
    pieces = []
    for number, entry in enumerate(layout):
        noise = jax.random.normal(jax.random.fold_in(key, number), (entry[0],), jnp.float32) * entry[2]
        pieces.append(noise + entry[1])
    return jnp.concatenate(pieces)


def draw_enc_params(key, part):
    base = jax.random.fold_in(key, 101)
    return jnp.stack([flat_draw(jax.random.fold_in(base, modality), encoder_layout()) for modality in range(MODS)])


def draw_enc_average(key, part):
    base = jax.random.fold_in(key, 102)
    return jnp.stack([flat_draw(jax.random.fold_in(base, modality), encoder_layout()) for modality in range(MODS)])


def draw_enc_momentum(key, part):
    scale = 0.055 * math.sqrt(SAMPLES * LAT_E * LON)
    return jax.random.normal(jax.random.fold_in(key, 103), (MODS, ENC_P), jnp.float32) * scale


def draw_fus_params(key, part):
    return flat_draw(jax.random.fold_in(key, 201), merging_layout())


def draw_fus_average(key, part):
    return flat_draw(jax.random.fold_in(key, 202), merging_layout())


def draw_fus_momentum(key, part):
    scale = 0.055 * math.sqrt(MODS * SAMPLES * LAT_E * LON)
    return jax.random.normal(jax.random.fold_in(key, 203), (FUS_P,), jnp.float32) * scale


def draw_bias_momentum(key, part):
    scale = 0.011 * math.sqrt(SAMPLES * LON / WIN_LON)
    return jax.random.normal(jax.random.fold_in(key, 301), (TABLE,), jnp.float32) * scale


def block_levels(stream_key, dims, split, low, high):
    gain = 1.0
    for axis_at, blocks in split:
        heights = jax.random.uniform(jax.random.fold_in(jax.random.fold_in(stream_key, 6), axis_at), (blocks,), jnp.float32, low / len(split), high / len(split))
        gain = gain * jnp.repeat(jnp.exp(heights), dims[axis_at] // blocks).reshape((-1,) + (1,) * (len(dims) - 1 - axis_at))
    return gain


def normal_values(own_key, extent, deviation, reach, cuts=(), kind=jnp.bfloat16):
    array = deviation * jax.random.normal(own_key, extent, jnp.float32)
    if cuts:
        array = array * block_levels(own_key, extent, cuts, -0.22, 0.18)
    return jnp.clip(array, -reach, reach).astype(kind)


def setup_inputs(seed: int = 0) -> dict:
    splits = jax.random.split(jax.random.key(seed), 12)
    tokens = normal_values(splits[0], (MODS, SLOTS, WIN_LAT, LON, CE), 1.0, 6.0, ((0, 2), (1, 16)), jnp.float32)
    cotangent = normal_values(splits[1], (MODS, SLOTS, HALVES, WIN_LAT, HALF_LON, CF), 1.0, 6.0, ((1, 16), (2, 2)), jnp.float32)
    enc_params = draw_enc_params(jax.random.fold_in(splits[11], 71), 0)
    enc_momentum = draw_enc_momentum(jax.random.fold_in(splits[11], 71), 0)
    enc_average = draw_enc_average(jax.random.fold_in(splits[11], 71), 0)
    fus_params = draw_fus_params(jax.random.fold_in(splits[11], 71), 0)
    fus_momentum = draw_fus_momentum(jax.random.fold_in(splits[11], 71), 0)
    fus_average = draw_fus_average(jax.random.fold_in(splits[11], 71), 0)
    earth_bias = normal_values(splits[8], (BANDS, HEADS_F, REL), 0.7, 4.0, (), jnp.float32)
    bias_momentum = draw_bias_momentum(jax.random.fold_in(splits[11], 71), 0)
    bias_average = normal_values(splits[10], (TABLE,), 0.7, 4.0, ((0, 32),), jnp.float32)
    return {"tokens": tokens, "cotangent": cotangent, "enc_params": enc_params, "enc_momentum": enc_momentum, "enc_average": enc_average, "fus_params": fus_params, "fus_momentum": fus_momentum, "fus_average": fus_average, "earth_bias": earth_bias, "bias_momentum": bias_momentum, "bias_average": bias_average}


@jax.custom_vjp
def low(v):
    return lax.optimization_barrier(v.astype(jnp.bfloat16)).astype(jnp.float32)

@jax.custom_vjp
def low_back(v):
    return v

def low_keep(v):
    return (low(v), None)

def low_pass(kept, grad):
    return (grad,)

def back_keep(v):
    return (v, None)

def back_low(kept, grad):
    return (low(grad),)
low.defvjp(low_keep, low_pass)
low_back.defvjp(back_keep, back_low)
precise = lax.Precision.HIGHEST
MOMENTUM_DECAY = 0.9
AVERAGE_DECAY = 0.99

def project(values, matrix):
    return jnp.dot(values, matrix, precision=precise, preferred_element_type=jnp.float32)

def unpack(flat_params, shapes):
    pieces = []
    offset = 0
    for one_shape in shapes:
        amount = math.prod(one_shape)
        pieces.append(flat_params[offset:offset + amount].reshape(one_shape))
        offset = offset + amount
    return pieces

def encoder_shapes():
    return [(CE, 3 * CE), (CE, CE), (CE, MLP_E), (MLP_E, CE), (CE, CF), (CE,), (CE,), (CE,), (CE,), (CE,), (CE,), (CE,), (MLP_E,), (CE,), (CF,)]

def merging_shapes():
    return [(CF, 3 * CF), (CF, CF), (CF, MLP_F), (MLP_F, CF), (CF,), (CF,), (CF,), (CF,), (CF,), (CF,), (CF,), (MLP_F,), (CF,)]

def layer_norm(values, gain_vec, shift_vec):
    center = values - lax.optimization_barrier(jnp.mean(values, -1, keepdims=True))
    spread = lax.optimization_barrier(jnp.mean(center * center, -1, keepdims=True))
    return center * lax.rsqrt(spread + 1e-05) * gain_vec + shift_vec

def attend(normed, in_weight, query_bias, value_bias, out_weight, out_bias, score_bias, allowed, head_count):
    win_count, length, feat_width = normed.shape
    head_size = feat_width // head_count
    packed = project(normed, in_weight)
    queries = (packed[..., :feat_width] + query_bias).reshape(win_count, length, head_count, head_size)
    key_vecs = packed[..., feat_width:2 * feat_width].reshape(win_count, length, head_count, head_size)
    value_vecs = (packed[..., 2 * feat_width:] + value_bias).reshape(win_count, length, head_count, head_size)
    scores = jnp.einsum('wqhd,wkhd->whqk', queries, key_vecs, precision=precise) / math.sqrt(head_size) + score_bias
    scores = jnp.where(allowed, scores, -1000000000.0)
    weights = jax.nn.softmax(scores, axis=-1)
    mixed_out = jnp.einsum('whqk,wkhd->wqhd', weights, value_vecs, precision=precise)
    return project(mixed_out.reshape(win_count, length, feat_width), out_weight) + out_bias

def to_windows(values):
    row_count, col_count, feat_width = values.shape
    shaped = values.reshape(row_count // WIN_LAT, WIN_LAT, col_count // WIN_LON, WIN_LON, feat_width)
    return shaped.transpose(0, 2, 1, 3, 4).reshape(-1, WIN_LAT * WIN_LON, feat_width)

def from_windows(windows, row_count, col_count):
    feat_width = windows.shape[-1]
    shaped = windows.reshape(row_count // WIN_LAT, col_count // WIN_LON, WIN_LAT, WIN_LON, feat_width)
    return shaped.transpose(0, 2, 1, 3, 4).reshape(row_count, col_count, feat_width)

def encoder_block(flat_params, shifted, region):
    parts = unpack(flat_params, encoder_shapes())
    in_weight, out_weight, up_weight, down_weight = (parts[0], parts[1], parts[2], parts[3])
    gain_one, shift_one, query_bias, value_bias, out_bias = (parts[5], parts[6], parts[7], parts[8], parts[9])
    gain_two, shift_two, up_bias, down_bias = (parts[10], parts[11], parts[12], parts[13])
    row_count, col_count, feat_width = shifted.shape
    windows = to_windows(layer_norm(shifted, gain_one, shift_one))
    labels = to_windows(jnp.broadcast_to(region[:, None, None], (row_count, col_count, 1)))[..., 0]
    allowed = labels[:, None, :, None] == labels[:, None, None, :]
    attention = jax.checkpoint(partial(attend, head_count=HEADS_E))
    mixed_out = attention(windows, in_weight, query_bias, value_bias, out_weight, out_bias, 0.0, allowed)
    hidden = shifted + from_windows(mixed_out, row_count, col_count)
    inner_act = jax.nn.gelu(project(layer_norm(hidden, gain_two, shift_two), up_weight) + up_bias, approximate=False)
    return hidden + project(inner_act, down_weight) + down_bias

def encoder_linear(flat_params, values):
    parts = unpack(flat_params, encoder_shapes())
    return project(values, parts[4]) + parts[14]

def earth_index():
    positions = jnp.arange(WIN_MOD * WIN_LAT * WIN_LON, dtype=jnp.int32)
    level = positions // (WIN_LAT * WIN_LON)
    lat_pos = positions // WIN_LON % WIN_LAT
    lon_pos = positions % WIN_LON
    pair_level = level[:, None] * WIN_MOD + level[None, :]
    pair_lat = lat_pos[:, None] * WIN_LAT + lat_pos[None, :]
    return (pair_level * (WIN_LAT * WIN_LAT) + pair_lat) * (2 * WIN_LON - 1) + lon_pos[:, None] - lon_pos[None, :] + WIN_LON - 1

def merging_block(flat_params, bias_table, fields):
    parts = unpack(flat_params, merging_shapes())
    in_weight, out_weight, up_weight, down_weight = (parts[0], parts[1], parts[2], parts[3])
    gain_one, shift_one, query_bias, value_bias, out_bias = (parts[4], parts[5], parts[6], parts[7], parts[8])
    gain_two, shift_two, up_bias, down_bias = (parts[9], parts[10], parts[11], parts[12])
    mod_count, row_count, col_count, feat_width = fields.shape
    normed = layer_norm(fields, gain_one, shift_one)
    shaped = normed.reshape(mod_count, row_count // WIN_LAT, WIN_LAT, col_count // WIN_LON, WIN_LON, feat_width)
    windows = shaped.transpose(1, 3, 0, 2, 4, 5).reshape(-1, mod_count * WIN_LAT * WIN_LON, feat_width)
    table_full = bias_table[:, :, earth_index()]
    score_bias = jnp.broadcast_to(table_full[:, None], (row_count // WIN_LAT, col_count // WIN_LON) + table_full.shape[1:])
    score_bias = score_bias.reshape((-1,) + table_full.shape[1:])
    allowed = jnp.ones((1, 1, 1, 1), dtype=bool)
    attention = jax.checkpoint(partial(attend, head_count=HEADS_F))
    mixed_out = attention(windows, in_weight, query_bias, value_bias, out_weight, out_bias, score_bias, allowed)
    mixed_out = mixed_out.reshape(row_count // WIN_LAT, col_count // WIN_LON, mod_count, WIN_LAT, WIN_LON, feat_width)
    hidden = fields + mixed_out.transpose(2, 0, 3, 1, 4, 5).reshape(mod_count, row_count, col_count, feat_width)
    inner_act = jax.nn.gelu(project(layer_norm(hidden, gain_two, shift_two), up_weight) + up_bias, approximate=False)
    return hidden + project(inner_act, down_weight) + down_bias

def encoder_band(flat_params, band, number):
    global_rows = number * WIN_LAT + jnp.arange(WIN_LAT, dtype=jnp.int32)
    region = (global_rows >= LAT_E - WIN_LAT // 2).astype(jnp.int32)
    return encoder_block(flat_params, band, region)

def encode(flat_params, field):
    shifted = jnp.roll(field, (-(WIN_LAT // 2), -(WIN_LON // 2)), axis=(0, 1))
    band_list = shifted.reshape(LAT_E // WIN_LAT, WIN_LAT, LON, CE)
    checked = jax.checkpoint(encoder_band)
    numbers = jnp.arange(LAT_E // WIN_LAT, dtype=jnp.int32)
    outputs = lax.map(lambda pair: checked(flat_params, pair[0], pair[1]), (band_list, numbers))
    encoded = jnp.roll(outputs.reshape(LAT_E, LON, CE), (WIN_LAT // 2, WIN_LON // 2), axis=(0, 1))
    return encoder_linear(flat_params, encoded)

def merge(flat_params, bias_table, fields):
    band_list = fields.reshape(MODS, LAT_E // WIN_LAT, WIN_LAT, LON, CF).transpose(1, 0, 2, 3, 4)
    checked = jax.checkpoint(merging_block)
    outputs = lax.map(lambda pair: checked(flat_params, pair[1][None], pair[0]), (band_list, bias_table))
    return outputs.transpose(1, 0, 2, 3, 4).reshape(MODS, LAT_E, LON, CF)

def update(params, grads, momentum, average, rate):
    momentum_new = MOMENTUM_DECAY * momentum + grads
    params_new = params - rate * (grads + MOMENTUM_DECAY * momentum_new)
    average_new = AVERAGE_DECAY * average + (1.0 - AVERAGE_DECAY) * params_new
    return (params_new, momentum_new, average_new)

def reference(tokens, cotangent, enc_params, enc_momentum, enc_average, fus_params, fus_momentum, fus_average, earth_bias, bias_momentum, bias_average):

    def forward(enc_all, fus_flat, table_all, fields):
        grids = fields.reshape(MODS, BANDS, SAMPLES, WIN_LAT, LON, CE).transpose(0, 2, 1, 3, 4, 5)
        grids = grids.reshape(MODS, SAMPLES, LAT_E, LON, CE)
        results = []
        for sample in range(SAMPLES):
            latent = jnp.stack([encode(enc_all[modality], grids[modality, sample]) for modality in range(MODS)])
            results.append(merge(fus_flat, table_all, latent))
        stacked = jnp.stack(results).reshape(SAMPLES, MODS, BANDS, WIN_LAT, HALVES, HALF_LON, CF)
        return stacked.transpose(1, 2, 0, 4, 3, 5, 6).reshape(MODS, SLOTS, HALVES, WIN_LAT, HALF_LON, CF)
    merged, backward = jax.vjp(forward, enc_params, fus_params, earth_bias, tokens)
    enc_grad, fus_grad, table_grad, tokens_grad = backward(cotangent)
    bias_grad = table_grad.reshape(-1)
    enc_new, enc_momentum_new, enc_average_new = update(enc_params, enc_grad, enc_momentum, enc_average, 1.0 / math.sqrt(CE * SAMPLES * LAT_E * LON))
    fus_new, fus_momentum_new, fus_average_new = update(fus_params, fus_grad, fus_momentum, fus_average, 1.0 / math.sqrt(CF * MODS * SAMPLES * LAT_E * LON))
    bias_new, bias_momentum_new, bias_average_new = update(earth_bias.reshape(-1), bias_grad, bias_momentum, bias_average, 2.0 / math.sqrt(SAMPLES * LON / WIN_LON))
    return (merged, tokens_grad, enc_grad, enc_new, enc_momentum_new, enc_average_new, fus_grad, fus_new, fus_momentum_new, fus_average_new, bias_grad, bias_new, bias_momentum_new, bias_average_new)
```

```python
from functools import partial
import math

import jax
import jax.numpy as jnp
import numpy as np
from jax import lax
from jax.experimental import pallas as pl
from jax.experimental.pallas import tpu as pltpu
from jax.sharding import PartitionSpec as P

CE = 192
CF = 384
HEADS_E = 6
HEADS_F = 12
MLP_E = 768
MLP_F = 1536
WIN_LAT = 6
WIN_LON = 12
WIN_MOD = 2
SAMPLES = 2
HEAD = 32
CHUNK = 256
LANES = 128
ROWS_E = WIN_LAT * WIN_LON
ROWS_F = WIN_MOD * ROWS_E
SPAN = 2 * WIN_LON - 1
PAIRS = WIN_MOD * WIN_LAT
TAB_PAD = 384
EPS = 1e-05
NEG = -1000000000.0
VMEM_BYTES = 60 << 20

MOMENTUM_DECAY = 0.9
AVERAGE_DECAY = 0.99

F32 = jnp.float32
BF16 = jnp.bfloat16

ENC_MATS = {"in": (CE, 3 * CE), "out": (CE, CE), "up": (CE, MLP_E), "down": (MLP_E, CE), "lin": (CE, CF)}
ENC_VECS = {"g1": CE, "s1": CE, "qb": CE, "vb": CE, "ob": CE, "g2": CE, "s2": CE, "ub": MLP_E, "db": CE, "lb": CF}
FUS_MATS = {"in": (CF, 3 * CF), "out": (CF, CF), "up": (CF, MLP_F), "down": (MLP_F, CF)}
FUS_VECS = {"g1": CF, "s1": CF, "qb": CF, "vb": CF, "ob": CF, "g2": CF, "s2": CF, "ub": MLP_F, "db": CF}


def offsets(mats, vecs):
    places, at = {}, 0
    for name, shape in mats.items():
        places[name] = at // LANES
        at += shape[0] * shape[1]
    for name, amount in vecs.items():
        places[name] = at
        at += amount
    return places


ENC_AT = offsets(ENC_MATS, ENC_VECS)
FUS_AT = offsets(FUS_MATS, FUS_VECS)


def split(v):
    hi = v.astype(BF16)
    return hi, (v - hi.astype(F32)).astype(BF16)


def dot(a, b, ca=1, cb=0):
    return lax.dot_general(a, b, (((ca,), (cb,)), ((), ())), preferred_element_type=F32)


def dot3(a, b, ca=1, cb=0):
    return dot(a[0], b[0], ca, cb) + (dot(a[0], b[1], ca, cb) + dot(a[1], b[0], ca, cb))


def put(refs, index, v):
    hi, lo = split(v)
    refs[0][index] = hi
    refs[1][index] = lo


def get(refs, index):
    return refs[0][index], refs[1][index]


def half_lanes():
    return lax.broadcasted_iota(jnp.int32, (1, LANES), 1) < LANES // 2


def turn(v):
    return pltpu.roll(v, LANES // 2, 1)


def vector(flat, at, amount):
    tiles = []
    for c in range(-(-amount // LANES)):
        row, lane = divmod(at + c * LANES, LANES)
        one = flat[row : row + 1, :]
        if lane:
            one = turn(one)
            if c * LANES + LANES // 2 < amount:
                one = jnp.where(half_lanes(), one, turn(flat[row + 1 : row + 2, :]))
        tiles.append(one)
    return jnp.concatenate(tiles, 1)[:, :amount] if len(tiles) > 1 else tiles[0][:, :amount]


def put_vector(flat, at, v):
    amount = v.shape[1]
    if at % LANES == 0 and amount % LANES == 0:
        for c in range(amount // LANES):
            flat[at // LANES + c : at // LANES + c + 1, :] = v[:, c * LANES : (c + 1) * LANES]
        return
    half = LANES // 2
    for c in range(amount // half):
        row, lane = divmod(at + c * half, LANES)
        flat[row : row + 1, lane : lane + half] = v[:, c * half : (c + 1) * half]


def unpack_matrix(flat, at, shape, store, scratch):
    rows, width = shape
    if width % LANES == 0:
        n = width // LANES
        for c in range(n):
            store(slice(0, rows), c, flat[pl.ds(at + c, rows, stride=n), :])
        return
    pairs, n, full = rows // 2, 2 * width // LANES, width // LANES
    low = half_lanes()
    for c in range(full + 1):
        scratch[c, pl.ds(0, pairs, stride=2), :] = flat[pl.ds(at + c, pairs, stride=n), :]
        odd = turn(flat[pl.ds(at + full + c, pairs, stride=n), :])
        if c < full:
            odd = jnp.where(low, odd, turn(flat[pl.ds(at + full + c + 1, pairs, stride=n), :]))
        scratch[c, pl.ds(1, pairs, stride=2), :] = odd
    for c in range(full + 1):
        store(slice(0, rows), c, scratch[c, 0:rows, :])


def pack_matrix(flat, at, shape, source):
    rows, width = shape
    pairs, n, full = rows // 2, 2 * width // LANES, width // LANES
    low = half_lanes()

    def tile(odd, c):
        return source[c, pl.ds(odd, pairs, stride=2), :]

    for c in range(full):
        flat[pl.ds(at + c, pairs, stride=n), :] = tile(0, c)
        flat[pl.ds(at + full + 1 + c, pairs, stride=n), :] = jnp.where(low, turn(tile(1, c)), turn(tile(1, c + 1)))
    flat[pl.ds(at + full, pairs, stride=n), :] = jnp.where(low, tile(0, full), turn(tile(1, 0)))


def put_tiles(ref, rows, v):
    for c in range(-(-v.shape[1] // LANES)):
        one = v[:, c * LANES : (c + 1) * LANES]
        ref[c, rows, 0 : one.shape[1]] = one


def get_tiles(ref, rows, width):
    tiles = [ref[c, rows, 0 : min(width - c * LANES, LANES)] for c in range(-(-width // LANES))]
    return jnp.concatenate(tiles, 1)


def normalize(x):
    center = x - jnp.mean(x, 1, keepdims=True)
    scale = lax.rsqrt(jnp.mean(center * center, 1, keepdims=True) + EPS)
    return center * scale, scale


def normalize_back(dv, xhat, scale, gain):
    dxhat = dv * gain
    return scale * (dxhat - jnp.mean(dxhat, 1, keepdims=True) - xhat * jnp.mean(dxhat * xhat, 1, keepdims=True))


def gelu_parts(u):
    phi = 0.5 * (1.0 + lax.erf(u * (1.0 / math.sqrt(2.0))))
    return u * phi, phi + u * jnp.exp(-0.5 * u * u) * (1.0 / math.sqrt(2.0 * math.pi))


def head_masks(width):
    lane = lax.broadcasted_iota(jnp.int32, (1, width), 1)
    return [jnp.where((lane >= h * HEAD) & (lane < (h + 1) * HEAD), 1.0, 0.0) for h in range(width // HEAD)]


def stacked(pair, masks):
    return tuple(jnp.concatenate([part * m.astype(BF16) for m in masks], 0) for part in pair)


def unstacked(v, masks):
    rows = v.shape[0] // len(masks)
    total = v[:rows] * masks[0]
    for h in range(1, len(masks)):
        total = total + v[h * rows : (h + 1) * rows] * masks[h]
    return total


def softmax(s):
    e = jnp.exp(s - jnp.max(s, 1, keepdims=True))
    return e / jnp.sum(e, 1, keepdims=True)


def wide_nt(a, b):
    return dot(jnp.concatenate(a, 1), jnp.concatenate([b[0], b[0]], 1), 1, 1) + dot(a[0], b[1], 1, 1)


def wide_n(a, b, ca=1):
    n = b[0].shape[1]
    both = dot(a[0], jnp.concatenate(b, 1), ca, 0)
    return both[:, :n] + (both[:, n:] + dot(a[1], b[0], ca, 0))


def column_sum(v):
    return jnp.sum(v, 0, keepdims=True)


def encoder_slots():
    for r in range(WIN_LAT):
        for n in range(8):
            start = n * WIN_LON + WIN_LON // 2
            at = n * ROWS_E + r * WIN_LON
            if n < 7:
                yield r, at, start, WIN_LON
            else:
                yield r, at, start, WIN_LON // 2
                yield r, at + WIN_LON // 2, 0, WIN_LON // 2


def merging_slots():
    for z in range(WIN_MOD):
        for r in range(WIN_LAT):
            for n in range(4):
                yield z, r, n * ROWS_F + (z * WIN_LAT + r) * WIN_LON, n * WIN_LON


def encoder_forward(
    wrap_ref, own_ref, head_ref, flat,
    lat_ref, xhat_ref, rstd_ref, qkv_ref, p_h, p_l, o_ref, xhat2_ref, rstd2_ref, g_h, g_l, dg_ref, out_ref,
    win_h, win_l, wout_h, wout_l, wup_h, wup_l, wdn_h, wdn_l, wlin_h, wlin_l,
    x, wide, lat,
):
    for pair, name in (((win_h, win_l), "in"), ((wout_h, wout_l), "out"), ((wup_h, wup_l), "up"), ((wdn_h, wdn_l), "down"), ((wlin_h, wlin_l), "lin")):
        width = ENC_MATS[name][1]

        def store(rows, c, v, pair=pair, width=width):
            last = min(width - c * LANES, LANES)
            put(pair, (rows, slice(c * LANES, c * LANES + last)), v[:, :last])

        unpack_matrix(flat, ENC_AT[name], ENC_MATS[name], store, wide)
    vec = {name: vector(flat, ENC_AT[name], amount) for name, amount in ENC_VECS.items()}
    masks = head_masks(CE)
    for r, at, start, amount in encoder_slots():
        src = own_ref if r < 3 else head_ref
        x[at : at + amount, :] = src[r % 3, start : start + amount, :]
    wrapped = wrap_ref[0] > 0
    half = ROWS_E // 2
    upper = lax.broadcasted_iota(jnp.int32, (ROWS_E, ROWS_E), 0) >= half
    right = lax.broadcasted_iota(jnp.int32, (ROWS_E, ROWS_E), 1) >= half
    apart = jnp.where(jnp.logical_and(upper != right, wrapped), 1.0, 0.0)
    apart = jnp.concatenate([apart] * HEADS_E, 0)
    win, wout, wup, wdn, wlin = (win_h, win_l), (wout_h, wout_l), (wup_h, wup_l), (wdn_h, wdn_l), (wlin_h, wlin_l)
    scale = 1.0 / math.sqrt(HEAD)

    def step(i, carry):
        rows = pl.ds(pl.multiple_of(i * 2 * ROWS_E, 2 * ROWS_E), 2 * ROWS_E)
        xv = x[rows, :]
        xhat, rstd = normalize(xv)
        xhat_ref[rows, :] = xhat
        rstd_ref[rows, :] = rstd
        xn = split(xhat * vec["g1"] + vec["s1"])
        full = slice(None)
        qkv = dot3(xn, get(win, (full, full)))
        shift = jnp.concatenate([vec["qb"], jnp.zeros_like(vec["qb"]), vec["vb"]], 1)
        factor = jnp.concatenate([jnp.full((1, CE), scale, F32), jnp.ones((1, 2 * CE), F32)], 1)
        qkv = (qkv + shift) * factor
        qkv_ref[rows, :] = qkv
        parts = []
        for w in range(2):
            one = qkv[w * ROWS_E : (w + 1) * ROWS_E]
            q, k, v = (one[:, j * CE : (j + 1) * CE] for j in range(3))
            qm = split(jnp.concatenate([q * m for m in masks], 0))
            s = dot3(qm, split(k), 1, 1)
            s = jnp.where(apart > 0.5, NEG, s)
            p = split(softmax(s))
            p_h[i * 2 + w] = p[0]
            p_l[i * 2 + w] = p[1]
            parts.append(unstacked(dot3(p, split(v)), masks))
        o = jnp.concatenate(parts, 0)
        o_ref[rows, :] = o
        hidden = xv + dot3(split(o), get(wout, (full, full))) + vec["ob"]
        xhat2, rstd2 = normalize(hidden)
        xhat2_ref[rows, :] = xhat2
        rstd2_ref[rows, :] = rstd2
        hn = split(xhat2 * vec["g2"] + vec["s2"])
        out = hidden + vec["db"]
        for c in range(MLP_E // CHUNK):
            cols = slice(c * CHUNK, (c + 1) * CHUNK)
            u = dot3(hn, get(wup, (full, cols))) + vec["ub"][:, cols]
            g, slope = gelu_parts(u)
            dg_ref[rows, cols] = slope
            g = split(g)
            g_h[rows, cols] = g[0]
            g_l[rows, cols] = g[1]
            out = out + dot3(g, get(wdn, (cols, full)))
        out_ref[rows, :] = out
        lat[rows, :] = dot3(split(out), get(wlin, (full, full))) + vec["lb"]
        return carry

    lax.fori_loop(0, 4, step, 0)
    for r, at, start, amount in encoder_slots():
        lat_ref[r, start : start + amount, :] = lat[at : at + amount, :]


def vmem(*shape, dtype=F32):
    return pltpu.VMEM(shape, dtype)


def pair_of(*shape):
    return [vmem(*shape, dtype=BF16)] * 2


def call(kernel, name, inputs, outs, scratch, smem=0, flops=0):
    specs = [pl.BlockSpec(memory_space=pltpu.SMEM)] * smem
    specs += [pl.BlockSpec(memory_space=pltpu.VMEM)] * (len(inputs) - smem)
    moved = sum(v.size * v.dtype.itemsize for v in list(inputs) + list(outs))
    return pl.pallas_call(
        kernel,
        name=name,
        out_shape=outs,
        in_specs=specs,
        out_specs=[pl.BlockSpec(memory_space=pltpu.VMEM)] * len(outs),
        scratch_shapes=scratch,
        cost_estimate=pl.CostEstimate(flops=flops, bytes_accessed=moved, transcendentals=0),
        compiler_params=pltpu.CompilerParams(vmem_limit_bytes=VMEM_BYTES),
    )(*inputs)


def shape(*dims, dtype=F32):
    return jax.ShapeDtypeStruct(dims, dtype)


def encoder_forward_call(wrap, own, head, flat):
    n = 8 * ROWS_E
    outs = [
        shape(WIN_LAT, 96, CF), shape(n, CE), shape(n, 1), shape(n, 3 * CE),
        shape(8, HEADS_E * ROWS_E, ROWS_E, dtype=BF16), shape(8, HEADS_E * ROWS_E, ROWS_E, dtype=BF16),
        shape(n, CE), shape(n, CE), shape(n, 1), shape(n, MLP_E, dtype=BF16), shape(n, MLP_E, dtype=BF16),
        shape(n, MLP_E), shape(n, CE),
    ]
    scratch = (
        pair_of(CE, 3 * CE) + pair_of(CE, CE) + pair_of(CE, MLP_E) + pair_of(MLP_E, CE) + pair_of(CE, CF)
        + [vmem(n, CE), vmem(5, MLP_E, LANES), vmem(n, CF)]
    )
    return call(encoder_forward, "encoder_forward", [wrap, own, head, flat], outs, scratch, 1, 6 * n * 516096)


def encoder_backward(
    dlat_ref, flat, xhat_ref, rstd_ref, qkv_ref, p_h, p_l, o_ref, xhat2_ref, rstd2_ref, g_h, g_l, dg_ref, out_ref,
    dfield_ref, grad,
    win_h, win_l, wout_h, wout_l, wup_h, wup_l, wdn_h, wdn_l, wlin_h, wlin_l,
    dlat, wide, dout, dout_h, dout_l, dhn, du_h, du_l, hn_h, hn_l, dh_h, dh_l, dqkv_h, dqkv_l, xn_h, xn_l, sums, dx,
):
    win, wout, wup, wdn, wlin = (win_h, win_l), (wout_h, wout_l), (wup_h, wup_l), (wdn_h, wdn_l), (wlin_h, wlin_l)
    for pair, name in ((win, "in"), (wout, "out"), (wup, "up"), (wdn, "down"), (wlin, "lin")):
        width = ENC_MATS[name][1]

        def store(rows, c, v, pair=pair, width=width):
            last = min(width - c * LANES, LANES)
            put(pair, (rows, slice(c * LANES, c * LANES + last)), v[:, :last])

        unpack_matrix(flat, ENC_AT[name], ENC_MATS[name], store, wide)
    vec = {name: vector(flat, ENC_AT[name], ENC_VECS[name]) for name in ("g1", "s1", "g2", "s2")}
    masks = head_masks(CE)
    full = slice(None)
    scale = 1.0 / math.sqrt(HEAD)
    for r, at, start, amount in encoder_slots():
        dlat[at : at + amount, :] = dlat_ref[r, start : start + amount, :]
    dl = split(dlat[...])
    put_vector(grad, ENC_AT["lb"], column_sum(dlat[...]))
    d = dot3(dl, get(wlin, (full, full)), 1, 1)
    dout[...] = d
    put((dout_h, dout_l), (full, full), d)
    put_vector(grad, ENC_AT["db"], column_sum(d))
    dw = dot3(split(out_ref[...]), dl, 0, 0)
    for c in range(3):
        grad[pl.ds(ENC_AT["lin"] + c, CE, stride=3), :] = dw[:, c * LANES : (c + 1) * LANES]
    xhat2 = xhat2_ref[...]
    put((hn_h, hn_l), (full, full), xhat2 * vec["g2"] + vec["s2"])
    for c in range(MLP_E // CHUNK):
        cols = slice(c * CHUNK, (c + 1) * CHUNK)
        do = (dout_h[...], dout_l[...])
        du = dot3(do, get(wdn, (cols, full)), 1, 1) * dg_ref[:, cols]
        put_vector(grad, ENC_AT["ub"] + c * CHUNK, column_sum(du))
        du = split(du)
        part = dot3(du, get(wup, (full, cols)), 1, 1)
        dhn[...] = part if c == 0 else dhn[...] + part
        dw = dot3((hn_h[...], hn_l[...]), du, 0, 0)
        for t in range(2):
            grad[pl.ds(ENC_AT["up"] + 2 * c + t, CE, stride=6), :] = dw[:, t * LANES : (t + 1) * LANES]
        dw = dot3((g_h[:, cols], g_l[:, cols]), do, 0, 0)
        put_tiles(wide, slice(c * CHUNK, (c + 1) * CHUNK), dw)
    pack_matrix(grad, ENC_AT["down"], ENC_MATS["down"], wide)
    dv = dhn[...]
    put_vector(grad, ENC_AT["g2"], column_sum(dv * xhat2))
    put_vector(grad, ENC_AT["s2"], column_sum(dv))
    d = dout[...] + normalize_back(dv, xhat2, rstd2_ref[...], vec["g2"])
    dout[...] = d
    put((dh_h, dh_l), (full, full), d)
    put_vector(grad, ENC_AT["ob"], column_sum(d))
    dw = dot3(split(o_ref[...]), (dh_h[...], dh_l[...]), 0, 0)
    put_tiles(wide, slice(0, CE), dw)
    pack_matrix(grad, ENC_AT["out"], ENC_MATS["out"], wide)
    sums[...] = jnp.zeros_like(sums)

    def step(i, carry):
        rows = pl.ds(pl.multiple_of(i * 2 * ROWS_E, 2 * ROWS_E), 2 * ROWS_E)
        do = dot3((dh_h[rows, :], dh_l[rows, :]), get(wout, (full, full)), 1, 1)
        parts = []
        for w in range(2):
            one = qkv_ref[pl.ds(pl.multiple_of(i * 2 * ROWS_E, 2 * ROWS_E) + w * ROWS_E, ROWS_E), :]
            q, k, v = (one[:, j * CE : (j + 1) * CE] for j in range(3))
            dow = do[w * ROWS_E : (w + 1) * ROWS_E]
            dom = split(jnp.concatenate([dow * m for m in masks], 0))
            qm = split(jnp.concatenate([q * m for m in masks], 0))
            p = (p_h[i * 2 + w], p_l[i * 2 + w])
            dp = dot3(dom, split(v), 1, 1)
            pf = p[0].astype(F32) + p[1].astype(F32)
            t = pf * dp
            ds = split(t - pf * jnp.sum(t, 1, keepdims=True))
            dq = unstacked(dot3(ds, split(k)), masks) * scale
            dk = dot3(ds, qm, 0, 0)
            dvv = dot3(p, dom, 0, 0)
            parts.append(jnp.concatenate([dq, dk, dvv], 1))
        dqkv = jnp.concatenate(parts, 0)
        sums[0:1, :] = sums[0:1, :] + column_sum(dqkv)
        dqkv = split(dqkv)
        dqkv_h[rows, :] = dqkv[0]
        dqkv_l[rows, :] = dqkv[1]
        xhat = xhat_ref[rows, :]
        put((xn_h, xn_l), (rows, full), xhat * vec["g1"] + vec["s1"])
        dxn = dot3(dqkv, get(win, (full, full)), 1, 1)
        sums[1:2, 0:CE] = sums[1:2, 0:CE] + column_sum(dxn * xhat)
        sums[2:3, 0:CE] = sums[2:3, 0:CE] + column_sum(dxn)
        dx[rows, :] = dout[rows, :] + normalize_back(dxn, xhat, rstd_ref[rows, :], vec["g1"])
        return carry

    lax.fori_loop(0, 4, step, 0)
    put_vector(grad, ENC_AT["qb"], sums[0:1, 0:CE])
    put_vector(grad, ENC_AT["vb"], sums[0:1, 2 * CE : 3 * CE])
    put_vector(grad, ENC_AT["g1"], sums[1:2, 0:CE])
    put_vector(grad, ENC_AT["s1"], sums[2:3, 0:CE])
    dw = dot3((xn_h[...], xn_l[...]), (dqkv_h[...], dqkv_l[...]), 0, 0)
    put_tiles(wide, slice(0, CE), dw)
    pack_matrix(grad, ENC_AT["in"], ENC_MATS["in"], wide)
    for r, at, start, amount in encoder_slots():
        dfield_ref[r, start : start + amount, :] = dx[at : at + amount, :]


def encoder_backward_call(dlat, flat, saved):
    n = 8 * ROWS_E
    scratch = (
        pair_of(CE, 3 * CE) + pair_of(CE, CE) + pair_of(CE, MLP_E) + pair_of(MLP_E, CE) + pair_of(CE, CF)
        + [vmem(n, CF), vmem(5, MLP_E, LANES), vmem(n, CE)] + pair_of(n, CE) + [vmem(n, CE)] + pair_of(n, CHUNK)
        + pair_of(n, CE) + pair_of(n, CE) + pair_of(n, 3 * CE) + pair_of(n, CE) + [vmem(8, 3 * CE), vmem(n, CE)]
    )
    return call(
        encoder_backward, "encoder_backward", [dlat, flat] + list(saved),
        [shape(WIN_LAT, 96, CE), shape(*flat.shape)], scratch, 0, 12 * n * 516096,
    )


def merging(
    fld_ref, cot_ref, flat, tab_ref, base_ref,
    out_ref, dx_ref, grad, dtab_ref,
    win_h, win_l, wout_h, wout_l, wup_h, wup_l, wdn_h, wdn_l,
    bias, dbias, x, xhat1, rstd1, xn_h, xn_l, q_h, q_l, k_h, k_l, v_h, v_l, p_h, p_l, o_h, o_l,
    xhat2, rstd2, hn_h, hn_l, acc, dhn, dy, dy_h, dy_l, g_h, g_l, du_h, du_l, dh_h, dh_l, dqkv_h, dqkv_l, sums,
):
    win, wout, wup, wdn = (win_h, win_l), (wout_h, wout_l), (wup_h, wup_l), (wdn_h, wdn_l)
    full = slice(None)
    chunks = MLP_F // CHUNK
    scale = 1.0 / math.sqrt(HEAD)

    def store(pair):
        def one(rows, c, v):
            put(pair, (rows, slice(c * LANES, (c + 1) * LANES)), v)
        return one

    def store_up(rows, c, v):
        put(wup, (c // 2, full, slice(c % 2 * LANES, (c % 2 + 1) * LANES)), v)

    def store_down(rows, c, v):
        for j in range(chunks):
            put(wdn, (j, full, slice(c * LANES, (c + 1) * LANES)), v[j * CHUNK : (j + 1) * CHUNK])

    unpack_matrix(flat, FUS_AT["in"], FUS_MATS["in"], store(win), None)
    unpack_matrix(flat, FUS_AT["out"], FUS_MATS["out"], store(wout), None)
    unpack_matrix(flat, FUS_AT["up"], FUS_MATS["up"], store_up, None)
    unpack_matrix(flat, FUS_AT["down"], FUS_MATS["down"], store_down, None)
    vec = {name: vector(flat, FUS_AT[name], amount) for name, amount in FUS_VECS.items()}
    masks = head_masks(LANES)

    spots = jnp.where(lax.broadcasted_iota(jnp.int32, (TAB_PAD, 2 * LANES), 0) == base_ref[...], 1.0, 0.0).astype(BF16)
    table = tab_ref[...]
    for w in range(WIN_LON):
        turned = pltpu.roll(table, TAB_PAD - w, 1) if w else table
        hi, lo = split(turned)
        rest = (turned - hi.astype(F32) - lo.astype(F32)).astype(BF16)
        one = dot(hi, spots) + (dot(lo, spots) + dot(rest, spots))
        for c in range(2):
            bias[c, pl.ds(w, ROWS_F, stride=WIN_LON), :] = one[:, c * LANES : (c + 1) * LANES]
    dbias[...] = jnp.zeros_like(dbias)

    for z, r, at, start in merging_slots():
        x[at : at + WIN_LON, :] = fld_ref[z, r, start : start + WIN_LON, :]
        dy[at : at + WIN_LON, :] = cot_ref[z, r, start : start + WIN_LON, :]

    def rows_of(i):
        return pl.ds(pl.multiple_of(i * ROWS_F, ROWS_F), ROWS_F)

    def forward(i, carry):
        rows = rows_of(i)
        xv = x[rows, :]
        xhat, rstd = normalize(xv)
        xhat1[rows, :] = xhat
        rstd1[rows, :] = rstd
        xn = split(xhat * vec["g1"] + vec["s1"])
        xn_h[rows, :] = xn[0]
        xn_l[rows, :] = xn[1]
        for j, (pair, shift) in enumerate((((q_h, q_l), vec["qb"]), ((k_h, k_l), None), ((v_h, v_l), vec["vb"]))):
            one = dot3(xn, get(win, (full, slice(j * CF, (j + 1) * CF))))
            if shift is not None:
                one = one + shift
            if j == 0:
                one = one * scale
            put(pair, (rows, full), one)
        for g in range(3):
            cols = slice(g * LANES, (g + 1) * LANES)
            qm = stacked((q_h[rows, cols], q_l[rows, cols]), masks)
            some = slice(g * 4 * ROWS_F, (g + 1) * 4 * ROWS_F)
            s = wide_nt(qm, (k_h[rows, cols], k_l[rows, cols])) + get_tiles(bias, some, ROWS_F)
            p = split(softmax(s))
            p_h[i * 3 + g] = p[0]
            p_l[i * 3 + g] = p[1]
            o = unstacked(wide_n(p, (v_h[rows, cols], v_l[rows, cols])), masks)
            put((o_h, o_l), (rows, cols), o)
        hidden = xv + dot3((o_h[rows, :], o_l[rows, :]), get(wout, (full, full))) + vec["ob"]
        xh2, rstd = normalize(hidden)
        xhat2[rows, :] = xh2
        rstd2[rows, :] = rstd
        put((hn_h, hn_l), (rows, full), xh2 * vec["g2"] + vec["s2"])
        acc[rows, :] = hidden + vec["db"]
        put((dy_h, dy_l), (rows, full), dy[rows, :])
        return carry

    lax.fori_loop(0, 4, forward, 0)
    dhn[...] = jnp.zeros_like(dhn)
    for c in range(chunks):
        sums[8:9, c * CHUNK : (c + 1) * CHUNK] = vec["ub"][:, c * CHUNK : (c + 1) * CHUNK]

    def feed(c, carry):
        up = (wup_h[c], wup_l[c])
        down = (wdn_h[c], wdn_l[c])
        cols = pl.ds(pl.multiple_of(c * CHUNK, CHUNK), CHUNK)
        shift = sums[8:9, cols]

        def part(i, total):
            rows = rows_of(i)
            u = dot3((hn_h[rows, :], hn_l[rows, :]), up) + shift
            g, slope = gelu_parts(u)
            g = split(g)
            g_h[rows, :] = g[0]
            g_l[rows, :] = g[1]
            acc[rows, :] = acc[rows, :] + dot3(g, down)
            du = dot3((dy_h[rows, :], dy_l[rows, :]), down, 1, 1) * slope
            total = total + column_sum(du)
            du = split(du)
            du_h[rows, :] = du[0]
            du_l[rows, :] = du[1]
            dhn[rows, :] = dhn[rows, :] + dot3(du, up, 1, 1)
            return total

        sums[9:10, cols] = lax.fori_loop(0, 4, part, jnp.zeros((1, CHUNK), F32))
        dw = dot3((hn_h[...], hn_l[...]), (du_h[...], du_l[...]), 0, 0)
        for t in range(2):
            grad[pl.ds(FUS_AT["up"] + 2 * c + t, CF, stride=12), :] = dw[:, t * LANES : (t + 1) * LANES]
        dw = dot3((g_h[...], g_l[...]), (dy_h[...], dy_l[...]), 0, 0)
        for t in range(3):
            grad[pl.ds(FUS_AT["down"] + 3 * CHUNK * c + t, CHUNK, stride=3), :] = dw[:, t * LANES : (t + 1) * LANES]
        return carry

    lax.fori_loop(0, chunks, feed, 0)
    put_vector(grad, FUS_AT["ub"], sums[9:10, :])
    sums[0:8, :] = jnp.zeros((8, MLP_F), F32)

    def backward(i, carry):
        rows = rows_of(i)
        dv = dhn[rows, :]
        xh2 = xhat2[rows, :]
        d = dy[rows, :]
        sums[0:1, 0:CF] = sums[0:1, 0:CF] + column_sum(d)
        sums[1:2, 0:CF] = sums[1:2, 0:CF] + column_sum(dv * xh2)
        sums[2:3, 0:CF] = sums[2:3, 0:CF] + column_sum(dv)
        dh = d + normalize_back(dv, xh2, rstd2[rows, :], vec["g2"])
        sums[3:4, 0:CF] = sums[3:4, 0:CF] + column_sum(dh)
        dhs = split(dh)
        dh_h[rows, :] = dhs[0]
        dh_l[rows, :] = dhs[1]
        do = split(dot3(dhs, get(wout, (full, full)), 1, 1))
        for g in range(3):
            cols = slice(g * LANES, (g + 1) * LANES)
            dom = stacked((do[0][:, cols], do[1][:, cols]), masks)
            qm = stacked((q_h[rows, cols], q_l[rows, cols]), masks)
            p = (p_h[i * 3 + g], p_l[i * 3 + g])
            dp = wide_nt(dom, (v_h[rows, cols], v_l[rows, cols]))
            pf = p[0].astype(F32) + p[1].astype(F32)
            t = pf * dp
            ds = t - pf * jnp.sum(t, 1, keepdims=True)
            some = slice(g * 4 * ROWS_F, (g + 1) * 4 * ROWS_F)
            for c in range(2):
                one = ds[:, c * LANES : (c + 1) * LANES]
                dbias[c, some, 0 : one.shape[1]] = dbias[c, some, 0 : one.shape[1]] + one
            ds = split(ds)
            dq = unstacked(wide_n(ds, (k_h[rows, cols], k_l[rows, cols])), masks) * scale
            dk = wide_n(ds, qm, 0)
            dvv = wide_n(p, dom, 0)
            for j, one in enumerate((dq, dk, dvv)):
                at = slice(j * CF + g * LANES, j * CF + (g + 1) * LANES)
                put((dqkv_h, dqkv_l), (rows, at), one)
                if j != 1:
                    sums[4 + j // 2 : 5 + j // 2, cols] = sums[4 + j // 2 : 5 + j // 2, cols] + column_sum(one)
        xhat = xhat1[rows, :]
        dxn = dot3((dqkv_h[rows, :], dqkv_l[rows, :]), get(win, (full, full)), 1, 1)
        sums[6:7, 0:CF] = sums[6:7, 0:CF] + column_sum(dxn * xhat)
        sums[7:8, 0:CF] = sums[7:8, 0:CF] + column_sum(dxn)
        x[rows, :] = dh + normalize_back(dxn, xhat, rstd1[rows, :], vec["g1"])
        return carry

    lax.fori_loop(0, 4, backward, 0)
    for j, name in enumerate(("db", "g2", "s2", "ob", "qb", "vb", "g1", "s1")):
        put_vector(grad, FUS_AT[name], sums[j : j + 1, 0:CF])
    for c in range(3):
        cols = slice(c * CF, (c + 1) * CF)
        dw = dot3((xn_h[...], xn_l[...]), (dqkv_h[:, cols], dqkv_l[:, cols]), 0, 0)
        for t in range(3):
            grad[pl.ds(FUS_AT["in"] + 3 * c + t, CF, stride=9), :] = dw[:, t * LANES : (t + 1) * LANES]
    dw = dot3((o_h[...], o_l[...]), (dh_h[...], dh_l[...]), 0, 0)
    for t in range(3):
        grad[pl.ds(FUS_AT["out"] + t, CF, stride=3), :] = dw[:, t * LANES : (t + 1) * LANES]
    total = jnp.zeros((ROWS_F, TAB_PAD), F32)
    for w in range(WIN_LON):
        turned = jnp.concatenate([dbias[c, pl.ds(w, ROWS_F, stride=WIN_LON), :] for c in range(2)], 1)
        hi, lo = split(turned)
        one = dot(hi, spots, 1, 1) + dot(lo, spots, 1, 1)
        total = total + (pltpu.roll(one, w, 1) if w else one)
    dtab_ref[...] = total
    for z, r, at, start in merging_slots():
        out_ref[z, r, start : start + WIN_LON, :] = acc[at : at + WIN_LON, :]
        dx_ref[z, r, start : start + WIN_LON, :] = x[at : at + WIN_LON, :]


def merging_call(fields, cotangent, flat, table):
    n = 4 * ROWS_F
    m = HEADS_F * ROWS_F
    t = np.arange(ROWS_F)
    base = np.full((1, 2 * LANES), -1, np.int32)
    base[0, :ROWS_F] = t // WIN_LON * SPAN + WIN_LON - 1 - t % WIN_LON
    base = jnp.asarray(base)
    scratch = (
        pair_of(CF, 3 * CF) + pair_of(CF, CF) + pair_of(6, CF, CHUNK) + pair_of(6, CHUNK, CF)
        + [vmem(2, m, LANES), vmem(2, m, LANES), vmem(n, CF), vmem(n, CF), vmem(n, 1)]
        + pair_of(n, CF) + pair_of(n, CF) + pair_of(n, CF) + pair_of(n, CF) + pair_of(12, 4 * ROWS_F, ROWS_F) + pair_of(n, CF)
        + [vmem(n, CF), vmem(n, 1)] + pair_of(n, CF) + [vmem(n, CF), vmem(n, CF), vmem(n, CF)] + pair_of(n, CF)
        + pair_of(n, CHUNK) + pair_of(n, CHUNK) + pair_of(n, CF) + pair_of(n, 3 * CF) + [vmem(16, MLP_F)]
    )
    outs = [shape(*fields.shape), shape(*fields.shape), shape(*flat.shape), shape(ROWS_F, TAB_PAD)]
    return call(merging, "merging", [fields, cotangent, flat, table, base], outs, scratch, 0, 18 * n * 1769472)


def passed_along(block, axis, distance):
    devices = range(lax.axis_size(axis))
    route = [((i - distance) % len(devices), i) for i in devices]
    return lax.ppermute(block, axis, route)


def update(params, grads, momentum, average, rate):
    momentum_new = MOMENTUM_DECAY * momentum + grads
    params_new = params - rate * (grads + MOMENTUM_DECAY * momentum_new)
    average_new = AVERAGE_DECAY * average + (1.0 - AVERAGE_DECAY) * params_new
    return (params_new, momentum_new, average_new)


def table_rows(one):
    heads = one.shape[0]
    one = one.reshape(heads, WIN_MOD, WIN_MOD, WIN_LAT, WIN_LAT * SPAN).transpose(0, 1, 3, 2, 4)
    return one.reshape(heads * PAIRS, PAIRS * SPAN)


def table_back(rows):
    heads = rows.shape[0] // PAIRS
    one = rows.reshape(heads, WIN_MOD, WIN_LAT, WIN_MOD, WIN_LAT * SPAN).transpose(0, 1, 3, 2, 4)
    return one.reshape(heads, -1)


def shards(
    tokens,
    cotangent,
    enc_params,
    enc_momentum,
    enc_average,
    fus_params,
    fus_momentum,
    fus_average,
    earth_bias,
    bias_momentum,
    bias_average,
):
    field = tokens[0, 0]
    row_count, col_count, feat_width = field.shape
    half_rows = WIN_LAT // 2
    seq_count = lax.axis_size("seq")
    group_count = lax.axis_size("group")
    band_count = seq_count // SAMPLES
    place = lax.axis_index("seq")
    mine = lax.axis_index("group")
    band = place // SAMPLES
    enc_flat = enc_params[0].reshape(-1, LANES)
    fus_flat = fus_params.reshape(-1, LANES)
    head_rows = passed_along(field[:half_rows], "seq", -SAMPLES)
    wrap = (band == band_count - 1).astype(jnp.int32).reshape(1)
    latent, *saved = encoder_forward_call(wrap, field[half_rows:], head_rows, enc_flat)
    tail_rows = passed_along(latent[-half_rows:], "seq", SAMPLES)
    encoded = jnp.concatenate([tail_rows, latent[:-half_rows]], 0)
    fields = lax.all_to_all(
        encoded.reshape(row_count, group_count, -1, CF)[None],
        "group",
        split_axis=2,
        concat_axis=0,
        tiled=True,
    )[:, :, 0]
    table = lax.dynamic_slice_in_dim(earth_bias, band, 1, 0)[0]
    table = jnp.pad(table_rows(table), ((0, 0), (0, TAB_PAD - PAIRS * SPAN)))
    merged, fields_grad, fus_local, table_grad = merging_call(fields, cotangent[:, 0, 0], fus_flat, table)
    table_grad = table_back(table_grad[:, : PAIRS * SPAN])[None]
    latent_grad = lax.all_to_all(
        fields_grad[:, :, None], "group", split_axis=0, concat_axis=2, tiled=True
    )[0].reshape(row_count, col_count, CF)
    lower_rows = passed_along(latent_grad[:half_rows], "seq", -SAMPLES)
    block_grad = jnp.concatenate([latent_grad[half_rows:], lower_rows], 0)
    before_grad, enc_local = encoder_backward_call(block_grad, enc_flat, saved)
    upper_rows = passed_along(before_grad[-half_rows:], "seq", SAMPLES)
    field_grad = jnp.concatenate([upper_rows, before_grad[:-half_rows]], 0)
    enc_grad = lax.psum_scatter(enc_local.reshape(-1), "seq", scatter_dimension=0, tiled=True)
    enc_piece = enc_grad.shape[0]
    enc_own = lax.dynamic_slice_in_dim(enc_params[0], place * enc_piece, enc_piece)
    bias_term = jnp.zeros(earth_bias.shape, F32)
    bias_term = lax.dynamic_update_slice_in_dim(bias_term, table_grad, band, 0).reshape(-1)
    fus_grad, bias_grad = (
        lax.psum_scatter(fus_local.reshape(-1), ("group", "seq"), scatter_dimension=0, tiled=True),
        lax.psum_scatter(bias_term, ("group", "seq"), scatter_dimension=0, tiled=True),
    )
    slot = mine * seq_count + place
    fus_piece = fus_grad.shape[0]
    fus_own = lax.dynamic_slice_in_dim(fus_params, slot * fus_piece, fus_piece)
    bias_piece = bias_grad.shape[0]
    bias_own = lax.dynamic_slice_in_dim(earth_bias.reshape(-1), slot * bias_piece, bias_piece)
    lat_total = band_count * row_count
    enc_new, enc_momentum_new, enc_average_new = update(
        enc_own,
        enc_grad,
        enc_momentum[0],
        enc_average[0],
        1.0 / math.sqrt(CE * SAMPLES * lat_total * col_count),
    )
    fus_new, fus_momentum_new, fus_average_new = update(
        fus_own,
        fus_grad,
        fus_momentum,
        fus_average,
        1.0 / math.sqrt(CF * group_count * SAMPLES * lat_total * col_count),
    )
    bias_new, bias_momentum_new, bias_average_new = update(
        bias_own,
        bias_grad,
        bias_momentum,
        bias_average,
        2.0 / math.sqrt(SAMPLES * col_count / WIN_LON),
    )
    return (
        merged[:, None, None],
        field_grad[None, None],
        enc_grad[None],
        enc_new[None],
        enc_momentum_new[None],
        enc_average_new[None],
        fus_grad,
        fus_new,
        fus_momentum_new,
        fus_average_new,
        bias_grad,
        bias_new,
        bias_momentum_new,
        bias_average_new,
    )


def solution(mesh):
    both = P(("group", "seq"))
    rows = P("group", "seq")
    merged = P(None, "seq", "group", None, None, None)
    tokens = P("group", "seq", None, None, None)
    return jax.shard_map(
        shards,
        mesh=mesh,
        in_specs=(tokens, merged, P("group", None), rows, rows, P(), both, both, P(), both, both),
        out_specs=(merged, tokens, rows, rows, rows, rows) + (both,) * 8,
        check_vma=False,
    )
```

```python
from functools import partial
import math

import jax
import jax.numpy as jnp
import numpy as np
from jax import lax
from jax.experimental import pallas as pl
from jax.experimental.pallas import tpu as pltpu
from jax.sharding import PartitionSpec as P

CE = 192
CF = 384
HEADS_E = 6
HEADS_F = 12
MLP_E = 768
MLP_F = 1536
WIN_LAT = 6
WIN_LON = 12
WIN_MOD = 2
SAMPLES = 2
HEAD = 32
CHUNK = 256
LANES = 128
ROWS_E = WIN_LAT * WIN_LON
ROWS_F = WIN_MOD * ROWS_E
SPAN = 2 * WIN_LON - 1
PAIRS = WIN_MOD * WIN_LAT
TAB_PAD = 384
EPS = 1e-05
NEG = -1000000000.0
VMEM_BYTES = 60 << 20

MOMENTUM_DECAY = 0.9
AVERAGE_DECAY = 0.99

F32 = jnp.float32
BF16 = jnp.bfloat16

ENC_MATS = {"in": (CE, 3 * CE), "out": (CE, CE), "up": (CE, MLP_E), "down": (MLP_E, CE), "lin": (CE, CF)}
ENC_VECS = {"g1": CE, "s1": CE, "qb": CE, "vb": CE, "ob": CE, "g2": CE, "s2": CE, "ub": MLP_E, "db": CE, "lb": CF}
FUS_MATS = {"in": (CF, 3 * CF), "out": (CF, CF), "up": (CF, MLP_F), "down": (MLP_F, CF)}
FUS_VECS = {"g1": CF, "s1": CF, "qb": CF, "vb": CF, "ob": CF, "g2": CF, "s2": CF, "ub": MLP_F, "db": CF}


def offsets(mats, vecs):
    places, at = {}, 0
    for name, shape in mats.items():
        places[name] = at // LANES
        at += shape[0] * shape[1]
    for name, amount in vecs.items():
        places[name] = at
        at += amount
    return places


ENC_AT = offsets(ENC_MATS, ENC_VECS)
FUS_AT = offsets(FUS_MATS, FUS_VECS)


def split(v):
    hi = v.astype(BF16)
    return hi, (v - hi.astype(F32)).astype(BF16)


def dot(a, b, ca=1, cb=0):
    return lax.dot_general(a, b, (((ca,), (cb,)), ((), ())), preferred_element_type=F32)


def dot3(a, b, ca=1, cb=0):
    return dot(a[0], b[0], ca, cb) + (dot(a[0], b[1], ca, cb) + dot(a[1], b[0], ca, cb))


def put(refs, index, v):
    hi, lo = split(v)
    refs[0][index] = hi
    refs[1][index] = lo


def get(refs, index):
    return refs[0][index], refs[1][index]


def half_lanes():
    return lax.broadcasted_iota(jnp.int32, (1, LANES), 1) < LANES // 2


def turn(v):
    return pltpu.roll(v, LANES // 2, 1)


def vector(flat, at, amount):
    tiles = []
    for c in range(-(-amount // LANES)):
        row, lane = divmod(at + c * LANES, LANES)
        one = flat[row : row + 1, :]
        if lane:
            one = turn(one)
            if c * LANES + LANES // 2 < amount:
                one = jnp.where(half_lanes(), one, turn(flat[row + 1 : row + 2, :]))
        tiles.append(one)
    return jnp.concatenate(tiles, 1)[:, :amount] if len(tiles) > 1 else tiles[0][:, :amount]


def put_vector(flat, at, v):
    amount = v.shape[1]
    if at % LANES == 0 and amount % LANES == 0:
        for c in range(amount // LANES):
            flat[at // LANES + c : at // LANES + c + 1, :] = v[:, c * LANES : (c + 1) * LANES]
        return
    half = LANES // 2
    for c in range(amount // half):
        row, lane = divmod(at + c * half, LANES)
        flat[row : row + 1, lane : lane + half] = v[:, c * half : (c + 1) * half]


def unpack_matrix(flat, at, shape, store, scratch):
    rows, width = shape
    if width % LANES == 0:
        n = width // LANES
        for c in range(n):
            store(slice(0, rows), c, flat[pl.ds(at + c, rows, stride=n), :])
        return
    pairs, n, full = rows // 2, 2 * width // LANES, width // LANES
    low = half_lanes()
    for c in range(full + 1):
        scratch[c, pl.ds(0, pairs, stride=2), :] = flat[pl.ds(at + c, pairs, stride=n), :]
        odd = turn(flat[pl.ds(at + full + c, pairs, stride=n), :])
        if c < full:
            odd = jnp.where(low, odd, turn(flat[pl.ds(at + full + c + 1, pairs, stride=n), :]))
        scratch[c, pl.ds(1, pairs, stride=2), :] = odd
    for c in range(full + 1):
        store(slice(0, rows), c, scratch[c, 0:rows, :])


def pack_matrix(flat, at, shape, source):
    rows, width = shape
    pairs, n, full = rows // 2, 2 * width // LANES, width // LANES
    low = half_lanes()

    def tile(odd, c):
        return source[c, pl.ds(odd, pairs, stride=2), :]

    for c in range(full):
        flat[pl.ds(at + c, pairs, stride=n), :] = tile(0, c)
        flat[pl.ds(at + full + 1 + c, pairs, stride=n), :] = jnp.where(low, turn(tile(1, c)), turn(tile(1, c + 1)))
    flat[pl.ds(at + full, pairs, stride=n), :] = jnp.where(low, tile(0, full), turn(tile(1, 0)))


def put_tiles(ref, rows, v):
    for c in range(-(-v.shape[1] // LANES)):
        one = v[:, c * LANES : (c + 1) * LANES]
        ref[c, rows, 0 : one.shape[1]] = one


def get_tiles(ref, rows, width):
    tiles = [ref[c, rows, 0 : min(width - c * LANES, LANES)] for c in range(-(-width // LANES))]
    return jnp.concatenate(tiles, 1)


def normalize(x):
    center = x - jnp.mean(x, 1, keepdims=True)
    scale = lax.rsqrt(jnp.mean(center * center, 1, keepdims=True) + EPS)
    return center * scale, scale


def normalize_back(dv, xhat, scale, gain):
    dxhat = dv * gain
    return scale * (dxhat - jnp.mean(dxhat, 1, keepdims=True) - xhat * jnp.mean(dxhat * xhat, 1, keepdims=True))


def gelu_parts(u):
    phi = 0.5 * (1.0 + lax.erf(u * (1.0 / math.sqrt(2.0))))
    return u * phi, phi + u * jnp.exp(-0.5 * u * u) * (1.0 / math.sqrt(2.0 * math.pi))


def head_masks(width):
    lane = lax.broadcasted_iota(jnp.int32, (1, width), 1)
    return [jnp.where((lane >= h * HEAD) & (lane < (h + 1) * HEAD), 1.0, 0.0) for h in range(width // HEAD)]


def stacked(pair, masks):
    return tuple(jnp.concatenate([part * m.astype(BF16) for m in masks], 0) for part in pair)


def unstacked(v, masks):
    rows = v.shape[0] // len(masks)
    total = v[:rows] * masks[0]
    for h in range(1, len(masks)):
        total = total + v[h * rows : (h + 1) * rows] * masks[h]
    return total


def softmax(s):
    e = jnp.exp(s - jnp.max(s, 1, keepdims=True))
    return e / jnp.sum(e, 1, keepdims=True)


def wide_nt(a, b):
    return dot(jnp.concatenate(a, 1), jnp.concatenate([b[0], b[0]], 1), 1, 1) + dot(a[0], b[1], 1, 1)


def wide_n(a, b, ca=1):
    n = b[0].shape[1]
    both = dot(a[0], jnp.concatenate(b, 1), ca, 0)
    return both[:, :n] + (both[:, n:] + dot(a[1], b[0], ca, 0))


def column_sum(v):
    return jnp.sum(v, 0, keepdims=True)


def encoder_slots():
    for r in range(WIN_LAT):
        for n in range(8):
            start = n * WIN_LON + WIN_LON // 2
            at = n * ROWS_E + r * WIN_LON
            if n < 7:
                yield r, at, start, WIN_LON
            else:
                yield r, at, start, WIN_LON // 2
                yield r, at + WIN_LON // 2, 0, WIN_LON // 2


def merging_slots():
    for z in range(WIN_MOD):
        for r in range(WIN_LAT):
            for n in range(4):
                yield z, r, n * ROWS_F + (z * WIN_LAT + r) * WIN_LON, n * WIN_LON


def encoder_forward(
    wrap_ref, own_ref, head_ref, flat,
    lat_ref, xhat_ref, rstd_ref, qkv_ref, p_h, p_l, o_ref, xhat2_ref, rstd2_ref, g_h, g_l, dg_ref, out_ref,
    win_h, win_l, wout_h, wout_l, wup_h, wup_l, wdn_h, wdn_l, wlin_h, wlin_l,
    x, wide, lat,
):
    for pair, name in (((win_h, win_l), "in"), ((wout_h, wout_l), "out"), ((wup_h, wup_l), "up"), ((wdn_h, wdn_l), "down"), ((wlin_h, wlin_l), "lin")):
        width = ENC_MATS[name][1]

        def store(rows, c, v, pair=pair, width=width):
            last = min(width - c * LANES, LANES)
            put(pair, (rows, slice(c * LANES, c * LANES + last)), v[:, :last])

        unpack_matrix(flat, ENC_AT[name], ENC_MATS[name], store, wide)
    vec = {name: vector(flat, ENC_AT[name], amount) for name, amount in ENC_VECS.items()}
    masks = head_masks(CE)
    for r, at, start, amount in encoder_slots():
        src = own_ref if r < 3 else head_ref
        x[at : at + amount, :] = src[r % 3, start : start + amount, :]
    wrapped = wrap_ref[0] > 0
    half = ROWS_E // 2
    upper = lax.broadcasted_iota(jnp.int32, (ROWS_E, ROWS_E), 0) >= half
    right = lax.broadcasted_iota(jnp.int32, (ROWS_E, ROWS_E), 1) >= half
    apart = jnp.where(jnp.logical_and(upper != right, wrapped), 1.0, 0.0)
    apart = jnp.concatenate([apart] * HEADS_E, 0)
    win, wout, wup, wdn, wlin = (win_h, win_l), (wout_h, wout_l), (wup_h, wup_l), (wdn_h, wdn_l), (wlin_h, wlin_l)
    scale = 1.0 / math.sqrt(HEAD)

    def step(i, carry):
        rows = pl.ds(pl.multiple_of(i * 2 * ROWS_E, 2 * ROWS_E), 2 * ROWS_E)
        xv = x[rows, :]
        xhat, rstd = normalize(xv)
        xhat_ref[rows, :] = xhat
        rstd_ref[rows, :] = rstd
        xn = split(xhat * vec["g1"] + vec["s1"])
        full = slice(None)
        qkv = dot3(xn, get(win, (full, full)))
        shift = jnp.concatenate([vec["qb"], jnp.zeros_like(vec["qb"]), vec["vb"]], 1)
        factor = jnp.concatenate([jnp.full((1, CE), scale, F32), jnp.ones((1, 2 * CE), F32)], 1)
        qkv = (qkv + shift) * factor
        qkv_ref[rows, :] = qkv
        parts = []
        for w in range(2):
            one = qkv[w * ROWS_E : (w + 1) * ROWS_E]
            q, k, v = (one[:, j * CE : (j + 1) * CE] for j in range(3))
            qm = split(jnp.concatenate([q * m for m in masks], 0))
            s = dot3(qm, split(k), 1, 1)
            s = jnp.where(apart > 0.5, NEG, s)
            p = split(softmax(s))
            p_h[i * 2 + w] = p[0]
            p_l[i * 2 + w] = p[1]
            parts.append(unstacked(dot3(p, split(v)), masks))
        o = jnp.concatenate(parts, 0)
        o_ref[rows, :] = o
        hidden = xv + dot3(split(o), get(wout, (full, full))) + vec["ob"]
        xhat2, rstd2 = normalize(hidden)
        xhat2_ref[rows, :] = xhat2
        rstd2_ref[rows, :] = rstd2
        hn = split(xhat2 * vec["g2"] + vec["s2"])
        out = hidden + vec["db"]
        for c in range(MLP_E // CHUNK):
            cols = slice(c * CHUNK, (c + 1) * CHUNK)
            u = dot3(hn, get(wup, (full, cols))) + vec["ub"][:, cols]
            g, slope = gelu_parts(u)
            dg_ref[rows, cols] = slope
            g = split(g)
            g_h[rows, cols] = g[0]
            g_l[rows, cols] = g[1]
            out = out + dot3(g, get(wdn, (cols, full)))
        out_ref[rows, :] = out
        lat[rows, :] = dot3(split(out), get(wlin, (full, full))) + vec["lb"]
        return carry

    lax.fori_loop(0, 4, step, 0)
    for r, at, start, amount in encoder_slots():
        lat_ref[r, start : start + amount, :] = lat[at : at + amount, :]


def vmem(*shape, dtype=F32):
    return pltpu.VMEM(shape, dtype)


def pair_of(*shape):
    return [vmem(*shape, dtype=BF16)] * 2


def call(kernel, name, inputs, outs, scratch, smem=0, flops=0):
    specs = [pl.BlockSpec(memory_space=pltpu.SMEM)] * smem
    specs += [pl.BlockSpec(memory_space=pltpu.VMEM)] * (len(inputs) - smem)
    moved = sum(v.size * v.dtype.itemsize for v in list(inputs) + list(outs))
    return pl.pallas_call(
        kernel,
        name=name,
        out_shape=outs,
        in_specs=specs,
        out_specs=[pl.BlockSpec(memory_space=pltpu.VMEM)] * len(outs),
        scratch_shapes=scratch,
        cost_estimate=pl.CostEstimate(flops=flops, bytes_accessed=moved, transcendentals=0),
        compiler_params=pltpu.CompilerParams(vmem_limit_bytes=VMEM_BYTES),
    )(*inputs)


def shape(*dims, dtype=F32):
    return jax.ShapeDtypeStruct(dims, dtype)


def encoder_forward_call(wrap, own, head, flat):
    n = 8 * ROWS_E
    outs = [
        shape(WIN_LAT, 96, CF), shape(n, CE), shape(n, 1), shape(n, 3 * CE),
        shape(8, HEADS_E * ROWS_E, ROWS_E, dtype=BF16), shape(8, HEADS_E * ROWS_E, ROWS_E, dtype=BF16),
        shape(n, CE), shape(n, CE), shape(n, 1), shape(n, MLP_E, dtype=BF16), shape(n, MLP_E, dtype=BF16),
        shape(n, MLP_E), shape(n, CE),
    ]
    scratch = (
        pair_of(CE, 3 * CE) + pair_of(CE, CE) + pair_of(CE, MLP_E) + pair_of(MLP_E, CE) + pair_of(CE, CF)
        + [vmem(n, CE), vmem(5, MLP_E, LANES), vmem(n, CF)]
    )
    return call(encoder_forward, "encoder_forward", [wrap, own, head, flat], outs, scratch, 1, 6 * n * 516096)


def encoder_backward(
    dlat_ref, flat, xhat_ref, rstd_ref, qkv_ref, p_h, p_l, o_ref, xhat2_ref, rstd2_ref, g_h, g_l, dg_ref, out_ref,
    dfield_ref, grad,
    win_h, win_l, wout_h, wout_l, wup_h, wup_l, wdn_h, wdn_l, wlin_h, wlin_l,
    dlat, wide, dout, dout_h, dout_l, dhn, du_h, du_l, hn_h, hn_l, dh_h, dh_l, dqkv_h, dqkv_l, xn_h, xn_l, sums, dx,
):
    win, wout, wup, wdn, wlin = (win_h, win_l), (wout_h, wout_l), (wup_h, wup_l), (wdn_h, wdn_l), (wlin_h, wlin_l)
    for pair, name in ((win, "in"), (wout, "out"), (wup, "up"), (wdn, "down"), (wlin, "lin")):
        width = ENC_MATS[name][1]

        def store(rows, c, v, pair=pair, width=width):
            last = min(width - c * LANES, LANES)
            put(pair, (rows, slice(c * LANES, c * LANES + last)), v[:, :last])

        unpack_matrix(flat, ENC_AT[name], ENC_MATS[name], store, wide)
    vec = {name: vector(flat, ENC_AT[name], ENC_VECS[name]) for name in ("g1", "s1", "g2", "s2")}
    masks = head_masks(CE)
    full = slice(None)
    scale = 1.0 / math.sqrt(HEAD)
    for r, at, start, amount in encoder_slots():
        dlat[at : at + amount, :] = dlat_ref[r, start : start + amount, :]
    dl = split(dlat[...])
    put_vector(grad, ENC_AT["lb"], column_sum(dlat[...]))
    d = dot3(dl, get(wlin, (full, full)), 1, 1)
    dout[...] = d
    put((dout_h, dout_l), (full, full), d)
    put_vector(grad, ENC_AT["db"], column_sum(d))
    dw = dot3(split(out_ref[...]), dl, 0, 0)
    for c in range(3):
        grad[pl.ds(ENC_AT["lin"] + c, CE, stride=3), :] = dw[:, c * LANES : (c + 1) * LANES]
    xhat2 = xhat2_ref[...]
    put((hn_h, hn_l), (full, full), xhat2 * vec["g2"] + vec["s2"])
    for c in range(MLP_E // CHUNK):
        cols = slice(c * CHUNK, (c + 1) * CHUNK)
        do = (dout_h[...], dout_l[...])
        du = dot3(do, get(wdn, (cols, full)), 1, 1) * dg_ref[:, cols]
        put_vector(grad, ENC_AT["ub"] + c * CHUNK, column_sum(du))
        du = split(du)
        part = dot3(du, get(wup, (full, cols)), 1, 1)
        dhn[...] = part if c == 0 else dhn[...] + part
        dw = dot3((hn_h[...], hn_l[...]), du, 0, 0)
        for t in range(2):
            grad[pl.ds(ENC_AT["up"] + 2 * c + t, CE, stride=6), :] = dw[:, t * LANES : (t + 1) * LANES]
        dw = dot3((g_h[:, cols], g_l[:, cols]), do, 0, 0)
        put_tiles(wide, slice(c * CHUNK, (c + 1) * CHUNK), dw)
    pack_matrix(grad, ENC_AT["down"], ENC_MATS["down"], wide)
    dv = dhn[...]
    put_vector(grad, ENC_AT["g2"], column_sum(dv * xhat2))
    put_vector(grad, ENC_AT["s2"], column_sum(dv))
    d = dout[...] + normalize_back(dv, xhat2, rstd2_ref[...], vec["g2"])
    dout[...] = d
    put((dh_h, dh_l), (full, full), d)
    put_vector(grad, ENC_AT["ob"], column_sum(d))
    dw = dot3(split(o_ref[...]), (dh_h[...], dh_l[...]), 0, 0)
    put_tiles(wide, slice(0, CE), dw)
    pack_matrix(grad, ENC_AT["out"], ENC_MATS["out"], wide)
    sums[...] = jnp.zeros_like(sums)

    def step(i, carry):
        rows = pl.ds(pl.multiple_of(i * 2 * ROWS_E, 2 * ROWS_E), 2 * ROWS_E)
        do = dot3((dh_h[rows, :], dh_l[rows, :]), get(wout, (full, full)), 1, 1)
        parts = []
        for w in range(2):
            one = qkv_ref[pl.ds(pl.multiple_of(i * 2 * ROWS_E, 2 * ROWS_E) + w * ROWS_E, ROWS_E), :]
            q, k, v = (one[:, j * CE : (j + 1) * CE] for j in range(3))
            dow = do[w * ROWS_E : (w + 1) * ROWS_E]
            dom = split(jnp.concatenate([dow * m for m in masks], 0))
            qm = split(jnp.concatenate([q * m for m in masks], 0))
            p = (p_h[i * 2 + w], p_l[i * 2 + w])
            dp = dot3(dom, split(v), 1, 1)
            pf = p[0].astype(F32) + p[1].astype(F32)
            t = pf * dp
            ds = split(t - pf * jnp.sum(t, 1, keepdims=True))
            dq = unstacked(dot3(ds, split(k)), masks) * scale
            dk = dot3(ds, qm, 0, 0)
            dvv = dot3(p, dom, 0, 0)
            parts.append(jnp.concatenate([dq, dk, dvv], 1))
        dqkv = jnp.concatenate(parts, 0)
        sums[0:1, :] = sums[0:1, :] + column_sum(dqkv)
        dqkv = split(dqkv)
        dqkv_h[rows, :] = dqkv[0]
        dqkv_l[rows, :] = dqkv[1]
        xhat = xhat_ref[rows, :]
        put((xn_h, xn_l), (rows, full), xhat * vec["g1"] + vec["s1"])
        dxn = dot3(dqkv, get(win, (full, full)), 1, 1)
        sums[1:2, 0:CE] = sums[1:2, 0:CE] + column_sum(dxn * xhat)
        sums[2:3, 0:CE] = sums[2:3, 0:CE] + column_sum(dxn)
        dx[rows, :] = dout[rows, :] + normalize_back(dxn, xhat, rstd_ref[rows, :], vec["g1"])
        return carry

    lax.fori_loop(0, 4, step, 0)
    put_vector(grad, ENC_AT["qb"], sums[0:1, 0:CE])
    put_vector(grad, ENC_AT["vb"], sums[0:1, 2 * CE : 3 * CE])
    put_vector(grad, ENC_AT["g1"], sums[1:2, 0:CE])
    put_vector(grad, ENC_AT["s1"], sums[2:3, 0:CE])
    dw = dot3((xn_h[...], xn_l[...]), (dqkv_h[...], dqkv_l[...]), 0, 0)
    put_tiles(wide, slice(0, CE), dw)
    pack_matrix(grad, ENC_AT["in"], ENC_MATS["in"], wide)
    for r, at, start, amount in encoder_slots():
        dfield_ref[r, start : start + amount, :] = dx[at : at + amount, :]


def encoder_backward_call(dlat, flat, saved, grad_rows):
    n = 8 * ROWS_E
    scratch = (
        pair_of(CE, 3 * CE) + pair_of(CE, CE) + pair_of(CE, MLP_E) + pair_of(MLP_E, CE) + pair_of(CE, CF)
        + [vmem(n, CF), vmem(5, MLP_E, LANES), vmem(n, CE)] + pair_of(n, CE) + [vmem(n, CE)] + pair_of(n, CHUNK)
        + pair_of(n, CE) + pair_of(n, CE) + pair_of(n, 3 * CE) + pair_of(n, CE) + [vmem(8, 3 * CE), vmem(n, CE)]
    )
    return call(
        encoder_backward, "encoder_backward", [dlat, flat] + list(saved),
        [shape(WIN_LAT, 96, CE), shape(grad_rows, LANES)], scratch, 0, 12 * n * 516096,
    )


def merging(
    fld_ref, cot_ref, flat, tab_ref, base_ref,
    out_ref, dx_ref, grad, dtab_ref,
    win_h, win_l, wout_h, wout_l, wup_h, wup_l, wdn_h, wdn_l,
    bias, dbias, x, xhat1, rstd1, xn_h, xn_l, q_h, q_l, k_h, k_l, v_h, v_l, p_h, p_l, o_h, o_l,
    xhat2, rstd2, hn_h, hn_l, acc, dhn, dy, dy_h, dy_l, g_h, g_l, du_h, du_l, dh_h, dh_l, dqkv_h, dqkv_l, sums,
):
    win, wout, wup, wdn = (win_h, win_l), (wout_h, wout_l), (wup_h, wup_l), (wdn_h, wdn_l)
    full = slice(None)
    chunks = MLP_F // CHUNK
    scale = 1.0 / math.sqrt(HEAD)

    def store(pair):
        def one(rows, c, v):
            put(pair, (rows, slice(c * LANES, (c + 1) * LANES)), v)
        return one

    def store_up(rows, c, v):
        put(wup, (c // 2, full, slice(c % 2 * LANES, (c % 2 + 1) * LANES)), v)

    def store_down(rows, c, v):
        for j in range(chunks):
            put(wdn, (j, full, slice(c * LANES, (c + 1) * LANES)), v[j * CHUNK : (j + 1) * CHUNK])

    unpack_matrix(flat, FUS_AT["in"], FUS_MATS["in"], store(win), None)
    unpack_matrix(flat, FUS_AT["out"], FUS_MATS["out"], store(wout), None)
    unpack_matrix(flat, FUS_AT["up"], FUS_MATS["up"], store_up, None)
    unpack_matrix(flat, FUS_AT["down"], FUS_MATS["down"], store_down, None)
    vec = {name: vector(flat, FUS_AT[name], amount) for name, amount in FUS_VECS.items()}
    masks = head_masks(LANES)

    spots = jnp.where(lax.broadcasted_iota(jnp.int32, (TAB_PAD, 2 * LANES), 0) == base_ref[...], 1.0, 0.0).astype(BF16)
    table = tab_ref[...]
    for w in range(WIN_LON):
        turned = pltpu.roll(table, TAB_PAD - w, 1) if w else table
        hi, lo = split(turned)
        rest = (turned - hi.astype(F32) - lo.astype(F32)).astype(BF16)
        one = dot(hi, spots) + (dot(lo, spots) + dot(rest, spots))
        for c in range(2):
            bias[c, pl.ds(w, ROWS_F, stride=WIN_LON), :] = one[:, c * LANES : (c + 1) * LANES]
    dbias[...] = jnp.zeros_like(dbias)

    for z, r, at, start in merging_slots():
        x[at : at + WIN_LON, :] = fld_ref[z, r, start : start + WIN_LON, :]
        dy[at : at + WIN_LON, :] = cot_ref[z, r, start : start + WIN_LON, :]

    def rows_of(i):
        return pl.ds(pl.multiple_of(i * ROWS_F, ROWS_F), ROWS_F)

    def forward(i, carry):
        rows = rows_of(i)
        xv = x[rows, :]
        xhat, rstd = normalize(xv)
        xhat1[rows, :] = xhat
        rstd1[rows, :] = rstd
        xn = split(xhat * vec["g1"] + vec["s1"])
        xn_h[rows, :] = xn[0]
        xn_l[rows, :] = xn[1]
        for j, (pair, shift) in enumerate((((q_h, q_l), vec["qb"]), ((k_h, k_l), None), ((v_h, v_l), vec["vb"]))):
            one = dot3(xn, get(win, (full, slice(j * CF, (j + 1) * CF))))
            if shift is not None:
                one = one + shift
            if j == 0:
                one = one * scale
            put(pair, (rows, full), one)
        for g in range(3):
            cols = slice(g * LANES, (g + 1) * LANES)
            qm = stacked((q_h[rows, cols], q_l[rows, cols]), masks)
            some = slice(g * 4 * ROWS_F, (g + 1) * 4 * ROWS_F)
            s = wide_nt(qm, (k_h[rows, cols], k_l[rows, cols])) + get_tiles(bias, some, ROWS_F)
            p = split(softmax(s))
            p_h[i * 3 + g] = p[0]
            p_l[i * 3 + g] = p[1]
            o = unstacked(wide_n(p, (v_h[rows, cols], v_l[rows, cols])), masks)
            put((o_h, o_l), (rows, cols), o)
        hidden = xv + dot3((o_h[rows, :], o_l[rows, :]), get(wout, (full, full))) + vec["ob"]
        xh2, rstd = normalize(hidden)
        xhat2[rows, :] = xh2
        rstd2[rows, :] = rstd
        put((hn_h, hn_l), (rows, full), xh2 * vec["g2"] + vec["s2"])
        acc[rows, :] = hidden + vec["db"]
        put((dy_h, dy_l), (rows, full), dy[rows, :])
        return carry

    lax.fori_loop(0, 4, forward, 0)
    dhn[...] = jnp.zeros_like(dhn)
    for c in range(chunks):
        sums[8:9, c * CHUNK : (c + 1) * CHUNK] = vec["ub"][:, c * CHUNK : (c + 1) * CHUNK]

    def feed(c, carry):
        up = (wup_h[c], wup_l[c])
        down = (wdn_h[c], wdn_l[c])
        cols = pl.ds(pl.multiple_of(c * CHUNK, CHUNK), CHUNK)
        shift = sums[8:9, cols]

        def part(i, total):
            rows = rows_of(i)
            u = dot3((hn_h[rows, :], hn_l[rows, :]), up) + shift
            g, slope = gelu_parts(u)
            g = split(g)
            g_h[rows, :] = g[0]
            g_l[rows, :] = g[1]
            acc[rows, :] = acc[rows, :] + dot3(g, down)
            du = dot3((dy_h[rows, :], dy_l[rows, :]), down, 1, 1) * slope
            total = total + column_sum(du)
            du = split(du)
            du_h[rows, :] = du[0]
            du_l[rows, :] = du[1]
            dhn[rows, :] = dhn[rows, :] + dot3(du, up, 1, 1)
            return total

        sums[9:10, cols] = lax.fori_loop(0, 4, part, jnp.zeros((1, CHUNK), F32))
        dw = dot3((hn_h[...], hn_l[...]), (du_h[...], du_l[...]), 0, 0)
        for t in range(2):
            grad[pl.ds(FUS_AT["up"] + 2 * c + t, CF, stride=12), :] = dw[:, t * LANES : (t + 1) * LANES]
        dw = dot3((g_h[...], g_l[...]), (dy_h[...], dy_l[...]), 0, 0)
        for t in range(3):
            grad[pl.ds(FUS_AT["down"] + 3 * CHUNK * c + t, CHUNK, stride=3), :] = dw[:, t * LANES : (t + 1) * LANES]
        return carry

    lax.fori_loop(0, chunks, feed, 0)
    put_vector(grad, FUS_AT["ub"], sums[9:10, :])
    sums[0:8, :] = jnp.zeros((8, MLP_F), F32)

    def backward(i, carry):
        rows = rows_of(i)
        dv = dhn[rows, :]
        xh2 = xhat2[rows, :]
        d = dy[rows, :]
        sums[0:1, 0:CF] = sums[0:1, 0:CF] + column_sum(d)
        sums[1:2, 0:CF] = sums[1:2, 0:CF] + column_sum(dv * xh2)
        sums[2:3, 0:CF] = sums[2:3, 0:CF] + column_sum(dv)
        dh = d + normalize_back(dv, xh2, rstd2[rows, :], vec["g2"])
        sums[3:4, 0:CF] = sums[3:4, 0:CF] + column_sum(dh)
        dhs = split(dh)
        dh_h[rows, :] = dhs[0]
        dh_l[rows, :] = dhs[1]
        do = split(dot3(dhs, get(wout, (full, full)), 1, 1))
        for g in range(3):
            cols = slice(g * LANES, (g + 1) * LANES)
            dom = stacked((do[0][:, cols], do[1][:, cols]), masks)
            qm = stacked((q_h[rows, cols], q_l[rows, cols]), masks)
            p = (p_h[i * 3 + g], p_l[i * 3 + g])
            dp = wide_nt(dom, (v_h[rows, cols], v_l[rows, cols]))
            pf = p[0].astype(F32) + p[1].astype(F32)
            t = pf * dp
            ds = t - pf * jnp.sum(t, 1, keepdims=True)
            some = slice(g * 4 * ROWS_F, (g + 1) * 4 * ROWS_F)
            for c in range(2):
                one = ds[:, c * LANES : (c + 1) * LANES]
                dbias[c, some, 0 : one.shape[1]] = dbias[c, some, 0 : one.shape[1]] + one
            ds = split(ds)
            dq = unstacked(wide_n(ds, (k_h[rows, cols], k_l[rows, cols])), masks) * scale
            dk = wide_n(ds, qm, 0)
            dvv = wide_n(p, dom, 0)
            for j, one in enumerate((dq, dk, dvv)):
                at = slice(j * CF + g * LANES, j * CF + (g + 1) * LANES)
                put((dqkv_h, dqkv_l), (rows, at), one)
                if j != 1:
                    sums[4 + j // 2 : 5 + j // 2, cols] = sums[4 + j // 2 : 5 + j // 2, cols] + column_sum(one)
        xhat = xhat1[rows, :]
        dxn = dot3((dqkv_h[rows, :], dqkv_l[rows, :]), get(win, (full, full)), 1, 1)
        sums[6:7, 0:CF] = sums[6:7, 0:CF] + column_sum(dxn * xhat)
        sums[7:8, 0:CF] = sums[7:8, 0:CF] + column_sum(dxn)
        x[rows, :] = dh + normalize_back(dxn, xhat, rstd1[rows, :], vec["g1"])
        return carry

    lax.fori_loop(0, 4, backward, 0)
    for j, name in enumerate(("db", "g2", "s2", "ob", "qb", "vb", "g1", "s1")):
        put_vector(grad, FUS_AT[name], sums[j : j + 1, 0:CF])
    for c in range(3):
        cols = slice(c * CF, (c + 1) * CF)
        dw = dot3((xn_h[...], xn_l[...]), (dqkv_h[:, cols], dqkv_l[:, cols]), 0, 0)
        for t in range(3):
            grad[pl.ds(FUS_AT["in"] + 3 * c + t, CF, stride=9), :] = dw[:, t * LANES : (t + 1) * LANES]
    dw = dot3((o_h[...], o_l[...]), (dh_h[...], dh_l[...]), 0, 0)
    for t in range(3):
        grad[pl.ds(FUS_AT["out"] + t, CF, stride=3), :] = dw[:, t * LANES : (t + 1) * LANES]
    total = jnp.zeros((ROWS_F, TAB_PAD), F32)
    for w in range(WIN_LON):
        turned = jnp.concatenate([dbias[c, pl.ds(w, ROWS_F, stride=WIN_LON), :] for c in range(2)], 1)
        hi, lo = split(turned)
        one = dot(hi, spots, 1, 1) + dot(lo, spots, 1, 1)
        total = total + (pltpu.roll(one, w, 1) if w else one)
    dtab_ref[...] = total
    for z, r, at, start in merging_slots():
        out_ref[z, r, start : start + WIN_LON, :] = acc[at : at + WIN_LON, :]
        dx_ref[z, r, start : start + WIN_LON, :] = x[at : at + WIN_LON, :]


def merging_call(fields, cotangent, flat, table, grad_rows):
    n = 4 * ROWS_F
    m = HEADS_F * ROWS_F
    t = np.arange(ROWS_F)
    base = np.full((1, 2 * LANES), -1, np.int32)
    base[0, :ROWS_F] = t // WIN_LON * SPAN + WIN_LON - 1 - t % WIN_LON
    base = jnp.asarray(base)
    scratch = (
        pair_of(CF, 3 * CF) + pair_of(CF, CF) + pair_of(6, CF, CHUNK) + pair_of(6, CHUNK, CF)
        + [vmem(2, m, LANES), vmem(2, m, LANES), vmem(n, CF), vmem(n, CF), vmem(n, 1)]
        + pair_of(n, CF) + pair_of(n, CF) + pair_of(n, CF) + pair_of(n, CF) + pair_of(12, 4 * ROWS_F, ROWS_F) + pair_of(n, CF)
        + [vmem(n, CF), vmem(n, 1)] + pair_of(n, CF) + [vmem(n, CF), vmem(n, CF), vmem(n, CF)] + pair_of(n, CF)
        + pair_of(n, CHUNK) + pair_of(n, CHUNK) + pair_of(n, CF) + pair_of(n, 3 * CF) + [vmem(16, MLP_F)]
    )
    outs = [shape(*fields.shape), shape(*fields.shape), shape(grad_rows, LANES), shape(ROWS_F, TAB_PAD)]
    return call(merging, "merging", [fields, cotangent, flat, table, base], outs, scratch, 0, 18 * n * 1769472)


MESH = pl.DeviceIdType.MESH


def seq_digits(count):
    rest, digits = count // 2, []
    while rest > 1:
        digits.insert(0, 4 if rest % 4 == 0 else 2)
        rest //= digits[0]
    digits.sort()
    if count == 16:
        digits = [4, 2]
    return digits + [2]


class Places:
    def __init__(self, groups, seqs):
        self.sizes = [groups] + seq_digits(seqs)
        self.groups = groups
        self.strides = [1] * len(self.sizes)
        for i in range(len(self.sizes) - 2, 0, -1):
            self.strides[i] = self.strides[i + 1] * self.sizes[i + 1]

    def here(self):
        self.g, self.s = lax.axis_index("group"), lax.axis_index("seq")
        self.mine = [self.g] + [self.s // self.strides[i] % self.sizes[i] for i in range(1, len(self.sizes))]

    def peer(self, digit, value):
        if digit == 0:
            return (value, self.s)
        return (self.g, self.s + (value - self.mine[digit]) * self.strides[digit])

    def place(self, values):
        return sum(v * self.strides[i] for i, v in values.items() if i)


def windows(total, count):
    piece = total // count
    tiles = max(-(-(piece * (d + 1)) // 1024) - piece * d // 1024 for d in range(count))
    last = piece * (count - 1) // 1024
    return piece, tiles * 8, (last + tiles) * 8


def window_start(piece, d):
    return pl.multiple_of(piece * d // 1024 * 8, 8)


def start_copy(src, dst, sems, at, peer):
    one = pltpu.make_async_remote_copy(
        src_ref=src, dst_ref=dst, send_sem=sems[0].at[at], recv_sem=sems[1].at[at], device_id=peer, device_id_type=MESH
    )
    one.start()
    return one


class Stream:
    def __init__(self, places, order, piece, first, rows, refs, sems, base):
        self.places, self.order, self.piece, self.first, self.rows = places, order, piece, first, rows
        self.refs, self.sems, self.base = refs, sems, base
        self.sizes = [places.sizes[d] for d in order]

    def combos(self):
        out = [()]
        for n in self.sizes:
            out = [c + (v,) for c in out for v in range(n)]
        return out

    def piece_at(self, combo, core):
        values = dict(zip(self.order, combo))
        values[len(self.places.sizes) - 1] = core
        where = self.places.place(values)
        if 0 in values:
            where = where + values[0] * (self.places.sizes[1] * self.places.strides[1])
        return pl.ds(window_start(self.piece, where) + self.first, self.rows)

    def start_core(self, source):
        p = self.places
        last = len(p.sizes) - 1
        core = p.mine[last]
        self.copies = []
        for n, combo in enumerate(self.combos()):
            self.copies.append(
                start_copy(source.at[self.piece_at(combo, 1 - core)], self.refs[0].at[n], self.sems, self.base + n, p.peer(last, 1 - core))
            )

    def finish_core(self, source):
        p = self.places
        core = p.mine[len(p.sizes) - 1]
        for n, combo in enumerate(self.combos()):
            self.copies[n].wait()
            self.refs[0][n] = self.refs[0][n] + source[self.piece_at(combo, core), :]

    def blocks(self, i):
        return math.prod(self.sizes[i + 1 :])

    def start(self, i):
        p, digit, size = self.places, self.order[i], self.sizes[i]
        base = self.base + len(self.combos()) + sum(n - 1 for n in self.sizes[:i])
        held = self.refs[i] if i == 0 else self.refs[i].at[0]
        mine = p.mine[digit]
        self.copies = []
        for k in range(1, size):
            value = lax.rem(mine + k, size)
            src = held.at[pl.ds(value * self.blocks(i), self.blocks(i))]
            self.copies.append(start_copy(src, self.refs[i + 1].at[k - 1], self.sems, base + k - 1, p.peer(digit, value)))

    def finish(self, i):
        held = self.refs[i] if i == 0 else self.refs[i].at[0]
        first = self.places.mine[self.order[i]] * self.blocks(i)
        for one in self.copies:
            one.wait()

        def add(n, carry):
            total = held[first + n]
            for k in range(self.sizes[i] - 1):
                total = total + self.refs[i + 1][k, n]
            self.refs[i + 1][0, n] = total
            return carry

        lax.fori_loop(0, self.blocks(i), add, 0)

    def result(self):
        return self.refs[-1][0, 0]

    @staticmethod
    def scratch(sizes, rows):
        refs, count = [vmem(math.prod(sizes), rows, LANES)], math.prod(sizes)
        for i, n in enumerate(sizes):
            refs.append(vmem(n - 1, math.prod(sizes[i + 1 :]), rows, LANES))
            count += n - 1
        return refs, count


def sum_plan(groups, seqs, fus_total, enc_total):
    places = Places(groups, seqs)
    last = len(places.sizes) - 1
    seq_order = list(range(1, last))
    seq_order.sort(key=lambda d: places.sizes[d])
    fus_piece, fus_rows, fus_all = windows(fus_total, groups * seqs)
    enc_piece, enc_rows, enc_all = windows(enc_total, seqs)
    first = fus_rows // 16 * 8
    streams = [
        ([0] + seq_order, fus_piece, 0, first),
        (seq_order[:1] + [0] + seq_order[1:], fus_piece, first, fus_rows - first),
        (seq_order, enc_piece, 0, enc_rows),
    ]
    return places, streams, fus_rows, fus_all, enc_rows, enc_all


def sum_kernel(places, plans, fus, enc, tab, fus_out, enc_out, tab_out, tabs, send, recv, *refs):
    places.here()
    bands_per_owner = 4
    last = len(places.sizes) - 1
    g, s = places.g, places.s
    seqs = places.sizes[1] * places.strides[1]
    slot = g * seqs + s
    band = s // 2
    mine = g * 2 + lax.rem(s, 2)
    owners = [((4 * band + j) // seqs, lax.rem(4 * band + j, seqs)) for j in range(4)]
    givers = [(k // 2, slot // bands_per_owner * 2 + k % 2) for k in range(4)]

    barrier = pltpu.get_barrier_semaphore()
    expected = 0
    for digit, size in enumerate(places.sizes):
        for k in range(1, size):
            pl.semaphore_signal(barrier, inc=1, device_id=places.peer(digit, lax.rem(places.mine[digit] + k, size)), device_id_type=MESH)
            expected += 1
    for pg, ps in owners + givers:
        @pl.when(jnp.logical_or(pg != g, ps != s))
        def _(pg=pg, ps=ps):
            pl.semaphore_signal(barrier, inc=1, device_id=(pg, ps), device_id_type=MESH)
    alone = slot // 4 == band
    pl.semaphore_wait(barrier, expected + jnp.where(alone, 6, 8))

    streams, at, base = [], 0, 0
    for order, piece, first, rows in plans:
        sizes = [places.sizes[d] for d in order]
        own, count = Stream.scratch(sizes, rows)
        streams.append(Stream(places, order, piece, first, rows, refs[at : at + len(own)], (send, recv), base))
        at += len(own)
        base += count
    sources = [fus, fus, enc]
    for one, source in zip(streams, sources):
        one.start_core(source)
    for j, (pg, ps) in enumerate(owners):
        away = jnp.logical_or(pg != g, ps != s)

        def give(pg=pg, ps=ps, j=j):
            return pltpu.make_async_remote_copy(
                src_ref=tab.at[j], dst_ref=tabs.at[mine], send_sem=send.at[base + j], recv_sem=recv.at[base + mine],
                device_id=(pg, ps), device_id_type=MESH,
            )

        @pl.when(away)
        def _(give=give):
            give().start()

        @pl.when(jnp.logical_not(away))
        def _(j=j):
            tabs[mine] = tab[j]
    for one, source in zip(streams, sources):
        one.finish_core(source)
    stages = max(len(one.order) for one in streams)
    for i in range(stages):
        for one in streams:
            if i < len(one.order):
                one.start(i)
        for one in streams:
            if i < len(one.order):
                one.finish(i)
    split_at = plans[0][3]
    fus_out[0:split_at, :] = streams[0].result()
    fus_out[split_at : split_at + plans[1][3], :] = streams[1].result()
    enc_out[...] = streams[2].result()
    for j, (pg, ps) in enumerate(owners):
        @pl.when(jnp.logical_or(pg != g, ps != s))
        def _(j=j, pg=pg, ps=ps):
            pltpu.make_async_remote_copy(
                src_ref=tab.at[j], dst_ref=tabs.at[mine], send_sem=send.at[base + j], recv_sem=recv.at[base + mine],
                device_id=(pg, ps), device_id_type=MESH,
            ).wait_send()
    for k, (pg, ps) in enumerate(givers):
        @pl.when(jnp.logical_or(pg != g, ps != s))
        def _(k=k, pg=pg, ps=ps):
            pltpu.make_async_remote_copy(
                src_ref=tab.at[0], dst_ref=tabs.at[k], send_sem=send.at[base], recv_sem=recv.at[base + k],
                device_id=(pg, ps), device_id_type=MESH,
            ).wait_recv()
    tab_out[...] = (tabs[0] + tabs[1]) + (tabs[2] + tabs[3])


def sum_call(groups, seqs, fus_total, enc_total, fus, enc, tab):
    places, plans, fus_rows, _, enc_rows, _ = sum_plan(groups, seqs, fus_total, enc_total)
    refs, count = [], 4
    for order, piece, first, rows in plans:
        own, more = Stream.scratch([places.sizes[d] for d in order], rows)
        refs += own
        count += more
    return pl.pallas_call(
        partial(sum_kernel, places, plans),
        name="device_sums",
        out_shape=[shape(fus_rows, LANES), shape(enc_rows, LANES), shape(*tab.shape[1:])],
        in_specs=[pl.BlockSpec(memory_space=pltpu.VMEM)] * 3,
        out_specs=[pl.BlockSpec(memory_space=pltpu.VMEM)] * 3,
        scratch_shapes=[vmem(*tab.shape), pltpu.SemaphoreType.DMA((count,)), pltpu.SemaphoreType.DMA((count,))] + refs,
        compiler_params=pltpu.CompilerParams(collective_id=0, has_side_effects=True, vmem_limit_bytes=VMEM_BYTES),
    )(fus, enc, tab)


def own_piece(block, piece, d):
    return lax.dynamic_slice_in_dim(block.reshape(-1), piece * d - piece * d // 1024 * 1024, piece)


def passed_along(block, axis, distance):
    devices = range(lax.axis_size(axis))
    route = [((i - distance) % len(devices), i) for i in devices]
    return lax.ppermute(block, axis, route)


def update(params, grads, momentum, average, rate):
    momentum_new = MOMENTUM_DECAY * momentum + grads
    params_new = params - rate * (grads + MOMENTUM_DECAY * momentum_new)
    average_new = AVERAGE_DECAY * average + (1.0 - AVERAGE_DECAY) * params_new
    return (params_new, momentum_new, average_new)


def table_rows(one):
    heads = one.shape[0]
    one = one.reshape(heads, WIN_MOD, WIN_MOD, WIN_LAT, WIN_LAT * SPAN).transpose(0, 1, 3, 2, 4)
    return one.reshape(heads * PAIRS, PAIRS * SPAN)


def table_back(rows):
    heads = rows.shape[0] // PAIRS
    one = rows.reshape(heads, WIN_MOD, WIN_LAT, WIN_MOD, WIN_LAT * SPAN).transpose(0, 1, 3, 2, 4)
    return one.reshape(heads, -1)


def shards(
    tokens,
    cotangent,
    enc_params,
    enc_momentum,
    enc_average,
    fus_params,
    fus_momentum,
    fus_average,
    earth_bias,
    bias_momentum,
    bias_average,
):
    field = tokens[0, 0]
    row_count, col_count, feat_width = field.shape
    half_rows = WIN_LAT // 2
    seq_count = lax.axis_size("seq")
    group_count = lax.axis_size("group")
    band_count = seq_count // SAMPLES
    place = lax.axis_index("seq")
    mine = lax.axis_index("group")
    band = place // SAMPLES
    enc_flat = enc_params.reshape(-1, LANES)
    plan = sum_plan(group_count, seq_count, fus_params.size, enc_params.size)
    fus_flat = fus_params.reshape(-1, LANES)
    head_rows = passed_along(field[:half_rows], "seq", -SAMPLES)
    wrap = (band == band_count - 1).astype(jnp.int32).reshape(1)
    latent, *saved = encoder_forward_call(wrap, field[half_rows:], head_rows, enc_flat)
    tail_rows = passed_along(latent[-half_rows:], "seq", SAMPLES)
    encoded = jnp.concatenate([tail_rows, latent[:-half_rows]], 0)
    fields = lax.all_to_all(
        encoded.reshape(row_count, group_count, -1, CF)[None],
        "group",
        split_axis=2,
        concat_axis=0,
        tiled=True,
    )[:, :, 0]
    table = lax.dynamic_slice_in_dim(earth_bias, band, 1, 0)[0]
    table = jnp.pad(table_rows(table), ((0, 0), (0, TAB_PAD - PAIRS * SPAN)))
    merged, fields_grad, fus_local, table_grad = merging_call(fields, cotangent[:, 0, 0], fus_flat, table, plan[3])
    table_grad = table_back(table_grad[:, : PAIRS * SPAN])[None]
    latent_grad = lax.all_to_all(
        fields_grad[:, :, None], "group", split_axis=0, concat_axis=2, tiled=True
    )[0].reshape(row_count, col_count, CF)
    lower_rows = passed_along(latent_grad[:half_rows], "seq", -SAMPLES)
    block_grad = jnp.concatenate([latent_grad[half_rows:], lower_rows], 0)
    before_grad, enc_local = encoder_backward_call(block_grad, enc_flat, saved, plan[5])
    upper_rows = passed_along(before_grad[-half_rows:], "seq", SAMPLES)
    field_grad = jnp.concatenate([upper_rows, before_grad[:-half_rows]], 0)
    pieces = table_grad.size // 4
    padded = -(-pieces // 1024) * 1024
    tab_local = jnp.pad(table_grad.reshape(4, pieces), ((0, 0), (0, padded - pieces))).reshape(4, -1, LANES)
    fus_block, enc_block, tab_block = sum_call(
        group_count, seq_count, fus_params.size, enc_params.size, fus_local, enc_local, tab_local
    )
    slot = mine * seq_count + place
    fus_grad = own_piece(fus_block, fus_params.size // (group_count * seq_count), slot)
    enc_grad = own_piece(enc_block, enc_params.size // seq_count, place)
    bias_grad = tab_block.reshape(-1)[:pieces]
    enc_piece = enc_grad.shape[0]
    enc_own = lax.dynamic_slice_in_dim(enc_params[0], place * enc_piece, enc_piece)
    fus_piece = fus_grad.shape[0]
    fus_own = lax.dynamic_slice_in_dim(fus_params, slot * fus_piece, fus_piece)
    bias_piece = bias_grad.shape[0]
    bias_own = lax.dynamic_slice_in_dim(earth_bias.reshape(-1), slot * bias_piece, bias_piece)
    lat_total = band_count * row_count
    enc_new, enc_momentum_new, enc_average_new = update(
        enc_own,
        enc_grad,
        enc_momentum[0],
        enc_average[0],
        1.0 / math.sqrt(CE * SAMPLES * lat_total * col_count),
    )
    fus_new, fus_momentum_new, fus_average_new = update(
        fus_own,
        fus_grad,
        fus_momentum,
        fus_average,
        1.0 / math.sqrt(CF * group_count * SAMPLES * lat_total * col_count),
    )
    bias_new, bias_momentum_new, bias_average_new = update(
        bias_own,
        bias_grad,
        bias_momentum,
        bias_average,
        2.0 / math.sqrt(SAMPLES * col_count / WIN_LON),
    )
    return (
        merged[:, None, None],
        field_grad[None, None],
        enc_grad[None],
        enc_new[None],
        enc_momentum_new[None],
        enc_average_new[None],
        fus_grad,
        fus_new,
        fus_momentum_new,
        fus_average_new,
        bias_grad,
        bias_new,
        bias_momentum_new,
        bias_average_new,
    )


def solution(mesh):
    both = P(("group", "seq"))
    rows = P("group", "seq")
    merged = P(None, "seq", "group", None, None, None)
    tokens = P("group", "seq", None, None, None)
    return jax.shard_map(
        shards,
        mesh=mesh,
        in_specs=(tokens, merged, P("group", None), rows, rows, P(), both, both, P(), both, both),
        out_specs=(merged, tokens, rows, rows, rows, rows) + (both,) * 8,
        check_vma=False,
    )
```

```python
from functools import partial
import math

import jax
import jax.numpy as jnp
import numpy as np
from jax import lax
from jax.experimental import pallas as pl
from jax.experimental.pallas import tpu as pltpu
from jax.sharding import PartitionSpec as P

CE = 192
CF = 384
HEADS_E = 6
HEADS_F = 12
MLP_E = 768
MLP_F = 1536
WIN_LAT = 6
WIN_LON = 12
WIN_MOD = 2
SAMPLES = 2
HEAD = 32
CHUNK = 256
LANES = 128
ROWS_E = WIN_LAT * WIN_LON
ROWS_F = WIN_MOD * ROWS_E
SPAN = 2 * WIN_LON - 1
PAIRS = WIN_MOD * WIN_LAT
TAB_PAD = 384
EPS = 1e-05
NEG = -1000000000.0
VMEM_BYTES = 60 << 20

MOMENTUM_DECAY = 0.9
AVERAGE_DECAY = 0.99

F32 = jnp.float32
BF16 = jnp.bfloat16

ENC_MATS = {"in": (CE, 3 * CE), "out": (CE, CE), "up": (CE, MLP_E), "down": (MLP_E, CE), "lin": (CE, CF)}
ENC_VECS = {"g1": CE, "s1": CE, "qb": CE, "vb": CE, "ob": CE, "g2": CE, "s2": CE, "ub": MLP_E, "db": CE, "lb": CF}
FUS_MATS = {"in": (CF, 3 * CF), "out": (CF, CF), "up": (CF, MLP_F), "down": (MLP_F, CF)}
FUS_VECS = {"g1": CF, "s1": CF, "qb": CF, "vb": CF, "ob": CF, "g2": CF, "s2": CF, "ub": MLP_F, "db": CF}


def offsets(mats, vecs):
    places, at = {}, 0
    for name, shape in mats.items():
        places[name] = at // LANES
        at += shape[0] * shape[1]
    for name, amount in vecs.items():
        places[name] = at
        at += amount
    return places


ENC_AT = offsets(ENC_MATS, ENC_VECS)
FUS_AT = offsets(FUS_MATS, FUS_VECS)


def split(v):
    hi = v.astype(BF16)
    return hi, (v - hi.astype(F32)).astype(BF16)


def dot(a, b, ca=1, cb=0):
    return lax.dot_general(a, b, (((ca,), (cb,)), ((), ())), preferred_element_type=F32)


def dot3(a, b, ca=1, cb=0):
    return dot(a[0], b[0], ca, cb) + (dot(a[0], b[1], ca, cb) + dot(a[1], b[0], ca, cb))


def put(refs, index, v):
    hi, lo = split(v)
    refs[0][index] = hi
    refs[1][index] = lo


def get(refs, index):
    return refs[0][index], refs[1][index]


def half_lanes():
    return lax.broadcasted_iota(jnp.int32, (1, LANES), 1) < LANES // 2


def turn(v):
    return pltpu.roll(v, LANES // 2, 1)


def vector(flat, at, amount):
    tiles = []
    for c in range(-(-amount // LANES)):
        row, lane = divmod(at + c * LANES, LANES)
        one = flat[row : row + 1, :]
        if lane:
            one = turn(one)
            if c * LANES + LANES // 2 < amount:
                one = jnp.where(half_lanes(), one, turn(flat[row + 1 : row + 2, :]))
        tiles.append(one)
    return jnp.concatenate(tiles, 1)[:, :amount] if len(tiles) > 1 else tiles[0][:, :amount]


def put_vector(flat, at, v):
    amount = v.shape[1]
    if at % LANES == 0 and amount % LANES == 0:
        for c in range(amount // LANES):
            flat[at // LANES + c : at // LANES + c + 1, :] = v[:, c * LANES : (c + 1) * LANES]
        return
    half = LANES // 2
    for c in range(amount // half):
        row, lane = divmod(at + c * half, LANES)
        flat[row : row + 1, lane : lane + half] = v[:, c * half : (c + 1) * half]


def unpack_matrix(flat, at, shape, store, scratch):
    rows, width = shape
    if width % LANES == 0:
        n = width // LANES
        for c in range(n):
            store(slice(0, rows), c, flat[pl.ds(at + c, rows, stride=n), :])
        return
    pairs, n, full = rows // 2, 2 * width // LANES, width // LANES
    low = half_lanes()
    for c in range(full + 1):
        scratch[c, pl.ds(0, pairs, stride=2), :] = flat[pl.ds(at + c, pairs, stride=n), :]
        odd = turn(flat[pl.ds(at + full + c, pairs, stride=n), :])
        if c < full:
            odd = jnp.where(low, odd, turn(flat[pl.ds(at + full + c + 1, pairs, stride=n), :]))
        scratch[c, pl.ds(1, pairs, stride=2), :] = odd
    for c in range(full + 1):
        store(slice(0, rows), c, scratch[c, 0:rows, :])


def pack_matrix(flat, at, shape, source):
    rows, width = shape
    pairs, n, full = rows // 2, 2 * width // LANES, width // LANES
    low = half_lanes()

    def tile(odd, c):
        return source[c, pl.ds(odd, pairs, stride=2), :]

    for c in range(full):
        flat[pl.ds(at + c, pairs, stride=n), :] = tile(0, c)
        flat[pl.ds(at + full + 1 + c, pairs, stride=n), :] = jnp.where(low, turn(tile(1, c)), turn(tile(1, c + 1)))
    flat[pl.ds(at + full, pairs, stride=n), :] = jnp.where(low, tile(0, full), turn(tile(1, 0)))


def put_tiles(ref, rows, v):
    for c in range(-(-v.shape[1] // LANES)):
        one = v[:, c * LANES : (c + 1) * LANES]
        ref[c, rows, 0 : one.shape[1]] = one


def get_tiles(ref, rows, width):
    tiles = [ref[c, rows, 0 : min(width - c * LANES, LANES)] for c in range(-(-width // LANES))]
    return jnp.concatenate(tiles, 1)


def normalize(x):
    center = x - jnp.mean(x, 1, keepdims=True)
    scale = lax.rsqrt(jnp.mean(center * center, 1, keepdims=True) + EPS)
    return center * scale, scale


def normalize_back(dv, xhat, scale, gain):
    dxhat = dv * gain
    return scale * (dxhat - jnp.mean(dxhat, 1, keepdims=True) - xhat * jnp.mean(dxhat * xhat, 1, keepdims=True))


def gelu_parts(u):
    phi = 0.5 * (1.0 + lax.erf(u * (1.0 / math.sqrt(2.0))))
    return u * phi, phi + u * jnp.exp(-0.5 * u * u) * (1.0 / math.sqrt(2.0 * math.pi))


def head_masks(width):
    lane = lax.broadcasted_iota(jnp.int32, (1, width), 1)
    return [jnp.where((lane >= h * HEAD) & (lane < (h + 1) * HEAD), 1.0, 0.0) for h in range(width // HEAD)]


def stacked(pair, masks):
    return tuple(jnp.concatenate([part * m.astype(BF16) for m in masks], 0) for part in pair)


def unstacked(v, masks):
    rows = v.shape[0] // len(masks)
    total = v[:rows] * masks[0]
    for h in range(1, len(masks)):
        total = total + v[h * rows : (h + 1) * rows] * masks[h]
    return total


def softmax(s):
    e = jnp.exp(s - jnp.max(s, 1, keepdims=True))
    return e / jnp.sum(e, 1, keepdims=True)


def wide_nt(a, b):
    return dot(jnp.concatenate(a, 1), jnp.concatenate([b[0], b[0]], 1), 1, 1) + dot(a[0], b[1], 1, 1)


def wide_n(a, b, ca=1):
    n = b[0].shape[1]
    both = dot(a[0], jnp.concatenate(b, 1), ca, 0)
    return both[:, :n] + (both[:, n:] + dot(a[1], b[0], ca, 0))


def column_sum(v):
    return jnp.sum(v, 0, keepdims=True)


def encoder_slots():
    for r in range(WIN_LAT):
        for n in range(8):
            start = n * WIN_LON + WIN_LON // 2
            at = n * ROWS_E + r * WIN_LON
            if n < 7:
                yield r, at, start, WIN_LON
            else:
                yield r, at, start, WIN_LON // 2
                yield r, at + WIN_LON // 2, 0, WIN_LON // 2


def merging_slots():
    for z in range(WIN_MOD):
        for r in range(WIN_LAT):
            for n in range(4):
                yield z, r, n * ROWS_F + (z * WIN_LAT + r) * WIN_LON, n * WIN_LON


MESH = pl.DeviceIdType.MESH


def seq_digits(count):
    rest, digits = count // 2, []
    while rest > 1:
        digits.insert(0, 4 if rest % 4 == 0 else 2)
        rest //= digits[0]
    digits.sort()
    if count == 16:
        digits = [4, 2]
    return digits + [2]


class Places:
    def __init__(self, groups, seqs):
        self.sizes = [groups] + seq_digits(seqs)
        self.groups = groups
        self.strides = [1] * len(self.sizes)
        for i in range(len(self.sizes) - 2, 0, -1):
            self.strides[i] = self.strides[i + 1] * self.sizes[i + 1]

    def here(self):
        self.g, self.s = lax.axis_index("group"), lax.axis_index("seq")
        self.mine = [self.g] + [self.s // self.strides[i] % self.sizes[i] for i in range(1, len(self.sizes))]

    def peer(self, digit, value):
        if digit == 0:
            return (value, self.s)
        return (self.g, self.s + (value - self.mine[digit]) * self.strides[digit])

    def place(self, values):
        return sum(v * self.strides[i] for i, v in values.items() if i)


def windows(total, count):
    piece = total // count
    tiles = max(-(-(piece * (d + 1)) // 1024) - piece * d // 1024 for d in range(count))
    last = piece * (count - 1) // 1024
    return piece, tiles * 8, (last + tiles) * 8


def window_start(piece, d):
    return pl.multiple_of(piece * d // 1024 * 8, 8)


def start_copy(src, dst, sems, at, peer):
    one = pltpu.make_async_remote_copy(
        src_ref=src, dst_ref=dst, send_sem=sems[0].at[at], recv_sem=sems[1].at[at], device_id=peer, device_id_type=MESH
    )
    one.start()
    return one


class Stream:
    def __init__(self, places, order, piece, first, rows, refs, sems, base):
        self.places, self.order, self.piece, self.first, self.rows = places, order, piece, first, rows
        self.refs, self.sems, self.base = refs, sems, base
        self.sizes = [places.sizes[d] for d in order]

    def combos(self):
        out = [()]
        for n in self.sizes:
            out = [c + (v,) for c in out for v in range(n)]
        return out

    def piece_at(self, combo, core):
        values = dict(zip(self.order, combo))
        values[len(self.places.sizes) - 1] = core
        where = self.places.place(values)
        if 0 in values:
            where = where + values[0] * (self.places.sizes[1] * self.places.strides[1])
        return pl.ds(window_start(self.piece, where) + self.first, self.rows)

    def start_core(self, source):
        p = self.places
        last = len(p.sizes) - 1
        core = p.mine[last]
        self.copies = []
        for n, combo in enumerate(self.combos()):
            self.copies.append(
                start_copy(source.at[self.piece_at(combo, 1 - core)], self.refs[0].at[n], self.sems, self.base + n, p.peer(last, 1 - core))
            )

    def finish_core(self, source):
        p = self.places
        core = p.mine[len(p.sizes) - 1]
        for n, combo in enumerate(self.combos()):
            self.copies[n].wait()
            self.refs[0][n] = self.refs[0][n] + source[self.piece_at(combo, core), :]

    def blocks(self, i):
        return math.prod(self.sizes[i + 1 :])

    def start(self, i):
        p, digit, size = self.places, self.order[i], self.sizes[i]
        base = self.base + len(self.combos()) + sum(n - 1 for n in self.sizes[:i])
        held = self.refs[i] if i == 0 else self.refs[i].at[0]
        mine = p.mine[digit]
        self.copies = []
        for k in range(1, size):
            value = lax.rem(mine + k, size)
            src = held.at[pl.ds(value * self.blocks(i), self.blocks(i))]
            self.copies.append(start_copy(src, self.refs[i + 1].at[k - 1], self.sems, base + k - 1, p.peer(digit, value)))

    def finish(self, i):
        held = self.refs[i] if i == 0 else self.refs[i].at[0]
        first = self.places.mine[self.order[i]] * self.blocks(i)
        for one in self.copies:
            one.wait()

        def add(n, carry):
            total = held[first + n]
            for k in range(self.sizes[i] - 1):
                total = total + self.refs[i + 1][k, n]
            self.refs[i + 1][0, n] = total
            return carry

        lax.fori_loop(0, self.blocks(i), add, 0)

    def result(self):
        return self.refs[-1][0, 0]

    @staticmethod
    def scratch(sizes, rows):
        refs, count = [vmem(math.prod(sizes), rows, LANES)], math.prod(sizes)
        for i, n in enumerate(sizes):
            refs.append(vmem(n - 1, math.prod(sizes[i + 1 :]), rows, LANES))
            count += n - 1
        return refs, count


def sum_plan(groups, seqs, fus_total, enc_total):
    places = Places(groups, seqs)
    last = len(places.sizes) - 1
    seq_order = list(range(1, last))
    seq_order.sort(key=lambda d: places.sizes[d])
    fus_piece, fus_rows, fus_all = windows(fus_total, groups * seqs)
    enc_piece, enc_rows, enc_all = windows(enc_total, seqs)
    first = fus_rows * 5 // 64 * 8
    streams = [
        ([0] + seq_order, fus_piece, 0, first),
        (seq_order[:1] + [0] + seq_order[1:], fus_piece, first, fus_rows - first),
        (seq_order, enc_piece, 0, enc_rows),
    ]
    return places, streams, fus_rows, fus_all, enc_rows, enc_all


def encoder_forward(
    field_ref, flat,
    lat_ref, xhat_ref, rstd_ref, qkv_ref, p_h, p_l, o_ref, xhat2_ref, rstd2_ref, g_h, g_l, dg_ref, out_ref,
    win_h, win_l, wout_h, wout_l, wup_h, wup_l, wdn_h, wdn_l, wlin_h, wlin_l,
    x, wide, lat, head_ref, send, recv,
):
    g, s = lax.axis_index("group"), lax.axis_index("seq")
    seqs = lax.axis_size("seq")
    before, after = lax.rem(s + seqs - SAMPLES, seqs), lax.rem(s + SAMPLES, seqs)
    barrier = pltpu.get_barrier_semaphore()
    for other in (before, after):
        pl.semaphore_signal(barrier, inc=1, device_id=(g, other), device_id_type=MESH)
    pl.semaphore_wait(barrier, 2)
    halo = start_copy(field_ref.at[pl.ds(0, 3)], head_ref, (send, recv), 0, (g, before))
    for pair, name in (((win_h, win_l), "in"), ((wout_h, wout_l), "out"), ((wup_h, wup_l), "up"), ((wdn_h, wdn_l), "down"), ((wlin_h, wlin_l), "lin")):
        width = ENC_MATS[name][1]

        def store(rows, c, v, pair=pair, width=width):
            last = min(width - c * LANES, LANES)
            put(pair, (rows, slice(c * LANES, c * LANES + last)), v[:, :last])

        unpack_matrix(flat, ENC_AT[name], ENC_MATS[name], store, wide)
    vec = {name: vector(flat, ENC_AT[name], amount) for name, amount in ENC_VECS.items()}
    masks = head_masks(CE)
    halo.wait()
    for r, at, start, amount in encoder_slots():
        x[at : at + amount, :] = (field_ref[r + 3, start : start + amount, :] if r < 3 else head_ref[r - 3, start : start + amount, :])
    wrapped = s // SAMPLES == seqs // SAMPLES - 1
    half = ROWS_E // 2
    upper = lax.broadcasted_iota(jnp.int32, (ROWS_E, ROWS_E), 0) >= half
    right = lax.broadcasted_iota(jnp.int32, (ROWS_E, ROWS_E), 1) >= half
    apart = jnp.where(jnp.logical_and(upper != right, wrapped), 1.0, 0.0)
    apart = jnp.concatenate([apart] * HEADS_E, 0)
    win, wout, wup, wdn, wlin = (win_h, win_l), (wout_h, wout_l), (wup_h, wup_l), (wdn_h, wdn_l), (wlin_h, wlin_l)
    scale = 1.0 / math.sqrt(HEAD)

    def step(i, carry):
        rows = pl.ds(pl.multiple_of(i * 2 * ROWS_E, 2 * ROWS_E), 2 * ROWS_E)
        xv = x[rows, :]
        xhat, rstd = normalize(xv)
        xhat_ref[rows, :] = xhat
        rstd_ref[rows, :] = rstd
        xn = split(xhat * vec["g1"] + vec["s1"])
        full = slice(None)
        qkv = dot3(xn, get(win, (full, full)))
        shift = jnp.concatenate([vec["qb"], jnp.zeros_like(vec["qb"]), vec["vb"]], 1)
        factor = jnp.concatenate([jnp.full((1, CE), scale, F32), jnp.ones((1, 2 * CE), F32)], 1)
        qkv = (qkv + shift) * factor
        qkv_ref[rows, :] = qkv
        parts = []
        for w in range(2):
            one = qkv[w * ROWS_E : (w + 1) * ROWS_E]
            q, k, v = (one[:, j * CE : (j + 1) * CE] for j in range(3))
            qm = split(jnp.concatenate([q * m for m in masks], 0))
            s = dot3(qm, split(k), 1, 1)
            s = jnp.where(apart > 0.5, NEG, s)
            p = split(softmax(s))
            p_h[i * 2 + w] = p[0]
            p_l[i * 2 + w] = p[1]
            parts.append(unstacked(dot3(p, split(v)), masks))
        o = jnp.concatenate(parts, 0)
        o_ref[rows, :] = o
        hidden = xv + dot3(split(o), get(wout, (full, full))) + vec["ob"]
        xhat2, rstd2 = normalize(hidden)
        xhat2_ref[rows, :] = xhat2
        rstd2_ref[rows, :] = rstd2
        hn = split(xhat2 * vec["g2"] + vec["s2"])
        out = hidden + vec["db"]
        for c in range(MLP_E // CHUNK):
            cols = slice(c * CHUNK, (c + 1) * CHUNK)
            u = dot3(hn, get(wup, (full, cols))) + vec["ub"][:, cols]
            g, slope = gelu_parts(u)
            dg_ref[rows, cols] = slope
            g = split(g)
            g_h[rows, cols] = g[0]
            g_l[rows, cols] = g[1]
            out = out + dot3(g, get(wdn, (cols, full)))
        out_ref[rows, :] = out
        lat[rows, :] = dot3(split(out), get(wlin, (full, full))) + vec["lb"]
        return carry

    lax.fori_loop(0, 4, step, 0)
    for r, at, start, amount in encoder_slots():
        lat_ref[r, start : start + amount, :] = lat[at : at + amount, :]


def vmem(*shape, dtype=F32):
    return pltpu.VMEM(shape, dtype)


def pair_of(*shape):
    return [vmem(*shape, dtype=BF16)] * 2


def call(kernel, name, inputs, outs, scratch, number, flops=0, far=()):
    specs = [pl.BlockSpec(memory_space=pl.ANY if n in far else pltpu.VMEM) for n in range(len(inputs))]
    moved = sum(v.size * v.dtype.itemsize for v in list(inputs) + list(outs))
    return pl.pallas_call(
        kernel,
        name=name,
        out_shape=outs,
        in_specs=specs,
        out_specs=[pl.BlockSpec(memory_space=pltpu.VMEM)] * len(outs),
        scratch_shapes=scratch,
        cost_estimate=pl.CostEstimate(flops=flops, bytes_accessed=moved, transcendentals=0),
        compiler_params=pltpu.CompilerParams(collective_id=number, has_side_effects=True, vmem_limit_bytes=VMEM_BYTES),
    )(*inputs)


def sems(count):
    return [pltpu.SemaphoreType.DMA((count,)), pltpu.SemaphoreType.DMA((count,))]


def shape(*dims, dtype=F32):
    return jax.ShapeDtypeStruct(dims, dtype)


def rows_kernel(line_ref, rows_ref):
    rows_ref[...] = line_ref.reshape(*rows_ref.shape)[...]


def rows_of_lanes(line):
    return pl.pallas_call(
        rows_kernel,
        name="rows_of_lanes",
        out_shape=shape(line.size // LANES, LANES),
        compiler_params=pltpu.CompilerParams(vmem_limit_bytes=16 << 20),
    )(line)


def encoder_forward_call(field, flat):
    n = 8 * ROWS_E
    outs = [
        shape(WIN_LAT, 96, CF), shape(n, CE), shape(n, 1), shape(n, 3 * CE),
        shape(8, HEADS_E * ROWS_E, ROWS_E, dtype=BF16), shape(8, HEADS_E * ROWS_E, ROWS_E, dtype=BF16),
        shape(n, CE), shape(n, CE), shape(n, 1), shape(n, MLP_E, dtype=BF16), shape(n, MLP_E, dtype=BF16),
        shape(n, MLP_E), shape(n, CE),
    ]
    scratch = (
        pair_of(CE, 3 * CE) + pair_of(CE, CE) + pair_of(CE, MLP_E) + pair_of(MLP_E, CE) + pair_of(CE, CF)
        + [vmem(n, CE), vmem(5, MLP_E, LANES), vmem(n, CF), vmem(3, 96, CE)] + sems(1)
    )
    return call(encoder_forward, "encoder_forward", [field, flat], outs, scratch, 0, 6 * n * 516096)


def encoder_backward(
    places, plans,
    dfld_ref, flat, fus, tab, xhat_ref, rstd_ref, qkv_ref, p_h, p_l, o_ref, xhat2_ref, rstd2_ref, g_h, g_l, dg_ref, out_ref,
    field_grad, fus_out, enc_out, tab_out,
    grad, dlat_ref, tabs, send, recv, win_h, win_l, wout_h, wout_l, wup_h, wup_l, wdn_h, wdn_l, wlin_h, wlin_l,
    dlat, wide, dout, dout_h, dout_l, dhn, du_h, du_l, hn_h, hn_l, dh_h, dh_l, dqkv_h, dqkv_l, xn_h, xn_l, sums, dx, dback,
    *refs,
):
    places.here()
    g, s = places.g, places.s
    seqs = places.sizes[1] * places.strides[1]
    before, after = lax.rem(s + seqs - SAMPLES, seqs), lax.rem(s + SAMPLES, seqs)
    slot, band = g * seqs + s, s // SAMPLES
    mine = g * SAMPLES + lax.rem(s, SAMPLES)
    owners = [((4 * band + j) // seqs, lax.rem(4 * band + j, seqs)) for j in range(4)]
    givers = [(k // 2, slot // 4 * SAMPLES + k % 2) for k in range(4)]

    def other(pg, ps):
        return jnp.logical_or(pg != g, ps != s)

    barrier = pltpu.get_barrier_semaphore()
    peers = [(1 - g, s), (g, before), (g, after), (1 - g, before), (1 - g, after)]
    for digit, size in enumerate(places.sizes):
        if digit:
            peers += [places.peer(digit, lax.rem(places.mine[digit] + k, size)) for k in range(1, size)]
    for peer in peers:
        pl.semaphore_signal(barrier, inc=1, device_id=peer, device_id_type=MESH)
    for pg, ps in owners + givers:
        @pl.when(other(pg, ps))
        def _(pg=pg, ps=ps):
            pl.semaphore_signal(barrier, inc=1, device_id=(pg, ps), device_id_type=MESH)
    pl.semaphore_wait(barrier, len(peers) + jnp.where(slot // 4 == band, 6, 8))

    columns = pl.ds(pl.multiple_of(g * 48, 48), 48)
    far = [
        start_copy(dfld_ref.at[1 - g, pl.ds(3, 3)], dlat_ref.at[pl.ds(0, 3), columns], (send, recv), 0, (1 - g, s)),
        start_copy(dfld_ref.at[g, pl.ds(0, 3)], dlat_ref.at[pl.ds(3, 3), columns], (send, recv), 1, (g, before)),
        start_copy(dfld_ref.at[1 - g, pl.ds(0, 3)], dlat_ref.at[pl.ds(3, 3), columns], (send, recv), 2, (1 - g, before)),
    ]
    dlat_ref[0:3, columns, :] = dfld_ref[g, 3:6]
    streams, at, base = [], 0, 8
    for order, piece, first, rows in plans:
        own, count = Stream.scratch([places.sizes[d] for d in order], rows)
        streams.append(Stream(places, order, piece, first, rows, refs[at : at + len(own)], (send, recv), base))
        at, base = at + len(own), base + count
    first_part, second_part, enc_part = streams
    first_part.start_core(fus)
    second_part.start_core(fus)

    def give(j, pg, ps):
        return pltpu.make_async_remote_copy(
            src_ref=tab.at[j], dst_ref=tabs.at[mine], send_sem=send.at[4 + j], recv_sem=recv.at[4 + mine],
            device_id=(pg, ps), device_id_type=MESH,
        )

    for j, (pg, ps) in enumerate(owners):
        @pl.when(other(pg, ps))
        def _(j=j, pg=pg, ps=ps):
            give(j, pg, ps).start()

        @pl.when(jnp.logical_not(other(pg, ps)))
        def _(j=j):
            tabs[mine] = tab[j]

    win, wout, wup, wdn, wlin = (win_h, win_l), (wout_h, wout_l), (wup_h, wup_l), (wdn_h, wdn_l), (wlin_h, wlin_l)
    for pair, name in ((win, "in"), (wout, "out"), (wup, "up"), (wdn, "down"), (wlin, "lin")):
        width = ENC_MATS[name][1]

        def store(rows, c, v, pair=pair, width=width):
            last = min(width - c * LANES, LANES)
            put(pair, (rows, slice(c * LANES, c * LANES + last)), v[:, :last])

        unpack_matrix(flat, ENC_AT[name], ENC_MATS[name], store, wide)
    vec = {name: vector(flat, ENC_AT[name], ENC_VECS[name]) for name in ("g1", "s1", "g2", "s2")}
    masks = head_masks(CE)
    full = slice(None)
    scale = 1.0 / math.sqrt(HEAD)
    first_part.finish_core(fus)
    second_part.finish_core(fus)
    for one in far:
        one.wait()
    first_part.start(0)
    second_part.start(0)
    for r, at, start, amount in encoder_slots():
        dlat[at : at + amount, :] = dlat_ref[r, start : start + amount, :]
    dl = split(dlat[...])
    put_vector(grad, ENC_AT["lb"], column_sum(dlat[...]))
    d = dot3(dl, get(wlin, (full, full)), 1, 1)
    dout[...] = d
    put((dout_h, dout_l), (full, full), d)
    put_vector(grad, ENC_AT["db"], column_sum(d))
    dw = dot3(split(out_ref[...]), dl, 0, 0)
    for c in range(3):
        grad[pl.ds(ENC_AT["lin"] + c, CE, stride=3), :] = dw[:, c * LANES : (c + 1) * LANES]
    xhat2 = xhat2_ref[...]
    put((hn_h, hn_l), (full, full), xhat2 * vec["g2"] + vec["s2"])
    for c in range(MLP_E // CHUNK):
        cols = slice(c * CHUNK, (c + 1) * CHUNK)
        do = (dout_h[...], dout_l[...])
        du = dot3(do, get(wdn, (cols, full)), 1, 1) * dg_ref[:, cols]
        put_vector(grad, ENC_AT["ub"] + c * CHUNK, column_sum(du))
        du = split(du)
        part = dot3(du, get(wup, (full, cols)), 1, 1)
        dhn[...] = part if c == 0 else dhn[...] + part
        dw = dot3((hn_h[...], hn_l[...]), du, 0, 0)
        for t in range(2):
            grad[pl.ds(ENC_AT["up"] + 2 * c + t, CE, stride=6), :] = dw[:, t * LANES : (t + 1) * LANES]
        dw = dot3((g_h[:, cols], g_l[:, cols]), do, 0, 0)
        put_tiles(wide, slice(c * CHUNK, (c + 1) * CHUNK), dw)
    pack_matrix(grad, ENC_AT["down"], ENC_MATS["down"], wide)
    dv = dhn[...]
    put_vector(grad, ENC_AT["g2"], column_sum(dv * xhat2))
    put_vector(grad, ENC_AT["s2"], column_sum(dv))
    d = dout[...] + normalize_back(dv, xhat2, rstd2_ref[...], vec["g2"])
    dout[...] = d
    put((dh_h, dh_l), (full, full), d)
    put_vector(grad, ENC_AT["ob"], column_sum(d))
    dw = dot3(split(o_ref[...]), (dh_h[...], dh_l[...]), 0, 0)
    put_tiles(wide, slice(0, CE), dw)
    pack_matrix(grad, ENC_AT["out"], ENC_MATS["out"], wide)
    sums[...] = jnp.zeros_like(sums)

    def step(i, carry):
        rows = pl.ds(pl.multiple_of(i * 2 * ROWS_E, 2 * ROWS_E), 2 * ROWS_E)
        do = dot3((dh_h[rows, :], dh_l[rows, :]), get(wout, (full, full)), 1, 1)
        parts = []
        for w in range(2):
            one = qkv_ref[pl.ds(pl.multiple_of(i * 2 * ROWS_E, 2 * ROWS_E) + w * ROWS_E, ROWS_E), :]
            q, k, v = (one[:, j * CE : (j + 1) * CE] for j in range(3))
            dow = do[w * ROWS_E : (w + 1) * ROWS_E]
            dom = split(jnp.concatenate([dow * m for m in masks], 0))
            qm = split(jnp.concatenate([q * m for m in masks], 0))
            p = (p_h[i * 2 + w], p_l[i * 2 + w])
            dp = dot3(dom, split(v), 1, 1)
            pf = p[0].astype(F32) + p[1].astype(F32)
            t = pf * dp
            ds = split(t - pf * jnp.sum(t, 1, keepdims=True))
            dq = unstacked(dot3(ds, split(k)), masks) * scale
            dk = dot3(ds, qm, 0, 0)
            dvv = dot3(p, dom, 0, 0)
            parts.append(jnp.concatenate([dq, dk, dvv], 1))
        dqkv = jnp.concatenate(parts, 0)
        sums[0:1, :] = sums[0:1, :] + column_sum(dqkv)
        dqkv = split(dqkv)
        dqkv_h[rows, :] = dqkv[0]
        dqkv_l[rows, :] = dqkv[1]
        xhat = xhat_ref[rows, :]
        put((xn_h, xn_l), (rows, full), xhat * vec["g1"] + vec["s1"])
        dxn = dot3(dqkv, get(win, (full, full)), 1, 1)
        sums[1:2, 0:CE] = sums[1:2, 0:CE] + column_sum(dxn * xhat)
        sums[2:3, 0:CE] = sums[2:3, 0:CE] + column_sum(dxn)
        dx[rows, :] = dout[rows, :] + normalize_back(dxn, xhat, rstd_ref[rows, :], vec["g1"])
        return carry

    lax.fori_loop(0, 2, step, 0)
    second_part.finish(0)
    second_part.start(1)
    lax.fori_loop(2, 4, step, 0)
    for r, at, start, amount in encoder_slots():
        if r < 3:
            field_grad[r + 3, start : start + amount, :] = dx[at : at + amount, :]
        else:
            dback[r - 3, start : start + amount, :] = dx[at : at + amount, :]
    back = start_copy(dback, field_grad.at[pl.ds(0, 3)], (send, recv), 3, (g, after))
    put_vector(grad, ENC_AT["qb"], sums[0:1, 0:CE])
    put_vector(grad, ENC_AT["vb"], sums[0:1, 2 * CE : 3 * CE])
    put_vector(grad, ENC_AT["g1"], sums[1:2, 0:CE])
    put_vector(grad, ENC_AT["s1"], sums[2:3, 0:CE])
    dw = dot3((xn_h[...], xn_l[...]), (dqkv_h[...], dqkv_l[...]), 0, 0)
    put_tiles(wide, slice(0, CE), dw)
    pack_matrix(grad, ENC_AT["in"], ENC_MATS["in"], wide)
    enc_part.start_core(grad)
    first_part.finish(0)
    first_part.start(1)
    enc_part.finish_core(grad)
    enc_part.start(0)
    second_part.finish(1)
    second_part.start(2)
    first_part.finish(1)
    first_part.start(2)
    enc_part.finish(0)
    enc_part.start(1)
    back.wait()
    for j, (pg, ps) in enumerate(owners):
        @pl.when(other(pg, ps))
        def _(j=j, pg=pg, ps=ps):
            give(j, pg, ps).wait_send()
    for k, (pg, ps) in enumerate(givers):
        @pl.when(other(pg, ps))
        def _(k=k, pg=pg, ps=ps):
            pltpu.make_async_remote_copy(
                src_ref=tab.at[0], dst_ref=tabs.at[k], send_sem=send.at[4], recv_sem=recv.at[4 + k],
                device_id=(pg, ps), device_id_type=MESH,
            ).wait_recv()
    tab_out[...] = (tabs[0] + tabs[1]) + (tabs[2] + tabs[3])
    for i in range(2, len(second_part.order)):
        second_part.finish(i)
        first_part.finish(i)
        if i + 1 < len(second_part.order):
            second_part.start(i + 1)
            first_part.start(i + 1)
    for i in range(1, len(enc_part.order)):
        enc_part.finish(i)
        if i + 1 < len(enc_part.order):
            enc_part.start(i + 1)
    split_at = first_part.rows
    fus_out[0:split_at, :] = first_part.result()
    fus_out[split_at : split_at + second_part.rows, :] = second_part.result()
    enc_out[...] = enc_part.result()


def encoder_backward_call(dfld, flat, fus, tab, saved, groups, seqs, fus_total):
    n = 8 * ROWS_E
    places, plans, fus_rows, _, enc_rows, enc_all = sum_plan(groups, seqs, fus_total, flat.size)
    refs, count = [], 8
    for order, piece, first, rows in plans:
        own, more = Stream.scratch([places.sizes[d] for d in order], rows)
        refs += own
        count += more
    scratch = (
        [vmem(enc_all, LANES), vmem(WIN_LAT, 96, CF), vmem(*tab.shape)] + sems(count)
        + pair_of(CE, 3 * CE) + pair_of(CE, CE) + pair_of(CE, MLP_E) + pair_of(MLP_E, CE) + pair_of(CE, CF)
        + [vmem(n, CF), vmem(5, MLP_E, LANES), vmem(n, CE)] + pair_of(n, CE) + [vmem(n, CE)] + pair_of(n, CHUNK)
        + pair_of(n, CE) + pair_of(n, CE) + pair_of(n, 3 * CE) + pair_of(n, CE) + [vmem(8, 3 * CE), vmem(n, CE), vmem(3, 96, CE)]
        + refs
    )
    return call(
        partial(encoder_backward, places, plans), "encoder_backward", [dfld, flat, fus, tab] + list(saved),
        [shape(WIN_LAT, 96, CE), shape(fus_rows, LANES), shape(enc_rows, LANES), shape(*tab.shape[1:])], scratch, 2, 12 * n * 516096,
    )


def merging(
    lat_ref, cot_ref, flat, tab_ref, base_ref,
    out_ref, dx_ref, grad, dtab_ref,
    fld_ref, send, recv, lines, bands, bands_sem,
    win_h, win_l, wout_h, wout_l, wup_h, wup_l, wdn_h, wdn_l,
    bias, dbias, x, xhat1, rstd1, xn_h, xn_l, q_h, q_l, k_h, k_l, v_h, v_l, p_h, p_l, o_h, o_l,
    xhat2, rstd2, hn_h, hn_l, acc, dhn, dy, dy_h, dy_l, g_h, g_l, du_h, du_l, dh_h, dh_l, dqkv_h, dqkv_l, sums,
):
    win, wout, wup, wdn = (win_h, win_l), (wout_h, wout_l), (wup_h, wup_l), (wdn_h, wdn_l)
    full = slice(None)
    chunks = MLP_F // CHUNK
    g, s = lax.axis_index("group"), lax.axis_index("seq")
    seqs = lax.axis_size("seq")
    before, after = lax.rem(s + seqs - SAMPLES, seqs), lax.rem(s + SAMPLES, seqs)
    band = s // SAMPLES
    picked = pltpu.make_async_copy(tab_ref.at[:, pl.ds(pl.multiple_of(band // 8 * 8, 8), 8)], bands, bands_sem)
    picked.start()
    barrier = pltpu.get_barrier_semaphore()
    for peer in ((1 - g, s), (g, before), (g, after), (1 - g, before), (1 - g, after)):
        pl.semaphore_signal(barrier, inc=1, device_id=peer, device_id_type=MESH)
    pl.semaphore_wait(barrier, 5)

    def half(one):
        return pl.ds(pl.multiple_of(one * 48, 48), 48)

    far = [
        start_copy(lat_ref.at[pl.ds(0, 3), half(1 - g)], fld_ref.at[g, pl.ds(3, 3)], (send, recv), 0, (1 - g, s)),
        start_copy(lat_ref.at[pl.ds(3, 3), half(g)], fld_ref.at[g, pl.ds(0, 3)], (send, recv), 1, (g, after)),
        start_copy(lat_ref.at[pl.ds(3, 3), half(1 - g)], fld_ref.at[g, pl.ds(0, 3)], (send, recv), 2, (1 - g, after)),
    ]
    fld_ref[g, 3:6] = lat_ref[0:3, half(g), :]
    scale = 1.0 / math.sqrt(HEAD)

    def store(pair):
        def one(rows, c, v):
            put(pair, (rows, slice(c * LANES, (c + 1) * LANES)), v)
        return one

    def store_up(rows, c, v):
        put(wup, (c // 2, full, slice(c % 2 * LANES, (c % 2 + 1) * LANES)), v)

    def store_down(rows, c, v):
        for j in range(chunks):
            put(wdn, (j, full, slice(c * LANES, (c + 1) * LANES)), v[j * CHUNK : (j + 1) * CHUNK])

    unpack_matrix(flat, FUS_AT["in"], FUS_MATS["in"], store(win), None)
    unpack_matrix(flat, FUS_AT["out"], FUS_MATS["out"], store(wout), None)
    unpack_matrix(flat, FUS_AT["up"], FUS_MATS["up"], store_up, None)
    unpack_matrix(flat, FUS_AT["down"], FUS_MATS["down"], store_down, None)
    vec = {name: vector(flat, FUS_AT[name], amount) for name, amount in FUS_VECS.items()}
    masks = head_masks(LANES)

    spots = jnp.where(lax.broadcasted_iota(jnp.int32, (TAB_PAD, 2 * LANES), 0) == base_ref[...], 1.0, 0.0).astype(BF16)
    picked.wait()
    for h in range(HEADS_F):
        lines[h : h + 1, :] = bands[h, pl.ds(lax.rem(band, 8), 1), :]
    pad = jnp.zeros((HEADS_F, TAB_PAD - PAIRS * SPAN), F32)
    table = []
    for z in range(WIN_MOD):
        for r in range(WIN_LAT):
            at = [((z * WIN_MOD + y) * WIN_LAT * WIN_LAT + r * WIN_LAT) * SPAN for y in range(WIN_MOD)]
            one = jnp.concatenate([lines[0:HEADS_F, t : t + WIN_LAT * SPAN] for t in at] + [pad], 1)
            table.append(jnp.concatenate([one, jnp.zeros((16 - HEADS_F, TAB_PAD), F32)], 0))
    table = jnp.concatenate(table, 0)
    for w in range(WIN_LON):
        turned = pltpu.roll(table, TAB_PAD - w, 1) if w else table
        hi, lo = split(turned)
        rest = (turned - hi.astype(F32) - lo.astype(F32)).astype(BF16)
        one = dot(hi, spots) + (dot(lo, spots) + dot(rest, spots))
        for n in range(PAIRS):
            for c in range(2):
                bias[c, pl.ds(n * WIN_LON + w, HEADS_F, stride=ROWS_F), :] = one[n * 16 : n * 16 + HEADS_F, c * LANES : (c + 1) * LANES]
    dbias[...] = jnp.zeros_like(dbias)

    for one in far:
        one.wait()
    for z, r, at, start in merging_slots():
        x[at : at + WIN_LON, :] = fld_ref[z, r, start : start + WIN_LON, :]
        dy[at : at + WIN_LON, :] = cot_ref[z, r, start : start + WIN_LON, :]

    def rows_of(i):
        return pl.ds(pl.multiple_of(i * ROWS_F, ROWS_F), ROWS_F)

    def forward(i, carry):
        rows = rows_of(i)
        xv = x[rows, :]
        xhat, rstd = normalize(xv)
        xhat1[rows, :] = xhat
        rstd1[rows, :] = rstd
        xn = split(xhat * vec["g1"] + vec["s1"])
        xn_h[rows, :] = xn[0]
        xn_l[rows, :] = xn[1]
        for j, (pair, shift) in enumerate((((q_h, q_l), vec["qb"]), ((k_h, k_l), None), ((v_h, v_l), vec["vb"]))):
            one = dot3(xn, get(win, (full, slice(j * CF, (j + 1) * CF))))
            if shift is not None:
                one = one + shift
            if j == 0:
                one = one * scale
            put(pair, (rows, full), one)
        for g in range(3):
            cols = slice(g * LANES, (g + 1) * LANES)
            qm = stacked((q_h[rows, cols], q_l[rows, cols]), masks)
            some = slice(g * 4 * ROWS_F, (g + 1) * 4 * ROWS_F)
            s = wide_nt(qm, (k_h[rows, cols], k_l[rows, cols])) + get_tiles(bias, some, ROWS_F)
            p = split(softmax(s))
            p_h[i * 3 + g] = p[0]
            p_l[i * 3 + g] = p[1]
            o = unstacked(wide_n(p, (v_h[rows, cols], v_l[rows, cols])), masks)
            put((o_h, o_l), (rows, cols), o)
        hidden = xv + dot3((o_h[rows, :], o_l[rows, :]), get(wout, (full, full))) + vec["ob"]
        xh2, rstd = normalize(hidden)
        xhat2[rows, :] = xh2
        rstd2[rows, :] = rstd
        put((hn_h, hn_l), (rows, full), xh2 * vec["g2"] + vec["s2"])
        acc[rows, :] = hidden + vec["db"]
        put((dy_h, dy_l), (rows, full), dy[rows, :])
        return carry

    lax.fori_loop(0, 4, forward, 0)
    dhn[...] = jnp.zeros_like(dhn)
    for c in range(chunks):
        sums[8:9, c * CHUNK : (c + 1) * CHUNK] = vec["ub"][:, c * CHUNK : (c + 1) * CHUNK]

    def feed(c, carry):
        up = (wup_h[c], wup_l[c])
        down = (wdn_h[c], wdn_l[c])
        cols = pl.ds(pl.multiple_of(c * CHUNK, CHUNK), CHUNK)
        shift = sums[8:9, cols]

        def part(i, total):
            rows = rows_of(i)
            u = dot3((hn_h[rows, :], hn_l[rows, :]), up) + shift
            g, slope = gelu_parts(u)
            g = split(g)
            g_h[rows, :] = g[0]
            g_l[rows, :] = g[1]
            acc[rows, :] = acc[rows, :] + dot3(g, down)
            du = dot3((dy_h[rows, :], dy_l[rows, :]), down, 1, 1) * slope
            total = total + column_sum(du)
            du = split(du)
            du_h[rows, :] = du[0]
            du_l[rows, :] = du[1]
            dhn[rows, :] = dhn[rows, :] + dot3(du, up, 1, 1)
            return total

        sums[9:10, cols] = lax.fori_loop(0, 4, part, jnp.zeros((1, CHUNK), F32))
        dw = dot3((hn_h[...], hn_l[...]), (du_h[...], du_l[...]), 0, 0)
        for t in range(2):
            grad[pl.ds(FUS_AT["up"] + 2 * c + t, CF, stride=12), :] = dw[:, t * LANES : (t + 1) * LANES]
        dw = dot3((g_h[...], g_l[...]), (dy_h[...], dy_l[...]), 0, 0)
        for t in range(3):
            grad[pl.ds(FUS_AT["down"] + 3 * CHUNK * c + t, CHUNK, stride=3), :] = dw[:, t * LANES : (t + 1) * LANES]
        return carry

    lax.fori_loop(0, chunks, feed, 0)
    put_vector(grad, FUS_AT["ub"], sums[9:10, :])
    sums[0:8, :] = jnp.zeros((8, MLP_F), F32)

    def backward(i, carry):
        rows = rows_of(i)
        dv = dhn[rows, :]
        xh2 = xhat2[rows, :]
        d = dy[rows, :]
        sums[0:1, 0:CF] = sums[0:1, 0:CF] + column_sum(d)
        sums[1:2, 0:CF] = sums[1:2, 0:CF] + column_sum(dv * xh2)
        sums[2:3, 0:CF] = sums[2:3, 0:CF] + column_sum(dv)
        dh = d + normalize_back(dv, xh2, rstd2[rows, :], vec["g2"])
        sums[3:4, 0:CF] = sums[3:4, 0:CF] + column_sum(dh)
        dhs = split(dh)
        dh_h[rows, :] = dhs[0]
        dh_l[rows, :] = dhs[1]
        do = split(dot3(dhs, get(wout, (full, full)), 1, 1))
        for g in range(3):
            cols = slice(g * LANES, (g + 1) * LANES)
            dom = stacked((do[0][:, cols], do[1][:, cols]), masks)
            qm = stacked((q_h[rows, cols], q_l[rows, cols]), masks)
            p = (p_h[i * 3 + g], p_l[i * 3 + g])
            dp = wide_nt(dom, (v_h[rows, cols], v_l[rows, cols]))
            pf = p[0].astype(F32) + p[1].astype(F32)
            t = pf * dp
            ds = t - pf * jnp.sum(t, 1, keepdims=True)
            some = slice(g * 4 * ROWS_F, (g + 1) * 4 * ROWS_F)
            for c in range(2):
                one = ds[:, c * LANES : (c + 1) * LANES]
                dbias[c, some, 0 : one.shape[1]] = dbias[c, some, 0 : one.shape[1]] + one
            ds = split(ds)
            dq = unstacked(wide_n(ds, (k_h[rows, cols], k_l[rows, cols])), masks) * scale
            dk = wide_n(ds, qm, 0)
            dvv = wide_n(p, dom, 0)
            for j, one in enumerate((dq, dk, dvv)):
                at = slice(j * CF + g * LANES, j * CF + (g + 1) * LANES)
                put((dqkv_h, dqkv_l), (rows, at), one)
                if j != 1:
                    sums[4 + j // 2 : 5 + j // 2, cols] = sums[4 + j // 2 : 5 + j // 2, cols] + column_sum(one)
        xhat = xhat1[rows, :]
        dxn = dot3((dqkv_h[rows, :], dqkv_l[rows, :]), get(win, (full, full)), 1, 1)
        sums[6:7, 0:CF] = sums[6:7, 0:CF] + column_sum(dxn * xhat)
        sums[7:8, 0:CF] = sums[7:8, 0:CF] + column_sum(dxn)
        x[rows, :] = dh + normalize_back(dxn, xhat, rstd1[rows, :], vec["g1"])
        return carry

    lax.fori_loop(0, 4, backward, 0)
    for j, name in enumerate(("db", "g2", "s2", "ob", "qb", "vb", "g1", "s1")):
        put_vector(grad, FUS_AT[name], sums[j : j + 1, 0:CF])
    for c in range(3):
        cols = slice(c * CF, (c + 1) * CF)
        dw = dot3((xn_h[...], xn_l[...]), (dqkv_h[:, cols], dqkv_l[:, cols]), 0, 0)
        for t in range(3):
            grad[pl.ds(FUS_AT["in"] + 3 * c + t, CF, stride=9), :] = dw[:, t * LANES : (t + 1) * LANES]
    dw = dot3((o_h[...], o_l[...]), (dh_h[...], dh_l[...]), 0, 0)
    for t in range(3):
        grad[pl.ds(FUS_AT["out"] + t, CF, stride=3), :] = dw[:, t * LANES : (t + 1) * LANES]
    total = jnp.zeros((PAIRS * 16, TAB_PAD), F32)
    blank = jnp.zeros((16 - HEADS_F, 2 * LANES), F32)
    for w in range(WIN_LON):
        rows = []
        for n in range(PAIRS):
            rows.append(jnp.concatenate([dbias[c, pl.ds(n * WIN_LON + w, HEADS_F, stride=ROWS_F), :] for c in range(2)], 1))
            rows.append(blank)
        hi, lo = split(jnp.concatenate(rows, 0))
        one = dot(hi, spots, 1, 1) + dot(lo, spots, 1, 1)
        total = total + (pltpu.roll(one, w, 1) if w else one)
    for z in range(WIN_MOD):
        for r in range(WIN_LAT):
            n = z * WIN_LAT + r
            for y in range(WIN_MOD):
                at = ((z * WIN_MOD + y) * WIN_LAT * WIN_LAT + r * WIN_LAT) * SPAN
                lines[0:HEADS_F, at : at + WIN_LAT * SPAN] = total[n * 16 : n * 16 + HEADS_F, y * WIN_LAT * SPAN : (y + 1) * WIN_LAT * SPAN]
    for j in range(4):
        dtab_ref[j, 0:3, :] = lines[3 * j : 3 * j + 3, :]
    for z, r, at, start in merging_slots():
        out_ref[z, r, start : start + WIN_LON, :] = acc[at : at + WIN_LON, :]
        dx_ref[z, r, start : start + WIN_LON, :] = x[at : at + WIN_LON, :]


def merging_call(latent, cotangent, flat, table, grad_rows):
    n = 4 * ROWS_F
    m = HEADS_F * ROWS_F
    t = np.arange(ROWS_F)
    base = np.full((1, 2 * LANES), -1, np.int32)
    base[0, :ROWS_F] = t // WIN_LON * SPAN + WIN_LON - 1 - t % WIN_LON
    base = jnp.asarray(base)
    scratch = (
        [vmem(*cotangent.shape)] + sems(3) + [vmem(16, table.shape[2]), vmem(HEADS_F, 8, table.shape[2]), pltpu.SemaphoreType.DMA] + pair_of(CF, 3 * CF) + pair_of(CF, CF) + pair_of(6, CF, CHUNK) + pair_of(6, CHUNK, CF)
        + [vmem(2, m, LANES), vmem(2, m, LANES), vmem(n, CF), vmem(n, CF), vmem(n, 1)]
        + pair_of(n, CF) + pair_of(n, CF) + pair_of(n, CF) + pair_of(n, CF) + pair_of(12, 4 * ROWS_F, ROWS_F) + pair_of(n, CF)
        + [vmem(n, CF), vmem(n, 1)] + pair_of(n, CF) + [vmem(n, CF), vmem(n, CF), vmem(n, CF)] + pair_of(n, CF)
        + pair_of(n, CHUNK) + pair_of(n, CHUNK) + pair_of(n, CF) + pair_of(n, 3 * CF) + [vmem(16, MLP_F)]
    )
    outs = [shape(*cotangent.shape), shape(*cotangent.shape), shape(grad_rows, LANES), shape(4, 3, table.shape[2])]
    return call(merging, "merging", [latent, cotangent, flat, table, base], outs, scratch, 1, 18 * n * 1769472, (3,))


def own_piece(block, piece, d):
    return lax.dynamic_slice_in_dim(block.reshape(-1), piece * d - piece * d // 1024 * 1024, piece)


def update(params, grads, momentum, average, rate):
    momentum_new = MOMENTUM_DECAY * momentum + grads
    params_new = params - rate * (grads + MOMENTUM_DECAY * momentum_new)
    average_new = AVERAGE_DECAY * average + (1.0 - AVERAGE_DECAY) * params_new
    return (params_new, momentum_new, average_new)


def shards(
    tokens,
    cotangent,
    enc_params,
    enc_momentum,
    enc_average,
    fus_params,
    fus_momentum,
    fus_average,
    earth_bias,
    bias_momentum,
    bias_average,
):
    field = tokens[0, 0]
    row_count, col_count, feat_width = field.shape
    seq_count = lax.axis_size("seq")
    group_count = lax.axis_size("group")
    band_count = seq_count // SAMPLES
    place = lax.axis_index("seq")
    mine = lax.axis_index("group")
    fus_flat = fus_params.reshape(-1, LANES)
    plan = sum_plan(group_count, seq_count, fus_params.size, enc_params.size)
    enc_flat = rows_of_lanes(enc_params)
    latent, *saved = encoder_forward_call(field, enc_flat)
    merged, fields_grad, fus_local, table_grad = merging_call(
        latent, cotangent[:, 0, 0], fus_flat, earth_bias.transpose(1, 0, 2), plan[3]
    )
    field_grad, fus_block, enc_block, tab_block = encoder_backward_call(
        fields_grad, enc_flat, fus_local, table_grad, saved, group_count, seq_count, fus_params.size
    )
    slot = mine * seq_count + place
    fus_grad = own_piece(fus_block, fus_params.size // (group_count * seq_count), slot)
    enc_grad = own_piece(enc_block, enc_params.size // seq_count, place)
    bias_grad = tab_block.reshape(-1)
    enc_piece = enc_grad.shape[0]
    enc_own = lax.dynamic_slice_in_dim(enc_params[0], place * enc_piece, enc_piece)
    fus_piece = fus_grad.shape[0]
    fus_own = lax.dynamic_slice_in_dim(fus_params, slot * fus_piece, fus_piece)
    bias_piece = bias_grad.shape[0]
    bias_own = lax.dynamic_slice_in_dim(earth_bias.reshape(-1), slot * bias_piece, bias_piece)
    lat_total = band_count * row_count
    enc_new, enc_momentum_new, enc_average_new = update(
        enc_own,
        enc_grad,
        enc_momentum[0],
        enc_average[0],
        1.0 / math.sqrt(CE * SAMPLES * lat_total * col_count),
    )
    fus_new, fus_momentum_new, fus_average_new = update(
        fus_own,
        fus_grad,
        fus_momentum,
        fus_average,
        1.0 / math.sqrt(CF * group_count * SAMPLES * lat_total * col_count),
    )
    bias_new, bias_momentum_new, bias_average_new = update(
        bias_own,
        bias_grad,
        bias_momentum,
        bias_average,
        2.0 / math.sqrt(SAMPLES * col_count / WIN_LON),
    )
    return (
        merged[:, None, None],
        field_grad[None, None],
        enc_grad[None],
        enc_new[None],
        enc_momentum_new[None],
        enc_average_new[None],
        fus_grad,
        fus_new,
        fus_momentum_new,
        fus_average_new,
        bias_grad,
        bias_new,
        bias_momentum_new,
        bias_average_new,
    )


def solution(mesh):
    both = P(("group", "seq"))
    rows = P("group", "seq")
    merged = P(None, "seq", "group", None, None, None)
    tokens = P("group", "seq", None, None, None)
    return jax.shard_map(
        shards,
        mesh=mesh,
        in_specs=(tokens, merged, P("group", None), rows, rows, P(), both, both, P(), both, both),
        out_specs=(merged, tokens, rows, rows, rows, rows) + (both,) * 8,
        check_vma=False,
    )
```

```python
from functools import partial
import math

import jax
import jax.numpy as jnp
import numpy as np
from jax import lax
from jax.experimental import pallas as pl
from jax.experimental.pallas import tpu as pltpu
from jax.sharding import PartitionSpec as P

CE = 192
CF = 384
HEADS_E = 6
HEADS_F = 12
MLP_E = 768
MLP_F = 1536
WIN_LAT = 6
WIN_LON = 12
WIN_MOD = 2
SAMPLES = 2
HEAD = 32
CHUNK = 256
FCH = 384
LANES = 128
ROWS_E = WIN_LAT * WIN_LON
ROWS_F = WIN_MOD * ROWS_E
SPAN = 2 * WIN_LON - 1
PAIRS = WIN_MOD * WIN_LAT
TAB_PAD = 384
EPS = 1e-05
NEG = -1000000000.0
VMEM_BYTES = 61 << 20

MOMENTUM_DECAY = 0.9
AVERAGE_DECAY = 0.99

F32 = jnp.float32
BF16 = jnp.bfloat16

ENC_MATS = {"in": (CE, 3 * CE), "out": (CE, CE), "up": (CE, MLP_E), "down": (MLP_E, CE), "lin": (CE, CF)}
ENC_VECS = {"g1": CE, "s1": CE, "qb": CE, "vb": CE, "ob": CE, "g2": CE, "s2": CE, "ub": MLP_E, "db": CE, "lb": CF}
FUS_MATS = {"in": (CF, 3 * CF), "out": (CF, CF), "up": (CF, MLP_F), "down": (MLP_F, CF)}
FUS_VECS = {"g1": CF, "s1": CF, "qb": CF, "vb": CF, "ob": CF, "g2": CF, "s2": CF, "ub": MLP_F, "db": CF}


def offsets(mats, vecs):
    places, at = {}, 0
    for name, shape in mats.items():
        places[name] = at // LANES
        at += shape[0] * shape[1]
    for name, amount in vecs.items():
        places[name] = at
        at += amount
    return places


ENC_AT = offsets(ENC_MATS, ENC_VECS)
FUS_AT = offsets(FUS_MATS, FUS_VECS)


def split(v):
    hi = v.astype(BF16)
    return hi, (v - hi.astype(F32)).astype(BF16)


def dot(a, b, ca=1, cb=0):
    return lax.dot_general(a, b, (((ca,), (cb,)), ((), ())), preferred_element_type=F32)


def dot3(a, b, ca=1, cb=0):
    return dot(a[0], b[0], ca, cb) + (dot(a[0], b[1], ca, cb) + dot(a[1], b[0], ca, cb))


def left3(a, axis=1):
    return jnp.concatenate([a[0], a[0], a[1]], axis)


def right3(b, axis=0):
    return jnp.concatenate([b[0], b[1], b[0]], axis)


def deep3(a, b, ca=1, cb=0):
    return dot(left3(a, ca), right3(b, cb), ca, cb)


def put(refs, index, v):
    hi, lo = split(v)
    refs[0][index] = hi
    refs[1][index] = lo


def get(refs, index):
    return refs[0][index], refs[1][index]


def half_lanes():
    return lax.broadcasted_iota(jnp.int32, (1, LANES), 1) < LANES // 2


def turn(v):
    return pltpu.roll(v, LANES // 2, 1)


def vector(flat, at, amount):
    tiles = []
    for c in range(-(-amount // LANES)):
        row, lane = divmod(at + c * LANES, LANES)
        one = flat[row : row + 1, :]
        if lane:
            one = turn(one)
            if c * LANES + LANES // 2 < amount:
                one = jnp.where(half_lanes(), one, turn(flat[row + 1 : row + 2, :]))
        tiles.append(one)
    return jnp.concatenate(tiles, 1)[:, :amount] if len(tiles) > 1 else tiles[0][:, :amount]


def put_vector(flat, at, v):
    amount = v.shape[1]
    if at % LANES == 0 and amount % LANES == 0:
        for c in range(amount // LANES):
            flat[at // LANES + c : at // LANES + c + 1, :] = v[:, c * LANES : (c + 1) * LANES]
        return
    half = LANES // 2
    for c in range(amount // half):
        row, lane = divmod(at + c * half, LANES)
        flat[row : row + 1, lane : lane + half] = v[:, c * half : (c + 1) * half]


def unpack_matrix(flat, at, shape, store, scratch):
    rows, width = shape
    if width % LANES == 0:
        n = width // LANES
        for c in range(n):
            store(slice(0, rows), c, flat[pl.ds(at + c, rows, stride=n), :])
        return
    pairs, n, full = rows // 2, 2 * width // LANES, width // LANES
    low = half_lanes()
    for c in range(full + 1):
        scratch[c, pl.ds(0, pairs, stride=2), :] = flat[pl.ds(at + c, pairs, stride=n), :]
        odd = turn(flat[pl.ds(at + full + c, pairs, stride=n), :])
        if c < full:
            odd = jnp.where(low, odd, turn(flat[pl.ds(at + full + c + 1, pairs, stride=n), :]))
        scratch[c, pl.ds(1, pairs, stride=2), :] = odd
    for c in range(full + 1):
        store(slice(0, rows), c, scratch[c, 0:rows, :])


def pack_matrix(flat, at, shape, source):
    rows, width = shape
    pairs, n, full = rows // 2, 2 * width // LANES, width // LANES
    low = half_lanes()

    def tile(odd, c):
        return source[c, pl.ds(odd, pairs, stride=2), :]

    for c in range(full):
        flat[pl.ds(at + c, pairs, stride=n), :] = tile(0, c)
        flat[pl.ds(at + full + 1 + c, pairs, stride=n), :] = jnp.where(low, turn(tile(1, c)), turn(tile(1, c + 1)))
    flat[pl.ds(at + full, pairs, stride=n), :] = jnp.where(low, tile(0, full), turn(tile(1, 0)))


def put_tiles(ref, rows, v):
    for c in range(-(-v.shape[1] // LANES)):
        one = v[:, c * LANES : (c + 1) * LANES]
        ref[c, rows, 0 : one.shape[1]] = one


def get_tiles(ref, rows, width):
    tiles = [ref[c, rows, 0 : min(width - c * LANES, LANES)] for c in range(-(-width // LANES))]
    return jnp.concatenate(tiles, 1)


def normalize(x):
    center = x - jnp.mean(x, 1, keepdims=True)
    scale = lax.rsqrt(jnp.mean(center * center, 1, keepdims=True) + EPS)
    return center * scale, scale


def normalize_back(dv, xhat, scale, gain):
    dxhat = dv * gain
    return scale * (dxhat - jnp.mean(dxhat, 1, keepdims=True) - xhat * jnp.mean(dxhat * xhat, 1, keepdims=True))


def gelu_parts(u):
    phi = 0.5 * (1.0 + lax.erf(u * (1.0 / math.sqrt(2.0))))
    return u * phi, phi + u * jnp.exp(-0.5 * u * u) * (1.0 / math.sqrt(2.0 * math.pi))


def head_masks(width):
    lane = lax.broadcasted_iota(jnp.int32, (1, width), 1)
    return [jnp.where((lane >= h * HEAD) & (lane < (h + 1) * HEAD), 1.0, 0.0) for h in range(width // HEAD)]


def stacked(pair, masks):
    return tuple(jnp.concatenate([part * m.astype(BF16) for m in masks], 0) for part in pair)


def unstacked(v, masks):
    rows = v.shape[0] // len(masks)
    total = v[:rows] * masks[0]
    for h in range(1, len(masks)):
        total = total + v[h * rows : (h + 1) * rows] * masks[h]
    return total


def softmax(s):
    e = jnp.exp(s - jnp.max(s, 1, keepdims=True))
    return e / jnp.sum(e, 1, keepdims=True)


def wide_nt(a, b):
    return dot(jnp.concatenate(a, 1), jnp.concatenate([b[0], b[0]], 1), 1, 1) + dot(a[0], b[1], 1, 1)


def wide_n(a, b, ca=1):
    n = b[0].shape[1]
    both = dot(a[0], jnp.concatenate(b, 1), ca, 0)
    return both[:, :n] + (both[:, n:] + dot(a[1], b[0], ca, 0))


def column_sum(v):
    return jnp.sum(v, 0, keepdims=True)


def encoder_slots():
    for r in range(WIN_LAT):
        for n in range(8):
            start = n * WIN_LON + WIN_LON // 2
            at = n * ROWS_E + r * WIN_LON
            if n < 7:
                yield r, at, start, WIN_LON
            else:
                yield r, at, start, WIN_LON // 2
                yield r, at + WIN_LON // 2, 0, WIN_LON // 2


def merging_slots():
    for z in range(WIN_MOD):
        for r in range(WIN_LAT):
            for n in range(4):
                yield z, r, n * ROWS_F + (z * WIN_LAT + r) * WIN_LON, n * WIN_LON


MESH = pl.DeviceIdType.MESH


def seq_digits(count):
    rest, digits = count // 2, []
    while rest > 1:
        digits.insert(0, 4 if rest % 4 == 0 else 2)
        rest //= digits[0]
    digits.sort()
    if count == 16:
        digits = [4, 2]
    return digits + [2]


class Places:
    def __init__(self, groups, seqs):
        self.sizes = [groups] + seq_digits(seqs)
        self.groups = groups
        self.strides = [1] * len(self.sizes)
        for i in range(len(self.sizes) - 2, 0, -1):
            self.strides[i] = self.strides[i + 1] * self.sizes[i + 1]

    def here(self):
        self.g, self.s = lax.axis_index("group"), lax.axis_index("seq")
        self.mine = [self.g] + [self.s // self.strides[i] % self.sizes[i] for i in range(1, len(self.sizes))]

    def peer(self, digit, value):
        if digit == 0:
            return (value, self.s)
        return (self.g, self.s + (value - self.mine[digit]) * self.strides[digit])

    def place(self, values):
        return sum(v * self.strides[i] for i, v in values.items() if i)


def windows(total, count):
    piece = total // count
    tiles = max(-(-(piece * (d + 1)) // 1024) - piece * d // 1024 for d in range(count))
    last = piece * (count - 1) // 1024
    return piece, tiles * 8, (last + tiles) * 8


def window_start(piece, d):
    return pl.multiple_of(piece * d // 1024 * 8, 8)


def start_copy(src, dst, sems, at, peer):
    one = pltpu.make_async_remote_copy(
        src_ref=src, dst_ref=dst, send_sem=sems[0].at[at], recv_sem=sems[1].at[at], device_id=peer, device_id_type=MESH
    )
    one.start()
    return one


class Stream:
    def __init__(self, places, plan, chosen, shift, sems, base):
        self.places, self.order, self.piece, self.first, self.rows = places, plan.order, plan.piece, plan.first, plan.rows
        self.chosen, self.shift, self.sems, self.base = chosen, shift, sems, base
        self.sizes = plan.sizes
        self.held, self.arrived = {}, {}
        self.last = len(places.sizes) - 1

    def buffers(self, held, arrived):
        self.held.update(held)
        self.arrived.update(arrived)
        return self

    def combos(self, i=0):
        out = [()]
        for n in self.sizes[i:]:
            out = [c + (v,) for c in out for v in range(n)]
        return out

    def number(self, values):
        where = self.places.place(values)
        if 0 in values:
            where = where + values[0] * (self.places.sizes[1] * self.places.strides[1])
        return where

    def target(self, i, combo, core):
        values = {d: self.places.mine[d] for d in self.order[:i]}
        values.update(zip(self.order[i:], combo))
        values[self.last] = core
        return self.number(values)

    def when(self, number, action):
        if self.chosen is None:
            action()
        else:
            pl.when(self.chosen(number))(action)

    def window(self, number):
        return pl.ds(pl.multiple_of(self.shift(window_start(self.piece, number)) + self.first, 8), self.rows)

    def core_copy(self, n, number, source):
        p = self.places
        core = p.mine[self.last]
        return pltpu.make_async_remote_copy(
            src_ref=source.at[self.window(number)], dst_ref=self.held[0].at[n], send_sem=self.sems[0].at[self.base + n],
            recv_sem=self.sems[1].at[self.base + n], device_id=p.peer(self.last, 1 - core), device_id_type=MESH,
        )

    def start_core(self, source):
        core = self.places.mine[self.last]
        for n, combo in enumerate(self.combos()):
            number = self.target(0, combo, 1 - core)
            self.when(number, lambda n=n, number=number: self.core_copy(n, number, source).start())

    def finish_core(self, source):
        core = self.places.mine[self.last]
        for n, combo in enumerate(self.combos()):
            number = self.target(0, combo, core)

            def add(n=n, number=number):
                self.core_copy(n, number, source).wait_recv()
                self.held[0][n] = self.held[0][n] + source[self.window(number), :]

            self.when(number, add)
        for n, combo in enumerate(self.combos()):
            number = self.target(0, combo, 1 - core)
            self.when(number, lambda n=n, number=number: self.core_copy(n, number, source).wait_send())

    def blocks(self, i):
        return math.prod(self.sizes[i + 1 :])

    def copy(self, i, k, n):
        p, digit, size = self.places, self.order[i], self.sizes[i]
        value = lax.rem(p.mine[digit] + k, size)
        at = self.base + len(self.combos()) + sum((self.sizes[j] - 1) * self.blocks(j) for j in range(i)) + (k - 1) * self.blocks(i) + n
        return pltpu.make_async_remote_copy(
            src_ref=self.held[i].at[value * self.blocks(i) + n], dst_ref=self.arrived[i].at[k - 1, n], send_sem=self.sems[0].at[at],
            recv_sem=self.sems[1].at[at], device_id=p.peer(digit, value), device_id_type=MESH,
        )

    def sent(self, i):
        core = self.places.mine[self.last]
        for k in range(1, self.sizes[i]):
            value = lax.rem(self.places.mine[self.order[i]] + k, self.sizes[i])
            for n, combo in enumerate(self.combos(i + 1)):
                yield k, n, self.target(i, (value,) + combo, core)

    def start(self, i):
        for k, n, number in self.sent(i):
            self.when(number, lambda k=k, n=n: self.copy(i, k, n).start())

    def finish(self, i, out=None):
        core = self.places.mine[self.last]
        mine = self.places.mine[self.order[i]]
        for n, combo in enumerate(self.combos(i + 1)):
            def add(n=n):
                total = self.held[i][mine * self.blocks(i) + n]
                for k in range(1, self.sizes[i]):
                    self.copy(i, k, n).wait_recv()
                    total = total + self.arrived[i][k - 1, n]
                if out is None:
                    self.held[i + 1][n] = total
                else:
                    out(total)

            self.when(self.target(i, (mine,) + combo, core), add)
        for k, n, number in self.sent(i):
            self.when(number, lambda k=k, n=n: self.copy(i, k, n).wait_send())

    def semaphores(self):
        return len(self.combos()) + sum((self.sizes[j] - 1) * self.blocks(j) for j in range(len(self.sizes)))


class Portion:
    def __init__(self, places, order, piece, first, rows):
        self.order, self.piece, self.first, self.rows = order, piece, first, rows
        self.sizes = [places.sizes[d] for d in order]

    def blocks(self, i):
        return math.prod(self.sizes[i + 1 :])

    def core_scratch(self):
        return vmem(math.prod(self.sizes), self.rows, LANES)

    def scratch(self, i):
        return vmem(self.sizes[i] - 1, self.blocks(i), self.rows, LANES)

    def semaphores(self):
        return math.prod(self.sizes) + sum((self.sizes[j] - 1) * self.blocks(j) for j in range(len(self.sizes)))


class Sums:
    def __init__(self, groups, seqs, fus_total, enc_total):
        self.places = places = Places(groups, seqs)
        last = len(places.sizes) - 1
        order = sorted(range(1, last), key=lambda d: places.sizes[d])
        piece, rows, self.fus_all = windows(fus_total, groups * seqs)
        enc_piece, enc_rows, self.enc_all = windows(enc_total, seqs)
        first = rows * 4 // 64 * 8
        self.fus = [
            Portion(places, [0] + order, piece, 0, first),
            Portion(places, order[:1] + [0] + order[1:], piece, first, rows - first),
        ]
        self.enc = [Portion(places, order, enc_piece, 0, enc_rows)]
        self.fus_rows, self.enc_rows = rows, enc_rows
        self.low, self.high = FUS_AT["up"], FUS_AT["g1"] // LANES
        starts = [piece * d // 1024 * 8 for d in range(groups * seqs)]
        self.early = [d for d, at in enumerate(starts) if at >= self.low and at + rows <= self.high]
        others = [at for d, at in enumerate(starts) if d not in self.early]
        self.rest_low = max(at for at in others if at < self.low) + rows
        self.rest_from = min(at for at in others if at >= self.low)
        self.rest_all = self.rest_low + self.fus_all - self.rest_from
        self.enc_low = 0

    def is_early(self, d):
        return jnp.logical_and(d >= self.early[0], d <= self.early[-1])

    def is_late(self, d):
        return jnp.logical_not(self.is_early(d))

    def rest_shift(self, at):
        return jnp.where(at < self.low, at, at - self.rest_from + self.rest_low)


def encoder_forward(
    field_ref, flat,
    lat_ref, xhat_ref, rstd_ref, qkv_ref, p_h, p_l, o_ref, xhat2_ref, rstd2_ref, g_h, g_l, dg_ref, out_ref,
    win_h, win_l, wout_h, wout_l, wup_h, wup_l, wdn_h, wdn_l, wlin_h, wlin_l,
    x, wide, lat, head_ref, send, recv,
):
    g, s = lax.axis_index("group"), lax.axis_index("seq")
    seqs = lax.axis_size("seq")
    before, after = lax.rem(s + seqs - SAMPLES, seqs), lax.rem(s + SAMPLES, seqs)
    barrier = pltpu.get_barrier_semaphore()
    for other in (before, after):
        pl.semaphore_signal(barrier, inc=1, device_id=(g, other), device_id_type=MESH)
    pl.semaphore_wait(barrier, 2)
    halo = start_copy(field_ref.at[pl.ds(0, 3)], head_ref, (send, recv), 0, (g, before))
    for pair, name in (((win_h, win_l), "in"), ((wout_h, wout_l), "out"), ((wup_h, wup_l), "up"), ((wdn_h, wdn_l), "down"), ((wlin_h, wlin_l), "lin")):
        width = ENC_MATS[name][1]

        def store(rows, c, v, pair=pair, width=width):
            last = min(width - c * LANES, LANES)
            put(pair, (rows, slice(c * LANES, c * LANES + last)), v[:, :last])

        unpack_matrix(flat, ENC_AT[name], ENC_MATS[name], store, wide)
    vec = {name: vector(flat, ENC_AT[name], amount) for name, amount in ENC_VECS.items()}
    masks = head_masks(CE)
    halo.wait()
    for r, at, start, amount in encoder_slots():
        x[at : at + amount, :] = (field_ref[r + 3, start : start + amount, :] if r < 3 else head_ref[r - 3, start : start + amount, :])
    wrapped = s // SAMPLES == seqs // SAMPLES - 1
    half = ROWS_E // 2
    upper = lax.broadcasted_iota(jnp.int32, (ROWS_E, ROWS_E), 0) >= half
    right = lax.broadcasted_iota(jnp.int32, (ROWS_E, ROWS_E), 1) >= half
    apart = jnp.where(jnp.logical_and(upper != right, wrapped), 1.0, 0.0)
    apart = jnp.concatenate([apart] * HEADS_E, 0)
    win, wout, wup, wdn, wlin = (win_h, win_l), (wout_h, wout_l), (wup_h, wup_l), (wdn_h, wdn_l), (wlin_h, wlin_l)
    scale = 1.0 / math.sqrt(HEAD)

    def step(i, carry):
        rows = pl.ds(pl.multiple_of(i * 2 * ROWS_E, 2 * ROWS_E), 2 * ROWS_E)
        xv = x[rows, :]
        xhat, rstd = normalize(xv)
        xhat_ref[rows, :] = xhat
        rstd_ref[rows, :] = rstd
        xn = split(xhat * vec["g1"] + vec["s1"])
        full = slice(None)
        qkv = dot3(xn, get(win, (full, full)))
        shift = jnp.concatenate([vec["qb"], jnp.zeros_like(vec["qb"]), vec["vb"]], 1)
        factor = jnp.concatenate([jnp.full((1, CE), scale, F32), jnp.ones((1, 2 * CE), F32)], 1)
        qkv = (qkv + shift) * factor
        qkv_ref[rows, :] = qkv
        parts = []
        for w in range(2):
            one = qkv[w * ROWS_E : (w + 1) * ROWS_E]
            q, k, v = (one[:, j * CE : (j + 1) * CE] for j in range(3))
            qm = split(jnp.concatenate([q * m for m in masks], 0))
            s = dot3(qm, split(k), 1, 1)
            s = jnp.where(apart > 0.5, NEG, s)
            p = split(softmax(s))
            p_h[i * 2 + w] = p[0]
            p_l[i * 2 + w] = p[1]
            parts.append(unstacked(dot3(p, split(v)), masks))
        o = jnp.concatenate(parts, 0)
        o_ref[rows, :] = o
        hidden = xv + dot3(split(o), get(wout, (full, full))) + vec["ob"]
        xhat2, rstd2 = normalize(hidden)
        xhat2_ref[rows, :] = xhat2
        rstd2_ref[rows, :] = rstd2
        hn = split(xhat2 * vec["g2"] + vec["s2"])
        out = hidden + vec["db"]
        for c in range(MLP_E // CHUNK):
            cols = slice(c * CHUNK, (c + 1) * CHUNK)
            u = dot3(hn, get(wup, (full, cols))) + vec["ub"][:, cols]
            g, slope = gelu_parts(u)
            dg_ref[rows, cols] = slope
            g = split(g)
            g_h[rows, cols] = g[0]
            g_l[rows, cols] = g[1]
            out = out + dot3(g, get(wdn, (cols, full)))
        out_ref[rows, :] = out
        lat[rows, :] = dot3(split(out), get(wlin, (full, full))) + vec["lb"]
        return carry

    lax.fori_loop(0, 4, step, 0)
    for r, at, start, amount in encoder_slots():
        lat_ref[r, start : start + amount, :] = lat[at : at + amount, :]


def vmem(*shape, dtype=F32):
    return pltpu.VMEM(shape, dtype)


def pair_of(*shape):
    return [vmem(*shape, dtype=BF16)] * 2


def call(kernel, name, inputs, outs, scratch, number, flops=0, far=(), far_outs=()):
    specs = [pl.BlockSpec(memory_space=pl.ANY if n in far else pltpu.VMEM) for n in range(len(inputs))]
    moved = sum(v.size * v.dtype.itemsize for v in list(inputs) + list(outs))
    return pl.pallas_call(
        kernel,
        name=name,
        out_shape=outs,
        in_specs=specs,
        out_specs=[pl.BlockSpec(memory_space=pl.ANY if n in far_outs else pltpu.VMEM) for n in range(len(outs))],
        scratch_shapes=scratch,
        cost_estimate=pl.CostEstimate(flops=flops, bytes_accessed=moved, transcendentals=0),
        compiler_params=pltpu.CompilerParams(collective_id=number, has_side_effects=True, vmem_limit_bytes=VMEM_BYTES),
    )(*inputs)


def sems(count):
    return [pltpu.SemaphoreType.DMA((count,)), pltpu.SemaphoreType.DMA((count,))]


def shape(*dims, dtype=F32):
    return jax.ShapeDtypeStruct(dims, dtype)


def rows_kernel(line_ref, rows_ref):
    rows_ref[...] = line_ref.reshape(*rows_ref.shape)[...]


def rows_of_lanes(line):
    return pl.pallas_call(
        rows_kernel,
        name="rows_of_lanes",
        out_shape=shape(line.size // LANES, LANES),
        compiler_params=pltpu.CompilerParams(vmem_limit_bytes=16 << 20),
    )(line)


def encoder_forward_call(field, flat):
    n = 8 * ROWS_E
    outs = [
        shape(WIN_LAT, 96, CF), shape(n, CE), shape(n, 1), shape(n, 3 * CE),
        shape(8, HEADS_E * ROWS_E, ROWS_E, dtype=BF16), shape(8, HEADS_E * ROWS_E, ROWS_E, dtype=BF16),
        shape(n, CE), shape(n, CE), shape(n, 1), shape(n, MLP_E, dtype=BF16), shape(n, MLP_E, dtype=BF16),
        shape(n, MLP_E), shape(n, CE),
    ]
    scratch = (
        pair_of(CE, 3 * CE) + pair_of(CE, CE) + pair_of(CE, MLP_E) + pair_of(MLP_E, CE) + pair_of(CE, CF)
        + [vmem(n, CE), vmem(5, MLP_E, LANES), vmem(n, CF), vmem(3, 96, CE)] + sems(1)
    )
    return call(encoder_forward, "encoder_forward", [field, flat], outs, scratch, 0, 6 * n * 516096)


def encoder_backward(
    plan,
    dlat_ref, flat, rest, tab, early_a, early_b,
    xhat_ref, rstd_ref, qkv_far, ph_far, pl_far, o_ref, xhat2_ref, rstd2_ref, gh_far, gl_far, dg_far, out_ref,
    field_grad, fus_out, enc_out, tab_out,
    qkv_ref, p_h, p_l, g_h, g_l, dg_ref,
    grad, tabs, send, recv, local_sems, win_h, win_l, wout_h, wout_l, wup_h, wup_l, wdn_h, wdn_l, wlin_h, wlin_l,
    dlat, wide, dout, dout_h, dout_l, dhn, du_h, du_l, hn_h, hn_l, dh_h, dh_l, dqkv_h, dqkv_l, xn_h, xn_l, sums, dx, dback,
    *refs,
):
    loads = [
        pltpu.make_async_copy(src, dst, local_sems.at[n])
        for n, (src, dst) in enumerate(
            ((gh_far, g_h), (gl_far, g_l), (dg_far, dg_ref), (qkv_far, qkv_ref), (ph_far, p_h), (pl_far, p_l))
        )
    ]
    for one in loads:
        one.start()
    places = plan.places
    places.here()
    g, s = places.g, places.s
    seqs = places.sizes[1] * places.strides[1]
    before, after = lax.rem(s + seqs - SAMPLES, seqs), lax.rem(s + SAMPLES, seqs)
    slot, band = g * seqs + s, s // SAMPLES
    mine = g * SAMPLES + lax.rem(s, SAMPLES)
    owners = [((4 * band + j) // seqs, lax.rem(4 * band + j, seqs)) for j in range(4)]
    givers = [(k // 2, slot // 4 * SAMPLES + k % 2) for k in range(4)]

    def other(pg, ps):
        return jnp.logical_or(pg != g, ps != s)

    barrier = pltpu.get_barrier_semaphore()
    peers = [(g, before), (g, after)]
    for digit, size in enumerate(places.sizes):
        peers += [places.peer(digit, lax.rem(places.mine[digit] + k, size)) for k in range(1, size)]
    for peer in peers:
        pl.semaphore_signal(barrier, inc=1, device_id=peer, device_id_type=MESH)
    for pg, ps in owners + givers:
        @pl.when(other(pg, ps))
        def _(pg=pg, ps=ps):
            pl.semaphore_signal(barrier, inc=1, device_id=(pg, ps), device_id_type=MESH)
    pl.semaphore_wait(barrier, len(peers) + jnp.where(slot // 4 == band, 6, 8))

    refs = list(refs)
    base = 8
    early, late, encs = [], [], []
    for portion, held in zip(plan.fus, (early_a, early_b)):
        one = Stream(places, portion, plan.is_early, lambda at: at, (send, recv), base)
        arrived = {i: refs.pop(0) for i in range(1, len(portion.order))}
        early.append(one.buffers({1: held}, arrived).buffers({i + 1: arrived[i].at[0] for i in arrived}, {}))
        base += portion.semaphores()
    for group, portions, chosen, shift in ((late, plan.fus, plan.is_late, plan.rest_shift), (encs, plan.enc, None, lambda at: at)):
        for portion in portions:
            one = Stream(places, portion, chosen, shift, (send, recv), base)
            held = {0: refs.pop(0)}
            arrived = {i: refs.pop(0) for i in range(len(portion.order))}
            group.append(one.buffers(held, arrived).buffers({i + 1: arrived[i].at[0] for i in arrived}, {}))
            base += portion.semaphores()

    def keep(one, split_at):
        def store(total):
            fus_out[split_at : split_at + one.rows, :] = total
        return store

    stages = len(plan.fus[0].order)
    keeps = [keep(one, one.first) for one in early]

    def go(streams, i):
        for n, one in enumerate(streams):
            if i == 0:
                one.finish_core(grad if one in encs else rest)
            else:
                one.finish(i - 1, keeps[n] if one not in encs and i == stages else None)
            if i < len(one.order):
                one.start(i)

    for one in late:
        one.start_core(rest)
    for one in early:
        one.start(1)

    def give(j, pg, ps):
        return pltpu.make_async_remote_copy(
            src_ref=tab.at[j], dst_ref=tabs.at[mine], send_sem=send.at[4 + j], recv_sem=recv.at[4 + mine],
            device_id=(pg, ps), device_id_type=MESH,
        )

    for j, (pg, ps) in enumerate(owners):
        @pl.when(other(pg, ps))
        def _(j=j, pg=pg, ps=ps):
            give(j, pg, ps).start()

        @pl.when(jnp.logical_not(other(pg, ps)))
        def _(j=j):
            tabs[mine] = tab[j]

    win, wout, wup, wdn, wlin = (win_h, win_l), (wout_h, wout_l), (wup_h, wup_l), (wdn_h, wdn_l), (wlin_h, wlin_l)
    for pair, name in ((win, "in"), (wout, "out"), (wup, "up"), (wdn, "down"), (wlin, "lin")):
        width = ENC_MATS[name][1]

        def store(rows, c, v, pair=pair, width=width):
            last = min(width - c * LANES, LANES)
            put(pair, (rows, slice(c * LANES, c * LANES + last)), v[:, :last])

        unpack_matrix(flat, ENC_AT[name], ENC_MATS[name], store, wide)
    vec = {name: vector(flat, ENC_AT[name], ENC_VECS[name]) for name in ("g1", "s1", "g2", "s2")}
    masks = head_masks(CE)
    full = slice(None)
    scale = 1.0 / math.sqrt(HEAD)
    go(late, 0)
    for r, at, start, amount in encoder_slots():
        dlat[at : at + amount, :] = dlat_ref[r, start : start + amount, :]
    for one in loads[:3]:
        one.wait()
    dl = split(dlat[...])
    put_vector(grad, ENC_AT["lb"], column_sum(dlat[...]))
    d = dot3(dl, get(wlin, (full, full)), 1, 1)
    dout[...] = d
    put((dout_h, dout_l), (full, full), d)
    put_vector(grad, ENC_AT["db"], column_sum(d))
    dw = dot3(split(out_ref[...]), dl, 0, 0)
    for c in range(3):
        grad[pl.ds(ENC_AT["lin"] + c, CE, stride=3), :] = dw[:, c * LANES : (c + 1) * LANES]
    xhat2 = xhat2_ref[...]
    put((hn_h, hn_l), (full, full), xhat2 * vec["g2"] + vec["s2"])
    for c in range(MLP_E // CHUNK):
        cols = slice(c * CHUNK, (c + 1) * CHUNK)
        do = (dout_h[...], dout_l[...])
        du = dot3(do, get(wdn, (cols, full)), 1, 1) * dg_ref[:, cols]
        put_vector(grad, ENC_AT["ub"] + c * CHUNK, column_sum(du))
        du = split(du)
        part = dot3(du, get(wup, (full, cols)), 1, 1)
        dhn[...] = part if c == 0 else dhn[...] + part
        dw = dot3((hn_h[...], hn_l[...]), du, 0, 0)
        for t in range(2):
            grad[pl.ds(ENC_AT["up"] + 2 * c + t, CE, stride=6), :] = dw[:, t * LANES : (t + 1) * LANES]
        dw = dot3((g_h[:, cols], g_l[:, cols]), do, 0, 0)
        put_tiles(wide, slice(c * CHUNK, (c + 1) * CHUNK), dw)
    pack_matrix(grad, ENC_AT["down"], ENC_MATS["down"], wide)
    dv = dhn[...]
    put_vector(grad, ENC_AT["g2"], column_sum(dv * xhat2))
    put_vector(grad, ENC_AT["s2"], column_sum(dv))
    d = dout[...] + normalize_back(dv, xhat2, rstd2_ref[...], vec["g2"])
    dout[...] = d
    put((dh_h, dh_l), (full, full), d)
    put_vector(grad, ENC_AT["ob"], column_sum(d))
    dw = dot3(split(o_ref[...]), (dh_h[...], dh_l[...]), 0, 0)
    put_tiles(wide, slice(0, CE), dw)
    pack_matrix(grad, ENC_AT["out"], ENC_MATS["out"], wide)
    sums[...] = jnp.zeros_like(sums)
    go(early, 2)
    for one in loads[3:]:
        one.wait()

    def step(i, carry):
        rows = pl.ds(pl.multiple_of(i * 2 * ROWS_E, 2 * ROWS_E), 2 * ROWS_E)
        do = dot3((dh_h[rows, :], dh_l[rows, :]), get(wout, (full, full)), 1, 1)
        parts = []
        for w in range(2):
            one = qkv_ref[pl.ds(pl.multiple_of(i * 2 * ROWS_E, 2 * ROWS_E) + w * ROWS_E, ROWS_E), :]
            q, k, v = (one[:, j * CE : (j + 1) * CE] for j in range(3))
            dow = do[w * ROWS_E : (w + 1) * ROWS_E]
            dom = split(jnp.concatenate([dow * m for m in masks], 0))
            qm = split(jnp.concatenate([q * m for m in masks], 0))
            p = (p_h[i * 2 + w], p_l[i * 2 + w])
            dp = dot3(dom, split(v), 1, 1)
            pf = p[0].astype(F32) + p[1].astype(F32)
            t = pf * dp
            ds = split(t - pf * jnp.sum(t, 1, keepdims=True))
            dq = unstacked(dot3(ds, split(k)), masks) * scale
            dk = dot3(ds, qm, 0, 0)
            dvv = dot3(p, dom, 0, 0)
            parts.append(jnp.concatenate([dq, dk, dvv], 1))
        dqkv = jnp.concatenate(parts, 0)
        sums[0:1, :] = sums[0:1, :] + column_sum(dqkv)
        dqkv = split(dqkv)
        dqkv_h[rows, :] = dqkv[0]
        dqkv_l[rows, :] = dqkv[1]
        xhat = xhat_ref[rows, :]
        put((xn_h, xn_l), (rows, full), xhat * vec["g1"] + vec["s1"])
        dxn = dot3(dqkv, get(win, (full, full)), 1, 1)
        sums[1:2, 0:CE] = sums[1:2, 0:CE] + column_sum(dxn * xhat)
        sums[2:3, 0:CE] = sums[2:3, 0:CE] + column_sum(dxn)
        dx[rows, :] = dout[rows, :] + normalize_back(dxn, xhat, rstd_ref[rows, :], vec["g1"])
        return carry

    lax.fori_loop(0, 2, step, 0)
    go(late, 1)
    lax.fori_loop(2, 4, step, 0)
    for r, at, start, amount in encoder_slots():
        if r < 3:
            field_grad[r + 3, start : start + amount, :] = dx[at : at + amount, :]
        else:
            dback[r - 3, start : start + amount, :] = dx[at : at + amount, :]
    back = start_copy(dback, field_grad.at[pl.ds(0, 3)], (send, recv), 3, (g, after))
    put_vector(grad, ENC_AT["qb"], sums[0:1, 0:CE])
    put_vector(grad, ENC_AT["vb"], sums[0:1, 2 * CE : 3 * CE])
    put_vector(grad, ENC_AT["g1"], sums[1:2, 0:CE])
    put_vector(grad, ENC_AT["s1"], sums[2:3, 0:CE])
    dw = dot3((xn_h[...], xn_l[...]), (dqkv_h[...], dqkv_l[...]), 0, 0)
    put_tiles(wide, slice(0, CE), dw)
    pack_matrix(grad, ENC_AT["in"], ENC_MATS["in"], wide)
    for one in encs:
        one.start_core(grad)
    go(late, 2)
    go(encs, 0)
    if stages > 3:
        go(early, 3)
    go(encs, 1)
    back.wait()
    for j, (pg, ps) in enumerate(owners):
        @pl.when(other(pg, ps))
        def _(j=j, pg=pg, ps=ps):
            give(j, pg, ps).wait_send()
    for k, (pg, ps) in enumerate(givers):
        @pl.when(other(pg, ps))
        def _(k=k, pg=pg, ps=ps):
            pltpu.make_async_remote_copy(
                src_ref=tab.at[0], dst_ref=tabs.at[k], send_sem=send.at[4], recv_sem=recv.at[4 + k],
                device_id=(pg, ps), device_id_type=MESH,
            ).wait_recv()
    tab_out[...] = (tabs[0] + tabs[1]) + (tabs[2] + tabs[3])
    for i in range(4, stages + 1):
        go(early, i)
    if stages <= 3:
        go(early, stages)
    for i in range(3, stages + 1):
        go(late, i)
    for i in range(2, len(encs[0].order)):
        go(encs, i)
    for one in encs:
        i = len(one.order) - 1

        def store(total):
            enc_out[...] = total

        one.finish(i, store)


def encoder_backward_call(plan, dlat, flat, rest, tab, early_a, early_b, saved):
    n = 8 * ROWS_E
    refs, count = [], 8
    for portion in plan.fus:
        refs += [portion.scratch(i) for i in range(1, len(portion.order))]
        count += portion.semaphores()
    for portion in plan.fus + plan.enc:
        refs += [portion.core_scratch()] + [portion.scratch(i) for i in range(len(portion.order))]
        count += portion.semaphores()
    xhat, rstd, qkv, p_h, p_l, o, xhat2, rstd2, g_h, g_l, dg, out = saved
    scratch = (
        [pltpu.VMEM(v.shape, v.dtype) for v in (qkv, p_h, p_l, g_h, g_l, dg)]
        + [vmem(plan.enc_all, LANES), vmem(*tab.shape)] + sems(count) + [pltpu.SemaphoreType.DMA((6,))]
        + pair_of(CE, 3 * CE) + pair_of(CE, CE) + pair_of(CE, MLP_E) + pair_of(MLP_E, CE) + pair_of(CE, CF)
        + [vmem(n, CF), vmem(5, MLP_E, LANES), vmem(n, CE)] + pair_of(n, CE) + [vmem(n, CE)] + pair_of(n, CHUNK)
        + pair_of(n, CE) + pair_of(n, CE) + pair_of(n, 3 * CE) + pair_of(n, CE) + [vmem(8, 3 * CE), vmem(n, CE), vmem(3, 96, CE)]
        + refs
    )
    return call(
        partial(encoder_backward, plan), "encoder_backward", [dlat, flat, rest, tab, early_a, early_b] + list(saved),
        [shape(WIN_LAT, 96, CE), shape(plan.fus_rows, LANES), shape(plan.enc_rows, LANES), shape(*tab.shape[1:])],
        scratch, 2, 12 * n * 516096, tuple(6 + j for j in (2, 3, 4, 8, 9, 10)),
    )


def merging(
    plan,
    lat_ref, cot_ref, flat_ref, tab_ref, base_ref,
    out_ref, dlat_ref, rest_ref, dtab_ref, early_a, early_b,
    grad, core_a, core_b, first_a, first_b, fld_ref, send, recv, lines, bands, vectors, local_sems,
    win_h, win_l, wout_h, wout_l, wup_h, wup_l, wdn_h, wdn_l,
    bias, dbias, x, xhat1, rstd1, xn_h, xn_l, q_h, q_l, k_h, k_l, v_h, v_l, p_h, p_l, o_h, o_l,
    xhat2, rstd2, hn_h, hn_l, acc, dhn, dy, dy_h, dy_l, hn_t, dy_t, dh_h, dh_l, dqkv_h, dqkv_l, sums,
):
    win, wout, wup, wdn = (win_h, win_l), (wout_h, wout_l), (wup_h, wup_l), (wdn_h, wdn_l)
    full = slice(None)
    chunks = MLP_F // FCH
    g, s = lax.axis_index("group"), lax.axis_index("seq")
    seqs = lax.axis_size("seq")
    before, after = lax.rem(s + seqs - SAMPLES, seqs), lax.rem(s + SAMPLES, seqs)
    band = s // SAMPLES
    picked = pltpu.make_async_copy(tab_ref.at[:, pl.ds(pl.multiple_of(band // 8 * 8, 8), 8)], bands, local_sems.at[0])
    picked.start()
    loads = {}
    for n, name in enumerate(FUS_MATS):
        some = pl.ds(FUS_AT[name], math.prod(FUS_MATS[name]) // LANES)
        loads[name] = pltpu.make_async_copy(flat_ref.at[some], grad.at[some], local_sems.at[n + 1])
    at = FUS_AT["g1"] // LANES
    loads["g1"] = pltpu.make_async_copy(flat_ref.at[pl.ds(at, flat_ref.shape[0] - at)], vectors, local_sems.at[5])
    for one in loads.values():
        one.start()
    barrier = pltpu.get_barrier_semaphore()
    places = plan.places
    places.here()
    peers = [(1 - g, s), (g, before), (g, after), (1 - g, before), (1 - g, after)]
    for digit in (len(places.sizes) - 1, plan.fus[1].order[0]):
        size = places.sizes[digit]
        peers += [places.peer(digit, lax.rem(places.mine[digit] + k, size)) for k in range(1, size)]
    for peer in peers:
        pl.semaphore_signal(barrier, inc=1, device_id=peer, device_id_type=MESH)
    pl.semaphore_wait(barrier, len(peers))
    early, base = [], 6
    for portion, core, first, out in zip(plan.fus, (core_a, core_b), (first_a, first_b), (early_a, early_b)):
        early.append(Stream(places, portion, plan.is_early, lambda at: at, (send, recv), base).buffers({0: core, 1: out}, {0: first}))
        base += portion.semaphores()

    def half(one):
        return pl.ds(pl.multiple_of(one * 48, 48), 48)

    far = [
        start_copy(lat_ref.at[pl.ds(0, 3), half(1 - g)], fld_ref.at[g, pl.ds(3, 3)], (send, recv), 0, (1 - g, s)),
        start_copy(lat_ref.at[pl.ds(3, 3), half(g)], fld_ref.at[g, pl.ds(0, 3)], (send, recv), 1, (g, after)),
        start_copy(lat_ref.at[pl.ds(3, 3), half(1 - g)], fld_ref.at[g, pl.ds(0, 3)], (send, recv), 2, (1 - g, after)),
    ]
    fld_ref[g, 3:6] = lat_ref[0:3, half(g), :]
    scale = 1.0 / math.sqrt(HEAD)

    def store(pair):
        def one(rows, c, v):
            put(pair, (rows, slice(c * LANES, (c + 1) * LANES)), v)
        return one

    def store_up(rows, c, v):
        put(wup, (c // (FCH // LANES), full, slice(c % (FCH // LANES) * LANES, (c % (FCH // LANES) + 1) * LANES)), v)

    def store_down(rows, c, v):
        for j in range(chunks):
            put(wdn, (j, full, slice(c * LANES, (c + 1) * LANES)), v[j * FCH : (j + 1) * FCH])

    loads["in"].wait()
    unpack_matrix(grad, FUS_AT["in"], FUS_MATS["in"], store(win), None)
    loads["out"].wait()
    unpack_matrix(grad, FUS_AT["out"], FUS_MATS["out"], store(wout), None)
    loads["up"].wait()
    unpack_matrix(grad, FUS_AT["up"], FUS_MATS["up"], store_up, None)
    loads["down"].wait()
    unpack_matrix(grad, FUS_AT["down"], FUS_MATS["down"], store_down, None)
    loads["g1"].wait()
    vec = {name: vector(vectors, FUS_AT[name] - FUS_AT["g1"], amount) for name, amount in FUS_VECS.items()}
    masks = head_masks(LANES)

    spots = jnp.where(lax.broadcasted_iota(jnp.int32, (TAB_PAD, 2 * LANES), 0) == base_ref[...], 1.0, 0.0).astype(BF16)
    picked.wait()
    for h in range(HEADS_F):
        lines[h : h + 1, :] = bands[h, pl.ds(lax.rem(band, 8), 1), :]
    pad = jnp.zeros((HEADS_F, TAB_PAD - PAIRS * SPAN), F32)
    table = []
    for z in range(WIN_MOD):
        for r in range(WIN_LAT):
            at = [((z * WIN_MOD + y) * WIN_LAT * WIN_LAT + r * WIN_LAT) * SPAN for y in range(WIN_MOD)]
            one = jnp.concatenate([lines[0:HEADS_F, t : t + WIN_LAT * SPAN] for t in at] + [pad], 1)
            table.append(jnp.concatenate([one, jnp.zeros((16 - HEADS_F, TAB_PAD), F32)], 0))
    table = jnp.concatenate(table, 0)
    for w in range(WIN_LON):
        turned = pltpu.roll(table, TAB_PAD - w, 1) if w else table
        hi, lo = split(turned)
        rest = (turned - hi.astype(F32) - lo.astype(F32)).astype(BF16)
        one = dot(hi, spots) + (dot(lo, spots) + dot(rest, spots))
        for n in range(PAIRS):
            for c in range(2):
                bias[c, pl.ds(n * WIN_LON + w, HEADS_F, stride=ROWS_F), :] = one[n * 16 : n * 16 + HEADS_F, c * LANES : (c + 1) * LANES]
    dbias[...] = jnp.zeros_like(dbias)

    for one in far:
        one.wait()
    for z, r, at, start in merging_slots():
        x[at : at + WIN_LON, :] = fld_ref[z, r, start : start + WIN_LON, :]
        dy[at : at + WIN_LON, :] = cot_ref[z, r, start : start + WIN_LON, :]

    def rows_of(i):
        return pl.ds(pl.multiple_of(i * ROWS_F, ROWS_F), ROWS_F)

    xhat, rstd = normalize(x[...])
    xhat1[...] = xhat
    rstd1[...] = rstd
    put((xn_h, xn_l), (full, full), xhat * vec["g1"] + vec["s1"])
    for j, (pair, shift) in enumerate((((q_h, q_l), vec["qb"]), ((k_h, k_l), None), ((v_h, v_l), vec["vb"]))):
        one = deep3((xn_h[...], xn_l[...]), get(win, (full, slice(j * CF, (j + 1) * CF))))
        if shift is not None:
            one = one + shift
        if j == 0:
            one = one * scale
        put(pair, (full, full), one)

    def forward(i, carry):
        rows = rows_of(i)
        for b in range(3):
            cols = slice(b * LANES, (b + 1) * LANES)
            qm = stacked((q_h[rows, cols], q_l[rows, cols]), masks)
            some = slice(b * 4 * ROWS_F, (b + 1) * 4 * ROWS_F)
            s = deep3(qm, (k_h[rows, cols], k_l[rows, cols]), 1, 1) + get_tiles(bias, some, ROWS_F)
            p = split(softmax(s))
            p_h[i * 3 + b] = p[0]
            p_l[i * 3 + b] = p[1]
            o = unstacked(wide_n(p, (v_h[rows, cols], v_l[rows, cols])), masks)
            put((o_h, o_l), (rows, cols), o)
        return carry

    lax.fori_loop(0, 4, forward, 0)
    hidden = x[...] + deep3((o_h[...], o_l[...]), get(wout, (full, full))) + vec["ob"]
    xh2, rstd = normalize(hidden)
    xhat2[...] = xh2
    rstd2[...] = rstd
    put((hn_h, hn_l), (full, full), xh2 * vec["g2"] + vec["s2"])
    acc[...] = hidden + vec["db"]
    put((dy_h, dy_l), (full, full), dy[...])
    dhn[...] = jnp.zeros_like(dhn)
    hn_t[...] = left3((hn_h[...], hn_l[...]), 0).T
    dy_t[...] = left3((dy_h[...], dy_l[...]), 0).T
    for c in range(chunks):
        sums[8:9, c * FCH : (c + 1) * FCH] = vec["ub"][:, c * FCH : (c + 1) * FCH]

    def feed(c, carry):
        up = (wup_h[c], wup_l[c])
        down = (wdn_h[c], wdn_l[c])
        cols = pl.ds(pl.multiple_of(c * FCH, FCH), FCH)
        shift = sums[8:9, cols]

        u = deep3((hn_h[...], hn_l[...]), up) + shift
        gl, slope = gelu_parts(u)
        gl = split(gl)
        acc[...] = acc[...] + deep3(gl, down)
        du = deep3((dy_h[...], dy_l[...]), down, 1, 1) * slope
        sums[9:10, cols] = column_sum(du)
        du = split(du)
        dhn[...] = dhn[...] + deep3(du, up, 1, 1)
        dw = dot(hn_t[...], right3(du))
        for t in range(FCH // LANES):
            grad[pl.ds(FUS_AT["up"] + FCH // LANES * c + t, CF, stride=12), :] = dw[:, t * LANES : (t + 1) * LANES]
        dw = dot(dy_t[...], right3(gl)).T
        for t in range(3):
            grad[pl.ds(FUS_AT["down"] + 3 * FCH * c + t, FCH, stride=3), :] = dw[:, t * LANES : (t + 1) * LANES]
        return carry

    lax.fori_loop(0, chunks, feed, 0)
    for one in early:
        one.start_core(grad)
    put_vector(grad, FUS_AT["ub"], sums[9:10, :])
    sums[0:8, :] = jnp.zeros((8, MLP_F), F32)

    dv = dhn[...]
    sums[0:1, 0:CF] = column_sum(dy[...])
    sums[1:2, 0:CF] = column_sum(dv * xhat2[...])
    sums[2:3, 0:CF] = column_sum(dv)
    dh = dy[...] + normalize_back(dv, xhat2[...], rstd2[...], vec["g2"])
    sums[3:4, 0:CF] = column_sum(dh)
    dy[...] = dh
    put((dh_h, dh_l), (full, full), dh)
    do_h, do_l = hn_h, hn_l
    put((do_h, do_l), (full, full), deep3((dh_h[...], dh_l[...]), get(wout, (full, full)), 1, 1))

    for one in early:
        one.finish_core(grad)
        one.start(0)

    def backward(i, carry):
        rows = rows_of(i)
        for b in range(3):
            cols = slice(b * LANES, (b + 1) * LANES)
            dom = stacked((do_h[rows, cols], do_l[rows, cols]), masks)
            qm = stacked((q_h[rows, cols], q_l[rows, cols]), masks)
            p = (p_h[i * 3 + b], p_l[i * 3 + b])
            dp = deep3(dom, (v_h[rows, cols], v_l[rows, cols]), 1, 1)
            pf = p[0].astype(F32) + p[1].astype(F32)
            t = pf * dp
            ds = t - pf * jnp.sum(t, 1, keepdims=True)
            some = slice(b * 4 * ROWS_F, (b + 1) * 4 * ROWS_F)
            for c in range(2):
                one = ds[:, c * LANES : (c + 1) * LANES]
                dbias[c, some, 0 : one.shape[1]] = dbias[c, some, 0 : one.shape[1]] + one
            ds = split(ds)
            dq = unstacked(wide_n(ds, (k_h[rows, cols], k_l[rows, cols])), masks) * scale
            dk = dot(left3(qm, 0).T, right3(ds)).T
            dvv = dot(left3(dom, 0).T, right3(p)).T
            for j, one in enumerate((dq, dk, dvv)):
                at = slice(j * CF + b * LANES, j * CF + (b + 1) * LANES)
                put((dqkv_h, dqkv_l), (rows, at), one)
                if j != 1:
                    sums[4 + j // 2 : 5 + j // 2, cols] = sums[4 + j // 2 : 5 + j // 2, cols] + column_sum(one)
        return carry

    lax.fori_loop(0, 4, backward, 0)
    dxn = deep3((dqkv_h[...], dqkv_l[...]), get(win, (full, full)), 1, 1)
    sums[6:7, 0:CF] = column_sum(dxn * xhat1[...])
    sums[7:8, 0:CF] = column_sum(dxn)
    x[...] = dy[...] + normalize_back(dxn, xhat1[...], rstd1[...], vec["g1"])
    dx_ref = fld_ref
    for z, r, at, start in merging_slots():
        dx_ref[z, r, start : start + WIN_LON, :] = x[at : at + WIN_LON, :]
    back = [
        start_copy(dx_ref.at[1 - g, pl.ds(3, 3)], dlat_ref.at[pl.ds(0, 3), half(g)], (send, recv), 3, (1 - g, s)),
        start_copy(dx_ref.at[g, pl.ds(0, 3)], dlat_ref.at[pl.ds(3, 3), half(g)], (send, recv), 4, (g, before)),
        start_copy(dx_ref.at[1 - g, pl.ds(0, 3)], dlat_ref.at[pl.ds(3, 3), half(g)], (send, recv), 5, (1 - g, before)),
    ]
    dlat_ref[0:3, half(g), :] = dx_ref[g, 3:6]
    for j, name in enumerate(("db", "g2", "s2", "ob", "qb", "vb", "g1", "s1")):
        put_vector(grad, FUS_AT[name], sums[j : j + 1, 0:CF])
    for c in range(3):
        cols = slice(c * CF, (c + 1) * CF)
        dw = dot3((xn_h[...], xn_l[...]), (dqkv_h[:, cols], dqkv_l[:, cols]), 0, 0)
        for t in range(3):
            grad[pl.ds(FUS_AT["in"] + 3 * c + t, CF, stride=9), :] = dw[:, t * LANES : (t + 1) * LANES]
    dw = dot3((o_h[...], o_l[...]), (dh_h[...], dh_l[...]), 0, 0)
    for t in range(3):
        grad[pl.ds(FUS_AT["out"] + t, CF, stride=3), :] = dw[:, t * LANES : (t + 1) * LANES]
    rest = [
        pltpu.make_async_copy(grad.at[pl.ds(0, plan.rest_low)], rest_ref.at[pl.ds(0, plan.rest_low)], local_sems.at[6]),
        pltpu.make_async_copy(
            grad.at[pl.ds(plan.rest_from, plan.rest_all - plan.rest_low)],
            rest_ref.at[pl.ds(plan.rest_low, plan.rest_all - plan.rest_low)], local_sems.at[7],
        ),
    ]
    for one in rest:
        one.start()
    for one in early:
        one.finish(0)
    total = jnp.zeros((PAIRS * 16, TAB_PAD), F32)
    blank = jnp.zeros((16 - HEADS_F, 2 * LANES), F32)
    for w in range(WIN_LON):
        rows = []
        for n in range(PAIRS):
            rows.append(jnp.concatenate([dbias[c, pl.ds(n * WIN_LON + w, HEADS_F, stride=ROWS_F), :] for c in range(2)], 1))
            rows.append(blank)
        hi, lo = split(jnp.concatenate(rows, 0))
        one = dot(hi, spots, 1, 1) + dot(lo, spots, 1, 1)
        total = total + (pltpu.roll(one, w, 1) if w else one)
    for z in range(WIN_MOD):
        for r in range(WIN_LAT):
            n = z * WIN_LAT + r
            for y in range(WIN_MOD):
                at = ((z * WIN_MOD + y) * WIN_LAT * WIN_LAT + r * WIN_LAT) * SPAN
                lines[0:HEADS_F, at : at + WIN_LAT * SPAN] = total[n * 16 : n * 16 + HEADS_F, y * WIN_LAT * SPAN : (y + 1) * WIN_LAT * SPAN]
    for j in range(4):
        dtab_ref[j, 0:3, :] = lines[3 * j : 3 * j + 3, :]
    for z, r, at, start in merging_slots():
        out_ref[z, r, start : start + WIN_LON, :] = acc[at : at + WIN_LON, :]
    for one in back + rest:
        one.wait()


def merging_call(plan, latent, cotangent, flat, table):
    n = 4 * ROWS_F
    m = HEADS_F * ROWS_F
    t = np.arange(ROWS_F)
    base = np.full((1, 2 * LANES), -1, np.int32)
    base[0, :ROWS_F] = t // WIN_LON * SPAN + WIN_LON - 1 - t % WIN_LON
    base = jnp.asarray(base)
    scratch = (
        [vmem(plan.fus_all, LANES)]
        + [portion.core_scratch() for portion in plan.fus] + [portion.scratch(0) for portion in plan.fus]
        + [vmem(*cotangent.shape)] + sems(6 + sum(portion.semaphores() for portion in plan.fus)) + [vmem(16, table.shape[2]), vmem(HEADS_F, 8, table.shape[2]), vmem(flat.shape[0] - FUS_AT["g1"] // LANES, LANES), pltpu.SemaphoreType.DMA((8,))] + pair_of(CF, 3 * CF) + pair_of(CF, CF) + pair_of(MLP_F // FCH, CF, FCH) + pair_of(MLP_F // FCH, FCH, CF)
        + [vmem(2, m, LANES), vmem(2, m, LANES), vmem(n, CF), vmem(n, CF), vmem(n, 1)]
        + pair_of(n, CF) + pair_of(n, CF) + pair_of(n, CF) + pair_of(n, CF) + pair_of(12, 4 * ROWS_F, ROWS_F) + pair_of(n, CF)
        + [vmem(n, CF), vmem(n, 1)] + pair_of(n, CF) + [vmem(n, CF), vmem(n, CF), vmem(n, CF)] + pair_of(n, CF)
        + [vmem(CF, 3 * n, dtype=BF16)] * 2 + pair_of(n, CF) + pair_of(n, 3 * CF) + [vmem(16, MLP_F)]
    )
    outs = [shape(*cotangent.shape), shape(*latent.shape), shape(plan.rest_all, LANES), shape(4, 3, table.shape[2])]
    outs += [shape(portion.blocks(0), portion.rows, LANES) for portion in plan.fus]
    return call(partial(merging, plan), "merging", [latent, cotangent, flat, table, base], outs, scratch, 1, 18 * n * 1769472, (2, 3), (2,))


def own_piece(block, piece, d):
    return lax.dynamic_slice_in_dim(block.reshape(-1), piece * d - piece * d // 1024 * 1024, piece)


def update(params, grads, momentum, average, rate):
    momentum_new = MOMENTUM_DECAY * momentum + grads
    params_new = params - rate * (grads + MOMENTUM_DECAY * momentum_new)
    average_new = AVERAGE_DECAY * average + (1.0 - AVERAGE_DECAY) * params_new
    return (params_new, momentum_new, average_new)


def shards(
    tokens,
    cotangent,
    enc_params,
    enc_momentum,
    enc_average,
    fus_params,
    fus_momentum,
    fus_average,
    earth_bias,
    bias_momentum,
    bias_average,
):
    field = tokens[0, 0]
    row_count, col_count, feat_width = field.shape
    seq_count = lax.axis_size("seq")
    group_count = lax.axis_size("group")
    band_count = seq_count // SAMPLES
    place = lax.axis_index("seq")
    mine = lax.axis_index("group")
    fus_flat = fus_params.reshape(-1, LANES)
    plan = Sums(group_count, seq_count, fus_params.size, enc_params.size)
    enc_flat = rows_of_lanes(enc_params)
    latent, *saved = encoder_forward_call(field, enc_flat)
    merged, latent_grad, rest, table_grad, early_a, early_b = merging_call(
        plan, latent, cotangent[:, 0, 0], fus_flat, earth_bias.transpose(1, 0, 2)
    )
    field_grad, fus_block, enc_block, tab_block = encoder_backward_call(
        plan, latent_grad, enc_flat, rest, table_grad, early_a, early_b, saved
    )
    slot = mine * seq_count + place
    fus_grad = own_piece(fus_block, fus_params.size // (group_count * seq_count), slot)
    enc_grad = own_piece(enc_block, enc_params.size // seq_count, place)
    bias_grad = tab_block.reshape(-1)
    enc_piece = enc_grad.shape[0]
    enc_own = lax.dynamic_slice_in_dim(enc_params[0], place * enc_piece, enc_piece)
    fus_piece = fus_grad.shape[0]
    fus_own = lax.dynamic_slice_in_dim(fus_params, slot * fus_piece, fus_piece)
    bias_piece = bias_grad.shape[0]
    bias_own = lax.dynamic_slice_in_dim(earth_bias.reshape(-1), slot * bias_piece, bias_piece)
    lat_total = band_count * row_count
    enc_new, enc_momentum_new, enc_average_new = update(
        enc_own,
        enc_grad,
        enc_momentum[0],
        enc_average[0],
        1.0 / math.sqrt(CE * SAMPLES * lat_total * col_count),
    )
    fus_new, fus_momentum_new, fus_average_new = update(
        fus_own,
        fus_grad,
        fus_momentum,
        fus_average,
        1.0 / math.sqrt(CF * group_count * SAMPLES * lat_total * col_count),
    )
    bias_new, bias_momentum_new, bias_average_new = update(
        bias_own,
        bias_grad,
        bias_momentum,
        bias_average,
        2.0 / math.sqrt(SAMPLES * col_count / WIN_LON),
    )
    return (
        merged[:, None, None],
        field_grad[None, None],
        enc_grad[None],
        enc_new[None],
        enc_momentum_new[None],
        enc_average_new[None],
        fus_grad,
        fus_new,
        fus_momentum_new,
        fus_average_new,
        bias_grad,
        bias_new,
        bias_momentum_new,
        bias_average_new,
    )


def solution(mesh):
    both = P(("group", "seq"))
    rows = P("group", "seq")
    merged = P(None, "seq", "group", None, None, None)
    tokens = P("group", "seq", None, None, None)
    return jax.shard_map(
        shards,
        mesh=mesh,
        in_specs=(tokens, merged, P("group", None), rows, rows, P(), both, both, P(), both, both),
        out_specs=(merged, tokens, rows, rows, rows, rows) + (both,) * 8,
        check_vma=False,
    )
```

```python
from functools import partial
import math

import jax
import jax.numpy as jnp
import numpy as np
from jax import lax
from jax.experimental import pallas as pl
from jax.experimental.pallas import tpu as pltpu
from jax.sharding import PartitionSpec as P

CE = 192
CF = 384
HEADS_E = 6
HEADS_F = 12
MLP_E = 768
MLP_F = 1536
WIN_LAT = 6
WIN_LON = 12
WIN_MOD = 2
SAMPLES = 2
HEAD = 32
CHUNK = 256
FCH = 384
LANES = 128
ROWS_E = WIN_LAT * WIN_LON
ROWS_F = WIN_MOD * ROWS_E
SPAN = 2 * WIN_LON - 1
PAIRS = WIN_MOD * WIN_LAT
TAB_PAD = 384
EPS = 1e-05
NEG = -1000000000.0
VMEM_BYTES = 61 << 20

MOMENTUM_DECAY = 0.9
AVERAGE_DECAY = 0.99

F32 = jnp.float32
BF16 = jnp.bfloat16

ENC_MATS = {"in": (CE, 3 * CE), "out": (CE, CE), "up": (CE, MLP_E), "down": (MLP_E, CE), "lin": (CE, CF)}
ENC_VECS = {"g1": CE, "s1": CE, "qb": CE, "vb": CE, "ob": CE, "g2": CE, "s2": CE, "ub": MLP_E, "db": CE, "lb": CF}
FUS_MATS = {"in": (CF, 3 * CF), "out": (CF, CF), "up": (CF, MLP_F), "down": (MLP_F, CF)}
FUS_VECS = {"g1": CF, "s1": CF, "qb": CF, "vb": CF, "ob": CF, "g2": CF, "s2": CF, "ub": MLP_F, "db": CF}


def offsets(mats, vecs):
    places, at = {}, 0
    for name, shape in mats.items():
        places[name] = at // LANES
        at += shape[0] * shape[1]
    for name, amount in vecs.items():
        places[name] = at
        at += amount
    return places


ENC_AT = offsets(ENC_MATS, ENC_VECS)
FUS_AT = offsets(FUS_MATS, FUS_VECS)


def split(v):
    hi = v.astype(BF16)
    return hi, (v - hi.astype(F32)).astype(BF16)


def dot(a, b, ca=1, cb=0):
    return lax.dot_general(a, b, (((ca,), (cb,)), ((), ())), preferred_element_type=F32)


def dot3(a, b, ca=1, cb=0):
    return dot(a[0], b[0], ca, cb) + (dot(a[0], b[1], ca, cb) + dot(a[1], b[0], ca, cb))


def left3(a, axis=1):
    return jnp.concatenate([a[0], a[0], a[1]], axis)


def right3(b, axis=0):
    return jnp.concatenate([b[0], b[1], b[0]], axis)


def deep3(a, b, ca=1, cb=0):
    return dot(left3(a, ca), right3(b, cb), ca, cb)


def put(refs, index, v):
    hi, lo = split(v)
    refs[0][index] = hi
    refs[1][index] = lo


def get(refs, index):
    return refs[0][index], refs[1][index]


def half_lanes():
    return lax.broadcasted_iota(jnp.int32, (1, LANES), 1) < LANES // 2


def turn(v):
    return pltpu.roll(v, LANES // 2, 1)


def vector(flat, at, amount):
    tiles = []
    for c in range(-(-amount // LANES)):
        row, lane = divmod(at + c * LANES, LANES)
        one = flat[row : row + 1, :]
        if lane:
            one = turn(one)
            if c * LANES + LANES // 2 < amount:
                one = jnp.where(half_lanes(), one, turn(flat[row + 1 : row + 2, :]))
        tiles.append(one)
    return jnp.concatenate(tiles, 1)[:, :amount] if len(tiles) > 1 else tiles[0][:, :amount]


def put_vector(flat, at, v):
    amount = v.shape[1]
    if at % LANES == 0 and amount % LANES == 0:
        for c in range(amount // LANES):
            flat[at // LANES + c : at // LANES + c + 1, :] = v[:, c * LANES : (c + 1) * LANES]
        return
    half = LANES // 2
    for c in range(amount // half):
        row, lane = divmod(at + c * half, LANES)
        flat[row : row + 1, lane : lane + half] = v[:, c * half : (c + 1) * half]


def unpack_matrix(flat, at, shape, store, scratch):
    rows, width = shape
    if width % LANES == 0:
        n = width // LANES
        for c in range(n):
            store(slice(0, rows), c, flat[pl.ds(at + c, rows, stride=n), :])
        return
    pairs, n, full = rows // 2, 2 * width // LANES, width // LANES
    low = half_lanes()
    for c in range(full + 1):
        scratch[c, pl.ds(0, pairs, stride=2), :] = flat[pl.ds(at + c, pairs, stride=n), :]
        odd = turn(flat[pl.ds(at + full + c, pairs, stride=n), :])
        if c < full:
            odd = jnp.where(low, odd, turn(flat[pl.ds(at + full + c + 1, pairs, stride=n), :]))
        scratch[c, pl.ds(1, pairs, stride=2), :] = odd
    for c in range(full + 1):
        store(slice(0, rows), c, scratch[c, 0:rows, :])


def pack_matrix(flat, at, shape, source):
    rows, width = shape
    pairs, n, full = rows // 2, 2 * width // LANES, width // LANES
    low = half_lanes()

    def tile(odd, c):
        return source[c, pl.ds(odd, pairs, stride=2), :]

    for c in range(full):
        flat[pl.ds(at + c, pairs, stride=n), :] = tile(0, c)
        flat[pl.ds(at + full + 1 + c, pairs, stride=n), :] = jnp.where(low, turn(tile(1, c)), turn(tile(1, c + 1)))
    flat[pl.ds(at + full, pairs, stride=n), :] = jnp.where(low, tile(0, full), turn(tile(1, 0)))


def put_tiles(ref, rows, v):
    for c in range(-(-v.shape[1] // LANES)):
        one = v[:, c * LANES : (c + 1) * LANES]
        ref[c, rows, 0 : one.shape[1]] = one


def get_tiles(ref, rows, width):
    tiles = [ref[c, rows, 0 : min(width - c * LANES, LANES)] for c in range(-(-width // LANES))]
    return jnp.concatenate(tiles, 1)


def normalize(x):
    center = x - jnp.mean(x, 1, keepdims=True)
    scale = lax.rsqrt(jnp.mean(center * center, 1, keepdims=True) + EPS)
    return center * scale, scale


def normalize_back(dv, xhat, scale, gain):
    dxhat = dv * gain
    return scale * (dxhat - jnp.mean(dxhat, 1, keepdims=True) - xhat * jnp.mean(dxhat * xhat, 1, keepdims=True))


def gelu_parts(u):
    phi = 0.5 * (1.0 + lax.erf(u * (1.0 / math.sqrt(2.0))))
    return u * phi, phi + u * jnp.exp(-0.5 * u * u) * (1.0 / math.sqrt(2.0 * math.pi))


def head_masks(width):
    lane = lax.broadcasted_iota(jnp.int32, (1, width), 1)
    return [jnp.where((lane >= h * HEAD) & (lane < (h + 1) * HEAD), 1.0, 0.0) for h in range(width // HEAD)]


def stacked(pair, masks):
    return tuple(jnp.concatenate([part * m.astype(BF16) for m in masks], 0) for part in pair)


def unstacked(v, masks):
    rows = v.shape[0] // len(masks)
    total = v[:rows] * masks[0]
    for h in range(1, len(masks)):
        total = total + v[h * rows : (h + 1) * rows] * masks[h]
    return total


def softmax(s):
    e = jnp.exp(s - jnp.max(s, 1, keepdims=True))
    return e / jnp.sum(e, 1, keepdims=True)


def wide_nt(a, b):
    return dot(jnp.concatenate(a, 1), jnp.concatenate([b[0], b[0]], 1), 1, 1) + dot(a[0], b[1], 1, 1)


def wide_n(a, b, ca=1):
    n = b[0].shape[1]
    both = dot(a[0], jnp.concatenate(b, 1), ca, 0)
    return both[:, :n] + (both[:, n:] + dot(a[1], b[0], ca, 0))


def column_sum(v):
    return jnp.sum(v, 0, keepdims=True)


def encoder_slots():
    for r in range(WIN_LAT):
        for n in range(8):
            start = n * WIN_LON + WIN_LON // 2
            at = n * ROWS_E + r * WIN_LON
            if n < 7:
                yield r, at, start, WIN_LON
            else:
                yield r, at, start, WIN_LON // 2
                yield r, at + WIN_LON // 2, 0, WIN_LON // 2


def merging_slots():
    for z in range(WIN_MOD):
        for r in range(WIN_LAT):
            for n in range(4):
                yield z, r, n * ROWS_F + (z * WIN_LAT + r) * WIN_LON, n * WIN_LON


MESH = pl.DeviceIdType.MESH


def seq_digits(count):
    rest, digits = count // 2, []
    while rest > 1:
        digits.insert(0, 4 if rest % 4 == 0 else 2)
        rest //= digits[0]
    digits.sort()
    if count == 16:
        digits = [4, 2]
    return digits + [2]


class Places:
    def __init__(self, groups, seqs):
        self.sizes = [groups] + seq_digits(seqs)
        self.groups = groups
        self.strides = [1] * len(self.sizes)
        for i in range(len(self.sizes) - 2, 0, -1):
            self.strides[i] = self.strides[i + 1] * self.sizes[i + 1]

    def here(self):
        self.g, self.s = lax.axis_index("group"), lax.axis_index("seq")
        self.mine = [self.g] + [self.s // self.strides[i] % self.sizes[i] for i in range(1, len(self.sizes))]

    def peer(self, digit, value):
        if digit == 0:
            return (value, self.s)
        return (self.g, self.s + (value - self.mine[digit]) * self.strides[digit])

    def place(self, values):
        return sum(v * self.strides[i] for i, v in values.items() if i)


def windows(total, count):
    piece = total // count
    tiles = max(-(-(piece * (d + 1)) // 1024) - piece * d // 1024 for d in range(count))
    last = piece * (count - 1) // 1024
    return piece, tiles * 8, (last + tiles) * 8


def window_start(piece, d):
    return pl.multiple_of(piece * d // 1024 * 8, 8)


def start_copy(src, dst, sems, at, peer):
    one = pltpu.make_async_remote_copy(
        src_ref=src, dst_ref=dst, send_sem=sems[0].at[at], recv_sem=sems[1].at[at], device_id=peer, device_id_type=MESH
    )
    one.start()
    return one


class Stream:
    def __init__(self, places, plan, chosen, shift, sems, base):
        self.places, self.order, self.piece, self.first, self.rows = places, plan.order, plan.piece, plan.first, plan.rows
        self.chosen, self.shift, self.sems, self.base = chosen, shift, sems, base
        self.sizes = plan.sizes
        self.held, self.arrived = {}, {}
        self.last = len(places.sizes) - 1

    def buffers(self, held, arrived):
        self.held.update(held)
        self.arrived.update(arrived)
        return self

    def combos(self, i=0):
        out = [()]
        for n in self.sizes[i:]:
            out = [c + (v,) for c in out for v in range(n)]
        return out

    def number(self, values):
        where = self.places.place(values)
        if 0 in values:
            where = where + values[0] * (self.places.sizes[1] * self.places.strides[1])
        return where

    def target(self, i, combo, core):
        values = {d: self.places.mine[d] for d in self.order[:i]}
        values.update(zip(self.order[i:], combo))
        values[self.last] = core
        return self.number(values)

    def when(self, number, action):
        if self.chosen is None:
            action()
        else:
            pl.when(self.chosen(number))(action)

    def window(self, number):
        return pl.ds(pl.multiple_of(self.shift(window_start(self.piece, number)) + self.first, 8), self.rows)

    def core_copy(self, n, number, source):
        p = self.places
        core = p.mine[self.last]
        return pltpu.make_async_remote_copy(
            src_ref=source.at[self.window(number)], dst_ref=self.held[0].at[n], send_sem=self.sems[0].at[self.base + n],
            recv_sem=self.sems[1].at[self.base + n], device_id=p.peer(self.last, 1 - core), device_id_type=MESH,
        )

    def start_core(self, source):
        core = self.places.mine[self.last]
        for n, combo in enumerate(self.combos()):
            number = self.target(0, combo, 1 - core)
            self.when(number, lambda n=n, number=number: self.core_copy(n, number, source).start())

    def finish_core(self, source):
        core = self.places.mine[self.last]
        for n, combo in enumerate(self.combos()):
            number = self.target(0, combo, core)

            def add(n=n, number=number):
                self.core_copy(n, number, source).wait_recv()
                self.held[0][n] = self.held[0][n] + source[self.window(number), :]

            self.when(number, add)
        for n, combo in enumerate(self.combos()):
            number = self.target(0, combo, 1 - core)
            self.when(number, lambda n=n, number=number: self.core_copy(n, number, source).wait_send())

    def blocks(self, i):
        return math.prod(self.sizes[i + 1 :])

    def copy(self, i, k, n):
        p, digit, size = self.places, self.order[i], self.sizes[i]
        value = lax.rem(p.mine[digit] + k, size)
        at = self.base + len(self.combos()) + sum((self.sizes[j] - 1) * self.blocks(j) for j in range(i)) + (k - 1) * self.blocks(i) + n
        return pltpu.make_async_remote_copy(
            src_ref=self.held[i].at[value * self.blocks(i) + n], dst_ref=self.arrived[i].at[k - 1, n], send_sem=self.sems[0].at[at],
            recv_sem=self.sems[1].at[at], device_id=p.peer(digit, value), device_id_type=MESH,
        )

    def sent(self, i):
        core = self.places.mine[self.last]
        for k in range(1, self.sizes[i]):
            value = lax.rem(self.places.mine[self.order[i]] + k, self.sizes[i])
            for n, combo in enumerate(self.combos(i + 1)):
                yield k, n, self.target(i, (value,) + combo, core)

    def start(self, i):
        for k, n, number in self.sent(i):
            self.when(number, lambda k=k, n=n: self.copy(i, k, n).start())

    def finish(self, i, out=None):
        core = self.places.mine[self.last]
        mine = self.places.mine[self.order[i]]
        for n, combo in enumerate(self.combos(i + 1)):
            def add(n=n):
                total = self.held[i][mine * self.blocks(i) + n]
                for k in range(1, self.sizes[i]):
                    self.copy(i, k, n).wait_recv()
                    total = total + self.arrived[i][k - 1, n]
                if out is None:
                    self.held[i + 1][n] = total
                else:
                    out(total)

            self.when(self.target(i, (mine,) + combo, core), add)
        for k, n, number in self.sent(i):
            self.when(number, lambda k=k, n=n: self.copy(i, k, n).wait_send())

    def semaphores(self):
        return len(self.combos()) + sum((self.sizes[j] - 1) * self.blocks(j) for j in range(len(self.sizes)))


class Portion:
    def __init__(self, places, order, piece, first, rows):
        self.order, self.piece, self.first, self.rows = order, piece, first, rows
        self.sizes = [places.sizes[d] for d in order]

    def blocks(self, i):
        return math.prod(self.sizes[i + 1 :])

    def core_scratch(self):
        return vmem(math.prod(self.sizes), self.rows, LANES)

    def scratch(self, i):
        return vmem(self.sizes[i] - 1, self.blocks(i), self.rows, LANES)

    def semaphores(self):
        return math.prod(self.sizes) + sum((self.sizes[j] - 1) * self.blocks(j) for j in range(len(self.sizes)))


class Sums:
    def __init__(self, groups, seqs, fus_total, enc_total):
        self.places = places = Places(groups, seqs)
        last = len(places.sizes) - 1
        order = sorted(range(1, last), key=lambda d: places.sizes[d])
        piece, rows, self.fus_all = windows(fus_total, groups * seqs)
        enc_piece, enc_rows, self.enc_all = windows(enc_total, seqs)
        first = rows * 4 // 64 * 8
        self.fus = [
            Portion(places, [0] + order, piece, 0, first),
            Portion(places, order[:1] + [0] + order[1:], piece, first, rows - first),
        ]
        cut_a, cut_b = rows * 5 // 96 * 8 // 1, rows * 9 // 96 * 8 // 1
        cut_a, cut_b = cut_a // 8 * 8, cut_b // 8 * 8
        self.late = [
            Portion(places, [0] + order, piece, 0, cut_a),
            Portion(places, order[:1] + [0] + order[1:], piece, cut_a, cut_b - cut_a),
            Portion(places, order[-1:] + [0] + order[:-1], piece, cut_b, rows - cut_b),
        ]
        self.enc = [Portion(places, order, enc_piece, 0, enc_rows)] * 2
        self.fus_rows, self.enc_rows = rows, enc_rows
        self.low, self.high = FUS_AT["up"], FUS_AT["g1"] // LANES
        starts = [piece * d // 1024 * 8 for d in range(groups * seqs)]
        self.early = [d for d, at in enumerate(starts) if at >= self.low and at + rows <= self.high]
        others = [at for d, at in enumerate(starts) if d not in self.early]
        self.rest_low = max(at for at in others if at < self.low) + rows
        self.rest_from = min(at for at in others if at >= self.low)
        self.rest_all = self.rest_low + self.fus_all - self.rest_from
        enc_starts = [enc_piece * d // 1024 * 8 for d in range(seqs)]
        low, high = ENC_AT["up"], ENC_AT["g1"] // LANES
        self.enc_early = [d for d, at in enumerate(enc_starts) if at >= low and at + enc_rows <= high]

    def is_early(self, d):
        return jnp.logical_and(d >= self.early[0], d <= self.early[-1])

    def is_late(self, d):
        return jnp.logical_not(self.is_early(d))

    def is_enc_early(self, d):
        return jnp.logical_and(d >= self.enc_early[0], d <= self.enc_early[-1])

    def is_enc_late(self, d):
        return jnp.logical_not(self.is_enc_early(d))

    def rest_shift(self, at):
        return jnp.where(at < self.low, at, at - self.rest_from + self.rest_low)


def encoder_forward(
    field_ref, flat,
    lat_ref, xhat_ref, rstd_ref, qkv_ref, p_h, p_l, o_ref, xhat2_ref, rstd2_ref, g_h, g_l, dg_ref, out_ref,
    win_h, win_l, wout_h, wout_l, wup_h, wup_l, wdn_h, wdn_l, wlin_h, wlin_l,
    x, wide, lat, head_ref, send, recv,
):
    g, s = lax.axis_index("group"), lax.axis_index("seq")
    seqs = lax.axis_size("seq")
    before, after = lax.rem(s + seqs - SAMPLES, seqs), lax.rem(s + SAMPLES, seqs)
    barrier = pltpu.get_barrier_semaphore()
    for other in (before, after):
        pl.semaphore_signal(barrier, inc=1, device_id=(g, other), device_id_type=MESH)
    pl.semaphore_wait(barrier, 2)
    halo = start_copy(field_ref.at[pl.ds(0, 3)], head_ref, (send, recv), 0, (g, before))
    for pair, name in (((win_h, win_l), "in"), ((wout_h, wout_l), "out"), ((wup_h, wup_l), "up"), ((wdn_h, wdn_l), "down"), ((wlin_h, wlin_l), "lin")):
        width = ENC_MATS[name][1]

        def store(rows, c, v, pair=pair, width=width):
            last = min(width - c * LANES, LANES)
            put(pair, (rows, slice(c * LANES, c * LANES + last)), v[:, :last])

        unpack_matrix(flat, ENC_AT[name], ENC_MATS[name], store, wide)
    vec = {name: vector(flat, ENC_AT[name], amount) for name, amount in ENC_VECS.items()}
    masks = head_masks(CE)
    halo.wait()
    for r, at, start, amount in encoder_slots():
        x[at : at + amount, :] = (field_ref[r + 3, start : start + amount, :] if r < 3 else head_ref[r - 3, start : start + amount, :])
    wrapped = s // SAMPLES == seqs // SAMPLES - 1
    half = ROWS_E // 2
    upper = lax.broadcasted_iota(jnp.int32, (ROWS_E, ROWS_E), 0) >= half
    right = lax.broadcasted_iota(jnp.int32, (ROWS_E, ROWS_E), 1) >= half
    apart = jnp.where(jnp.logical_and(upper != right, wrapped), 1.0, 0.0)
    apart = jnp.concatenate([apart] * HEADS_E, 0)
    win, wout, wup, wdn, wlin = (win_h, win_l), (wout_h, wout_l), (wup_h, wup_l), (wdn_h, wdn_l), (wlin_h, wlin_l)
    scale = 1.0 / math.sqrt(HEAD)

    full = slice(None)
    xhat, rstd = normalize(x[...])
    xhat_ref[...] = xhat
    rstd_ref[...] = rstd
    xn = split(xhat * vec["g1"] + vec["s1"])
    for j, name in enumerate(("qb", None, "vb")):
        cols = slice(j * CE, (j + 1) * CE)
        one = dot3(xn, get(win, (full, cols)))
        if name is not None:
            one = one + vec[name]
        qkv_ref[:, cols] = one * scale if j == 0 else one

    def step(i, carry):
        rows = pl.ds(pl.multiple_of(i * 2 * ROWS_E, 2 * ROWS_E), 2 * ROWS_E)
        qkv = qkv_ref[rows, :]
        parts = []
        for w in range(2):
            one = qkv[w * ROWS_E : (w + 1) * ROWS_E]
            q, k, v = (one[:, j * CE : (j + 1) * CE] for j in range(3))
            qm = split(jnp.concatenate([q * m for m in masks], 0))
            s = dot3(qm, split(k), 1, 1)
            s = jnp.where(apart > 0.5, NEG, s)
            p = split(softmax(s))
            p_h[i * 2 + w] = p[0]
            p_l[i * 2 + w] = p[1]
            parts.append(unstacked(dot3(p, split(v)), masks))
        o_ref[rows, :] = jnp.concatenate(parts, 0)
        return carry

    lax.fori_loop(0, 4, step, 0)
    hidden = x[...] + dot3(split(o_ref[...]), get(wout, (full, full))) + vec["ob"]
    xhat2, rstd2 = normalize(hidden)
    xhat2_ref[...] = xhat2
    rstd2_ref[...] = rstd2
    hn = split(xhat2 * vec["g2"] + vec["s2"])
    out_ref[...] = hidden + vec["db"]
    for c in range(MLP_E // CHUNK):
        cols = slice(c * CHUNK, (c + 1) * CHUNK)
        u = dot3(hn, get(wup, (full, cols))) + vec["ub"][:, cols]
        one, slope = gelu_parts(u)
        dg_ref[:, cols] = slope
        one = split(one)
        g_h[:, cols] = one[0]
        g_l[:, cols] = one[1]
        out_ref[...] = out_ref[...] + deep3(one, get(wdn, (cols, full)))
    lat[...] = dot3(split(out_ref[...]), get(wlin, (full, full))) + vec["lb"]
    for r, at, start, amount in encoder_slots():
        lat_ref[r, start : start + amount, :] = lat[at : at + amount, :]


def vmem(*shape, dtype=F32):
    return pltpu.VMEM(shape, dtype)


def pair_of(*shape):
    return [vmem(*shape, dtype=BF16)] * 2


def call(kernel, name, inputs, outs, scratch, number, flops=0, far=(), far_outs=()):
    specs = [pl.BlockSpec(memory_space=pl.ANY if n in far else pltpu.VMEM) for n in range(len(inputs))]
    moved = sum(v.size * v.dtype.itemsize for v in list(inputs) + list(outs))
    return pl.pallas_call(
        kernel,
        name=name,
        out_shape=outs,
        in_specs=specs,
        out_specs=[pl.BlockSpec(memory_space=pl.ANY if n in far_outs else pltpu.VMEM) for n in range(len(outs))],
        scratch_shapes=scratch,
        cost_estimate=pl.CostEstimate(flops=flops, bytes_accessed=moved, transcendentals=0),
        compiler_params=pltpu.CompilerParams(collective_id=number, has_side_effects=True, vmem_limit_bytes=VMEM_BYTES),
    )(*inputs)


def sems(count):
    return [pltpu.SemaphoreType.DMA((count,)), pltpu.SemaphoreType.DMA((count,))]


def shape(*dims, dtype=F32):
    return jax.ShapeDtypeStruct(dims, dtype)


def rows_kernel(line_ref, rows_ref):
    amount = line_ref.shape[1] // LANES
    rows_ref[0:amount, :] = line_ref.reshape(amount, LANES)[...]


def rows_of_lanes(line, amount):
    return pl.pallas_call(
        rows_kernel,
        name="rows_of_lanes",
        out_shape=shape(amount, LANES),
        compiler_params=pltpu.CompilerParams(vmem_limit_bytes=VMEM_BYTES),
    )(line)


def encoder_forward_call(field, flat):
    n = 8 * ROWS_E
    outs = [
        shape(WIN_LAT, 96, CF), shape(n, CE), shape(n, 1), shape(n, 3 * CE),
        shape(8, HEADS_E * ROWS_E, ROWS_E, dtype=BF16), shape(8, HEADS_E * ROWS_E, ROWS_E, dtype=BF16),
        shape(n, CE), shape(n, CE), shape(n, 1), shape(n, MLP_E, dtype=BF16), shape(n, MLP_E, dtype=BF16),
        shape(n, MLP_E), shape(n, CE),
    ]
    scratch = (
        pair_of(CE, 3 * CE) + pair_of(CE, CE) + pair_of(CE, MLP_E) + pair_of(MLP_E, CE) + pair_of(CE, CF)
        + [vmem(n, CE), vmem(5, MLP_E, LANES), vmem(n, CF), vmem(3, 96, CE)] + sems(1)
    )
    return call(encoder_forward, "encoder_forward", [field, flat], outs, scratch, 0, 6 * n * 516096)


def encoder_backward(
    plan,
    dlat_ref, flat, rest, tab, early_a, early_b,
    xhat_ref, rstd_ref, qkv_far, ph_far, pl_far, o_ref, xhat2_ref, rstd2_ref, gh_far, gl_far, dg_far, out_ref,
    field_grad, fus_out, enc_out, tab_out,
    qkv_ref, p_h, p_l, g_h, g_l, dg_ref,
    grad, tabs, send, recv, local_sems, win_h, win_l, wout_h, wout_l, wup_h, wup_l, wdn_h, wdn_l, wlin_h, wlin_l,
    dlat, wide, dout, dout_h, dout_l, dhn, du_h, du_l, hn_h, hn_l, dh_h, dh_l, dqkv_h, dqkv_l, xn_h, xn_l, sums, dx, dback,
    *refs,
):
    loads = [
        pltpu.make_async_copy(src, dst, local_sems.at[n])
        for n, (src, dst) in enumerate(
            ((gh_far, g_h), (gl_far, g_l), (dg_far, dg_ref), (qkv_far, qkv_ref), (ph_far, p_h), (pl_far, p_l))
        )
    ]
    for one in loads:
        one.start()
    places = plan.places
    places.here()
    g, s = places.g, places.s
    seqs = places.sizes[1] * places.strides[1]
    before, after = lax.rem(s + seqs - SAMPLES, seqs), lax.rem(s + SAMPLES, seqs)
    slot, band = g * seqs + s, s // SAMPLES
    mine = g * SAMPLES + lax.rem(s, SAMPLES)
    owners = [((4 * band + j) // seqs, lax.rem(4 * band + j, seqs)) for j in range(4)]
    givers = [(k // 2, slot // 4 * SAMPLES + k % 2) for k in range(4)]

    def other(pg, ps):
        return jnp.logical_or(pg != g, ps != s)

    barrier = pltpu.get_barrier_semaphore()
    peers = [(g, before), (g, after)]
    for digit, size in enumerate(places.sizes):
        peers += [places.peer(digit, lax.rem(places.mine[digit] + k, size)) for k in range(1, size)]
    for peer in peers:
        pl.semaphore_signal(barrier, inc=1, device_id=peer, device_id_type=MESH)
    for pg, ps in owners + givers:
        @pl.when(other(pg, ps))
        def _(pg=pg, ps=ps):
            pl.semaphore_signal(barrier, inc=1, device_id=(pg, ps), device_id_type=MESH)
    pl.semaphore_wait(barrier, len(peers) + jnp.where(slot // 4 == band, 6, 8))

    refs = list(refs)
    base = 8
    early, late, encs = [], [], []
    for portion, held in zip(plan.fus, (early_a, early_b)):
        one = Stream(places, portion, plan.is_early, lambda at: at, (send, recv), base)
        arrived = {i: refs.pop(0) for i in range(1, len(portion.order))}
        early.append(one.buffers({1: held}, arrived).buffers({i + 1: arrived[i].at[0] for i in arrived}, {}))
        base += portion.semaphores()
    for group, portions, choices, shift in (
        (late, plan.late, [plan.is_late] * 3, plan.rest_shift),
        (encs, plan.enc, [plan.is_enc_early, plan.is_enc_late], lambda at: at),
    ):
        for portion, chosen in zip(portions, choices):
            one = Stream(places, portion, chosen, shift, (send, recv), base)
            held = {0: refs.pop(0)}
            arrived = {i: refs.pop(0) for i in range(len(portion.order))}
            group.append(one.buffers(held, arrived).buffers({i + 1: arrived[i].at[0] for i in arrived}, {}))
            base += portion.semaphores()

    def keep(one, split_at):
        def store(total):
            fus_out[split_at : split_at + one.rows, :] = total
        return store

    stages = len(plan.fus[0].order)

    def keep_enc(total):
        enc_out[...] = total

    def go(streams, i):
        for one in streams:
            if i == 0:
                one.finish_core(grad if one in encs else rest)
            else:
                last = keep_enc if one in encs else keep(one, one.first)
                one.finish(i - 1, last if i == len(one.order) else None)
            if i < len(one.order):
                one.start(i)

    for one in late:
        one.start_core(rest)
    for one in early:
        one.start(1)

    def give(j, pg, ps):
        return pltpu.make_async_remote_copy(
            src_ref=tab.at[j], dst_ref=tabs.at[mine], send_sem=send.at[4 + j], recv_sem=recv.at[4 + mine],
            device_id=(pg, ps), device_id_type=MESH,
        )

    for j, (pg, ps) in enumerate(owners):
        @pl.when(other(pg, ps))
        def _(j=j, pg=pg, ps=ps):
            give(j, pg, ps).start()

        @pl.when(jnp.logical_not(other(pg, ps)))
        def _(j=j):
            tabs[mine] = tab[j]

    win, wout, wup, wdn, wlin = (win_h, win_l), (wout_h, wout_l), (wup_h, wup_l), (wdn_h, wdn_l), (wlin_h, wlin_l)
    for pair, name in ((win, "in"), (wout, "out"), (wup, "up"), (wdn, "down"), (wlin, "lin")):
        width = ENC_MATS[name][1]

        def store(rows, c, v, pair=pair, width=width):
            last = min(width - c * LANES, LANES)
            put(pair, (rows, slice(c * LANES, c * LANES + last)), v[:, :last])

        unpack_matrix(flat, ENC_AT[name], ENC_MATS[name], store, wide)
    vec = {name: vector(flat, ENC_AT[name], ENC_VECS[name]) for name in ("g1", "s1", "g2", "s2")}
    masks = head_masks(CE)
    full = slice(None)
    scale = 1.0 / math.sqrt(HEAD)
    go(late, 0)
    for r, at, start, amount in encoder_slots():
        dlat[at : at + amount, :] = dlat_ref[r, start : start + amount, :]
    for one in loads[:3]:
        one.wait()
    dl = split(dlat[...])
    put_vector(grad, ENC_AT["lb"], column_sum(dlat[...]))
    d = dot3(dl, get(wlin, (full, full)), 1, 1)
    dout[...] = d
    put((dout_h, dout_l), (full, full), d)
    put_vector(grad, ENC_AT["db"], column_sum(d))
    dw = deep3(split(out_ref[...]), dl, 0, 0)
    for c in range(3):
        grad[pl.ds(ENC_AT["lin"] + c, CE, stride=3), :] = dw[:, c * LANES : (c + 1) * LANES]
    xhat2 = xhat2_ref[...]
    put((hn_h, hn_l), (full, full), xhat2 * vec["g2"] + vec["s2"])
    hn_t = left3((hn_h[...], hn_l[...]), 0).T
    do_t = left3((dout_h[...], dout_l[...]), 0).T
    for c in range(MLP_E // CHUNK):
        cols = slice(c * CHUNK, (c + 1) * CHUNK)
        do = (dout_h[...], dout_l[...])
        du = dot3(do, get(wdn, (cols, full)), 1, 1) * dg_ref[:, cols]
        put_vector(grad, ENC_AT["ub"] + c * CHUNK, column_sum(du))
        du = split(du)
        if c == 2:
            go(early, 2)
        part = deep3(du, get(wup, (full, cols)), 1, 1)
        dhn[...] = part if c == 0 else dhn[...] + part
        dw = dot(hn_t, right3(du))
        for t in range(2):
            grad[pl.ds(ENC_AT["up"] + 2 * c + t, CE, stride=6), :] = dw[:, t * LANES : (t + 1) * LANES]
        dw = dot(do_t, right3((g_h[:, cols], g_l[:, cols]))).T
        put_tiles(wide, slice(c * CHUNK, (c + 1) * CHUNK), dw)
    pack_matrix(grad, ENC_AT["down"], ENC_MATS["down"], wide)
    dv = dhn[...]
    put_vector(grad, ENC_AT["g2"], column_sum(dv * xhat2))
    put_vector(grad, ENC_AT["s2"], column_sum(dv))
    d = dout[...] + normalize_back(dv, xhat2, rstd2_ref[...], vec["g2"])
    dout[...] = d
    put((dh_h, dh_l), (full, full), d)
    put_vector(grad, ENC_AT["ob"], column_sum(d))
    dw = deep3(split(o_ref[...]), (dh_h[...], dh_l[...]), 0, 0)
    put_tiles(wide, slice(0, CE), dw)
    pack_matrix(grad, ENC_AT["out"], ENC_MATS["out"], wide)
    sums[...] = jnp.zeros_like(sums)
    encs[0].start_core(grad)
    go(late, 1)
    go(encs[:1], 0)
    for one in loads[3:]:
        one.wait()

    def step(i, carry):
        rows = pl.ds(pl.multiple_of(i * 2 * ROWS_E, 2 * ROWS_E), 2 * ROWS_E)
        do = dhn[rows, :]
        parts = []
        for w in range(2):
            one = qkv_ref[pl.ds(pl.multiple_of(i * 2 * ROWS_E, 2 * ROWS_E) + w * ROWS_E, ROWS_E), :]
            q, k, v = (one[:, j * CE : (j + 1) * CE] for j in range(3))
            dow = do[w * ROWS_E : (w + 1) * ROWS_E]
            dom = split(jnp.concatenate([dow * m for m in masks], 0))
            qm = split(jnp.concatenate([q * m for m in masks], 0))
            p = (p_h[i * 2 + w], p_l[i * 2 + w])
            dp = dot3(dom, split(v), 1, 1)
            pf = p[0].astype(F32) + p[1].astype(F32)
            t = pf * dp
            ds = split(t - pf * jnp.sum(t, 1, keepdims=True))
            dq = unstacked(dot3(ds, split(k)), masks) * scale
            dk = dot(left3(qm, 0).T, right3(ds)).T
            dvv = dot(left3(dom, 0).T, right3(p)).T
            parts.append(jnp.concatenate([dq, dk, dvv], 1))
        dqkv = jnp.concatenate(parts, 0)
        sums[0:1, :] = sums[0:1, :] + column_sum(dqkv)
        put((dqkv_h, dqkv_l), (rows, full), dqkv)
        return carry

    dhn[...] = dot3((dh_h[...], dh_l[...]), get(wout, (full, full)), 1, 1)
    lax.fori_loop(0, 2, step, 0)
    go(late, 2)
    lax.fori_loop(2, 4, step, 0)
    go(encs[:1], 1)
    xhat = xhat_ref[...]
    put((xn_h, xn_l), (full, full), xhat * vec["g1"] + vec["s1"])
    dxn = dot3((dqkv_h[...], dqkv_l[...]), get(win, (full, full)), 1, 1)
    sums[1:2, 0:CE] = column_sum(dxn * xhat)
    sums[2:3, 0:CE] = column_sum(dxn)
    dx[...] = dout[...] + normalize_back(dxn, xhat, rstd_ref[...], vec["g1"])
    for r, at, start, amount in encoder_slots():
        if r < 3:
            field_grad[r + 3, start : start + amount, :] = dx[at : at + amount, :]
        else:
            dback[r - 3, start : start + amount, :] = dx[at : at + amount, :]
    back = start_copy(dback, field_grad.at[pl.ds(0, 3)], (send, recv), 3, (g, after))
    put_vector(grad, ENC_AT["qb"], sums[0:1, 0:CE])
    put_vector(grad, ENC_AT["vb"], sums[0:1, 2 * CE : 3 * CE])
    put_vector(grad, ENC_AT["g1"], sums[1:2, 0:CE])
    put_vector(grad, ENC_AT["s1"], sums[2:3, 0:CE])
    dw = deep3((xn_h[...], xn_l[...]), (dqkv_h[...], dqkv_l[...]), 0, 0)
    put_tiles(wide, slice(0, CE), dw)
    pack_matrix(grad, ENC_AT["in"], ENC_MATS["in"], wide)
    encs[1].start_core(grad)
    go(encs[1:], 0)
    back.wait()
    for j, (pg, ps) in enumerate(owners):
        @pl.when(other(pg, ps))
        def _(j=j, pg=pg, ps=ps):
            give(j, pg, ps).wait_send()
    for k, (pg, ps) in enumerate(givers):
        @pl.when(other(pg, ps))
        def _(k=k, pg=pg, ps=ps):
            pltpu.make_async_remote_copy(
                src_ref=tab.at[0], dst_ref=tabs.at[k], send_sem=send.at[4], recv_sem=recv.at[4 + k],
                device_id=(pg, ps), device_id_type=MESH,
            ).wait_recv()
    tab_out[...] = (tabs[0] + tabs[1]) + (tabs[2] + tabs[3])
    for i in range(3, stages + 1):
        go(early, i)
    go(encs[1:], 1)
    for i in range(3, stages + 1):
        go(late, i)
    for i in range(2, len(encs[0].order) + 1):
        go(encs, i)


def encoder_backward_call(plan, dlat, flat, rest, tab, early_a, early_b, saved):
    n = 8 * ROWS_E
    refs, count = [], 8
    for portion in plan.fus:
        refs += [portion.scratch(i) for i in range(1, len(portion.order))]
        count += portion.semaphores()
    for portion in plan.late + plan.enc:
        refs += [portion.core_scratch()] + [portion.scratch(i) for i in range(len(portion.order))]
        count += portion.semaphores()
    xhat, rstd, qkv, p_h, p_l, o, xhat2, rstd2, g_h, g_l, dg, out = saved
    scratch = (
        [pltpu.VMEM(v.shape, v.dtype) for v in (qkv, p_h, p_l, g_h, g_l, dg)]
        + [vmem(plan.enc_all, LANES), vmem(*tab.shape)] + sems(count) + [pltpu.SemaphoreType.DMA((6,))]
        + pair_of(CE, 3 * CE) + pair_of(CE, CE) + pair_of(CE, MLP_E) + pair_of(MLP_E, CE) + pair_of(CE, CF)
        + [vmem(n, CF), vmem(5, MLP_E, LANES), vmem(n, CE)] + pair_of(n, CE) + [vmem(n, CE)] + pair_of(n, CHUNK)
        + pair_of(n, CE) + pair_of(n, CE) + pair_of(n, 3 * CE) + pair_of(n, CE) + [vmem(8, 3 * CE), vmem(n, CE), vmem(3, 96, CE)]
        + refs
    )
    return call(
        partial(encoder_backward, plan), "encoder_backward", [dlat, flat, rest, tab, early_a, early_b] + list(saved),
        [shape(WIN_LAT, 96, CE), shape(plan.fus_rows, LANES), shape(plan.enc_rows, LANES), shape(*tab.shape[1:])],
        scratch, 2, 12 * n * 516096, tuple(6 + j for j in (2, 3, 4, 8, 9, 10)),
    )


def merging(
    plan,
    lat_ref, cot_ref, flat_ref, tab_ref, base_ref,
    out_ref, dlat_ref, rest_ref, dtab_ref, early_a, early_b,
    grad, core_a, core_b, first_a, first_b, fld_ref, send, recv, lines, bands, vectors, local_sems,
    win_h, win_l, wout_h, wout_l, wup_h, wup_l, wdn_h, wdn_l,
    bias, dbias, x, xhat1, rstd1, xn_h, xn_l, q_h, q_l, k_h, k_l, v_h, v_l, p_h, p_l, o_h, o_l,
    xhat2, rstd2, hn_h, hn_l, acc, dhn, dy, dy_h, dy_l, hn_t, dy_t, dh_h, dh_l, dqkv_h, dqkv_l, sums,
):
    win, wout, wup, wdn = (win_h, win_l), (wout_h, wout_l), (wup_h, wup_l), (wdn_h, wdn_l)
    full = slice(None)
    chunks = MLP_F // FCH
    g, s = lax.axis_index("group"), lax.axis_index("seq")
    seqs = lax.axis_size("seq")
    before, after = lax.rem(s + seqs - SAMPLES, seqs), lax.rem(s + SAMPLES, seqs)
    band = s // SAMPLES
    picked = pltpu.make_async_copy(tab_ref.at[:, pl.ds(pl.multiple_of(band // 8 * 8, 8), 8)], bands, local_sems.at[0])
    picked.start()
    loads = {}
    for n, name in enumerate(FUS_MATS):
        some = pl.ds(FUS_AT[name], math.prod(FUS_MATS[name]) // LANES)
        loads[name] = pltpu.make_async_copy(flat_ref.at[some], grad.at[some], local_sems.at[n + 1])
    at = FUS_AT["g1"] // LANES
    loads["g1"] = pltpu.make_async_copy(flat_ref.at[pl.ds(at, flat_ref.shape[0] - at)], vectors, local_sems.at[5])
    for one in loads.values():
        one.start()
    barrier = pltpu.get_barrier_semaphore()
    places = plan.places
    places.here()
    peers = [(1 - g, s), (g, before), (g, after), (1 - g, before), (1 - g, after)]
    for digit in (len(places.sizes) - 1, plan.fus[1].order[0]):
        size = places.sizes[digit]
        peers += [places.peer(digit, lax.rem(places.mine[digit] + k, size)) for k in range(1, size)]
    for peer in peers:
        pl.semaphore_signal(barrier, inc=1, device_id=peer, device_id_type=MESH)
    pl.semaphore_wait(barrier, len(peers))
    early, base = [], 6
    for portion, core, first, out in zip(plan.fus, (core_a, core_b), (first_a, first_b), (early_a, early_b)):
        early.append(Stream(places, portion, plan.is_early, lambda at: at, (send, recv), base).buffers({0: core, 1: out}, {0: first}))
        base += portion.semaphores()

    def half(one):
        return pl.ds(pl.multiple_of(one * 48, 48), 48)

    far = [
        start_copy(lat_ref.at[pl.ds(0, 3), half(1 - g)], fld_ref.at[g, pl.ds(3, 3)], (send, recv), 0, (1 - g, s)),
        start_copy(lat_ref.at[pl.ds(3, 3), half(g)], fld_ref.at[g, pl.ds(0, 3)], (send, recv), 1, (g, after)),
        start_copy(lat_ref.at[pl.ds(3, 3), half(1 - g)], fld_ref.at[g, pl.ds(0, 3)], (send, recv), 2, (1 - g, after)),
    ]
    fld_ref[g, 3:6] = lat_ref[0:3, half(g), :]
    scale = 1.0 / math.sqrt(HEAD)

    def store(pair):
        def one(rows, c, v):
            put(pair, (rows, slice(c * LANES, (c + 1) * LANES)), v)
        return one

    def store_up(rows, c, v):
        put(wup, (c // (FCH // LANES), full, slice(c % (FCH // LANES) * LANES, (c % (FCH // LANES) + 1) * LANES)), v)

    def store_down(rows, c, v):
        for j in range(chunks):
            put(wdn, (j, full, slice(c * LANES, (c + 1) * LANES)), v[j * FCH : (j + 1) * FCH])

    loads["in"].wait()
    unpack_matrix(grad, FUS_AT["in"], FUS_MATS["in"], store(win), None)
    loads["out"].wait()
    unpack_matrix(grad, FUS_AT["out"], FUS_MATS["out"], store(wout), None)
    loads["up"].wait()
    unpack_matrix(grad, FUS_AT["up"], FUS_MATS["up"], store_up, None)
    loads["down"].wait()
    unpack_matrix(grad, FUS_AT["down"], FUS_MATS["down"], store_down, None)
    loads["g1"].wait()
    vec = {name: vector(vectors, FUS_AT[name] - FUS_AT["g1"], amount) for name, amount in FUS_VECS.items()}
    masks = head_masks(LANES)

    spots = jnp.where(lax.broadcasted_iota(jnp.int32, (TAB_PAD, 2 * LANES), 0) == base_ref[...], 1.0, 0.0).astype(BF16)
    picked.wait()
    for h in range(HEADS_F):
        lines[h : h + 1, :] = bands[h, pl.ds(lax.rem(band, 8), 1), :]
    pad = jnp.zeros((HEADS_F, TAB_PAD - PAIRS * SPAN), F32)
    table = []
    for z in range(WIN_MOD):
        for r in range(WIN_LAT):
            at = [((z * WIN_MOD + y) * WIN_LAT * WIN_LAT + r * WIN_LAT) * SPAN for y in range(WIN_MOD)]
            one = jnp.concatenate([lines[0:HEADS_F, t : t + WIN_LAT * SPAN] for t in at] + [pad], 1)
            table.append(jnp.concatenate([one, jnp.zeros((16 - HEADS_F, TAB_PAD), F32)], 0))
    table = jnp.concatenate(table, 0)
    for w in range(WIN_LON):
        turned = pltpu.roll(table, TAB_PAD - w, 1) if w else table
        hi, lo = split(turned)
        rest = (turned - hi.astype(F32) - lo.astype(F32)).astype(BF16)
        one = dot(hi, spots) + (dot(lo, spots) + dot(rest, spots))
        for n in range(PAIRS):
            for c in range(2):
                bias[c, pl.ds(n * WIN_LON + w, HEADS_F, stride=ROWS_F), :] = one[n * 16 : n * 16 + HEADS_F, c * LANES : (c + 1) * LANES]
    dbias[...] = jnp.zeros_like(dbias)

    for one in far:
        one.wait()
    for z, r, at, start in merging_slots():
        x[at : at + WIN_LON, :] = fld_ref[z, r, start : start + WIN_LON, :]
        dy[at : at + WIN_LON, :] = cot_ref[z, r, start : start + WIN_LON, :]

    def rows_of(i):
        return pl.ds(pl.multiple_of(i * ROWS_F, ROWS_F), ROWS_F)

    xhat, rstd = normalize(x[...])
    xhat1[...] = xhat
    rstd1[...] = rstd
    put((xn_h, xn_l), (full, full), xhat * vec["g1"] + vec["s1"])
    for j, (pair, shift) in enumerate((((q_h, q_l), vec["qb"]), ((k_h, k_l), None), ((v_h, v_l), vec["vb"]))):
        one = deep3((xn_h[...], xn_l[...]), get(win, (full, slice(j * CF, (j + 1) * CF))))
        if shift is not None:
            one = one + shift
        if j == 0:
            one = one * scale
        put(pair, (full, full), one)

    def forward(i, carry):
        rows = rows_of(i)
        for b in range(3):
            cols = slice(b * LANES, (b + 1) * LANES)
            qm = stacked((q_h[rows, cols], q_l[rows, cols]), masks)
            some = slice(b * 4 * ROWS_F, (b + 1) * 4 * ROWS_F)
            s = deep3(qm, (k_h[rows, cols], k_l[rows, cols]), 1, 1) + get_tiles(bias, some, ROWS_F)
            p = split(softmax(s))
            p_h[i * 3 + b] = p[0]
            p_l[i * 3 + b] = p[1]
            o = unstacked(wide_n(p, (v_h[rows, cols], v_l[rows, cols])), masks)
            put((o_h, o_l), (rows, cols), o)
        return carry

    lax.fori_loop(0, 4, forward, 0)
    hidden = x[...] + deep3((o_h[...], o_l[...]), get(wout, (full, full))) + vec["ob"]
    xh2, rstd = normalize(hidden)
    xhat2[...] = xh2
    rstd2[...] = rstd
    put((hn_h, hn_l), (full, full), xh2 * vec["g2"] + vec["s2"])
    acc[...] = hidden + vec["db"]
    put((dy_h, dy_l), (full, full), dy[...])
    dhn[...] = jnp.zeros_like(dhn)
    hn_t[...] = left3((hn_h[...], hn_l[...]), 0).T
    dy_t[...] = left3((dy_h[...], dy_l[...]), 0).T
    for c in range(chunks):
        sums[8:9, c * FCH : (c + 1) * FCH] = vec["ub"][:, c * FCH : (c + 1) * FCH]

    def feed(c, carry):
        up = (wup_h[c], wup_l[c])
        down = (wdn_h[c], wdn_l[c])
        cols = pl.ds(pl.multiple_of(c * FCH, FCH), FCH)
        shift = sums[8:9, cols]

        u = deep3((hn_h[...], hn_l[...]), up) + shift
        gl, slope = gelu_parts(u)
        gl = split(gl)
        acc[...] = acc[...] + deep3(gl, down)
        du = deep3((dy_h[...], dy_l[...]), down, 1, 1) * slope
        sums[9:10, cols] = column_sum(du)
        du = split(du)
        dhn[...] = dhn[...] + deep3(du, up, 1, 1)
        dw = dot(hn_t[...], right3(du))
        for t in range(FCH // LANES):
            grad[pl.ds(FUS_AT["up"] + FCH // LANES * c + t, CF, stride=12), :] = dw[:, t * LANES : (t + 1) * LANES]
        dw = dot(dy_t[...], right3(gl)).T
        for t in range(3):
            grad[pl.ds(FUS_AT["down"] + 3 * FCH * c + t, FCH, stride=3), :] = dw[:, t * LANES : (t + 1) * LANES]
        return carry

    lax.fori_loop(0, chunks, feed, 0)
    for one in early:
        one.start_core(grad)
    put_vector(grad, FUS_AT["ub"], sums[9:10, :])
    sums[0:8, :] = jnp.zeros((8, MLP_F), F32)

    dv = dhn[...]
    sums[0:1, 0:CF] = column_sum(dy[...])
    sums[1:2, 0:CF] = column_sum(dv * xhat2[...])
    sums[2:3, 0:CF] = column_sum(dv)
    dh = dy[...] + normalize_back(dv, xhat2[...], rstd2[...], vec["g2"])
    sums[3:4, 0:CF] = column_sum(dh)
    dy[...] = dh
    put((dh_h, dh_l), (full, full), dh)
    do_h, do_l = hn_h, hn_l
    put((do_h, do_l), (full, full), deep3((dh_h[...], dh_l[...]), get(wout, (full, full)), 1, 1))

    for one in early:
        one.finish_core(grad)
        one.start(0)

    def backward(i, carry):
        rows = rows_of(i)
        for b in range(3):
            cols = slice(b * LANES, (b + 1) * LANES)
            dom = stacked((do_h[rows, cols], do_l[rows, cols]), masks)
            qm = stacked((q_h[rows, cols], q_l[rows, cols]), masks)
            p = (p_h[i * 3 + b], p_l[i * 3 + b])
            dp = deep3(dom, (v_h[rows, cols], v_l[rows, cols]), 1, 1)
            pf = p[0].astype(F32) + p[1].astype(F32)
            t = pf * dp
            ds = t - pf * jnp.sum(t, 1, keepdims=True)
            some = slice(b * 4 * ROWS_F, (b + 1) * 4 * ROWS_F)
            for c in range(2):
                one = ds[:, c * LANES : (c + 1) * LANES]
                dbias[c, some, 0 : one.shape[1]] = dbias[c, some, 0 : one.shape[1]] + one
            ds = split(ds)
            dq = unstacked(wide_n(ds, (k_h[rows, cols], k_l[rows, cols])), masks) * scale
            dk = dot(left3(qm, 0).T, right3(ds)).T
            dvv = dot(left3(dom, 0).T, right3(p)).T
            for j, one in enumerate((dq, dk, dvv)):
                at = slice(j * CF + b * LANES, j * CF + (b + 1) * LANES)
                put((dqkv_h, dqkv_l), (rows, at), one)
                if j != 1:
                    sums[4 + j // 2 : 5 + j // 2, cols] = sums[4 + j // 2 : 5 + j // 2, cols] + column_sum(one)
        return carry

    lax.fori_loop(0, 4, backward, 0)
    dxn = deep3((dqkv_h[...], dqkv_l[...]), get(win, (full, full)), 1, 1)
    sums[6:7, 0:CF] = column_sum(dxn * xhat1[...])
    sums[7:8, 0:CF] = column_sum(dxn)
    x[...] = dy[...] + normalize_back(dxn, xhat1[...], rstd1[...], vec["g1"])
    dx_ref = fld_ref
    for z, r, at, start in merging_slots():
        dx_ref[z, r, start : start + WIN_LON, :] = x[at : at + WIN_LON, :]
    back = [
        start_copy(dx_ref.at[1 - g, pl.ds(3, 3)], dlat_ref.at[pl.ds(0, 3), half(g)], (send, recv), 3, (1 - g, s)),
        start_copy(dx_ref.at[g, pl.ds(0, 3)], dlat_ref.at[pl.ds(3, 3), half(g)], (send, recv), 4, (g, before)),
        start_copy(dx_ref.at[1 - g, pl.ds(0, 3)], dlat_ref.at[pl.ds(3, 3), half(g)], (send, recv), 5, (1 - g, before)),
    ]
    dlat_ref[0:3, half(g), :] = dx_ref[g, 3:6]
    for j, name in enumerate(("db", "g2", "s2", "ob", "qb", "vb", "g1", "s1")):
        put_vector(grad, FUS_AT[name], sums[j : j + 1, 0:CF])
    for c in range(3):
        cols = slice(c * CF, (c + 1) * CF)
        dw = dot3((xn_h[...], xn_l[...]), (dqkv_h[:, cols], dqkv_l[:, cols]), 0, 0)
        for t in range(3):
            grad[pl.ds(FUS_AT["in"] + 3 * c + t, CF, stride=9), :] = dw[:, t * LANES : (t + 1) * LANES]
    dw = dot3((o_h[...], o_l[...]), (dh_h[...], dh_l[...]), 0, 0)
    for t in range(3):
        grad[pl.ds(FUS_AT["out"] + t, CF, stride=3), :] = dw[:, t * LANES : (t + 1) * LANES]
    rest = [
        pltpu.make_async_copy(grad.at[pl.ds(0, plan.rest_low)], rest_ref.at[pl.ds(0, plan.rest_low)], local_sems.at[6]),
        pltpu.make_async_copy(
            grad.at[pl.ds(plan.rest_from, plan.rest_all - plan.rest_low)],
            rest_ref.at[pl.ds(plan.rest_low, plan.rest_all - plan.rest_low)], local_sems.at[7],
        ),
    ]
    for one in rest:
        one.start()
    for one in early:
        one.finish(0)
    total = jnp.zeros((PAIRS * 16, TAB_PAD), F32)
    blank = jnp.zeros((16 - HEADS_F, 2 * LANES), F32)
    for w in range(WIN_LON):
        rows = []
        for n in range(PAIRS):
            rows.append(jnp.concatenate([dbias[c, pl.ds(n * WIN_LON + w, HEADS_F, stride=ROWS_F), :] for c in range(2)], 1))
            rows.append(blank)
        hi, lo = split(jnp.concatenate(rows, 0))
        one = dot(hi, spots, 1, 1) + dot(lo, spots, 1, 1)
        total = total + (pltpu.roll(one, w, 1) if w else one)
    for z in range(WIN_MOD):
        for r in range(WIN_LAT):
            n = z * WIN_LAT + r
            for y in range(WIN_MOD):
                at = ((z * WIN_MOD + y) * WIN_LAT * WIN_LAT + r * WIN_LAT) * SPAN
                lines[0:HEADS_F, at : at + WIN_LAT * SPAN] = total[n * 16 : n * 16 + HEADS_F, y * WIN_LAT * SPAN : (y + 1) * WIN_LAT * SPAN]
    for j in range(4):
        dtab_ref[j, 0:3, :] = lines[3 * j : 3 * j + 3, :]
    for z, r, at, start in merging_slots():
        out_ref[z, r, start : start + WIN_LON, :] = acc[at : at + WIN_LON, :]
    for one in back + rest:
        one.wait()


def merging_call(plan, latent, cotangent, flat, table):
    n = 4 * ROWS_F
    m = HEADS_F * ROWS_F
    t = np.arange(ROWS_F)
    base = np.full((1, 2 * LANES), -1, np.int32)
    base[0, :ROWS_F] = t // WIN_LON * SPAN + WIN_LON - 1 - t % WIN_LON
    base = jnp.asarray(base)
    scratch = (
        [vmem(plan.fus_all, LANES)]
        + [portion.core_scratch() for portion in plan.fus] + [portion.scratch(0) for portion in plan.fus]
        + [vmem(*cotangent.shape)] + sems(6 + sum(portion.semaphores() for portion in plan.fus)) + [vmem(16, table.shape[2]), vmem(HEADS_F, 8, table.shape[2]), vmem(flat.shape[0] - FUS_AT["g1"] // LANES, LANES), pltpu.SemaphoreType.DMA((8,))] + pair_of(CF, 3 * CF) + pair_of(CF, CF) + pair_of(MLP_F // FCH, CF, FCH) + pair_of(MLP_F // FCH, FCH, CF)
        + [vmem(2, m, LANES), vmem(2, m, LANES), vmem(n, CF), vmem(n, CF), vmem(n, 1)]
        + pair_of(n, CF) + pair_of(n, CF) + pair_of(n, CF) + pair_of(n, CF) + pair_of(12, 4 * ROWS_F, ROWS_F) + pair_of(n, CF)
        + [vmem(n, CF), vmem(n, 1)] + pair_of(n, CF) + [vmem(n, CF), vmem(n, CF), vmem(n, CF)] + pair_of(n, CF)
        + [vmem(CF, 3 * n, dtype=BF16)] * 2 + pair_of(n, CF) + pair_of(n, 3 * CF) + [vmem(16, MLP_F)]
    )
    outs = [shape(*cotangent.shape), shape(*latent.shape), shape(plan.rest_all, LANES), shape(4, 3, table.shape[2])]
    outs += [shape(portion.blocks(0), portion.rows, LANES) for portion in plan.fus]
    return call(partial(merging, plan), "merging", [latent, cotangent, flat, table, base], outs, scratch, 1, 18 * n * 1769472, (2, 3), (2,))


def update(params, grads, momentum, average, rate):
    momentum_new = MOMENTUM_DECAY * momentum + grads
    params_new = params - rate * (grads + MOMENTUM_DECAY * momentum_new)
    average_new = AVERAGE_DECAY * average + (1.0 - AVERAGE_DECAY) * params_new
    return (params_new, momentum_new, average_new)


def shifted_piece(block, rows, at, piece):
    amount = -(-piece // LANES)
    first, lane = at // LANES, lax.rem(at, LANES)
    rows[0 : block.shape[0], :] = pltpu.roll(block[...], LANES - lane, 1)
    low = lax.broadcasted_iota(jnp.int32, (1, LANES), 1) < LANES - lane
    return jnp.where(low, rows[pl.ds(first, amount), :], rows[pl.ds(first + 1, amount), :])


def optimizer(
    rates, fus_start, enc_start,
    merged_in, field_in, fus_block, fus_flat, fus_mom, fus_avg, enc_block, enc_flat, enc_mom, enc_avg, tab_block, table, tab_mom, tab_avg,
    merged, field, enc_grad, enc_new, enc_mom_new, enc_avg_new, fus_grad, fus_new, fus_mom_new, fus_avg_new,
    tab_grad, tab_new, tab_mom_new, tab_avg_new,
    fus_own, enc_own, tab_own, rows, sems,
):
    g, s = lax.axis_index("group"), lax.axis_index("seq")
    slot = g * lax.axis_size("seq") + s
    band, part = slot // 4, lax.rem(slot, 4)
    fus_piece, enc_piece = fus_mom.shape[0], enc_mom.shape[1]
    fus_from = pl.multiple_of(jnp.minimum(fus_start(slot), fus_flat.shape[0] - fus_own.shape[0]), 8)
    enc_from = enc_start(s)
    copies = [
        pltpu.make_async_copy(fus_flat.at[pl.ds(fus_from, fus_own.shape[0])], fus_own, sems.at[0]),
        pltpu.make_async_copy(enc_flat.at[pl.ds(enc_from, enc_own.shape[0])], enc_own, sems.at[1]),
        pltpu.make_async_copy(table.at[pl.ds(3 * part, 3), pl.ds(pl.multiple_of(band // 8 * 8, 8), 8)], tab_own, sems.at[2]),
        pltpu.make_async_copy(merged_in, merged, sems.at[3]),
        pltpu.make_async_copy(field_in, field, sems.at[4]),
    ]
    for one in copies:
        one.start()

    def store(outs, values):
        for ref, value in zip(outs, values):
            ref[...] = value

    def step(own, grads, mom, avg, rate, outs):
        new, mom_new, avg_new = update(own, grads, mom[...], avg[...], rate)
        store(outs, (grads, new, mom_new, avg_new))

    fus_at = fus_piece * slot
    grads = shifted_piece(fus_block, rows, fus_at - fus_start(slot) * LANES, fus_piece).reshape(-1)[:fus_piece]
    copies[0].wait()
    own = shifted_piece(fus_own, rows, fus_at - fus_from * LANES, fus_piece).reshape(-1)[:fus_piece]
    step(own, grads, fus_mom, fus_avg, rates[1], (fus_grad, fus_new, fus_mom_new, fus_avg_new))
    enc_at = enc_piece * s - enc_from * LANES
    grads = shifted_piece(enc_block, rows, enc_at, enc_piece).reshape(1, -1)[:, :enc_piece]
    copies[1].wait()
    own = shifted_piece(enc_own, rows, enc_at, enc_piece).reshape(1, -1)[:, :enc_piece]
    step(own, grads, enc_mom, enc_avg, rates[0], (enc_grad, enc_new, enc_mom_new, enc_avg_new))
    grads = jnp.concatenate([tab_block[j : j + 1, :] for j in range(3)], 1).reshape(-1)
    copies[2].wait()
    own = jnp.concatenate([tab_own[j, pl.ds(lax.rem(band, 8), 1), :] for j in range(3)], 1).reshape(-1)
    step(own, grads, tab_mom, tab_avg, rates[2], (tab_grad, tab_new, tab_mom_new, tab_avg_new))
    for one in copies[3:]:
        one.wait()


def optimizer_call(plan, rates, merged, field, fus_block, fus_flat, fus_mom, fus_avg, enc_block, enc_flat, enc_mom, enc_avg, tab_block, table, tab_mom, tab_avg):
    inputs = [merged, field, fus_block, fus_flat, fus_mom, fus_avg, enc_block, enc_flat, enc_mom, enc_avg, tab_block, table, tab_mom, tab_avg]
    outs = [merged, field] + [enc_mom] * 4 + [fus_mom] * 4 + [tab_mom] * 4
    far, far_outs = (0, 1, 3, 7, 11), ()
    fus_rows = plan.fus_rows + fus_flat.shape[0] % 8
    return pl.pallas_call(
        partial(optimizer, rates, partial(window_start, fus_mom.size), partial(window_start, enc_mom.size)),
        name="optimizer",
        out_shape=[shape(*v.shape) for v in outs],
        in_specs=[pl.BlockSpec(memory_space=pl.ANY if n in far else pltpu.VMEM) for n in range(len(inputs))],
        out_specs=[pl.BlockSpec(memory_space=pl.ANY if n in far_outs else pltpu.VMEM) for n in range(len(outs))],
        scratch_shapes=[
            vmem(fus_rows, LANES), vmem(plan.enc_rows, LANES), vmem(3, 8, table.shape[2]),
            vmem(fus_rows + 16, LANES), pltpu.SemaphoreType.DMA((5,)),
        ],
        compiler_params=pltpu.CompilerParams(vmem_limit_bytes=VMEM_BYTES),
    )(*inputs)


def shards(
    tokens,
    cotangent,
    enc_params,
    enc_momentum,
    enc_average,
    fus_params,
    fus_momentum,
    fus_average,
    earth_bias,
    bias_momentum,
    bias_average,
):
    field = tokens[0, 0]
    row_count, col_count, feat_width = field.shape
    seq_count = lax.axis_size("seq")
    group_count = lax.axis_size("group")
    band_count = seq_count // SAMPLES
    fus_flat = fus_params.reshape(-1, LANES)
    plan = Sums(group_count, seq_count, fus_params.size, enc_params.size)
    enc_flat = rows_of_lanes(enc_params, plan.enc_all)
    latent, *saved = encoder_forward_call(field, enc_flat)
    table = earth_bias.transpose(1, 0, 2)
    merged, latent_grad, rest, table_grad, early_a, early_b = merging_call(plan, latent, cotangent[:, 0, 0], fus_flat, table)
    field_grad, fus_block, enc_block, tab_block = encoder_backward_call(
        plan, latent_grad, enc_flat, rest, table_grad, early_a, early_b, saved
    )
    lat_total = seq_count // SAMPLES * row_count
    rates = (
        1.0 / math.sqrt(CE * SAMPLES * lat_total * col_count),
        1.0 / math.sqrt(CF * group_count * SAMPLES * lat_total * col_count),
        2.0 / math.sqrt(SAMPLES * col_count / WIN_LON),
    )
    merged, field_grad, *others = optimizer_call(
        plan, rates, merged, field_grad, fus_block, fus_flat, fus_momentum, fus_average, enc_block, enc_flat,
        enc_momentum, enc_average, tab_block, table, bias_momentum, bias_average,
    )
    return (merged[:, None, None], field_grad[None, None], *others)


def solution(mesh):
    both = P(("group", "seq"))
    rows = P("group", "seq")
    merged = P(None, "seq", "group", None, None, None)
    tokens = P("group", "seq", None, None, None)
    return jax.shard_map(
        shards,
        mesh=mesh,
        in_specs=(tokens, merged, P("group", None), rows, rows, P(), both, both, P(), both, both),
        out_specs=(merged, tokens, rows, rows, rows, rows) + (both,) * 8,
        check_vma=False,
    )
```

```python
from functools import partial
import math

import jax
import jax.numpy as jnp
import numpy as np
from jax import lax
from jax.experimental import pallas as pl
from jax.experimental.pallas import tpu as pltpu
from jax.sharding import PartitionSpec as P

CE = 192
CF = 384
HEADS_E = 6
HEADS_F = 12
MLP_E = 768
MLP_F = 1536
WIN_LAT = 6
WIN_LON = 12
WIN_MOD = 2
SAMPLES = 2
HEAD = 32
CHUNK = 256
FCH = 384
LANES = 128
ROWS_E = WIN_LAT * WIN_LON
ROWS_F = WIN_MOD * ROWS_E
SPAN = 2 * WIN_LON - 1
PAIRS = WIN_MOD * WIN_LAT
TAB_PAD = 384
EPS = 1e-05
NEG = -1000000000.0
VMEM_BYTES = 61 << 20

MOMENTUM_DECAY = 0.9
AVERAGE_DECAY = 0.99

F32 = jnp.float32
BF16 = jnp.bfloat16

ENC_MATS = {"in": (CE, 3 * CE), "out": (CE, CE), "up": (CE, MLP_E), "down": (MLP_E, CE), "lin": (CE, CF)}
ENC_VECS = {"g1": CE, "s1": CE, "qb": CE, "vb": CE, "ob": CE, "g2": CE, "s2": CE, "ub": MLP_E, "db": CE, "lb": CF}
FUS_MATS = {"in": (CF, 3 * CF), "out": (CF, CF), "up": (CF, MLP_F), "down": (MLP_F, CF)}
FUS_VECS = {"g1": CF, "s1": CF, "qb": CF, "vb": CF, "ob": CF, "g2": CF, "s2": CF, "ub": MLP_F, "db": CF}


def offsets(mats, vecs):
    places, at = {}, 0
    for name, shape in mats.items():
        places[name] = at // LANES
        at += shape[0] * shape[1]
    for name, amount in vecs.items():
        places[name] = at
        at += amount
    return places


ENC_AT = offsets(ENC_MATS, ENC_VECS)
FUS_AT = offsets(FUS_MATS, FUS_VECS)


def split(v):
    hi = v.astype(BF16)
    return hi, (v - hi.astype(F32)).astype(BF16)


def dot(a, b, ca=1, cb=0):
    return lax.dot_general(a, b, (((ca,), (cb,)), ((), ())), preferred_element_type=F32)


def dot3(a, b, ca=1, cb=0):
    return dot(a[0], b[0], ca, cb) + (dot(a[0], b[1], ca, cb) + dot(a[1], b[0], ca, cb))


def left3(a, axis=1):
    return jnp.concatenate([a[0], a[0], a[1]], axis)


def right3(b, axis=0):
    return jnp.concatenate([b[0], b[1], b[0]], axis)


def deep3(a, b, ca=1, cb=0):
    return dot(left3(a, ca), right3(b, cb), ca, cb)


def put(refs, index, v):
    hi, lo = split(v)
    refs[0][index] = hi
    refs[1][index] = lo


def get(refs, index):
    return refs[0][index], refs[1][index]


def half_lanes():
    return lax.broadcasted_iota(jnp.int32, (1, LANES), 1) < LANES // 2


def turn(v):
    return pltpu.roll(v, LANES // 2, 1)


def vector(flat, at, amount):
    tiles = []
    for c in range(-(-amount // LANES)):
        row, lane = divmod(at + c * LANES, LANES)
        one = flat[row : row + 1, :]
        if lane:
            one = turn(one)
            if c * LANES + LANES // 2 < amount:
                one = jnp.where(half_lanes(), one, turn(flat[row + 1 : row + 2, :]))
        tiles.append(one)
    return jnp.concatenate(tiles, 1)[:, :amount] if len(tiles) > 1 else tiles[0][:, :amount]


def put_vector(flat, at, v):
    amount = v.shape[1]
    if at % LANES == 0 and amount % LANES == 0:
        for c in range(amount // LANES):
            flat[at // LANES + c : at // LANES + c + 1, :] = v[:, c * LANES : (c + 1) * LANES]
        return
    half = LANES // 2
    for c in range(amount // half):
        row, lane = divmod(at + c * half, LANES)
        flat[row : row + 1, lane : lane + half] = v[:, c * half : (c + 1) * half]


def unpack_matrix(flat, at, shape, store, scratch):
    rows, width = shape
    if width % LANES == 0:
        n = width // LANES
        for c in range(n):
            store(slice(0, rows), c, flat[pl.ds(at + c, rows, stride=n), :])
        return
    pairs, n, full = rows // 2, 2 * width // LANES, width // LANES
    low = half_lanes()
    for c in range(full + 1):
        scratch[c, pl.ds(0, pairs, stride=2), :] = flat[pl.ds(at + c, pairs, stride=n), :]
        odd = turn(flat[pl.ds(at + full + c, pairs, stride=n), :])
        if c < full:
            odd = jnp.where(low, odd, turn(flat[pl.ds(at + full + c + 1, pairs, stride=n), :]))
        scratch[c, pl.ds(1, pairs, stride=2), :] = odd
    for c in range(full + 1):
        store(slice(0, rows), c, scratch[c, 0:rows, :])


def pack_matrix(flat, at, shape, source):
    rows, width = shape
    pairs, n, full = rows // 2, 2 * width // LANES, width // LANES
    low = half_lanes()

    def tile(odd, c):
        return source[c, pl.ds(odd, pairs, stride=2), :]

    for c in range(full):
        flat[pl.ds(at + c, pairs, stride=n), :] = tile(0, c)
        flat[pl.ds(at + full + 1 + c, pairs, stride=n), :] = jnp.where(low, turn(tile(1, c)), turn(tile(1, c + 1)))
    flat[pl.ds(at + full, pairs, stride=n), :] = jnp.where(low, tile(0, full), turn(tile(1, 0)))


def put_tiles(ref, rows, v):
    for c in range(-(-v.shape[1] // LANES)):
        one = v[:, c * LANES : (c + 1) * LANES]
        ref[c, rows, 0 : one.shape[1]] = one


def get_tiles(ref, rows, width):
    tiles = [ref[c, rows, 0 : min(width - c * LANES, LANES)] for c in range(-(-width // LANES))]
    return jnp.concatenate(tiles, 1)


def normalize(x):
    center = x - jnp.mean(x, 1, keepdims=True)
    scale = lax.rsqrt(jnp.mean(center * center, 1, keepdims=True) + EPS)
    return center * scale, scale


def normalize_back(dv, xhat, scale, gain):
    dxhat = dv * gain
    return scale * (dxhat - jnp.mean(dxhat, 1, keepdims=True) - xhat * jnp.mean(dxhat * xhat, 1, keepdims=True))


def gelu_parts(u):
    phi = 0.5 * (1.0 + lax.erf(u * (1.0 / math.sqrt(2.0))))
    return u * phi, phi + u * jnp.exp(-0.5 * u * u) * (1.0 / math.sqrt(2.0 * math.pi))


def head_masks(width):
    lane = lax.broadcasted_iota(jnp.int32, (1, width), 1)
    return [jnp.where((lane >= h * HEAD) & (lane < (h + 1) * HEAD), 1.0, 0.0) for h in range(width // HEAD)]


def stacked(pair, masks):
    return tuple(jnp.concatenate([part * m.astype(BF16) for m in masks], 0) for part in pair)


def unstacked(v, masks):
    rows = v.shape[0] // len(masks)
    total = v[:rows] * masks[0]
    for h in range(1, len(masks)):
        total = total + v[h * rows : (h + 1) * rows] * masks[h]
    return total


def softmax(s):
    e = jnp.exp(s - jnp.max(s, 1, keepdims=True))
    return e / jnp.sum(e, 1, keepdims=True)


def wide_nt(a, b):
    return dot(jnp.concatenate(a, 1), jnp.concatenate([b[0], b[0]], 1), 1, 1) + dot(a[0], b[1], 1, 1)


def wide_n(a, b, ca=1):
    n = b[0].shape[1]
    both = dot(a[0], jnp.concatenate(b, 1), ca, 0)
    return both[:, :n] + (both[:, n:] + dot(a[1], b[0], ca, 0))


def column_sum(v):
    return jnp.sum(v, 0, keepdims=True)


def encoder_slots():
    for r in range(WIN_LAT):
        for n in range(8):
            start = n * WIN_LON + WIN_LON // 2
            at = n * ROWS_E + r * WIN_LON
            if n < 7:
                yield r, at, start, WIN_LON
            else:
                yield r, at, start, WIN_LON // 2
                yield r, at + WIN_LON // 2, 0, WIN_LON // 2


def merging_slots():
    for z in range(WIN_MOD):
        for r in range(WIN_LAT):
            for n in range(4):
                yield z, r, n * ROWS_F + (z * WIN_LAT + r) * WIN_LON, n * WIN_LON


MESH = pl.DeviceIdType.MESH


def seq_digits(count):
    rest, digits = count // 2, []
    while rest > 1:
        digits.insert(0, 4 if rest % 4 == 0 else 2)
        rest //= digits[0]
    digits.sort()
    if count == 16:
        digits = [4, 2]
    return digits + [2]


class Places:
    def __init__(self, groups, seqs):
        self.sizes = [groups] + seq_digits(seqs)
        self.groups = groups
        self.strides = [1] * len(self.sizes)
        for i in range(len(self.sizes) - 2, 0, -1):
            self.strides[i] = self.strides[i + 1] * self.sizes[i + 1]

    def here(self):
        self.g, self.s = lax.axis_index("group"), lax.axis_index("seq")
        self.mine = [self.g] + [self.s // self.strides[i] % self.sizes[i] for i in range(1, len(self.sizes))]

    def peer(self, digit, value):
        if digit == 0:
            return (value, self.s)
        return (self.g, self.s + (value - self.mine[digit]) * self.strides[digit])

    def place(self, values):
        return sum(v * self.strides[i] for i, v in values.items() if i)


def windows(total, count):
    piece = total // count
    tiles = max(-(-(piece * (d + 1)) // 1024) - piece * d // 1024 for d in range(count))
    last = piece * (count - 1) // 1024
    return piece, tiles * 8, (last + tiles) * 8


def window_start(piece, d):
    return pl.multiple_of(piece * d // 1024 * 8, 8)


def start_copy(src, dst, sems, at, peer):
    one = pltpu.make_async_remote_copy(
        src_ref=src, dst_ref=dst, send_sem=sems[0].at[at], recv_sem=sems[1].at[at], device_id=peer, device_id_type=MESH
    )
    one.start()
    return one


class Stream:
    def __init__(self, places, plan, chosen, shift, sems, base):
        self.places, self.order, self.piece, self.first, self.rows = places, plan.order, plan.piece, plan.first, plan.rows
        self.chosen, self.shift, self.sems, self.base = chosen, shift, sems, base
        self.sizes = plan.sizes
        self.held, self.arrived = {}, {}
        self.last = len(places.sizes) - 1

    def buffers(self, held, arrived):
        self.held.update(held)
        self.arrived.update(arrived)
        return self

    def combos(self, i=0):
        out = [()]
        for n in self.sizes[i:]:
            out = [c + (v,) for c in out for v in range(n)]
        return out

    def number(self, values):
        where = self.places.place(values)
        if 0 in values:
            where = where + values[0] * (self.places.sizes[1] * self.places.strides[1])
        return where

    def target(self, i, combo, core):
        values = {d: self.places.mine[d] for d in self.order[:i]}
        values.update(zip(self.order[i:], combo))
        values[self.last] = core
        return self.number(values)

    def when(self, number, action):
        if self.chosen is None:
            action()
        else:
            pl.when(self.chosen(number))(action)

    def window(self, number):
        return pl.ds(pl.multiple_of(self.shift(window_start(self.piece, number)) + self.first, 8), self.rows)

    def core_copy(self, n, number, source):
        p = self.places
        core = p.mine[self.last]
        return pltpu.make_async_remote_copy(
            src_ref=source.at[self.window(number)], dst_ref=self.held[0].at[n], send_sem=self.sems[0].at[self.base + n],
            recv_sem=self.sems[1].at[self.base + n], device_id=p.peer(self.last, 1 - core), device_id_type=MESH,
        )

    def start_core(self, source):
        core = self.places.mine[self.last]
        for n, combo in enumerate(self.combos()):
            number = self.target(0, combo, 1 - core)
            self.when(number, lambda n=n, number=number: self.core_copy(n, number, source).start())

    def finish_core(self, source):
        core = self.places.mine[self.last]
        for n, combo in enumerate(self.combos()):
            number = self.target(0, combo, core)

            def add(n=n, number=number):
                self.core_copy(n, number, source).wait_recv()
                self.held[0][n] = self.held[0][n] + source[self.window(number), :]

            self.when(number, add)
        for n, combo in enumerate(self.combos()):
            number = self.target(0, combo, 1 - core)
            self.when(number, lambda n=n, number=number: self.core_copy(n, number, source).wait_send())

    def blocks(self, i):
        return math.prod(self.sizes[i + 1 :])

    def copy(self, i, k, n):
        p, digit, size = self.places, self.order[i], self.sizes[i]
        value = lax.rem(p.mine[digit] + k, size)
        at = self.base + len(self.combos()) + sum((self.sizes[j] - 1) * self.blocks(j) for j in range(i)) + (k - 1) * self.blocks(i) + n
        return pltpu.make_async_remote_copy(
            src_ref=self.held[i].at[value * self.blocks(i) + n], dst_ref=self.arrived[i].at[k - 1, n], send_sem=self.sems[0].at[at],
            recv_sem=self.sems[1].at[at], device_id=p.peer(digit, value), device_id_type=MESH,
        )

    def sent(self, i):
        core = self.places.mine[self.last]
        for k in range(1, self.sizes[i]):
            value = lax.rem(self.places.mine[self.order[i]] + k, self.sizes[i])
            for n, combo in enumerate(self.combos(i + 1)):
                yield k, n, self.target(i, (value,) + combo, core)

    def start(self, i):
        for k, n, number in self.sent(i):
            self.when(number, lambda k=k, n=n: self.copy(i, k, n).start())

    def finish(self, i, out=None):
        core = self.places.mine[self.last]
        mine = self.places.mine[self.order[i]]
        for n, combo in enumerate(self.combos(i + 1)):
            def add(n=n):
                total = self.held[i][mine * self.blocks(i) + n]
                for k in range(1, self.sizes[i]):
                    self.copy(i, k, n).wait_recv()
                    total = total + self.arrived[i][k - 1, n]
                if out is None:
                    self.held[i + 1][n] = total
                else:
                    out(total)

            self.when(self.target(i, (mine,) + combo, core), add)
        for k, n, number in self.sent(i):
            self.when(number, lambda k=k, n=n: self.copy(i, k, n).wait_send())

    def semaphores(self):
        return len(self.combos()) + sum((self.sizes[j] - 1) * self.blocks(j) for j in range(len(self.sizes)))


class Portion:
    def __init__(self, places, order, piece, first, rows):
        self.order, self.piece, self.first, self.rows = order, piece, first, rows
        self.sizes = [places.sizes[d] for d in order]

    def blocks(self, i):
        return math.prod(self.sizes[i + 1 :])

    def core_scratch(self):
        return vmem(math.prod(self.sizes), self.rows, LANES)

    def scratch(self, i):
        return vmem(self.sizes[i] - 1, self.blocks(i), self.rows, LANES)

    def semaphores(self):
        return math.prod(self.sizes) + sum((self.sizes[j] - 1) * self.blocks(j) for j in range(len(self.sizes)))


class Sums:
    def __init__(self, groups, seqs, fus_total, enc_total):
        self.places = places = Places(groups, seqs)
        last = len(places.sizes) - 1
        order = sorted(range(1, last), key=lambda d: places.sizes[d])
        piece, rows, self.fus_all = windows(fus_total, groups * seqs)
        enc_piece, enc_rows, self.enc_all = windows(enc_total, seqs)
        first = rows * 4 // 64 * 8
        self.fus = [
            Portion(places, [0] + order, piece, 0, first),
            Portion(places, order[:1] + [0] + order[1:], piece, first, rows - first),
        ]
        cut_a, cut_b = rows * 5 // 96 * 8 // 1, rows * 9 // 96 * 8 // 1
        cut_a, cut_b = cut_a // 8 * 8, cut_b // 8 * 8
        self.late = [
            Portion(places, [0] + order, piece, 0, cut_a),
            Portion(places, order[:1] + [0] + order[1:], piece, cut_a, cut_b - cut_a),
            Portion(places, order[-1:] + [0] + order[:-1], piece, cut_b, rows - cut_b),
        ]
        self.enc = [Portion(places, order, enc_piece, 0, enc_rows)] * 2
        self.fus_rows, self.enc_rows = rows, enc_rows
        self.low, self.high = FUS_AT["up"], FUS_AT["g1"] // LANES
        starts = [piece * d // 1024 * 8 for d in range(groups * seqs)]
        self.early = [d for d, at in enumerate(starts) if at >= self.low and at + rows <= self.high]
        others = [at for d, at in enumerate(starts) if d not in self.early]
        self.rest_low = max(at for at in others if at < self.low) + rows
        self.rest_from = min(at for at in others if at >= self.low)
        self.rest_all = self.rest_low + self.fus_all - self.rest_from
        enc_starts = [enc_piece * d // 1024 * 8 for d in range(seqs)]
        low, high = ENC_AT["up"], ENC_AT["g1"] // LANES
        self.enc_early = [d for d, at in enumerate(enc_starts) if at >= low and at + enc_rows <= high]

    def is_early(self, d):
        return jnp.logical_and(d >= self.early[0], d <= self.early[-1])

    def is_late(self, d):
        return jnp.logical_not(self.is_early(d))

    def is_enc_early(self, d):
        return jnp.logical_and(d >= self.enc_early[0], d <= self.enc_early[-1])

    def is_enc_late(self, d):
        return jnp.logical_not(self.is_enc_early(d))

    def rest_shift(self, at):
        return jnp.where(at < self.low, at, at - self.rest_from + self.rest_low)


def encoder_forward(
    field_ref, line_ref,
    lat_ref, *outs_and_scratch,
):
    saved, scratch = outs_and_scratch[:13], outs_and_scratch[13:]
    kept, local_sems, others = scratch[:13], scratch[13], scratch[14:]
    encoder_forward_body(field_ref, line_ref, lat_ref, saved, local_sems, *kept, *others)


def encoder_forward_body(
    field_ref, line_ref, lat_ref, saved, local_sems, flat, xhat_ref, rstd_ref, qkv_ref, p_h, p_l, o_ref, xhat2_ref, rstd2_ref, g_h, g_l, dg_ref, out_ref,
    win_h, win_l, wout_h, wout_l, wup_h, wup_l, wdn_h, wdn_l, wlin_h, wlin_l,
    x, wide, lat, head_ref, send, recv,
):
    here = (flat, xhat_ref, rstd_ref, qkv_ref, p_h, p_l, o_ref, xhat2_ref, rstd2_ref, g_h, g_l, dg_ref, out_ref)
    leaving = []

    def leave(*numbers):
        for n in numbers:
            one = pltpu.make_async_copy(here[n], saved[n], local_sems.at[n])
            one.start()
            leaving.append(one)

    g, s = lax.axis_index("group"), lax.axis_index("seq")
    seqs = lax.axis_size("seq")
    before, after = lax.rem(s + seqs - SAMPLES, seqs), lax.rem(s + SAMPLES, seqs)
    barrier = pltpu.get_barrier_semaphore()
    for other in (before, after):
        pl.semaphore_signal(barrier, inc=1, device_id=(g, other), device_id_type=MESH)
    pl.semaphore_wait(barrier, 2)
    halo = start_copy(field_ref.at[pl.ds(0, 3)], head_ref, (send, recv), 0, (g, before))
    amount = line_ref.shape[1] // LANES
    flat[0:amount, :] = line_ref[...].reshape(amount, LANES)
    leave(0)
    for pair, name in (((win_h, win_l), "in"), ((wout_h, wout_l), "out"), ((wup_h, wup_l), "up"), ((wdn_h, wdn_l), "down"), ((wlin_h, wlin_l), "lin")):
        width = ENC_MATS[name][1]

        def store(rows, c, v, pair=pair, width=width):
            last = min(width - c * LANES, LANES)
            put(pair, (rows, slice(c * LANES, c * LANES + last)), v[:, :last])

        unpack_matrix(flat, ENC_AT[name], ENC_MATS[name], store, wide)
    vec = {name: vector(flat, ENC_AT[name], amount) for name, amount in ENC_VECS.items()}
    masks = head_masks(CE)
    halo.wait()
    for r, at, start, amount in encoder_slots():
        x[at : at + amount, :] = (field_ref[r + 3, start : start + amount, :] if r < 3 else head_ref[r - 3, start : start + amount, :])
    wrapped = s // SAMPLES == seqs // SAMPLES - 1
    half = ROWS_E // 2
    upper = lax.broadcasted_iota(jnp.int32, (ROWS_E, ROWS_E), 0) >= half
    right = lax.broadcasted_iota(jnp.int32, (ROWS_E, ROWS_E), 1) >= half
    apart = jnp.where(jnp.logical_and(upper != right, wrapped), 1.0, 0.0)
    apart = jnp.concatenate([apart] * HEADS_E, 0)
    win, wout, wup, wdn, wlin = (win_h, win_l), (wout_h, wout_l), (wup_h, wup_l), (wdn_h, wdn_l), (wlin_h, wlin_l)
    scale = 1.0 / math.sqrt(HEAD)

    full = slice(None)
    xhat, rstd = normalize(x[...])
    xhat_ref[...] = xhat
    rstd_ref[...] = rstd
    xn = split(xhat * vec["g1"] + vec["s1"])
    for j, name in enumerate(("qb", None, "vb")):
        cols = slice(j * CE, (j + 1) * CE)
        one = dot3(xn, get(win, (full, cols)))
        if name is not None:
            one = one + vec[name]
        qkv_ref[:, cols] = one * scale if j == 0 else one
    leave(1, 2, 3)

    def step(i, carry):
        rows = pl.ds(pl.multiple_of(i * 2 * ROWS_E, 2 * ROWS_E), 2 * ROWS_E)
        qkv = qkv_ref[rows, :]
        parts = []
        for w in range(2):
            one = qkv[w * ROWS_E : (w + 1) * ROWS_E]
            q, k, v = (one[:, j * CE : (j + 1) * CE] for j in range(3))
            qm = split(jnp.concatenate([q * m for m in masks], 0))
            s = dot3(qm, split(k), 1, 1)
            s = jnp.where(apart > 0.5, NEG, s)
            p = split(softmax(s))
            p_h[i * 2 + w] = p[0]
            p_l[i * 2 + w] = p[1]
            parts.append(unstacked(dot3(p, split(v)), masks))
        o_ref[rows, :] = jnp.concatenate(parts, 0)
        return carry

    lax.fori_loop(0, 4, step, 0)
    leave(4, 5, 6)
    hidden = x[...] + dot3(split(o_ref[...]), get(wout, (full, full))) + vec["ob"]
    xhat2, rstd2 = normalize(hidden)
    xhat2_ref[...] = xhat2
    rstd2_ref[...] = rstd2
    leave(7, 8)
    hn = split(xhat2 * vec["g2"] + vec["s2"])
    out_ref[...] = hidden + vec["db"]
    for c in range(MLP_E // CHUNK):
        cols = slice(c * CHUNK, (c + 1) * CHUNK)
        u = dot3(hn, get(wup, (full, cols))) + vec["ub"][:, cols]
        one, slope = gelu_parts(u)
        dg_ref[:, cols] = slope
        one = split(one)
        g_h[:, cols] = one[0]
        g_l[:, cols] = one[1]
        out_ref[...] = out_ref[...] + deep3(one, get(wdn, (cols, full)))
    leave(9, 10, 11, 12)
    lat[...] = dot3(split(out_ref[...]), get(wlin, (full, full))) + vec["lb"]
    for r, at, start, amount in encoder_slots():
        lat_ref[r, start : start + amount, :] = lat[at : at + amount, :]
    for one in leaving:
        one.wait()


def vmem(*shape, dtype=F32):
    return pltpu.VMEM(shape, dtype)


def pair_of(*shape):
    return [vmem(*shape, dtype=BF16)] * 2


def call(kernel, name, inputs, outs, scratch, number, flops=0, far=(), far_outs=()):
    specs = [pl.BlockSpec(memory_space=pl.ANY if n in far else pltpu.VMEM) for n in range(len(inputs))]
    moved = sum(v.size * v.dtype.itemsize for v in list(inputs) + list(outs))
    return pl.pallas_call(
        kernel,
        name=name,
        out_shape=outs,
        in_specs=specs,
        out_specs=[pl.BlockSpec(memory_space=pl.ANY if n in far_outs else pltpu.VMEM) for n in range(len(outs))],
        scratch_shapes=scratch,
        cost_estimate=pl.CostEstimate(flops=flops, bytes_accessed=moved, transcendentals=0),
        compiler_params=pltpu.CompilerParams(collective_id=number, has_side_effects=True, vmem_limit_bytes=VMEM_BYTES),
    )(*inputs)


def sems(count):
    return [pltpu.SemaphoreType.DMA((count,)), pltpu.SemaphoreType.DMA((count,))]


def shape(*dims, dtype=F32):
    return jax.ShapeDtypeStruct(dims, dtype)


def encoder_forward_call(field, line, amount):
    n = 8 * ROWS_E
    outs = [
        shape(WIN_LAT, 96, CF), shape(amount, LANES), shape(n, CE), shape(n, 1), shape(n, 3 * CE),
        shape(8, HEADS_E * ROWS_E, ROWS_E, dtype=BF16), shape(8, HEADS_E * ROWS_E, ROWS_E, dtype=BF16),
        shape(n, CE), shape(n, CE), shape(n, 1), shape(n, MLP_E, dtype=BF16), shape(n, MLP_E, dtype=BF16),
        shape(n, MLP_E), shape(n, CE),
    ]
    scratch = (
        pair_of(CE, 3 * CE) + pair_of(CE, CE) + pair_of(CE, MLP_E) + pair_of(MLP_E, CE) + pair_of(CE, CF)
        + [vmem(n, CE), vmem(5, MLP_E, LANES), vmem(n, CF), vmem(3, 96, CE)] + sems(1)
    )
    scratch = [pltpu.VMEM(v.shape, v.dtype) for v in outs[1:]] + [pltpu.SemaphoreType.DMA((13,))] + scratch
    return call(
        encoder_forward, "encoder_forward", [field, line], outs, scratch, 0, 6 * n * 516096, (), tuple(range(1, 14))
    )


def encoder_backward(
    plan,
    dlat_ref, flat, rest, tab, early_a, early_b,
    xhat_ref, rstd_ref, qkv_far, ph_far, pl_far, o_ref, xhat2_ref, rstd2_ref, gh_far, gl_far, dg_far, out_ref,
    field_grad, fus_out, enc_out, tab_out,
    qkv_ref, p_h, p_l, g_h, g_l, dg_ref,
    grad, tabs, send, recv, local_sems, win_h, win_l, wout_h, wout_l, wup_h, wup_l, wdn_h, wdn_l, wlin_h, wlin_l,
    dlat, wide, dout, dout_h, dout_l, dhn, du_h, du_l, hn_h, hn_l, dh_h, dh_l, dqkv_h, dqkv_l, xn_h, xn_l, sums, dx, dback,
    *refs,
):
    loads = [
        pltpu.make_async_copy(src, dst, local_sems.at[n])
        for n, (src, dst) in enumerate(
            ((gh_far, g_h), (gl_far, g_l), (dg_far, dg_ref), (qkv_far, qkv_ref), (ph_far, p_h), (pl_far, p_l))
        )
    ]
    for one in loads:
        one.start()
    places = plan.places
    places.here()
    g, s = places.g, places.s
    seqs = places.sizes[1] * places.strides[1]
    before, after = lax.rem(s + seqs - SAMPLES, seqs), lax.rem(s + SAMPLES, seqs)
    slot, band = g * seqs + s, s // SAMPLES
    mine = g * SAMPLES + lax.rem(s, SAMPLES)
    owners = [((4 * band + j) // seqs, lax.rem(4 * band + j, seqs)) for j in range(4)]
    givers = [(k // 2, slot // 4 * SAMPLES + k % 2) for k in range(4)]

    def other(pg, ps):
        return jnp.logical_or(pg != g, ps != s)

    barrier = pltpu.get_barrier_semaphore()
    peers = [(g, before), (g, after)]
    for digit, size in enumerate(places.sizes):
        peers += [places.peer(digit, lax.rem(places.mine[digit] + k, size)) for k in range(1, size)]
    for peer in peers:
        pl.semaphore_signal(barrier, inc=1, device_id=peer, device_id_type=MESH)
    for pg, ps in owners + givers:
        @pl.when(other(pg, ps))
        def _(pg=pg, ps=ps):
            pl.semaphore_signal(barrier, inc=1, device_id=(pg, ps), device_id_type=MESH)
    pl.semaphore_wait(barrier, len(peers) + jnp.where(slot // 4 == band, 6, 8))

    refs = list(refs)
    base = 8
    early, late, encs = [], [], []
    for portion, held in zip(plan.fus, (early_a, early_b)):
        one = Stream(places, portion, plan.is_early, lambda at: at, (send, recv), base)
        arrived = {i: refs.pop(0) for i in range(1, len(portion.order))}
        early.append(one.buffers({1: held}, arrived).buffers({i + 1: arrived[i].at[0] for i in arrived}, {}))
        base += portion.semaphores()
    for group, portions, choices, shift in (
        (late, plan.late, [plan.is_late] * 3, plan.rest_shift),
        (encs, plan.enc, [plan.is_enc_early, plan.is_enc_late], lambda at: at),
    ):
        for portion, chosen in zip(portions, choices):
            one = Stream(places, portion, chosen, shift, (send, recv), base)
            held = {0: refs.pop(0)}
            arrived = {i: refs.pop(0) for i in range(len(portion.order))}
            group.append(one.buffers(held, arrived).buffers({i + 1: arrived[i].at[0] for i in arrived}, {}))
            base += portion.semaphores()

    def keep(one, split_at):
        def store(total):
            fus_out[split_at : split_at + one.rows, :] = total
        return store

    stages = len(plan.fus[0].order)

    def keep_enc(total):
        enc_out[...] = total

    def go(streams, i):
        for one in streams:
            if i == 0:
                one.finish_core(grad if one in encs else rest)
            else:
                last = keep_enc if one in encs else keep(one, one.first)
                one.finish(i - 1, last if i == len(one.order) else None)
            if i < len(one.order):
                one.start(i)

    for one in late:
        one.start_core(rest)
    for one in early:
        one.start(1)

    def give(j, pg, ps):
        return pltpu.make_async_remote_copy(
            src_ref=tab.at[j], dst_ref=tabs.at[mine], send_sem=send.at[4 + j], recv_sem=recv.at[4 + mine],
            device_id=(pg, ps), device_id_type=MESH,
        )

    for j, (pg, ps) in enumerate(owners):
        @pl.when(other(pg, ps))
        def _(j=j, pg=pg, ps=ps):
            give(j, pg, ps).start()

        @pl.when(jnp.logical_not(other(pg, ps)))
        def _(j=j):
            tabs[mine] = tab[j]

    win, wout, wup, wdn, wlin = (win_h, win_l), (wout_h, wout_l), (wup_h, wup_l), (wdn_h, wdn_l), (wlin_h, wlin_l)
    for pair, name in ((win, "in"), (wout, "out"), (wup, "up"), (wdn, "down"), (wlin, "lin")):
        width = ENC_MATS[name][1]

        def store(rows, c, v, pair=pair, width=width):
            last = min(width - c * LANES, LANES)
            put(pair, (rows, slice(c * LANES, c * LANES + last)), v[:, :last])

        unpack_matrix(flat, ENC_AT[name], ENC_MATS[name], store, wide)
    vec = {name: vector(flat, ENC_AT[name], ENC_VECS[name]) for name in ("g1", "s1", "g2", "s2")}
    masks = head_masks(CE)
    full = slice(None)
    scale = 1.0 / math.sqrt(HEAD)
    go(late, 0)
    for r, at, start, amount in encoder_slots():
        dlat[at : at + amount, :] = dlat_ref[r, start : start + amount, :]
    for one in loads[:3]:
        one.wait()
    dl = split(dlat[...])
    put_vector(grad, ENC_AT["lb"], column_sum(dlat[...]))
    d = dot3(dl, get(wlin, (full, full)), 1, 1)
    dout[...] = d
    put((dout_h, dout_l), (full, full), d)
    put_vector(grad, ENC_AT["db"], column_sum(d))
    dw = deep3(split(out_ref[...]), dl, 0, 0)
    for c in range(3):
        grad[pl.ds(ENC_AT["lin"] + c, CE, stride=3), :] = dw[:, c * LANES : (c + 1) * LANES]
    xhat2 = xhat2_ref[...]
    put((hn_h, hn_l), (full, full), xhat2 * vec["g2"] + vec["s2"])
    hn_t = left3((hn_h[...], hn_l[...]), 0).T
    do_t = left3((dout_h[...], dout_l[...]), 0).T
    for c in range(MLP_E // CHUNK):
        cols = slice(c * CHUNK, (c + 1) * CHUNK)
        do = (dout_h[...], dout_l[...])
        du = dot3(do, get(wdn, (cols, full)), 1, 1) * dg_ref[:, cols]
        put_vector(grad, ENC_AT["ub"] + c * CHUNK, column_sum(du))
        du = split(du)
        if c == 2:
            go(early, 2)
        part = deep3(du, get(wup, (full, cols)), 1, 1)
        dhn[...] = part if c == 0 else dhn[...] + part
        dw = dot(hn_t, right3(du))
        for t in range(2):
            grad[pl.ds(ENC_AT["up"] + 2 * c + t, CE, stride=6), :] = dw[:, t * LANES : (t + 1) * LANES]
        dw = dot(do_t, right3((g_h[:, cols], g_l[:, cols]))).T
        put_tiles(wide, slice(c * CHUNK, (c + 1) * CHUNK), dw)
    pack_matrix(grad, ENC_AT["down"], ENC_MATS["down"], wide)
    dv = dhn[...]
    put_vector(grad, ENC_AT["g2"], column_sum(dv * xhat2))
    put_vector(grad, ENC_AT["s2"], column_sum(dv))
    d = dout[...] + normalize_back(dv, xhat2, rstd2_ref[...], vec["g2"])
    dout[...] = d
    put((dh_h, dh_l), (full, full), d)
    put_vector(grad, ENC_AT["ob"], column_sum(d))
    dw = deep3(split(o_ref[...]), (dh_h[...], dh_l[...]), 0, 0)
    put_tiles(wide, slice(0, CE), dw)
    pack_matrix(grad, ENC_AT["out"], ENC_MATS["out"], wide)
    sums[...] = jnp.zeros_like(sums)
    encs[0].start_core(grad)
    for one in loads[3:]:
        one.wait()

    def step(i, carry):
        rows = pl.ds(pl.multiple_of(i * 2 * ROWS_E, 2 * ROWS_E), 2 * ROWS_E)
        do = dhn[rows, :]
        parts = []
        for w in range(2):
            one = qkv_ref[pl.ds(pl.multiple_of(i * 2 * ROWS_E, 2 * ROWS_E) + w * ROWS_E, ROWS_E), :]
            q, k, v = (one[:, j * CE : (j + 1) * CE] for j in range(3))
            dow = do[w * ROWS_E : (w + 1) * ROWS_E]
            dom = split(jnp.concatenate([dow * m for m in masks], 0))
            qm = split(jnp.concatenate([q * m for m in masks], 0))
            p = (p_h[i * 2 + w], p_l[i * 2 + w])
            dp = dot3(dom, split(v), 1, 1)
            pf = p[0].astype(F32) + p[1].astype(F32)
            t = pf * dp
            ds = split(t - pf * jnp.sum(t, 1, keepdims=True))
            dq = unstacked(dot3(ds, split(k)), masks) * scale
            dk = dot(left3(qm, 0).T, right3(ds)).T
            dvv = dot(left3(dom, 0).T, right3(p)).T
            parts.append(jnp.concatenate([dq, dk, dvv], 1))
        dqkv = jnp.concatenate(parts, 0)
        sums[0:1, :] = sums[0:1, :] + column_sum(dqkv)
        put((dqkv_h, dqkv_l), (rows, full), dqkv)
        return carry

    dhn[...] = dot3((dh_h[...], dh_l[...]), get(wout, (full, full)), 1, 1)
    lax.fori_loop(0, 2, step, 0)
    go(late, 1)
    go(encs[:1], 0)
    lax.fori_loop(2, 4, step, 0)
    go(late, 2)
    go(encs[:1], 1)
    xhat = xhat_ref[...]
    put((xn_h, xn_l), (full, full), xhat * vec["g1"] + vec["s1"])
    dxn = dot3((dqkv_h[...], dqkv_l[...]), get(win, (full, full)), 1, 1)
    sums[1:2, 0:CE] = column_sum(dxn * xhat)
    sums[2:3, 0:CE] = column_sum(dxn)
    put_vector(grad, ENC_AT["qb"], sums[0:1, 0:CE])
    put_vector(grad, ENC_AT["vb"], sums[0:1, 2 * CE : 3 * CE])
    put_vector(grad, ENC_AT["g1"], sums[1:2, 0:CE])
    put_vector(grad, ENC_AT["s1"], sums[2:3, 0:CE])
    dw = deep3((xn_h[...], xn_l[...]), (dqkv_h[...], dqkv_l[...]), 0, 0)
    put_tiles(wide, slice(0, CE), dw)
    pack_matrix(grad, ENC_AT["in"], ENC_MATS["in"], wide)
    encs[1].start_core(grad)
    dx[...] = dout[...] + normalize_back(dxn, xhat, rstd_ref[...], vec["g1"])
    for r, at, start, amount in encoder_slots():
        if r < 3:
            field_grad[r + 3, start : start + amount, :] = dx[at : at + amount, :]
        else:
            dback[r - 3, start : start + amount, :] = dx[at : at + amount, :]
    back = start_copy(dback, field_grad.at[pl.ds(0, 3)], (send, recv), 3, (g, after))
    go(encs[1:], 0)
    back.wait()
    for j, (pg, ps) in enumerate(owners):
        @pl.when(other(pg, ps))
        def _(j=j, pg=pg, ps=ps):
            give(j, pg, ps).wait_send()
    for k, (pg, ps) in enumerate(givers):
        @pl.when(other(pg, ps))
        def _(k=k, pg=pg, ps=ps):
            pltpu.make_async_remote_copy(
                src_ref=tab.at[0], dst_ref=tabs.at[k], send_sem=send.at[4], recv_sem=recv.at[4 + k],
                device_id=(pg, ps), device_id_type=MESH,
            ).wait_recv()
    tab_out[...] = (tabs[0] + tabs[1]) + (tabs[2] + tabs[3])
    for i in range(3, stages + 1):
        go(early, i)
    go(encs[1:], 1)
    for i in range(3, stages + 1):
        go(late, i)
    for i in range(2, len(encs[0].order) + 1):
        go(encs, i)


def encoder_backward_call(plan, dlat, flat, rest, tab, early_a, early_b, saved):
    n = 8 * ROWS_E
    refs, count = [], 8
    for portion in plan.fus:
        refs += [portion.scratch(i) for i in range(1, len(portion.order))]
        count += portion.semaphores()
    for portion in plan.late + plan.enc:
        refs += [portion.core_scratch()] + [portion.scratch(i) for i in range(len(portion.order))]
        count += portion.semaphores()
    xhat, rstd, qkv, p_h, p_l, o, xhat2, rstd2, g_h, g_l, dg, out = saved
    scratch = (
        [pltpu.VMEM(v.shape, v.dtype) for v in (qkv, p_h, p_l, g_h, g_l, dg)]
        + [vmem(plan.enc_all, LANES), vmem(*tab.shape)] + sems(count) + [pltpu.SemaphoreType.DMA((6,))]
        + pair_of(CE, 3 * CE) + pair_of(CE, CE) + pair_of(CE, MLP_E) + pair_of(MLP_E, CE) + pair_of(CE, CF)
        + [vmem(n, CF), vmem(5, MLP_E, LANES), vmem(n, CE)] + pair_of(n, CE) + [vmem(n, CE)] + pair_of(n, CHUNK)
        + pair_of(n, CE) + pair_of(n, CE) + pair_of(n, 3 * CE) + pair_of(n, CE) + [vmem(8, 3 * CE), vmem(n, CE), vmem(3, 96, CE)]
        + refs
    )
    return call(
        partial(encoder_backward, plan), "encoder_backward", [dlat, flat, rest, tab, early_a, early_b] + list(saved),
        [shape(WIN_LAT, 96, CE), shape(plan.fus_rows, LANES), shape(plan.enc_rows, LANES), shape(*tab.shape[1:])],
        scratch, 2, 12 * n * 516096, tuple(6 + j for j in (2, 3, 4, 8, 9, 10)),
    )


def merging(
    plan,
    lat_ref, cot_far, flat_ref, tab_ref, base_ref,
    out_ref, dlat_ref, rest_ref, dtab_ref, early_a, early_b,
    grad, cot_ref, core_a, core_b, first_a, first_b, fld_ref, send, recv, lines, bands, vectors, local_sems,
    win_h, win_l, wout_h, wout_l, wup_h, wup_l, wdn_h, wdn_l,
    bias, dbias, x, xhat1, rstd1, xn_h, xn_l, q_h, q_l, k_h, k_l, v_h, v_l, p_h, p_l, o_h, o_l,
    xhat2, rstd2, hn_h, hn_l, acc, dhn, dy, dy_h, dy_l, hn_t, dy_t, dh_h, dh_l, dqkv_h, dqkv_l, sums,
):
    win, wout, wup, wdn = (win_h, win_l), (wout_h, wout_l), (wup_h, wup_l), (wdn_h, wdn_l)
    full = slice(None)
    chunks = MLP_F // FCH
    g, s = lax.axis_index("group"), lax.axis_index("seq")
    seqs = lax.axis_size("seq")
    before, after = lax.rem(s + seqs - SAMPLES, seqs), lax.rem(s + SAMPLES, seqs)
    band = s // SAMPLES
    picked = pltpu.make_async_copy(tab_ref.at[:, pl.ds(pl.multiple_of(band // 8 * 8, 8), 8)], bands, local_sems.at[0])
    picked.start()
    loads = {}
    for n, name in enumerate(FUS_MATS):
        some = pl.ds(FUS_AT[name], math.prod(FUS_MATS[name]) // LANES)
        loads[name] = pltpu.make_async_copy(flat_ref.at[some], grad.at[some], local_sems.at[n + 1])
    at = FUS_AT["g1"] // LANES
    loads["g1"] = pltpu.make_async_copy(flat_ref.at[pl.ds(at, flat_ref.shape[0] - at)], vectors, local_sems.at[5])
    loads["cot"] = pltpu.make_async_copy(cot_far, cot_ref, local_sems.at[8])
    for one in loads.values():
        one.start()
    barrier = pltpu.get_barrier_semaphore()
    places = plan.places
    places.here()
    peers = [(1 - g, s), (g, before), (g, after), (1 - g, before), (1 - g, after)]
    for digit in (len(places.sizes) - 1, plan.fus[1].order[0]):
        size = places.sizes[digit]
        peers += [places.peer(digit, lax.rem(places.mine[digit] + k, size)) for k in range(1, size)]
    for peer in peers:
        pl.semaphore_signal(barrier, inc=1, device_id=peer, device_id_type=MESH)
    pl.semaphore_wait(barrier, len(peers))
    early, base = [], 6
    for portion, core, first, out in zip(plan.fus, (core_a, core_b), (first_a, first_b), (early_a, early_b)):
        early.append(Stream(places, portion, plan.is_early, lambda at: at, (send, recv), base).buffers({0: core, 1: out}, {0: first}))
        base += portion.semaphores()

    def half(one):
        return pl.ds(pl.multiple_of(one * 48, 48), 48)

    far = [
        start_copy(lat_ref.at[pl.ds(0, 3), half(1 - g)], fld_ref.at[g, pl.ds(3, 3)], (send, recv), 0, (1 - g, s)),
        start_copy(lat_ref.at[pl.ds(3, 3), half(g)], fld_ref.at[g, pl.ds(0, 3)], (send, recv), 1, (g, after)),
        start_copy(lat_ref.at[pl.ds(3, 3), half(1 - g)], fld_ref.at[g, pl.ds(0, 3)], (send, recv), 2, (1 - g, after)),
    ]
    far.append(pltpu.make_async_copy(lat_ref.at[pl.ds(0, 3), half(g)], fld_ref.at[g, pl.ds(3, 3)], local_sems.at[9]))
    far[-1].start()
    scale = 1.0 / math.sqrt(HEAD)

    def store(pair):
        def one(rows, c, v):
            put(pair, (rows, slice(c * LANES, (c + 1) * LANES)), v)
        return one

    def store_up(rows, c, v):
        put(wup, (c // (FCH // LANES), full, slice(c % (FCH // LANES) * LANES, (c % (FCH // LANES) + 1) * LANES)), v)

    def store_down(rows, c, v):
        for j in range(chunks):
            put(wdn, (j, full, slice(c * LANES, (c + 1) * LANES)), v[j * FCH : (j + 1) * FCH])

    loads["in"].wait()
    unpack_matrix(grad, FUS_AT["in"], FUS_MATS["in"], store(win), None)
    loads["out"].wait()
    unpack_matrix(grad, FUS_AT["out"], FUS_MATS["out"], store(wout), None)
    loads["up"].wait()
    unpack_matrix(grad, FUS_AT["up"], FUS_MATS["up"], store_up, None)
    loads["down"].wait()
    unpack_matrix(grad, FUS_AT["down"], FUS_MATS["down"], store_down, None)
    loads["g1"].wait()
    vec = {name: vector(vectors, FUS_AT[name] - FUS_AT["g1"], amount) for name, amount in FUS_VECS.items()}
    masks = head_masks(LANES)

    spots = jnp.where(lax.broadcasted_iota(jnp.int32, (TAB_PAD, 2 * LANES), 0) == base_ref[...], 1.0, 0.0).astype(BF16)
    picked.wait()
    for h in range(HEADS_F):
        lines[h : h + 1, :] = bands[h, pl.ds(lax.rem(band, 8), 1), :]
    pad = jnp.zeros((HEADS_F, TAB_PAD - PAIRS * SPAN), F32)
    table = []
    for z in range(WIN_MOD):
        for r in range(WIN_LAT):
            at = [((z * WIN_MOD + y) * WIN_LAT * WIN_LAT + r * WIN_LAT) * SPAN for y in range(WIN_MOD)]
            one = jnp.concatenate([lines[0:HEADS_F, t : t + WIN_LAT * SPAN] for t in at] + [pad], 1)
            table.append(jnp.concatenate([one, jnp.zeros((16 - HEADS_F, TAB_PAD), F32)], 0))
    table = jnp.concatenate(table, 0)
    for w in range(WIN_LON):
        turned = pltpu.roll(table, TAB_PAD - w, 1) if w else table
        hi, lo = split(turned)
        rest = (turned - hi.astype(F32) - lo.astype(F32)).astype(BF16)
        one = dot(hi, spots) + (dot(lo, spots) + dot(rest, spots))
        for n in range(PAIRS):
            for c in range(2):
                bias[c, pl.ds(n * WIN_LON + w, HEADS_F, stride=ROWS_F), :] = one[n * 16 : n * 16 + HEADS_F, c * LANES : (c + 1) * LANES]
    dbias[...] = jnp.zeros_like(dbias)

    loads["cot"].wait()
    for z, r, at, start in merging_slots():
        dy[at : at + WIN_LON, :] = cot_ref[z, r, start : start + WIN_LON, :]
    put((dy_h, dy_l), (full, full), dy[...])
    dy_t[...] = left3((dy_h[...], dy_l[...]), 0).T
    sums[10:11, 0:CF] = column_sum(dy[...])
    for one in far:
        one.wait()
    for z, r, at, start in merging_slots():
        x[at : at + WIN_LON, :] = fld_ref[z, r, start : start + WIN_LON, :]

    def rows_of(i):
        return pl.ds(pl.multiple_of(i * ROWS_F, ROWS_F), ROWS_F)

    xhat, rstd = normalize(x[...])
    xhat1[...] = xhat
    rstd1[...] = rstd
    put((xn_h, xn_l), (full, full), xhat * vec["g1"] + vec["s1"])
    for j, (pair, shift) in enumerate((((q_h, q_l), vec["qb"]), ((k_h, k_l), None), ((v_h, v_l), vec["vb"]))):
        one = deep3((xn_h[...], xn_l[...]), get(win, (full, slice(j * CF, (j + 1) * CF))))
        if shift is not None:
            one = one + shift
        if j == 0:
            one = one * scale
        put(pair, (full, full), one)

    def forward(i, carry):
        rows = rows_of(i)
        for b in range(3):
            cols = slice(b * LANES, (b + 1) * LANES)
            qm = stacked((q_h[rows, cols], q_l[rows, cols]), masks)
            some = slice(b * 4 * ROWS_F, (b + 1) * 4 * ROWS_F)
            s = deep3(qm, (k_h[rows, cols], k_l[rows, cols]), 1, 1) + get_tiles(bias, some, ROWS_F)
            p = split(softmax(s))
            p_h[i * 3 + b] = p[0]
            p_l[i * 3 + b] = p[1]
            o = unstacked(wide_n(p, (v_h[rows, cols], v_l[rows, cols])), masks)
            put((o_h, o_l), (rows, cols), o)
        return carry

    lax.fori_loop(0, 4, forward, 0)
    hidden = x[...] + deep3((o_h[...], o_l[...]), get(wout, (full, full))) + vec["ob"]
    xh2, rstd = normalize(hidden)
    xhat2[...] = xh2
    rstd2[...] = rstd
    put((hn_h, hn_l), (full, full), xh2 * vec["g2"] + vec["s2"])
    acc[...] = hidden + vec["db"]
    dhn[...] = jnp.zeros_like(dhn)
    hn_t[...] = left3((hn_h[...], hn_l[...]), 0).T
    for c in range(chunks):
        sums[8:9, c * FCH : (c + 1) * FCH] = vec["ub"][:, c * FCH : (c + 1) * FCH]

    def feed(c, carry):
        up = (wup_h[c], wup_l[c])
        down = (wdn_h[c], wdn_l[c])
        cols = pl.ds(pl.multiple_of(c * FCH, FCH), FCH)
        shift = sums[8:9, cols]

        u = deep3((hn_h[...], hn_l[...]), up) + shift
        gl, slope = gelu_parts(u)
        gl = split(gl)
        acc[...] = acc[...] + deep3(gl, down)
        du = deep3((dy_h[...], dy_l[...]), down, 1, 1) * slope
        sums[9:10, cols] = column_sum(du)
        du = split(du)
        dhn[...] = dhn[...] + deep3(du, up, 1, 1)
        dw = dot(hn_t[...], right3(du))
        for t in range(FCH // LANES):
            grad[pl.ds(FUS_AT["up"] + FCH // LANES * c + t, CF, stride=12), :] = dw[:, t * LANES : (t + 1) * LANES]
        dw = dot(dy_t[...], right3(gl)).T
        for t in range(3):
            grad[pl.ds(FUS_AT["down"] + 3 * FCH * c + t, FCH, stride=3), :] = dw[:, t * LANES : (t + 1) * LANES]
        return carry

    lax.fori_loop(0, chunks, feed, 0)
    for one in early:
        one.start_core(grad)
    put_vector(grad, FUS_AT["ub"], sums[9:10, :])
    sums[0:8, :] = jnp.zeros((8, MLP_F), F32)

    dv = dhn[...]
    sums[0:1, 0:CF] = sums[10:11, 0:CF]
    sums[1:2, 0:CF] = column_sum(dv * xhat2[...])
    sums[2:3, 0:CF] = column_sum(dv)
    dh = dy[...] + normalize_back(dv, xhat2[...], rstd2[...], vec["g2"])
    sums[3:4, 0:CF] = column_sum(dh)
    dy[...] = dh
    put((dh_h, dh_l), (full, full), dh)
    do_h, do_l = hn_h, hn_l
    put((do_h, do_l), (full, full), deep3((dh_h[...], dh_l[...]), get(wout, (full, full)), 1, 1))

    for one in early:
        one.finish_core(grad)
        one.start(0)

    def backward(i, carry):
        rows = rows_of(i)
        for b in range(3):
            cols = slice(b * LANES, (b + 1) * LANES)
            dom = stacked((do_h[rows, cols], do_l[rows, cols]), masks)
            qm = stacked((q_h[rows, cols], q_l[rows, cols]), masks)
            p = (p_h[i * 3 + b], p_l[i * 3 + b])
            dp = deep3(dom, (v_h[rows, cols], v_l[rows, cols]), 1, 1)
            pf = p[0].astype(F32) + p[1].astype(F32)
            t = pf * dp
            ds = t - pf * jnp.sum(t, 1, keepdims=True)
            some = slice(b * 4 * ROWS_F, (b + 1) * 4 * ROWS_F)
            for c in range(2):
                one = ds[:, c * LANES : (c + 1) * LANES]
                dbias[c, some, 0 : one.shape[1]] = dbias[c, some, 0 : one.shape[1]] + one
            ds = split(ds)
            dq = unstacked(wide_n(ds, (k_h[rows, cols], k_l[rows, cols])), masks) * scale
            dk = dot(left3(qm, 0).T, right3(ds)).T
            dvv = dot(left3(dom, 0).T, right3(p)).T
            for j, one in enumerate((dq, dk, dvv)):
                at = slice(j * CF + b * LANES, j * CF + (b + 1) * LANES)
                put((dqkv_h, dqkv_l), (rows, at), one)
                if j != 1:
                    sums[4 + j // 2 : 5 + j // 2, cols] = sums[4 + j // 2 : 5 + j // 2, cols] + column_sum(one)
        return carry

    lax.fori_loop(0, 4, backward, 0)
    dxn = deep3((dqkv_h[...], dqkv_l[...]), get(win, (full, full)), 1, 1)
    sums[6:7, 0:CF] = column_sum(dxn * xhat1[...])
    sums[7:8, 0:CF] = column_sum(dxn)
    x[...] = dy[...] + normalize_back(dxn, xhat1[...], rstd1[...], vec["g1"])
    dx_ref = fld_ref
    for z, r, at, start in merging_slots():
        dx_ref[z, r, start : start + WIN_LON, :] = x[at : at + WIN_LON, :]
    back = [
        start_copy(dx_ref.at[1 - g, pl.ds(3, 3)], dlat_ref.at[pl.ds(0, 3), half(g)], (send, recv), 3, (1 - g, s)),
        start_copy(dx_ref.at[g, pl.ds(0, 3)], dlat_ref.at[pl.ds(3, 3), half(g)], (send, recv), 4, (g, before)),
        start_copy(dx_ref.at[1 - g, pl.ds(0, 3)], dlat_ref.at[pl.ds(3, 3), half(g)], (send, recv), 5, (1 - g, before)),
    ]
    dlat_ref[0:3, half(g), :] = dx_ref[g, 3:6]
    for j, name in enumerate(("db", "g2", "s2", "ob", "qb", "vb", "g1", "s1")):
        put_vector(grad, FUS_AT[name], sums[j : j + 1, 0:CF])
    for c in range(3):
        cols = slice(c * CF, (c + 1) * CF)
        dw = dot3((xn_h[...], xn_l[...]), (dqkv_h[:, cols], dqkv_l[:, cols]), 0, 0)
        for t in range(3):
            grad[pl.ds(FUS_AT["in"] + 3 * c + t, CF, stride=9), :] = dw[:, t * LANES : (t + 1) * LANES]
    dw = dot3((o_h[...], o_l[...]), (dh_h[...], dh_l[...]), 0, 0)
    for t in range(3):
        grad[pl.ds(FUS_AT["out"] + t, CF, stride=3), :] = dw[:, t * LANES : (t + 1) * LANES]
    rest = [
        pltpu.make_async_copy(grad.at[pl.ds(0, plan.rest_low)], rest_ref.at[pl.ds(0, plan.rest_low)], local_sems.at[6]),
        pltpu.make_async_copy(
            grad.at[pl.ds(plan.rest_from, plan.rest_all - plan.rest_low)],
            rest_ref.at[pl.ds(plan.rest_low, plan.rest_all - plan.rest_low)], local_sems.at[7],
        ),
    ]
    for one in rest:
        one.start()
    for one in early:
        one.finish(0)
    total = jnp.zeros((PAIRS * 16, TAB_PAD), F32)
    blank = jnp.zeros((16 - HEADS_F, 2 * LANES), F32)
    for w in range(WIN_LON):
        rows = []
        for n in range(PAIRS):
            rows.append(jnp.concatenate([dbias[c, pl.ds(n * WIN_LON + w, HEADS_F, stride=ROWS_F), :] for c in range(2)], 1))
            rows.append(blank)
        hi, lo = split(jnp.concatenate(rows, 0))
        one = dot(hi, spots, 1, 1) + dot(lo, spots, 1, 1)
        total = total + (pltpu.roll(one, w, 1) if w else one)
    for z in range(WIN_MOD):
        for r in range(WIN_LAT):
            n = z * WIN_LAT + r
            for y in range(WIN_MOD):
                at = ((z * WIN_MOD + y) * WIN_LAT * WIN_LAT + r * WIN_LAT) * SPAN
                lines[0:HEADS_F, at : at + WIN_LAT * SPAN] = total[n * 16 : n * 16 + HEADS_F, y * WIN_LAT * SPAN : (y + 1) * WIN_LAT * SPAN]
    for j in range(4):
        dtab_ref[j, 0:3, :] = lines[3 * j : 3 * j + 3, :]
    for z, r, at, start in merging_slots():
        out_ref[z, r, start : start + WIN_LON, :] = acc[at : at + WIN_LON, :]
    for one in back + rest:
        one.wait()


def merging_call(plan, latent, cotangent, flat, table):
    n = 4 * ROWS_F
    m = HEADS_F * ROWS_F
    t = np.arange(ROWS_F)
    base = np.full((1, 2 * LANES), -1, np.int32)
    base[0, :ROWS_F] = t // WIN_LON * SPAN + WIN_LON - 1 - t % WIN_LON
    base = jnp.asarray(base)
    scratch = (
        [vmem(plan.fus_all, LANES), vmem(*cotangent.shape)]
        + [portion.core_scratch() for portion in plan.fus] + [portion.scratch(0) for portion in plan.fus]
        + [vmem(*cotangent.shape)] + sems(6 + sum(portion.semaphores() for portion in plan.fus)) + [vmem(16, table.shape[2]), vmem(HEADS_F, 8, table.shape[2]), vmem(flat.shape[0] - FUS_AT["g1"] // LANES, LANES), pltpu.SemaphoreType.DMA((10,))] + pair_of(CF, 3 * CF) + pair_of(CF, CF) + pair_of(MLP_F // FCH, CF, FCH) + pair_of(MLP_F // FCH, FCH, CF)
        + [vmem(2, m, LANES), vmem(2, m, LANES), vmem(n, CF), vmem(n, CF), vmem(n, 1)]
        + pair_of(n, CF) + pair_of(n, CF) + pair_of(n, CF) + pair_of(n, CF) + pair_of(12, 4 * ROWS_F, ROWS_F) + pair_of(n, CF)
        + [vmem(n, CF), vmem(n, 1)] + pair_of(n, CF) + [vmem(n, CF), vmem(n, CF), vmem(n, CF)] + pair_of(n, CF)
        + [vmem(CF, 3 * n, dtype=BF16)] * 2 + pair_of(n, CF) + pair_of(n, 3 * CF) + [vmem(16, MLP_F)]
    )
    outs = [shape(*cotangent.shape), shape(*latent.shape), shape(plan.rest_all, LANES), shape(4, 3, table.shape[2])]
    outs += [shape(portion.blocks(0), portion.rows, LANES) for portion in plan.fus]
    return call(partial(merging, plan), "merging", [latent, cotangent, flat, table, base], outs, scratch, 1, 18 * n * 1769472, (0, 1, 2, 3), (2,))


def update(params, grads, momentum, average, rate):
    momentum_new = MOMENTUM_DECAY * momentum + grads
    params_new = params - rate * (grads + MOMENTUM_DECAY * momentum_new)
    average_new = AVERAGE_DECAY * average + (1.0 - AVERAGE_DECAY) * params_new
    return (params_new, momentum_new, average_new)


def shifted_piece(block, rows, at, piece):
    amount = -(-piece // LANES)
    first, lane = at // LANES, lax.rem(at, LANES)
    rows[0 : block.shape[0], :] = pltpu.roll(block[...], LANES - lane, 1)
    low = lax.broadcasted_iota(jnp.int32, (1, LANES), 1) < LANES - lane
    return jnp.where(low, rows[pl.ds(first, amount), :], rows[pl.ds(first + 1, amount), :])


def optimizer(
    rates, fus_start, enc_start,
    merged_in, field_in, fus_block, fus_flat, fus_mom, fus_avg, enc_block, enc_flat, enc_mom, enc_avg, tab_block, table, tab_mom, tab_avg,
    merged, field, enc_grad, enc_new, enc_mom_new, enc_avg_new, fus_grad, fus_new, fus_mom_new, fus_avg_new,
    tab_grad, tab_new, tab_mom_new, tab_avg_new,
    fus_own, enc_own, tab_own, rows, sems,
):
    g, s = lax.axis_index("group"), lax.axis_index("seq")
    slot = g * lax.axis_size("seq") + s
    band, part = slot // 4, lax.rem(slot, 4)
    fus_piece, enc_piece = fus_mom.shape[0], enc_mom.shape[1]
    fus_from = pl.multiple_of(jnp.minimum(fus_start(slot), fus_flat.shape[0] - fus_own.shape[0]), 8)
    enc_from = enc_start(s)
    copies = [
        pltpu.make_async_copy(fus_flat.at[pl.ds(fus_from, fus_own.shape[0])], fus_own, sems.at[0]),
        pltpu.make_async_copy(enc_flat.at[pl.ds(enc_from, enc_own.shape[0])], enc_own, sems.at[1]),
        pltpu.make_async_copy(table.at[pl.ds(3 * part, 3), pl.ds(pl.multiple_of(band // 8 * 8, 8), 8)], tab_own, sems.at[2]),
        pltpu.make_async_copy(merged_in, merged, sems.at[3]),
        pltpu.make_async_copy(field_in, field, sems.at[4]),
    ]
    for one in copies:
        one.start()

    def store(outs, values):
        for ref, value in zip(outs, values):
            ref[...] = value

    def step(own, grads, mom, avg, rate, outs):
        new, mom_new, avg_new = update(own, grads, mom[...], avg[...], rate)
        store(outs, (grads, new, mom_new, avg_new))

    fus_at = fus_piece * slot
    grads = shifted_piece(fus_block, rows, fus_at - fus_start(slot) * LANES, fus_piece).reshape(-1)[:fus_piece]
    copies[0].wait()
    own = shifted_piece(fus_own, rows, fus_at - fus_from * LANES, fus_piece).reshape(-1)[:fus_piece]
    step(own, grads, fus_mom, fus_avg, rates[1], (fus_grad, fus_new, fus_mom_new, fus_avg_new))
    enc_at = enc_piece * s - enc_from * LANES
    grads = shifted_piece(enc_block, rows, enc_at, enc_piece).reshape(1, -1)[:, :enc_piece]
    copies[1].wait()
    own = shifted_piece(enc_own, rows, enc_at, enc_piece).reshape(1, -1)[:, :enc_piece]
    step(own, grads, enc_mom, enc_avg, rates[0], (enc_grad, enc_new, enc_mom_new, enc_avg_new))
    grads = jnp.concatenate([tab_block[j : j + 1, :] for j in range(3)], 1).reshape(-1)
    copies[2].wait()
    own = jnp.concatenate([tab_own[j, pl.ds(lax.rem(band, 8), 1), :] for j in range(3)], 1).reshape(-1)
    step(own, grads, tab_mom, tab_avg, rates[2], (tab_grad, tab_new, tab_mom_new, tab_avg_new))
    for one in copies[3:]:
        one.wait()


def optimizer_call(plan, rates, merged, field, fus_block, fus_flat, fus_mom, fus_avg, enc_block, enc_flat, enc_mom, enc_avg, tab_block, table, tab_mom, tab_avg):
    inputs = [merged, field, fus_block, fus_flat, fus_mom, fus_avg, enc_block, enc_flat, enc_mom, enc_avg, tab_block, table, tab_mom, tab_avg]
    outs = [merged, field] + [enc_mom] * 4 + [fus_mom] * 4 + [tab_mom] * 4
    far, far_outs = (0, 1, 3, 7, 11), ()
    fus_rows = plan.fus_rows + fus_flat.shape[0] % 8
    return pl.pallas_call(
        partial(optimizer, rates, partial(window_start, fus_mom.size), partial(window_start, enc_mom.size)),
        name="optimizer",
        out_shape=[shape(*v.shape) for v in outs],
        in_specs=[pl.BlockSpec(memory_space=pl.ANY if n in far else pltpu.VMEM) for n in range(len(inputs))],
        out_specs=[pl.BlockSpec(memory_space=pl.ANY if n in far_outs else pltpu.VMEM) for n in range(len(outs))],
        scratch_shapes=[
            vmem(fus_rows, LANES), vmem(plan.enc_rows, LANES), vmem(3, 8, table.shape[2]),
            vmem(fus_rows + 16, LANES), pltpu.SemaphoreType.DMA((5,)),
        ],
        compiler_params=pltpu.CompilerParams(vmem_limit_bytes=VMEM_BYTES),
    )(*inputs)


def shards(
    tokens,
    cotangent,
    enc_params,
    enc_momentum,
    enc_average,
    fus_params,
    fus_momentum,
    fus_average,
    earth_bias,
    bias_momentum,
    bias_average,
):
    field = tokens[0, 0]
    row_count, col_count, feat_width = field.shape
    seq_count = lax.axis_size("seq")
    group_count = lax.axis_size("group")
    band_count = seq_count // SAMPLES
    fus_flat = fus_params.reshape(-1, LANES)
    plan = Sums(group_count, seq_count, fus_params.size, enc_params.size)
    latent, enc_flat, *saved = encoder_forward_call(field, enc_params, plan.enc_all)
    table = earth_bias.transpose(1, 0, 2)
    merged, latent_grad, rest, table_grad, early_a, early_b = merging_call(plan, latent, cotangent[:, 0, 0], fus_flat, table)
    field_grad, fus_block, enc_block, tab_block = encoder_backward_call(
        plan, latent_grad, enc_flat, rest, table_grad, early_a, early_b, saved
    )
    lat_total = seq_count // SAMPLES * row_count
    rates = (
        1.0 / math.sqrt(CE * SAMPLES * lat_total * col_count),
        1.0 / math.sqrt(CF * group_count * SAMPLES * lat_total * col_count),
        2.0 / math.sqrt(SAMPLES * col_count / WIN_LON),
    )
    merged, field_grad, *others = optimizer_call(
        plan, rates, merged, field_grad, fus_block, fus_flat, fus_momentum, fus_average, enc_block, enc_flat,
        enc_momentum, enc_average, tab_block, table, bias_momentum, bias_average,
    )
    return (merged[:, None, None], field_grad[None, None], *others)


def solution(mesh):
    both = P(("group", "seq"))
    rows = P("group", "seq")
    merged = P(None, "seq", "group", None, None, None)
    tokens = P("group", "seq", None, None, None)
    return jax.shard_map(
        shards,
        mesh=mesh,
        in_specs=(tokens, merged, P("group", None), rows, rows, P(), both, both, P(), both, both),
        out_specs=(merged, tokens, rows, rows, rows, rows) + (both,) * 8,
        check_vma=False,
    )
```

```python
from functools import partial
import math

import jax
import jax.numpy as jnp
import numpy as np
from jax import lax
from jax.experimental import pallas as pl
from jax.experimental.pallas import tpu as pltpu
from jax.sharding import PartitionSpec as P

CE = 192
CF = 384
HEADS_E = 6
HEADS_F = 12
MLP_E = 768
MLP_F = 1536
WIN_LAT = 6
WIN_LON = 12
WIN_MOD = 2
SAMPLES = 2
HEAD = 32
CHUNK = 256
FCH = 384
LANES = 128
ROWS_E = WIN_LAT * WIN_LON
ROWS_F = WIN_MOD * ROWS_E
SPAN = 2 * WIN_LON - 1
PAIRS = WIN_MOD * WIN_LAT
TAB_PAD = 384
EPS = 1e-05
NEG = -1000000000.0
VMEM_BYTES = 61 << 20

MOMENTUM_DECAY = 0.9
AVERAGE_DECAY = 0.99

F32 = jnp.float32
BF16 = jnp.bfloat16

ENC_MATS = {"in": (CE, 3 * CE), "out": (CE, CE), "up": (CE, MLP_E), "down": (MLP_E, CE), "lin": (CE, CF)}
ENC_VECS = {"g1": CE, "s1": CE, "qb": CE, "vb": CE, "ob": CE, "g2": CE, "s2": CE, "ub": MLP_E, "db": CE, "lb": CF}
FUS_MATS = {"in": (CF, 3 * CF), "out": (CF, CF), "up": (CF, MLP_F), "down": (MLP_F, CF)}
FUS_VECS = {"g1": CF, "s1": CF, "qb": CF, "vb": CF, "ob": CF, "g2": CF, "s2": CF, "ub": MLP_F, "db": CF}


def offsets(mats, vecs):
    places, at = {}, 0
    for name, shape in mats.items():
        places[name] = at // LANES
        at += shape[0] * shape[1]
    for name, amount in vecs.items():
        places[name] = at
        at += amount
    return places


ENC_AT = offsets(ENC_MATS, ENC_VECS)
FUS_AT = offsets(FUS_MATS, FUS_VECS)


def split(v):
    hi = v.astype(BF16)
    return hi, (v - hi.astype(F32)).astype(BF16)


def dot(a, b, ca=1, cb=0):
    return lax.dot_general(a, b, (((ca,), (cb,)), ((), ())), preferred_element_type=F32)


def dot3(a, b, ca=1, cb=0):
    return dot(a[0], b[0], ca, cb) + (dot(a[0], b[1], ca, cb) + dot(a[1], b[0], ca, cb))


def left3(a, axis=1):
    return jnp.concatenate([a[0], a[0], a[1]], axis)


def right3(b, axis=0):
    return jnp.concatenate([b[0], b[1], b[0]], axis)


def deep3(a, b, ca=1, cb=0):
    return dot(left3(a, ca), right3(b, cb), ca, cb)


def put(refs, index, v):
    hi, lo = split(v)
    refs[0][index] = hi
    refs[1][index] = lo


def get(refs, index):
    return refs[0][index], refs[1][index]


def half_lanes():
    return lax.broadcasted_iota(jnp.int32, (1, LANES), 1) < LANES // 2


def turn(v):
    return pltpu.roll(v, LANES // 2, 1)


def vector(flat, at, amount):
    tiles = []
    for c in range(-(-amount // LANES)):
        row, lane = divmod(at + c * LANES, LANES)
        one = flat[row : row + 1, :]
        if lane:
            one = turn(one)
            if c * LANES + LANES // 2 < amount:
                one = jnp.where(half_lanes(), one, turn(flat[row + 1 : row + 2, :]))
        tiles.append(one)
    return jnp.concatenate(tiles, 1)[:, :amount] if len(tiles) > 1 else tiles[0][:, :amount]


def put_vector(flat, at, v):
    amount = v.shape[1]
    if at % LANES == 0 and amount % LANES == 0:
        for c in range(amount // LANES):
            flat[at // LANES + c : at // LANES + c + 1, :] = v[:, c * LANES : (c + 1) * LANES]
        return
    half = LANES // 2
    for c in range(amount // half):
        row, lane = divmod(at + c * half, LANES)
        flat[row : row + 1, lane : lane + half] = v[:, c * half : (c + 1) * half]


def unpack_matrix(flat, at, shape, store, scratch):
    rows, width = shape
    if width % LANES == 0:
        n = width // LANES
        for c in range(n):
            store(slice(0, rows), c, flat[pl.ds(at + c, rows, stride=n), :])
        return
    pairs, n, full = rows // 2, 2 * width // LANES, width // LANES
    low = half_lanes()
    for c in range(full + 1):
        scratch[c, pl.ds(0, pairs, stride=2), :] = flat[pl.ds(at + c, pairs, stride=n), :]
        odd = turn(flat[pl.ds(at + full + c, pairs, stride=n), :])
        if c < full:
            odd = jnp.where(low, odd, turn(flat[pl.ds(at + full + c + 1, pairs, stride=n), :]))
        scratch[c, pl.ds(1, pairs, stride=2), :] = odd
    for c in range(full + 1):
        store(slice(0, rows), c, scratch[c, 0:rows, :])


def pack_matrix(flat, at, shape, source):
    rows, width = shape
    pairs, n, full = rows // 2, 2 * width // LANES, width // LANES
    low = half_lanes()

    def tile(odd, c):
        return source[c, pl.ds(odd, pairs, stride=2), :]

    for c in range(full):
        flat[pl.ds(at + c, pairs, stride=n), :] = tile(0, c)
        flat[pl.ds(at + full + 1 + c, pairs, stride=n), :] = jnp.where(low, turn(tile(1, c)), turn(tile(1, c + 1)))
    flat[pl.ds(at + full, pairs, stride=n), :] = jnp.where(low, tile(0, full), turn(tile(1, 0)))


def put_tiles(ref, rows, v):
    for c in range(-(-v.shape[1] // LANES)):
        one = v[:, c * LANES : (c + 1) * LANES]
        ref[c, rows, 0 : one.shape[1]] = one


def get_tiles(ref, rows, width):
    tiles = [ref[c, rows, 0 : min(width - c * LANES, LANES)] for c in range(-(-width // LANES))]
    return jnp.concatenate(tiles, 1)


def normalize(x):
    center = x - jnp.mean(x, 1, keepdims=True)
    scale = lax.rsqrt(jnp.mean(center * center, 1, keepdims=True) + EPS)
    return center * scale, scale


def normalize_back(dv, xhat, scale, gain):
    dxhat = dv * gain
    return scale * (dxhat - jnp.mean(dxhat, 1, keepdims=True) - xhat * jnp.mean(dxhat * xhat, 1, keepdims=True))


def gelu_parts(u):
    phi = 0.5 * (1.0 + lax.erf(u * (1.0 / math.sqrt(2.0))))
    return u * phi, phi + u * jnp.exp(-0.5 * u * u) * (1.0 / math.sqrt(2.0 * math.pi))


def head_masks(width):
    lane = lax.broadcasted_iota(jnp.int32, (1, width), 1)
    return [jnp.where((lane >= h * HEAD) & (lane < (h + 1) * HEAD), 1.0, 0.0) for h in range(width // HEAD)]


def stacked(pair, masks):
    return tuple(jnp.concatenate([part * m.astype(BF16) for m in masks], 0) for part in pair)


def unstacked(v, masks):
    rows = v.shape[0] // len(masks)
    total = v[:rows] * masks[0]
    for h in range(1, len(masks)):
        total = total + v[h * rows : (h + 1) * rows] * masks[h]
    return total


def softmax(s):
    e = jnp.exp(s - jnp.max(s, 1, keepdims=True))
    return e / jnp.sum(e, 1, keepdims=True)


def wide_nt(a, b):
    return dot(jnp.concatenate(a, 1), jnp.concatenate([b[0], b[0]], 1), 1, 1) + dot(a[0], b[1], 1, 1)


def wide_n(a, b, ca=1):
    n = b[0].shape[1]
    both = dot(a[0], jnp.concatenate(b, 1), ca, 0)
    return both[:, :n] + (both[:, n:] + dot(a[1], b[0], ca, 0))


def column_sum(v):
    return jnp.sum(v, 0, keepdims=True)


def encoder_slots():
    for r in range(WIN_LAT):
        for n in range(8):
            start = n * WIN_LON + WIN_LON // 2
            at = n * ROWS_E + r * WIN_LON
            if n < 7:
                yield r, at, start, WIN_LON
            else:
                yield r, at, start, WIN_LON // 2
                yield r, at + WIN_LON // 2, 0, WIN_LON // 2


def merging_slots():
    for z in range(WIN_MOD):
        for r in range(WIN_LAT):
            for n in range(4):
                yield z, r, n * ROWS_F + (z * WIN_LAT + r) * WIN_LON, n * WIN_LON


MESH = pl.DeviceIdType.MESH


def seq_digits(count):
    rest, digits = count // 2, []
    while rest > 1:
        digits.insert(0, 4 if rest % 4 == 0 else 2)
        rest //= digits[0]
    digits.sort()
    if count == 16:
        digits = [4, 2]
    return digits + [2]


class Places:
    def __init__(self, groups, seqs):
        self.sizes = [groups] + seq_digits(seqs)
        self.groups = groups
        self.strides = [1] * len(self.sizes)
        for i in range(len(self.sizes) - 2, 0, -1):
            self.strides[i] = self.strides[i + 1] * self.sizes[i + 1]

    def here(self):
        self.g, self.s = lax.axis_index("group"), lax.axis_index("seq")
        self.mine = [self.g] + [self.s // self.strides[i] % self.sizes[i] for i in range(1, len(self.sizes))]

    def peer(self, digit, value):
        if digit == 0:
            return (value, self.s)
        return (self.g, self.s + (value - self.mine[digit]) * self.strides[digit])

    def place(self, values):
        return sum(v * self.strides[i] for i, v in values.items() if i)


def windows(total, count):
    piece = total // count
    tiles = max(-(-(piece * (d + 1)) // 1024) - piece * d // 1024 for d in range(count))
    last = piece * (count - 1) // 1024
    return piece, tiles * 8, (last + tiles) * 8


def window_start(piece, d):
    return pl.multiple_of(piece * d // 1024 * 8, 8)


def start_copy(src, dst, sems, at, peer):
    one = pltpu.make_async_remote_copy(
        src_ref=src, dst_ref=dst, send_sem=sems[0].at[at], recv_sem=sems[1].at[at], device_id=peer, device_id_type=MESH
    )
    one.start()
    return one


class Stream:
    def __init__(self, places, plan, chosen, shift, sems, base):
        self.places, self.order, self.piece, self.first, self.rows = places, plan.order, plan.piece, plan.first, plan.rows
        self.chosen, self.shift, self.sems, self.base = chosen, shift, sems, base
        self.sizes = plan.sizes
        self.held, self.arrived = {}, {}
        self.last = len(places.sizes) - 1

    def buffers(self, held, arrived):
        self.held.update(held)
        self.arrived.update(arrived)
        return self

    def combos(self, i=0):
        out = [()]
        for n in self.sizes[i:]:
            out = [c + (v,) for c in out for v in range(n)]
        return out

    def number(self, values):
        where = self.places.place(values)
        if 0 in values:
            where = where + values[0] * (self.places.sizes[1] * self.places.strides[1])
        return where

    def target(self, i, combo, core):
        values = {d: self.places.mine[d] for d in self.order[:i]}
        values.update(zip(self.order[i:], combo))
        values[self.last] = core
        return self.number(values)

    def when(self, number, action):
        if self.chosen is None:
            action()
        else:
            pl.when(self.chosen(number))(action)

    def window(self, number):
        return pl.ds(pl.multiple_of(self.shift(window_start(self.piece, number)) + self.first, 8), self.rows)

    def core_copy(self, n, number, source):
        p = self.places
        core = p.mine[self.last]
        return pltpu.make_async_remote_copy(
            src_ref=source.at[self.window(number)], dst_ref=self.held[0].at[n], send_sem=self.sems[0].at[self.base + n],
            recv_sem=self.sems[1].at[self.base + n], device_id=p.peer(self.last, 1 - core), device_id_type=MESH,
        )

    def start_core(self, source):
        core = self.places.mine[self.last]
        for n, combo in enumerate(self.combos()):
            number = self.target(0, combo, 1 - core)
            self.when(number, lambda n=n, number=number: self.core_copy(n, number, source).start())

    def finish_core(self, source):
        core = self.places.mine[self.last]
        for n, combo in enumerate(self.combos()):
            number = self.target(0, combo, core)

            def add(n=n, number=number):
                self.core_copy(n, number, source).wait_recv()
                self.held[0][n] = self.held[0][n] + source[self.window(number), :]

            self.when(number, add)
        for n, combo in enumerate(self.combos()):
            number = self.target(0, combo, 1 - core)
            self.when(number, lambda n=n, number=number: self.core_copy(n, number, source).wait_send())

    def blocks(self, i):
        return math.prod(self.sizes[i + 1 :])

    def copy(self, i, k, n):
        p, digit, size = self.places, self.order[i], self.sizes[i]
        value = lax.rem(p.mine[digit] + k, size)
        at = self.base + len(self.combos()) + sum((self.sizes[j] - 1) * self.blocks(j) for j in range(i)) + (k - 1) * self.blocks(i) + n
        return pltpu.make_async_remote_copy(
            src_ref=self.held[i].at[value * self.blocks(i) + n], dst_ref=self.arrived[i].at[k - 1, n], send_sem=self.sems[0].at[at],
            recv_sem=self.sems[1].at[at], device_id=p.peer(digit, value), device_id_type=MESH,
        )

    def sent(self, i):
        core = self.places.mine[self.last]
        for k in range(1, self.sizes[i]):
            value = lax.rem(self.places.mine[self.order[i]] + k, self.sizes[i])
            for n, combo in enumerate(self.combos(i + 1)):
                yield k, n, self.target(i, (value,) + combo, core)

    def start(self, i):
        for k, n, number in self.sent(i):
            self.when(number, lambda k=k, n=n: self.copy(i, k, n).start())

    def finish(self, i, out=None):
        core = self.places.mine[self.last]
        mine = self.places.mine[self.order[i]]
        for n, combo in enumerate(self.combos(i + 1)):
            def add(n=n):
                total = self.held[i][mine * self.blocks(i) + n]
                for k in range(1, self.sizes[i]):
                    self.copy(i, k, n).wait_recv()
                    total = total + self.arrived[i][k - 1, n]
                if out is None:
                    self.held[i + 1][n] = total
                else:
                    out(total)

            self.when(self.target(i, (mine,) + combo, core), add)
        for k, n, number in self.sent(i):
            self.when(number, lambda k=k, n=n: self.copy(i, k, n).wait_send())

    def semaphores(self):
        return len(self.combos()) + sum((self.sizes[j] - 1) * self.blocks(j) for j in range(len(self.sizes)))


class Portion:
    def __init__(self, places, order, piece, first, rows):
        self.order, self.piece, self.first, self.rows = order, piece, first, rows
        self.sizes = [places.sizes[d] for d in order]

    def blocks(self, i):
        return math.prod(self.sizes[i + 1 :])

    def core_scratch(self):
        return vmem(math.prod(self.sizes), self.rows, LANES)

    def scratch(self, i):
        return vmem(self.sizes[i] - 1, self.blocks(i), self.rows, LANES)

    def semaphores(self):
        return math.prod(self.sizes) + sum((self.sizes[j] - 1) * self.blocks(j) for j in range(len(self.sizes)))


class Sums:
    def __init__(self, groups, seqs, fus_total, enc_total):
        self.places = places = Places(groups, seqs)
        last = len(places.sizes) - 1
        order = sorted(range(1, last), key=lambda d: places.sizes[d])
        piece, rows, self.fus_all = windows(fus_total, groups * seqs)
        enc_piece, enc_rows, self.enc_all = windows(enc_total, seqs)
        first = rows * 4 // 64 * 8
        self.fus = [
            Portion(places, [0] + order, piece, 0, first),
            Portion(places, order[:1] + [0] + order[1:], piece, first, rows - first),
        ]
        cut_a, cut_b = rows * 4 // 96 * 8, rows * 9 // 96 * 8
        cut_a, cut_b = cut_a // 8 * 8, cut_b // 8 * 8
        self.late = [
            Portion(places, [0] + order, piece, 0, cut_a),
            Portion(places, order[:1] + [0] + order[1:], piece, cut_a, cut_b - cut_a),
            Portion(places, order[-1:] + [0] + order[:-1], piece, cut_b, rows - cut_b),
        ]
        self.enc = [Portion(places, order, enc_piece, 0, enc_rows)] * 2
        self.fus_rows, self.enc_rows = rows, enc_rows
        self.low, self.high = FUS_AT["out"], FUS_AT["g1"] // LANES
        starts = [piece * d // 1024 * 8 for d in range(groups * seqs)]
        self.early = [d for d, at in enumerate(starts) if at >= self.low and at + rows <= self.high]
        others = [at for d, at in enumerate(starts) if d not in self.early]
        self.rest_low = max(at for at in others if at < self.low) + rows
        self.rest_from = min(at for at in others if at >= self.low)
        self.rest_all = self.rest_low + self.fus_all - self.rest_from
        enc_starts = [enc_piece * d // 1024 * 8 for d in range(seqs)]
        low, high = ENC_AT["up"], ENC_AT["g1"] // LANES
        self.enc_early = [d for d, at in enumerate(enc_starts) if at >= low and at + enc_rows <= high]

    def is_early(self, d):
        return jnp.logical_and(d >= self.early[0], d <= self.early[-1])

    def is_late(self, d):
        return jnp.logical_not(self.is_early(d))

    def is_enc_early(self, d):
        return jnp.logical_and(d >= self.enc_early[0], d <= self.enc_early[-1])

    def is_enc_late(self, d):
        return jnp.logical_not(self.is_enc_early(d))

    def rest_shift(self, at):
        return jnp.where(at < self.low, at, at - self.rest_from + self.rest_low)


def encoder_forward(
    field_ref, line_ref,
    lat_ref, *outs_and_scratch,
):
    saved, scratch = outs_and_scratch[:13], outs_and_scratch[13:]
    kept, local_sems, others = scratch[:13], scratch[13], scratch[14:]
    encoder_forward_body(field_ref, line_ref, lat_ref, saved, local_sems, *kept, *others)


def encoder_forward_body(
    field_ref, line_ref, lat_ref, saved, local_sems, flat, xhat_ref, rstd_ref, qkv_ref, p_h, p_l, o_ref, xhat2_ref, rstd2_ref, g_h, g_l, dg_ref, out_ref,
    win_h, win_l, wout_h, wout_l, wup_h, wup_l, wdn_h, wdn_l, wlin_h, wlin_l,
    x, wide, lat, head_ref, send, recv,
):
    here = (flat, xhat_ref, rstd_ref, qkv_ref, p_h, p_l, o_ref, xhat2_ref, rstd2_ref, g_h, g_l, dg_ref, out_ref)
    leaving = []

    def leave(*numbers):
        for n in numbers:
            one = pltpu.make_async_copy(here[n], saved[n], local_sems.at[n])
            one.start()
            leaving.append(one)

    g, s = lax.axis_index("group"), lax.axis_index("seq")
    seqs = lax.axis_size("seq")
    before, after = lax.rem(s + seqs - SAMPLES, seqs), lax.rem(s + SAMPLES, seqs)
    barrier = pltpu.get_barrier_semaphore()
    for other in (before, after):
        pl.semaphore_signal(barrier, inc=1, device_id=(g, other), device_id_type=MESH)
    pl.semaphore_wait(barrier, 2)
    halo = start_copy(field_ref.at[pl.ds(0, 3)], head_ref, (send, recv), 0, (g, before))
    amount = line_ref.shape[1] // LANES
    flat[0:amount, :] = line_ref[...].reshape(amount, LANES)
    leave(0)
    for pair, name in (((win_h, win_l), "in"), ((wout_h, wout_l), "out"), ((wup_h, wup_l), "up"), ((wdn_h, wdn_l), "down"), ((wlin_h, wlin_l), "lin")):
        width = ENC_MATS[name][1]

        def store(rows, c, v, pair=pair, width=width):
            last = min(width - c * LANES, LANES)
            put(pair, (rows, slice(c * LANES, c * LANES + last)), v[:, :last])

        unpack_matrix(flat, ENC_AT[name], ENC_MATS[name], store, wide)
    vec = {name: vector(flat, ENC_AT[name], amount) for name, amount in ENC_VECS.items()}
    masks = head_masks(CE)
    halo.wait()
    for r, at, start, amount in encoder_slots():
        x[at : at + amount, :] = (field_ref[r + 3, start : start + amount, :] if r < 3 else head_ref[r - 3, start : start + amount, :])
    wrapped = s // SAMPLES == seqs // SAMPLES - 1
    half = ROWS_E // 2
    upper = lax.broadcasted_iota(jnp.int32, (ROWS_E, ROWS_E), 0) >= half
    right = lax.broadcasted_iota(jnp.int32, (ROWS_E, ROWS_E), 1) >= half
    apart = jnp.where(jnp.logical_and(upper != right, wrapped), 1.0, 0.0)
    apart = jnp.concatenate([apart] * HEADS_E, 0)
    win, wout, wup, wdn, wlin = (win_h, win_l), (wout_h, wout_l), (wup_h, wup_l), (wdn_h, wdn_l), (wlin_h, wlin_l)
    scale = 1.0 / math.sqrt(HEAD)

    full = slice(None)
    xhat, rstd = normalize(x[...])
    xhat_ref[...] = xhat
    rstd_ref[...] = rstd
    xn = split(xhat * vec["g1"] + vec["s1"])
    for j, name in enumerate(("qb", None, "vb")):
        cols = slice(j * CE, (j + 1) * CE)
        one = dot3(xn, get(win, (full, cols)))
        if name is not None:
            one = one + vec[name]
        qkv_ref[:, cols] = one * scale if j == 0 else one
    leave(1, 2, 3)

    def step(i, carry):
        rows = pl.ds(pl.multiple_of(i * 2 * ROWS_E, 2 * ROWS_E), 2 * ROWS_E)
        qkv = qkv_ref[rows, :]
        parts = []
        for w in range(2):
            one = qkv[w * ROWS_E : (w + 1) * ROWS_E]
            q, k, v = (one[:, j * CE : (j + 1) * CE] for j in range(3))
            qm = split(jnp.concatenate([q * m for m in masks], 0))
            s = dot3(qm, split(k), 1, 1)
            s = jnp.where(apart > 0.5, NEG, s)
            p = split(softmax(s))
            p_h[i * 2 + w] = p[0]
            p_l[i * 2 + w] = p[1]
            parts.append(unstacked(dot3(p, split(v)), masks))
        o_ref[rows, :] = jnp.concatenate(parts, 0)
        return carry

    lax.fori_loop(0, 4, step, 0)
    leave(4, 5, 6)
    hidden = x[...] + dot3(split(o_ref[...]), get(wout, (full, full))) + vec["ob"]
    xhat2, rstd2 = normalize(hidden)
    xhat2_ref[...] = xhat2
    rstd2_ref[...] = rstd2
    leave(7, 8)
    hn = split(xhat2 * vec["g2"] + vec["s2"])
    out_ref[...] = hidden + vec["db"]
    for c in range(MLP_E // CHUNK):
        cols = slice(c * CHUNK, (c + 1) * CHUNK)
        u = dot3(hn, get(wup, (full, cols))) + vec["ub"][:, cols]
        one, slope = gelu_parts(u)
        dg_ref[:, cols] = slope
        one = split(one)
        g_h[:, cols] = one[0]
        g_l[:, cols] = one[1]
        out_ref[...] = out_ref[...] + deep3(one, get(wdn, (cols, full)))
    leave(9, 10, 11, 12)
    lat[...] = dot3(split(out_ref[...]), get(wlin, (full, full))) + vec["lb"]
    for r, at, start, amount in encoder_slots():
        lat_ref[r, start : start + amount, :] = lat[at : at + amount, :]
    for one in leaving:
        one.wait()


def vmem(*shape, dtype=F32):
    return pltpu.VMEM(shape, dtype)


def pair_of(*shape):
    return [vmem(*shape, dtype=BF16)] * 2


def call(kernel, name, inputs, outs, scratch, number, flops=0, far=(), far_outs=()):
    specs = [pl.BlockSpec(memory_space=pl.ANY if n in far else pltpu.VMEM) for n in range(len(inputs))]
    moved = sum(v.size * v.dtype.itemsize for v in list(inputs) + list(outs))
    return pl.pallas_call(
        kernel,
        name=name,
        out_shape=outs,
        in_specs=specs,
        out_specs=[pl.BlockSpec(memory_space=pl.ANY if n in far_outs else pltpu.VMEM) for n in range(len(outs))],
        scratch_shapes=scratch,
        cost_estimate=pl.CostEstimate(flops=flops, bytes_accessed=moved, transcendentals=0),
        compiler_params=pltpu.CompilerParams(collective_id=number, has_side_effects=True, vmem_limit_bytes=VMEM_BYTES),
    )(*inputs)


def sems(count):
    return [pltpu.SemaphoreType.DMA((count,)), pltpu.SemaphoreType.DMA((count,))]


def shape(*dims, dtype=F32):
    return jax.ShapeDtypeStruct(dims, dtype)


def encoder_forward_call(field, line, amount):
    n = 8 * ROWS_E
    outs = [
        shape(WIN_LAT, 96, CF), shape(amount, LANES), shape(n, CE), shape(n, 1), shape(n, 3 * CE),
        shape(8, HEADS_E * ROWS_E, ROWS_E, dtype=BF16), shape(8, HEADS_E * ROWS_E, ROWS_E, dtype=BF16),
        shape(n, CE), shape(n, CE), shape(n, 1), shape(n, MLP_E, dtype=BF16), shape(n, MLP_E, dtype=BF16),
        shape(n, MLP_E), shape(n, CE),
    ]
    scratch = (
        pair_of(CE, 3 * CE) + pair_of(CE, CE) + pair_of(CE, MLP_E) + pair_of(MLP_E, CE) + pair_of(CE, CF)
        + [vmem(n, CE), vmem(5, MLP_E, LANES), vmem(n, CF), vmem(3, 96, CE)] + sems(1)
    )
    scratch = [pltpu.VMEM(v.shape, v.dtype) for v in outs[1:]] + [pltpu.SemaphoreType.DMA((13,))] + scratch
    return call(
        encoder_forward, "encoder_forward", [field, line], outs, scratch, 0, 6 * n * 516096, (), tuple(range(1, 14))
    )


def encoder_backward(
    plan,
    dlat_ref, flat, rest, tab, early_a, early_b,
    xhat_ref, rstd_ref, qkv_far, ph_far, pl_far, o_ref, xhat2_ref, rstd2_ref, gh_far, gl_far, dg_far, out_ref,
    field_grad, fus_out, enc_out, tab_out,
    qkv_ref, p_h, p_l, g_h, g_l, dg_ref,
    grad, tabs, send, recv, local_sems, win_h, win_l, wout_h, wout_l, wup_h, wup_l, wdn_h, wdn_l, wlin_h, wlin_l,
    dlat, wide, dout, dout_h, dout_l, dhn, du_h, du_l, hn_h, hn_l, dh_h, dh_l, dqkv_h, dqkv_l, xn_h, xn_l, sums, dx, dback,
    *refs,
):
    loads = [
        pltpu.make_async_copy(src, dst, local_sems.at[n])
        for n, (src, dst) in enumerate(
            ((gh_far, g_h), (gl_far, g_l), (dg_far, dg_ref), (qkv_far, qkv_ref), (ph_far, p_h), (pl_far, p_l))
        )
    ]
    for one in loads:
        one.start()
    places = plan.places
    places.here()
    g, s = places.g, places.s
    seqs = places.sizes[1] * places.strides[1]
    before, after = lax.rem(s + seqs - SAMPLES, seqs), lax.rem(s + SAMPLES, seqs)
    slot, band = g * seqs + s, s // SAMPLES
    mine = g * SAMPLES + lax.rem(s, SAMPLES)
    owners = [((4 * band + j) // seqs, lax.rem(4 * band + j, seqs)) for j in range(4)]
    givers = [(k // 2, slot // 4 * SAMPLES + k % 2) for k in range(4)]

    def other(pg, ps):
        return jnp.logical_or(pg != g, ps != s)

    barrier = pltpu.get_barrier_semaphore()
    peers = [(g, before), (g, after)]
    for digit, size in enumerate(places.sizes):
        peers += [places.peer(digit, lax.rem(places.mine[digit] + k, size)) for k in range(1, size)]
    for peer in peers:
        pl.semaphore_signal(barrier, inc=1, device_id=peer, device_id_type=MESH)
    for pg, ps in owners + givers:
        @pl.when(other(pg, ps))
        def _(pg=pg, ps=ps):
            pl.semaphore_signal(barrier, inc=1, device_id=(pg, ps), device_id_type=MESH)
    pl.semaphore_wait(barrier, len(peers) + jnp.where(slot // 4 == band, 6, 8))

    refs = list(refs)
    base = 8
    early, late, encs = [], [], []
    for portion, held in zip(plan.fus, (early_a, early_b)):
        one = Stream(places, portion, plan.is_early, lambda at: at, (send, recv), base)
        arrived = {i: refs.pop(0) for i in range(1, len(portion.order))}
        early.append(one.buffers({1: held}, arrived).buffers({i + 1: arrived[i].at[0] for i in arrived}, {}))
        base += portion.semaphores()
    for group, portions, choices, shift in (
        (late, plan.late, [plan.is_late] * 3, plan.rest_shift),
        (encs, plan.enc, [plan.is_enc_early, plan.is_enc_late], lambda at: at),
    ):
        for portion, chosen in zip(portions, choices):
            one = Stream(places, portion, chosen, shift, (send, recv), base)
            held = {0: refs.pop(0)}
            arrived = {i: refs.pop(0) for i in range(len(portion.order))}
            group.append(one.buffers(held, arrived).buffers({i + 1: arrived[i].at[0] for i in arrived}, {}))
            base += portion.semaphores()

    def keep(one, split_at):
        def store(total):
            fus_out[split_at : split_at + one.rows, :] = total
        return store

    stages = len(plan.fus[0].order)

    def keep_enc(total):
        enc_out[...] = total

    def go(streams, i):
        for one in streams:
            if i == 0:
                one.finish_core(grad if one in encs else rest)
            else:
                last = keep_enc if one in encs else keep(one, one.first)
                one.finish(i - 1, last if i == len(one.order) else None)
            if i < len(one.order):
                one.start(i)

    for one in late:
        one.start_core(rest)
    for one in early:
        one.start(1)

    def give(j, pg, ps):
        return pltpu.make_async_remote_copy(
            src_ref=tab.at[j], dst_ref=tabs.at[mine], send_sem=send.at[4 + j], recv_sem=recv.at[4 + mine],
            device_id=(pg, ps), device_id_type=MESH,
        )

    for j, (pg, ps) in enumerate(owners):
        @pl.when(other(pg, ps))
        def _(j=j, pg=pg, ps=ps):
            give(j, pg, ps).start()

        @pl.when(jnp.logical_not(other(pg, ps)))
        def _(j=j):
            tabs[mine] = tab[j]

    win, wout, wup, wdn, wlin = (win_h, win_l), (wout_h, wout_l), (wup_h, wup_l), (wdn_h, wdn_l), (wlin_h, wlin_l)
    for pair, name in ((win, "in"), (wout, "out"), (wup, "up"), (wdn, "down"), (wlin, "lin")):
        width = ENC_MATS[name][1]

        def store(rows, c, v, pair=pair, width=width):
            last = min(width - c * LANES, LANES)
            put(pair, (rows, slice(c * LANES, c * LANES + last)), v[:, :last])

        unpack_matrix(flat, ENC_AT[name], ENC_MATS[name], store, wide)
    vec = {name: vector(flat, ENC_AT[name], ENC_VECS[name]) for name in ("g1", "s1", "g2", "s2")}
    masks = head_masks(CE)
    full = slice(None)
    scale = 1.0 / math.sqrt(HEAD)
    go(late, 0)
    for r, at, start, amount in encoder_slots():
        dlat[at : at + amount, :] = dlat_ref[r, start : start + amount, :]
    for one in loads[:3]:
        one.wait()
    dl = split(dlat[...])
    put_vector(grad, ENC_AT["lb"], column_sum(dlat[...]))
    d = dot3(dl, get(wlin, (full, full)), 1, 1)
    dout[...] = d
    put((dout_h, dout_l), (full, full), d)
    put_vector(grad, ENC_AT["db"], column_sum(d))
    dw = deep3(split(out_ref[...]), dl, 0, 0)
    for c in range(3):
        grad[pl.ds(ENC_AT["lin"] + c, CE, stride=3), :] = dw[:, c * LANES : (c + 1) * LANES]
    xhat2 = xhat2_ref[...]
    put((hn_h, hn_l), (full, full), xhat2 * vec["g2"] + vec["s2"])
    hn_t = left3((hn_h[...], hn_l[...]), 0).T
    do_t = left3((dout_h[...], dout_l[...]), 0).T
    for c in range(MLP_E // CHUNK):
        cols = slice(c * CHUNK, (c + 1) * CHUNK)
        do = (dout_h[...], dout_l[...])
        du = dot3(do, get(wdn, (cols, full)), 1, 1) * dg_ref[:, cols]
        put_vector(grad, ENC_AT["ub"] + c * CHUNK, column_sum(du))
        du = split(du)
        if c == 2:
            go(early, 2)
        part = deep3(du, get(wup, (full, cols)), 1, 1)
        dhn[...] = part if c == 0 else dhn[...] + part
        dw = dot(hn_t, right3(du))
        for t in range(2):
            grad[pl.ds(ENC_AT["up"] + 2 * c + t, CE, stride=6), :] = dw[:, t * LANES : (t + 1) * LANES]
        dw = dot(do_t, right3((g_h[:, cols], g_l[:, cols]))).T
        put_tiles(wide, slice(c * CHUNK, (c + 1) * CHUNK), dw)
    pack_matrix(grad, ENC_AT["down"], ENC_MATS["down"], wide)
    dv = dhn[...]
    put_vector(grad, ENC_AT["g2"], column_sum(dv * xhat2))
    put_vector(grad, ENC_AT["s2"], column_sum(dv))
    d = dout[...] + normalize_back(dv, xhat2, rstd2_ref[...], vec["g2"])
    dout[...] = d
    put((dh_h, dh_l), (full, full), d)
    put_vector(grad, ENC_AT["ob"], column_sum(d))
    dw = deep3(split(o_ref[...]), (dh_h[...], dh_l[...]), 0, 0)
    put_tiles(wide, slice(0, CE), dw)
    pack_matrix(grad, ENC_AT["out"], ENC_MATS["out"], wide)
    sums[...] = jnp.zeros_like(sums)
    encs[0].start_core(grad)
    for one in loads[3:]:
        one.wait()

    def step(i, carry):
        rows = pl.ds(pl.multiple_of(i * 2 * ROWS_E, 2 * ROWS_E), 2 * ROWS_E)
        do = dhn[rows, :]
        parts = []
        for w in range(2):
            one = qkv_ref[pl.ds(pl.multiple_of(i * 2 * ROWS_E, 2 * ROWS_E) + w * ROWS_E, ROWS_E), :]
            q, k, v = (one[:, j * CE : (j + 1) * CE] for j in range(3))
            dow = do[w * ROWS_E : (w + 1) * ROWS_E]
            dom = split(jnp.concatenate([dow * m for m in masks], 0))
            qm = split(jnp.concatenate([q * m for m in masks], 0))
            p = (p_h[i * 2 + w], p_l[i * 2 + w])
            dp = dot3(dom, split(v), 1, 1)
            pf = p[0].astype(F32) + p[1].astype(F32)
            t = pf * dp
            ds = split(t - pf * jnp.sum(t, 1, keepdims=True))
            dq = unstacked(dot3(ds, split(k)), masks) * scale
            dk = dot(left3(qm, 0).T, right3(ds)).T
            dvv = dot(left3(dom, 0).T, right3(p)).T
            parts.append(jnp.concatenate([dq, dk, dvv], 1))
        dqkv = jnp.concatenate(parts, 0)
        sums[0:1, :] = sums[0:1, :] + column_sum(dqkv)
        put((dqkv_h, dqkv_l), (rows, full), dqkv)
        return carry

    dhn[...] = dot3((dh_h[...], dh_l[...]), get(wout, (full, full)), 1, 1)
    lax.fori_loop(0, 2, step, 0)
    go(late, 1)
    go(encs[:1], 0)
    lax.fori_loop(2, 4, step, 0)
    go(late, 2)
    go(encs[:1], 1)
    xhat = xhat_ref[...]
    put((xn_h, xn_l), (full, full), xhat * vec["g1"] + vec["s1"])
    dxn = dot3((dqkv_h[...], dqkv_l[...]), get(win, (full, full)), 1, 1)
    sums[1:2, 0:CE] = column_sum(dxn * xhat)
    sums[2:3, 0:CE] = column_sum(dxn)
    put_vector(grad, ENC_AT["qb"], sums[0:1, 0:CE])
    put_vector(grad, ENC_AT["vb"], sums[0:1, 2 * CE : 3 * CE])
    put_vector(grad, ENC_AT["g1"], sums[1:2, 0:CE])
    put_vector(grad, ENC_AT["s1"], sums[2:3, 0:CE])
    dw = deep3((xn_h[...], xn_l[...]), (dqkv_h[...], dqkv_l[...]), 0, 0)
    put_tiles(wide, slice(0, CE), dw)
    pack_matrix(grad, ENC_AT["in"], ENC_MATS["in"], wide)
    encs[1].start_core(grad)
    dx[...] = dout[...] + normalize_back(dxn, xhat, rstd_ref[...], vec["g1"])
    for r, at, start, amount in encoder_slots():
        if r < 3:
            field_grad[r + 3, start : start + amount, :] = dx[at : at + amount, :]
        else:
            dback[r - 3, start : start + amount, :] = dx[at : at + amount, :]
    back = start_copy(dback, field_grad.at[pl.ds(0, 3)], (send, recv), 3, (g, after))
    go(encs[1:], 0)
    back.wait()
    for j, (pg, ps) in enumerate(owners):
        @pl.when(other(pg, ps))
        def _(j=j, pg=pg, ps=ps):
            give(j, pg, ps).wait_send()
    for k, (pg, ps) in enumerate(givers):
        @pl.when(other(pg, ps))
        def _(k=k, pg=pg, ps=ps):
            pltpu.make_async_remote_copy(
                src_ref=tab.at[0], dst_ref=tabs.at[k], send_sem=send.at[4], recv_sem=recv.at[4 + k],
                device_id=(pg, ps), device_id_type=MESH,
            ).wait_recv()
    tab_out[...] = (tabs[0] + tabs[1]) + (tabs[2] + tabs[3])
    for i in range(3, stages + 1):
        go(early, i)
    go(encs[1:], 1)
    for i in range(3, stages + 1):
        go(late, i)
    for i in range(2, len(encs[0].order) + 1):
        go(encs, i)


def encoder_backward_call(plan, dlat, flat, rest, tab, early_a, early_b, saved):
    n = 8 * ROWS_E
    refs, count = [], 8
    for portion in plan.fus:
        refs += [portion.scratch(i) for i in range(1, len(portion.order))]
        count += portion.semaphores()
    for portion in plan.late + plan.enc:
        refs += [portion.core_scratch()] + [portion.scratch(i) for i in range(len(portion.order))]
        count += portion.semaphores()
    xhat, rstd, qkv, p_h, p_l, o, xhat2, rstd2, g_h, g_l, dg, out = saved
    scratch = (
        [pltpu.VMEM(v.shape, v.dtype) for v in (qkv, p_h, p_l, g_h, g_l, dg)]
        + [vmem(plan.enc_all, LANES), vmem(*tab.shape)] + sems(count) + [pltpu.SemaphoreType.DMA((6,))]
        + pair_of(CE, 3 * CE) + pair_of(CE, CE) + pair_of(CE, MLP_E) + pair_of(MLP_E, CE) + pair_of(CE, CF)
        + [vmem(n, CF), vmem(5, MLP_E, LANES), vmem(n, CE)] + pair_of(n, CE) + [vmem(n, CE)] + pair_of(n, CHUNK)
        + pair_of(n, CE) + pair_of(n, CE) + pair_of(n, 3 * CE) + pair_of(n, CE) + [vmem(8, 3 * CE), vmem(n, CE), vmem(3, 96, CE)]
        + refs
    )
    return call(
        partial(encoder_backward, plan), "encoder_backward", [dlat, flat, rest, tab, early_a, early_b] + list(saved),
        [shape(WIN_LAT, 96, CE), shape(plan.fus_rows, LANES), shape(plan.enc_rows, LANES), shape(*tab.shape[1:])],
        scratch, 2, 12 * n * 516096, tuple(6 + j for j in (2, 3, 4, 8, 9, 10)),
    )


def merging(
    plan,
    lat_ref, cot_far, flat_ref, tab_ref, base_ref,
    out_ref, dlat_ref, rest_ref, dtab_ref, early_a, early_b,
    grad, cot_ref, core_a, core_b, first_a, first_b, fld_ref, send, recv, lines, bands, vectors, local_sems,
    win_h, win_l, wout_h, wout_l, wup_h, wup_l, wdn_h, wdn_l,
    bias, dbias, x, xhat1, rstd1, xn_h, xn_l, q_h, q_l, k_h, k_l, v_h, v_l, p_h, p_l, o_h, o_l,
    xhat2, rstd2, hn_h, hn_l, acc, dhn, dy, dy_h, dy_l, hn_t, dy_t, dh_h, dh_l, dqkv_h, dqkv_l, sums,
):
    win, wout, wup, wdn = (win_h, win_l), (wout_h, wout_l), (wup_h, wup_l), (wdn_h, wdn_l)
    full = slice(None)
    chunks = MLP_F // FCH
    g, s = lax.axis_index("group"), lax.axis_index("seq")
    seqs = lax.axis_size("seq")
    before, after = lax.rem(s + seqs - SAMPLES, seqs), lax.rem(s + SAMPLES, seqs)
    band = s // SAMPLES
    picked = pltpu.make_async_copy(tab_ref.at[:, pl.ds(pl.multiple_of(band // 8 * 8, 8), 8)], bands, local_sems.at[0])
    picked.start()
    loads = {}
    for n, name in enumerate(FUS_MATS):
        some = pl.ds(FUS_AT[name], math.prod(FUS_MATS[name]) // LANES)
        loads[name] = pltpu.make_async_copy(flat_ref.at[some], grad.at[some], local_sems.at[n + 1])
    at = FUS_AT["g1"] // LANES
    loads["g1"] = pltpu.make_async_copy(flat_ref.at[pl.ds(at, flat_ref.shape[0] - at)], vectors, local_sems.at[5])
    loads["cot"] = pltpu.make_async_copy(cot_far, cot_ref, local_sems.at[8])
    for one in loads.values():
        one.start()
    barrier = pltpu.get_barrier_semaphore()
    places = plan.places
    places.here()
    peers = [(1 - g, s), (g, before), (g, after), (1 - g, before), (1 - g, after)]
    for digit in (len(places.sizes) - 1, plan.fus[1].order[0]):
        size = places.sizes[digit]
        peers += [places.peer(digit, lax.rem(places.mine[digit] + k, size)) for k in range(1, size)]
    for peer in peers:
        pl.semaphore_signal(barrier, inc=1, device_id=peer, device_id_type=MESH)
    pl.semaphore_wait(barrier, len(peers))
    early, base = [], 6
    for portion, core, first, out in zip(plan.fus, (core_a, core_b), (first_a, first_b), (early_a, early_b)):
        early.append(Stream(places, portion, plan.is_early, lambda at: at, (send, recv), base).buffers({0: core, 1: out}, {0: first}))
        base += portion.semaphores()

    def half(one):
        return pl.ds(pl.multiple_of(one * 48, 48), 48)

    far = [
        start_copy(lat_ref.at[pl.ds(0, 3), half(1 - g)], fld_ref.at[g, pl.ds(3, 3)], (send, recv), 0, (1 - g, s)),
        start_copy(lat_ref.at[pl.ds(3, 3), half(g)], fld_ref.at[g, pl.ds(0, 3)], (send, recv), 1, (g, after)),
        start_copy(lat_ref.at[pl.ds(3, 3), half(1 - g)], fld_ref.at[g, pl.ds(0, 3)], (send, recv), 2, (1 - g, after)),
    ]
    far.append(pltpu.make_async_copy(lat_ref.at[pl.ds(0, 3), half(g)], fld_ref.at[g, pl.ds(3, 3)], local_sems.at[9]))
    far[-1].start()
    scale = 1.0 / math.sqrt(HEAD)

    def store(pair):
        def one(rows, c, v):
            put(pair, (rows, slice(c * LANES, (c + 1) * LANES)), v)
        return one

    def store_up(rows, c, v):
        put(wup, (c // (FCH // LANES), full, slice(c % (FCH // LANES) * LANES, (c % (FCH // LANES) + 1) * LANES)), v)

    def store_down(rows, c, v):
        for j in range(chunks):
            put(wdn, (j, full, slice(c * LANES, (c + 1) * LANES)), v[j * FCH : (j + 1) * FCH])

    loads["in"].wait()
    unpack_matrix(grad, FUS_AT["in"], FUS_MATS["in"], store(win), None)
    loads["out"].wait()
    unpack_matrix(grad, FUS_AT["out"], FUS_MATS["out"], store(wout), None)
    loads["up"].wait()
    unpack_matrix(grad, FUS_AT["up"], FUS_MATS["up"], store_up, None)
    loads["down"].wait()
    unpack_matrix(grad, FUS_AT["down"], FUS_MATS["down"], store_down, None)
    loads["g1"].wait()
    vec = {name: vector(vectors, FUS_AT[name] - FUS_AT["g1"], amount) for name, amount in FUS_VECS.items()}
    masks = head_masks(LANES)

    spots = jnp.where(lax.broadcasted_iota(jnp.int32, (TAB_PAD, 2 * LANES), 0) == base_ref[...], 1.0, 0.0).astype(BF16)
    picked.wait()
    for h in range(HEADS_F):
        lines[h : h + 1, :] = bands[h, pl.ds(lax.rem(band, 8), 1), :]
    pad = jnp.zeros((HEADS_F, TAB_PAD - PAIRS * SPAN), F32)
    table = []
    for z in range(WIN_MOD):
        for r in range(WIN_LAT):
            at = [((z * WIN_MOD + y) * WIN_LAT * WIN_LAT + r * WIN_LAT) * SPAN for y in range(WIN_MOD)]
            one = jnp.concatenate([lines[0:HEADS_F, t : t + WIN_LAT * SPAN] for t in at] + [pad], 1)
            table.append(jnp.concatenate([one, jnp.zeros((16 - HEADS_F, TAB_PAD), F32)], 0))
    table = jnp.concatenate(table, 0)
    for w in range(WIN_LON):
        turned = pltpu.roll(table, TAB_PAD - w, 1) if w else table
        hi, lo = split(turned)
        rest = (turned - hi.astype(F32) - lo.astype(F32)).astype(BF16)
        one = dot(hi, spots) + (dot(lo, spots) + dot(rest, spots))
        for n in range(PAIRS):
            for c in range(2):
                bias[c, pl.ds(n * WIN_LON + w, HEADS_F, stride=ROWS_F), :] = one[n * 16 : n * 16 + HEADS_F, c * LANES : (c + 1) * LANES]
    dbias[...] = jnp.zeros_like(dbias)

    loads["cot"].wait()
    for z, r, at, start in merging_slots():
        dy[at : at + WIN_LON, :] = cot_ref[z, r, start : start + WIN_LON, :]
    put((dy_h, dy_l), (full, full), dy[...])
    dy_t[...] = left3((dy_h[...], dy_l[...]), 0).T
    sums[10:11, 0:CF] = column_sum(dy[...])
    for one in far:
        one.wait()
    for z, r, at, start in merging_slots():
        x[at : at + WIN_LON, :] = fld_ref[z, r, start : start + WIN_LON, :]

    def rows_of(i):
        return pl.ds(pl.multiple_of(i * ROWS_F, ROWS_F), ROWS_F)

    xhat, rstd = normalize(x[...])
    xhat1[...] = xhat
    rstd1[...] = rstd
    put((xn_h, xn_l), (full, full), xhat * vec["g1"] + vec["s1"])
    for j, (pair, shift) in enumerate((((q_h, q_l), vec["qb"]), ((k_h, k_l), None), ((v_h, v_l), vec["vb"]))):
        one = deep3((xn_h[...], xn_l[...]), get(win, (full, slice(j * CF, (j + 1) * CF))))
        if shift is not None:
            one = one + shift
        if j == 0:
            one = one * scale
        put(pair, (full, full), one)

    def forward(i, carry):
        rows = rows_of(i)
        for b in range(3):
            cols = slice(b * LANES, (b + 1) * LANES)
            qm = stacked((q_h[rows, cols], q_l[rows, cols]), masks)
            some = slice(b * 4 * ROWS_F, (b + 1) * 4 * ROWS_F)
            s = deep3(qm, (k_h[rows, cols], k_l[rows, cols]), 1, 1) + get_tiles(bias, some, ROWS_F)
            p = split(softmax(s))
            p_h[i * 3 + b] = p[0]
            p_l[i * 3 + b] = p[1]
            o = unstacked(wide_n(p, (v_h[rows, cols], v_l[rows, cols])), masks)
            put((o_h, o_l), (rows, cols), o)
        return carry

    lax.fori_loop(0, 4, forward, 0)
    hidden = x[...] + deep3((o_h[...], o_l[...]), get(wout, (full, full))) + vec["ob"]
    xh2, rstd = normalize(hidden)
    xhat2[...] = xh2
    rstd2[...] = rstd
    put((hn_h, hn_l), (full, full), xh2 * vec["g2"] + vec["s2"])
    acc[...] = hidden + vec["db"]
    dhn[...] = jnp.zeros_like(dhn)
    hn_t[...] = left3((hn_h[...], hn_l[...]), 0).T
    for c in range(chunks):
        sums[8:9, c * FCH : (c + 1) * FCH] = vec["ub"][:, c * FCH : (c + 1) * FCH]

    def feed(c, carry):
        up = (wup_h[c], wup_l[c])
        down = (wdn_h[c], wdn_l[c])
        cols = pl.ds(pl.multiple_of(c * FCH, FCH), FCH)
        shift = sums[8:9, cols]

        u = deep3((hn_h[...], hn_l[...]), up) + shift
        gl, slope = gelu_parts(u)
        gl = split(gl)
        acc[...] = acc[...] + deep3(gl, down)
        du = deep3((dy_h[...], dy_l[...]), down, 1, 1) * slope
        sums[9:10, cols] = column_sum(du)
        du = split(du)
        dhn[...] = dhn[...] + deep3(du, up, 1, 1)
        dw = dot(hn_t[...], right3(du))
        for t in range(FCH // LANES):
            grad[pl.ds(FUS_AT["up"] + FCH // LANES * c + t, CF, stride=12), :] = dw[:, t * LANES : (t + 1) * LANES]
        dw = dot(dy_t[...], right3(gl)).T
        for t in range(3):
            grad[pl.ds(FUS_AT["down"] + 3 * FCH * c + t, FCH, stride=3), :] = dw[:, t * LANES : (t + 1) * LANES]
        return carry

    lax.fori_loop(0, chunks, feed, 0)
    put_vector(grad, FUS_AT["ub"], sums[9:10, :])
    sums[0:8, :] = jnp.zeros((8, MLP_F), F32)

    dv = dhn[...]
    sums[0:1, 0:CF] = sums[10:11, 0:CF]
    sums[1:2, 0:CF] = column_sum(dv * xhat2[...])
    sums[2:3, 0:CF] = column_sum(dv)
    dh = dy[...] + normalize_back(dv, xhat2[...], rstd2[...], vec["g2"])
    sums[3:4, 0:CF] = column_sum(dh)
    dy[...] = dh
    put((dh_h, dh_l), (full, full), dh)
    dw = dot3((o_h[...], o_l[...]), (dh_h[...], dh_l[...]), 0, 0)
    for t in range(3):
        grad[pl.ds(FUS_AT["out"] + t, CF, stride=3), :] = dw[:, t * LANES : (t + 1) * LANES]
    for one in early:
        one.start_core(grad)
    do_h, do_l = hn_h, hn_l
    put((do_h, do_l), (full, full), deep3((dh_h[...], dh_l[...]), get(wout, (full, full)), 1, 1))


    def backward(i, carry):
        rows = rows_of(i)
        for b in range(3):
            cols = slice(b * LANES, (b + 1) * LANES)
            dom = stacked((do_h[rows, cols], do_l[rows, cols]), masks)
            qm = stacked((q_h[rows, cols], q_l[rows, cols]), masks)
            p = (p_h[i * 3 + b], p_l[i * 3 + b])
            dp = deep3(dom, (v_h[rows, cols], v_l[rows, cols]), 1, 1)
            pf = p[0].astype(F32) + p[1].astype(F32)
            t = pf * dp
            ds = t - pf * jnp.sum(t, 1, keepdims=True)
            some = slice(b * 4 * ROWS_F, (b + 1) * 4 * ROWS_F)
            for c in range(2):
                one = ds[:, c * LANES : (c + 1) * LANES]
                dbias[c, some, 0 : one.shape[1]] = dbias[c, some, 0 : one.shape[1]] + one
            ds = split(ds)
            dq = unstacked(wide_n(ds, (k_h[rows, cols], k_l[rows, cols])), masks) * scale
            dk = dot(left3(qm, 0).T, right3(ds)).T
            dvv = dot(left3(dom, 0).T, right3(p)).T
            for j, one in enumerate((dq, dk, dvv)):
                at = slice(j * CF + b * LANES, j * CF + (b + 1) * LANES)
                put((dqkv_h, dqkv_l), (rows, at), one)
                if j != 1:
                    sums[4 + j // 2 : 5 + j // 2, cols] = sums[4 + j // 2 : 5 + j // 2, cols] + column_sum(one)
        return carry

    for one in early:
        one.finish_core(grad)
        one.start(0)
    lax.fori_loop(0, 4, backward, 0)
    dxn = deep3((dqkv_h[...], dqkv_l[...]), get(win, (full, full)), 1, 1)
    sums[6:7, 0:CF] = column_sum(dxn * xhat1[...])
    sums[7:8, 0:CF] = column_sum(dxn)
    x[...] = dy[...] + normalize_back(dxn, xhat1[...], rstd1[...], vec["g1"])
    dx_ref = fld_ref
    for z, r, at, start in merging_slots():
        dx_ref[z, r, start : start + WIN_LON, :] = x[at : at + WIN_LON, :]
    back = [
        start_copy(dx_ref.at[1 - g, pl.ds(3, 3)], dlat_ref.at[pl.ds(0, 3), half(g)], (send, recv), 3, (1 - g, s)),
        start_copy(dx_ref.at[g, pl.ds(0, 3)], dlat_ref.at[pl.ds(3, 3), half(g)], (send, recv), 4, (g, before)),
        start_copy(dx_ref.at[1 - g, pl.ds(0, 3)], dlat_ref.at[pl.ds(3, 3), half(g)], (send, recv), 5, (1 - g, before)),
    ]
    dlat_ref[0:3, half(g), :] = dx_ref[g, 3:6]
    for j, name in enumerate(("db", "g2", "s2", "ob", "qb", "vb", "g1", "s1")):
        put_vector(grad, FUS_AT[name], sums[j : j + 1, 0:CF])
    for c in range(3):
        cols = slice(c * CF, (c + 1) * CF)
        dw = dot3((xn_h[...], xn_l[...]), (dqkv_h[:, cols], dqkv_l[:, cols]), 0, 0)
        for t in range(3):
            grad[pl.ds(FUS_AT["in"] + 3 * c + t, CF, stride=9), :] = dw[:, t * LANES : (t + 1) * LANES]
    rest = [
        pltpu.make_async_copy(grad.at[pl.ds(0, plan.rest_low)], rest_ref.at[pl.ds(0, plan.rest_low)], local_sems.at[6]),
        pltpu.make_async_copy(
            grad.at[pl.ds(plan.rest_from, plan.rest_all - plan.rest_low)],
            rest_ref.at[pl.ds(plan.rest_low, plan.rest_all - plan.rest_low)], local_sems.at[7],
        ),
    ]
    for one in rest:
        one.start()
    for one in early:
        one.finish(0)
    total = jnp.zeros((PAIRS * 16, TAB_PAD), F32)
    blank = jnp.zeros((16 - HEADS_F, 2 * LANES), F32)
    for w in range(WIN_LON):
        rows = []
        for n in range(PAIRS):
            rows.append(jnp.concatenate([dbias[c, pl.ds(n * WIN_LON + w, HEADS_F, stride=ROWS_F), :] for c in range(2)], 1))
            rows.append(blank)
        hi, lo = split(jnp.concatenate(rows, 0))
        one = dot(hi, spots, 1, 1) + dot(lo, spots, 1, 1)
        total = total + (pltpu.roll(one, w, 1) if w else one)
    for z in range(WIN_MOD):
        for r in range(WIN_LAT):
            n = z * WIN_LAT + r
            for y in range(WIN_MOD):
                at = ((z * WIN_MOD + y) * WIN_LAT * WIN_LAT + r * WIN_LAT) * SPAN
                lines[0:HEADS_F, at : at + WIN_LAT * SPAN] = total[n * 16 : n * 16 + HEADS_F, y * WIN_LAT * SPAN : (y + 1) * WIN_LAT * SPAN]
    for j in range(4):
        dtab_ref[j, 0:3, :] = lines[3 * j : 3 * j + 3, :]
    for z, r, at, start in merging_slots():
        out_ref[z, r, start : start + WIN_LON, :] = acc[at : at + WIN_LON, :]
    for one in back + rest:
        one.wait()


def merging_call(plan, latent, cotangent, flat, table):
    n = 4 * ROWS_F
    m = HEADS_F * ROWS_F
    t = np.arange(ROWS_F)
    base = np.full((1, 2 * LANES), -1, np.int32)
    base[0, :ROWS_F] = t // WIN_LON * SPAN + WIN_LON - 1 - t % WIN_LON
    base = jnp.asarray(base)
    scratch = (
        [vmem(plan.fus_all, LANES), vmem(*cotangent.shape)]
        + [portion.core_scratch() for portion in plan.fus] + [portion.scratch(0) for portion in plan.fus]
        + [vmem(*cotangent.shape)] + sems(6 + sum(portion.semaphores() for portion in plan.fus)) + [vmem(16, table.shape[2]), vmem(HEADS_F, 8, table.shape[2]), vmem(flat.shape[0] - FUS_AT["g1"] // LANES, LANES), pltpu.SemaphoreType.DMA((10,))] + pair_of(CF, 3 * CF) + pair_of(CF, CF) + pair_of(MLP_F // FCH, CF, FCH) + pair_of(MLP_F // FCH, FCH, CF)
        + [vmem(2, m, LANES), vmem(2, m, LANES), vmem(n, CF), vmem(n, CF), vmem(n, 1)]
        + pair_of(n, CF) + pair_of(n, CF) + pair_of(n, CF) + pair_of(n, CF) + pair_of(12, 4 * ROWS_F, ROWS_F) + pair_of(n, CF)
        + [vmem(n, CF), vmem(n, 1)] + pair_of(n, CF) + [vmem(n, CF), vmem(n, CF), vmem(n, CF)] + pair_of(n, CF)
        + [vmem(CF, 3 * n, dtype=BF16)] * 2 + pair_of(n, CF) + pair_of(n, 3 * CF) + [vmem(16, MLP_F)]
    )
    outs = [shape(*cotangent.shape), shape(*latent.shape), shape(plan.rest_all, LANES), shape(4, 3, table.shape[2])]
    outs += [shape(portion.blocks(0), portion.rows, LANES) for portion in plan.fus]
    return call(partial(merging, plan), "merging", [latent, cotangent, flat, table, base], outs, scratch, 1, 18 * n * 1769472, (0, 1, 2, 3), (2,))


def update(params, grads, momentum, average, rate):
    momentum_new = MOMENTUM_DECAY * momentum + grads
    params_new = params - rate * (grads + MOMENTUM_DECAY * momentum_new)
    average_new = AVERAGE_DECAY * average + (1.0 - AVERAGE_DECAY) * params_new
    return (params_new, momentum_new, average_new)


def shifted_piece(block, rows, at, piece):
    amount = -(-piece // LANES)
    first, lane = at // LANES, lax.rem(at, LANES)
    rows[0 : block.shape[0], :] = pltpu.roll(block[...], LANES - lane, 1)
    low = lax.broadcasted_iota(jnp.int32, (1, LANES), 1) < LANES - lane
    return jnp.where(low, rows[pl.ds(first, amount), :], rows[pl.ds(first + 1, amount), :])


def optimizer(
    rates, fus_start, enc_start,
    merged_in, field_in, fus_block, fus_flat, fus_mom, fus_avg, enc_block, enc_flat, enc_mom, enc_avg, tab_block, table, tab_mom, tab_avg,
    merged, field, enc_grad, enc_new, enc_mom_new, enc_avg_new, fus_grad, fus_new, fus_mom_new, fus_avg_new,
    tab_grad, tab_new, tab_mom_new, tab_avg_new,
    fus_own, enc_own, tab_own, rows, sems,
):
    g, s = lax.axis_index("group"), lax.axis_index("seq")
    slot = g * lax.axis_size("seq") + s
    band, part = slot // 4, lax.rem(slot, 4)
    fus_piece, enc_piece = fus_mom.shape[0], enc_mom.shape[1]
    fus_from = pl.multiple_of(jnp.minimum(fus_start(slot), fus_flat.shape[0] - fus_own.shape[0]), 8)
    enc_from = enc_start(s)
    copies = [
        pltpu.make_async_copy(fus_flat.at[pl.ds(fus_from, fus_own.shape[0])], fus_own, sems.at[0]),
        pltpu.make_async_copy(enc_flat.at[pl.ds(enc_from, enc_own.shape[0])], enc_own, sems.at[1]),
        pltpu.make_async_copy(table.at[pl.ds(3 * part, 3), pl.ds(pl.multiple_of(band // 8 * 8, 8), 8)], tab_own, sems.at[2]),
        pltpu.make_async_copy(merged_in, merged, sems.at[3]),
        pltpu.make_async_copy(field_in, field, sems.at[4]),
    ]
    for one in copies:
        one.start()

    def store(outs, values):
        for ref, value in zip(outs, values):
            ref[...] = value

    def step(own, grads, mom, avg, rate, outs):
        new, mom_new, avg_new = update(own, grads, mom[...], avg[...], rate)
        store(outs, (grads, new, mom_new, avg_new))

    fus_at = fus_piece * slot
    grads = shifted_piece(fus_block, rows, fus_at - fus_start(slot) * LANES, fus_piece).reshape(-1)[:fus_piece]
    copies[0].wait()
    own = shifted_piece(fus_own, rows, fus_at - fus_from * LANES, fus_piece).reshape(-1)[:fus_piece]
    step(own, grads, fus_mom, fus_avg, rates[1], (fus_grad, fus_new, fus_mom_new, fus_avg_new))
    enc_at = enc_piece * s - enc_from * LANES
    grads = shifted_piece(enc_block, rows, enc_at, enc_piece).reshape(1, -1)[:, :enc_piece]
    copies[1].wait()
    own = shifted_piece(enc_own, rows, enc_at, enc_piece).reshape(1, -1)[:, :enc_piece]
    step(own, grads, enc_mom, enc_avg, rates[0], (enc_grad, enc_new, enc_mom_new, enc_avg_new))
    grads = jnp.concatenate([tab_block[j : j + 1, :] for j in range(3)], 1).reshape(-1)
    copies[2].wait()
    own = jnp.concatenate([tab_own[j, pl.ds(lax.rem(band, 8), 1), :] for j in range(3)], 1).reshape(-1)
    step(own, grads, tab_mom, tab_avg, rates[2], (tab_grad, tab_new, tab_mom_new, tab_avg_new))
    for one in copies[3:]:
        one.wait()


def optimizer_call(plan, rates, merged, field, fus_block, fus_flat, fus_mom, fus_avg, enc_block, enc_flat, enc_mom, enc_avg, tab_block, table, tab_mom, tab_avg):
    inputs = [merged, field, fus_block, fus_flat, fus_mom, fus_avg, enc_block, enc_flat, enc_mom, enc_avg, tab_block, table, tab_mom, tab_avg]
    outs = [merged, field] + [enc_mom] * 4 + [fus_mom] * 4 + [tab_mom] * 4
    far, far_outs = (0, 1, 3, 7, 11), ()
    fus_rows = plan.fus_rows + fus_flat.shape[0] % 8
    return pl.pallas_call(
        partial(optimizer, rates, partial(window_start, fus_mom.size), partial(window_start, enc_mom.size)),
        name="optimizer",
        out_shape=[shape(*v.shape) for v in outs],
        in_specs=[pl.BlockSpec(memory_space=pl.ANY if n in far else pltpu.VMEM) for n in range(len(inputs))],
        out_specs=[pl.BlockSpec(memory_space=pl.ANY if n in far_outs else pltpu.VMEM) for n in range(len(outs))],
        scratch_shapes=[
            vmem(fus_rows, LANES), vmem(plan.enc_rows, LANES), vmem(3, 8, table.shape[2]),
            vmem(fus_rows + 16, LANES), pltpu.SemaphoreType.DMA((5,)),
        ],
        compiler_params=pltpu.CompilerParams(vmem_limit_bytes=VMEM_BYTES),
    )(*inputs)


def shards(
    tokens,
    cotangent,
    enc_params,
    enc_momentum,
    enc_average,
    fus_params,
    fus_momentum,
    fus_average,
    earth_bias,
    bias_momentum,
    bias_average,
):
    field = tokens[0, 0]
    row_count, col_count, feat_width = field.shape
    seq_count = lax.axis_size("seq")
    group_count = lax.axis_size("group")
    band_count = seq_count // SAMPLES
    fus_flat = fus_params.reshape(-1, LANES)
    plan = Sums(group_count, seq_count, fus_params.size, enc_params.size)
    latent, enc_flat, *saved = encoder_forward_call(field, enc_params, plan.enc_all)
    table = earth_bias.transpose(1, 0, 2)
    merged, latent_grad, rest, table_grad, early_a, early_b = merging_call(plan, latent, cotangent[:, 0, 0], fus_flat, table)
    field_grad, fus_block, enc_block, tab_block = encoder_backward_call(
        plan, latent_grad, enc_flat, rest, table_grad, early_a, early_b, saved
    )
    lat_total = seq_count // SAMPLES * row_count
    rates = (
        1.0 / math.sqrt(CE * SAMPLES * lat_total * col_count),
        1.0 / math.sqrt(CF * group_count * SAMPLES * lat_total * col_count),
        2.0 / math.sqrt(SAMPLES * col_count / WIN_LON),
    )
    merged, field_grad, *others = optimizer_call(
        plan, rates, merged, field_grad, fus_block, fus_flat, fus_momentum, fus_average, enc_block, enc_flat,
        enc_momentum, enc_average, tab_block, table, bias_momentum, bias_average,
    )
    return (merged[:, None, None], field_grad[None, None], *others)


def solution(mesh):
    both = P(("group", "seq"))
    rows = P("group", "seq")
    merged = P(None, "seq", "group", None, None, None)
    tokens = P("group", "seq", None, None, None)
    return jax.shard_map(
        shards,
        mesh=mesh,
        in_specs=(tokens, merged, P("group", None), rows, rows, P(), both, both, P(), both, both),
        out_specs=(merged, tokens, rows, rows, rows, rows) + (both,) * 8,
        check_vma=False,
    )
```
